32 devices in a mesh: seq: 4 (over x, core), fsdp: 8 (over z, y).
Axes of the slice: x: 2, y: 2, z: 4, core: 2. Of those that a mesh axis runs over, the one named last changes fastest.
Arguments:
- tokens: bfloat16 [2, 8, 1024, 1024], P(None, 'fsdp', 'seq'), may hold values from -6 to 6
- positions: int32 [2, 8, 1024], P(None, 'fsdp'), may hold values from 0 to 1023, as said below
- input_gain: bfloat16 [1024], P(('seq', 'fsdp')), may hold values from 0.5 to 1.5
- post_gain: bfloat16 [1024], P(('seq', 'fsdp')), may hold values from 0.5 to 1.5
- query_gain: bfloat16 [128], P(('seq', 'fsdp')), may hold values from 0.5 to 1.5
- key_gain: bfloat16 [128], P(('seq', 'fsdp')), may hold values from 0.5 to 1.5
- w_query: bfloat16 [1024, 2048], P(('seq', 'fsdp')), may hold values from -0.1875 to 0.1875
- w_key: bfloat16 [1024, 1024], P(('seq', 'fsdp')), may hold values from -0.1875 to 0.1875
- w_value: bfloat16 [1024, 1024], P(('seq', 'fsdp')), may hold values from -0.1875 to 0.1875
- w_out: bfloat16 [2048, 1024], P(('seq', 'fsdp')), may hold values from -1.5 to 1.5
- w_gate: bfloat16 [1024, 3072], P(('seq', 'fsdp')), may hold values from -0.1875 to 0.1875
- w_up: bfloat16 [1024, 3072], P(('seq', 'fsdp')), may hold values from -0.1875 to 0.1875
- w_down: bfloat16 [3072, 1024], P(('seq', 'fsdp')), may hold values from -0.109375 to 0.109375
- cotangent: bfloat16 [2, 8, 1024, 1024], P(None, 'fsdp', 'seq'), may hold values from -6 to 6
Outputs:
- block_out: bfloat16 [2, 8, 1024, 1024], P(None, 'fsdp', 'seq')
- tokens_grad: float32 [2, 8, 1024, 1024], P(None, 'fsdp', 'seq')
- input_gain_grad: float32 [1024], P(('seq', 'fsdp'))
- post_gain_grad: float32 [1024], P(('seq', 'fsdp'))
- query_gain_grad: float32 [128], P(('seq', 'fsdp'))
- key_gain_grad: float32 [128], P(('seq', 'fsdp'))
- w_query_grad: float32 [1024, 2048], P(('seq', 'fsdp'))
- w_key_grad: float32 [1024, 1024], P(('seq', 'fsdp'))
- w_value_grad: float32 [1024, 1024], P(('seq', 'fsdp'))
- w_out_grad: float32 [2048, 1024], P(('seq', 'fsdp'))
- w_gate_grad: float32 [1024, 3072], P(('seq', 'fsdp'))
- w_up_grad: float32 [1024, 3072], P(('seq', 'fsdp'))
- w_down_grad: float32 [3072, 1024], P(('seq', 'fsdp'))
The draws below stay inside these ranges and needn't reach their ends.
Inputs may be any that keep to these rules, and one draw needn't show every extreme that they name: In each sequence the positions are a permutation of 0 to 1023 made of runs of 128 consecutive positions, each run starting at a multiple of 128; the order of the runs is drawn at random for each sequence.
All inputs are finite; a program needn't handle non-finite values.
Results may differ from the reference program's by a relative error of at most 0.02.
Values may be sent and summed in bfloat16 or wider, within the bound.
A program may use at most 160 MiB of HBM per device.

```python
import jax
import jax.numpy as jnp
from jax import lax

D = 1024
HEADS = 16
KV_HEADS = 8
HEAD_DIM = 128
FF = 3072
MB = 2
SEQ_LEN = 1024
SPAN = 128
GROUPS = 8


def draw_positions(key, part):
    runs = SEQ_LEN // SPAN
    streams = jax.random.split(key, MB * GROUPS)
    orders = jax.vmap(lambda single: jax.random.permutation(single, runs))(streams)
    within = jnp.arange(SPAN, dtype=jnp.int32)
    spots = orders.astype(jnp.int32)[:, :, None] * SPAN + within[None, None, :]
    return spots.reshape(MB, GROUPS, SEQ_LEN).astype(jnp.int32)


def steps_of(key, dims, pieces, least, largest):
    def one(axis_at, parts):
        draws = jax.random.uniform(jax.random.fold_in(jax.random.fold_in(key, 6), axis_at), (parts,), jnp.float32, least / len(pieces), largest / len(pieces))
        return jnp.repeat(jnp.exp(draws), dims[axis_at] // parts).reshape((-1,) + (1,) * (len(dims) - axis_at - 1))

    loudness = one(*pieces[0])
    for cut in pieces[1:]:
        loudness = loudness * one(*cut)
    return loudness


def scatter_about(stream_key, extent, deviation, bound, shards=(), kind=jnp.bfloat16):
    values = jax.random.normal(stream_key, extent, jnp.float32) * deviation
    if len(shards) > 0:
        values = steps_of(stream_key, extent, shards, -0.22, 0.18) * values
    return jnp.clip(values, min=-bound, max=bound).astype(kind)


def setup_inputs(seed: int = 0) -> dict:
    streams_of = jax.random.split(jax.random.key(seed), 15)
    return {
        "tokens": scatter_about(streams_of[0], (MB, GROUPS, SEQ_LEN, D), 1.0, 6.0, ((1, 8), (2, 4))),
        "positions": draw_positions(jax.random.fold_in(streams_of[14], 71), 0),
        "input_gain": jnp.clip(1.0 + 0.1 * jax.random.normal(streams_of[2], (D,), jnp.float32), 0.5, 1.5).astype(jnp.bfloat16),
        "post_gain": jnp.clip(1.0 + 0.1 * jax.random.normal(streams_of[3], (D,), jnp.float32), 0.5, 1.5).astype(jnp.bfloat16),
        "query_gain": jnp.clip(1.0 + 0.1 * jax.random.normal(streams_of[4], (HEAD_DIM,), jnp.float32), 0.5, 1.5).astype(jnp.bfloat16),
        "key_gain": jnp.clip(1.0 + 0.1 * jax.random.normal(streams_of[5], (HEAD_DIM,), jnp.float32), 0.5, 1.5).astype(jnp.bfloat16),
        "w_query": scatter_about(streams_of[6], (D, HEADS * HEAD_DIM), D ** -0.5, 0.1875, ((0, 32),)),
        "w_key": scatter_about(streams_of[7], (D, KV_HEADS * HEAD_DIM), D ** -0.5, 0.1875, ((0, 32),)),
        "w_value": scatter_about(streams_of[8], (D, KV_HEADS * HEAD_DIM), D ** -0.5, 0.1875, ((0, 32),)),
        "w_out": scatter_about(streams_of[9], (HEADS * HEAD_DIM, D), 16 ** -0.5, 1.5, ((0, 32),)),
        "w_gate": scatter_about(streams_of[10], (D, FF), D ** -0.5, 0.1875, ((0, 32),)),
        "w_up": scatter_about(streams_of[11], (D, FF), D ** -0.5, 0.1875, ((0, 32),)),
        "w_down": scatter_about(streams_of[12], (FF, D), FF ** -0.5, 0.109375, ((0, 32),)),
        "cotangent": scatter_about(streams_of[13], (MB, GROUPS, SEQ_LEN, D), 1.0, 6.0, ((1, 8), (2, 4))),
    }


EPSILON = 1e-06
ROPE_BASE = 1000000.0
NEGATIVE = -1e+30

@jax.custom_vjp
def low(v):
    return lax.optimization_barrier(v.astype(jnp.bfloat16)).astype(jnp.float32)

@jax.custom_vjp
def low_back(v):
    return v

def low_keep(v):
    return (low(v), None)

def low_pass(kept, grad):
    return (grad,)

def back_keep(v):
    return (v, None)

def back_low(kept, grad):
    return (low(grad),)
low.defvjp(low_keep, low_pass)
low_back.defvjp(back_keep, back_low)

def high_dot(left, right):
    return jnp.dot(left, right, precision=lax.Precision.HIGHEST, preferred_element_type=jnp.float32)

def inverse_root(values):
    return lax.rsqrt(lax.optimization_barrier(jnp.mean(values * values, axis=-1, keepdims=True)) + EPSILON)

def rope_tables(token_pos):
    half_width = HEAD_DIM // 2
    frequency = ROPE_BASE ** (-(jnp.arange(half_width, dtype=jnp.float32) * 2.0 / HEAD_DIM))
    angles = token_pos.astype(jnp.float32)[:, None] * frequency[None, :]
    cosine = jnp.cos(angles)
    sine = jnp.sin(angles)
    return (jnp.concatenate([cosine, cosine], axis=-1)[:, None, :], jnp.concatenate([sine, sine], axis=-1)[:, None, :])

def rotate(values, cosine, sine):
    half_width = values.shape[-1] // 2
    turned = jnp.concatenate([-values[..., half_width:], values[..., :half_width]], axis=-1)
    return values * cosine + turned * sine

def attend_heads(queries, keys, values, token_pos):
    length = queries.shape[0]
    group = HEADS // KV_HEADS
    allowed = token_pos[None, :] <= token_pos[:, None]

    def one_head(item):
        query_group, key_head, value_head = item
        raw = jnp.einsum('qgd,kd->gqk', query_group, key_head, precision=lax.Precision.HIGHEST) * HEAD_DIM ** (-0.5)
        scores = jnp.where(allowed[None], low_back(raw), NEGATIVE)
        soft = low(jax.nn.softmax(scores, axis=-1))
        return jnp.einsum('gqk,kd->qgd', soft, value_head, precision=lax.Precision.HIGHEST)
    query_heads = queries.reshape(length, KV_HEADS, group, HEAD_DIM).transpose(1, 0, 2, 3)
    key_heads = keys.transpose(1, 0, 2)
    value_heads = values.transpose(1, 0, 2)
    mixed = lax.map(jax.checkpoint(one_head), (query_heads, key_heads, value_heads))
    return mixed.transpose(1, 0, 2, 3).reshape(length, HEADS * HEAD_DIM)

def forward(sequence, token_pos, params):
    input_gain, post_gain, query_gain, key_gain, w_query, w_key, w_value, w_out, w_gate, w_up, w_down = params
    length = sequence.shape[0]
    cosine, sine = rope_tables(token_pos)
    normed = low(sequence * inverse_root(sequence) * input_gain)
    q_raw = low_back(high_dot(normed, w_query)).reshape(length, HEADS, HEAD_DIM)
    k_raw = low_back(high_dot(normed, w_key)).reshape(length, KV_HEADS, HEAD_DIM)
    values = low(low_back(high_dot(normed, w_value))).reshape(length, KV_HEADS, HEAD_DIM)
    queries = low(rotate(q_raw * inverse_root(q_raw) * query_gain, cosine, sine))
    keys = low(rotate(k_raw * inverse_root(k_raw) * key_gain, cosine, sine))
    mixed = low(low_back(attend_heads(queries, keys, values, token_pos)))
    resid = sequence + low_back(high_dot(mixed, w_out))
    post = low(resid * inverse_root(resid) * post_gain)
    gate = low_back(high_dot(post, w_gate))
    upper = low_back(high_dot(post, w_up))
    hidden = low(jax.nn.silu(gate) * upper)
    return resid + low_back(high_dot(hidden, w_down))

def reference(tokens, positions, input_gain, post_gain, query_gain, key_gain, w_query, w_key, w_value, w_out, w_gate, w_up, w_down, cotangent):
    params = tuple((item.astype(jnp.float32) for item in (input_gain, post_gain, query_gain, key_gain, w_query, w_key, w_value, w_out, w_gate, w_up, w_down)))
    sequences = tokens.astype(jnp.float32).reshape(MB * GROUPS, SEQ_LEN, D)
    places = positions.reshape(MB * GROUPS, SEQ_LEN)
    backs = cotangent.astype(jnp.float32).reshape(MB * GROUPS, SEQ_LEN, D)

    def one_sequence(totals, item):
        sequence, token_pos, back = item
        result, pull = jax.vjp(lambda values, weights: forward(values, token_pos, weights), sequence, params)
        d_sequence, d_params = pull(back)
        return (tuple((left + right for left, right in zip(totals, d_params))), (result, d_sequence))
    empty = tuple((jnp.zeros(item.shape, jnp.float32) for item in params))
    grads, (results, d_inputs) = lax.scan(one_sequence, empty, (sequences, places, backs))
    return (results.reshape(tokens.shape).astype(jnp.bfloat16), d_inputs.reshape(tokens.shape), grads[0], grads[1], grads[2], grads[3], grads[4], grads[5], grads[6], grads[7], grads[8], grads[9], grads[10])
```

```python
import jax
import jax.numpy as jnp
from jax import lax
from jax.sharding import PartitionSpec as P

HEADS = 16
KV_HEADS = 8
HEAD_DIM = 128
EPSILON = 1e-06
ROPE_BASE = 1000000.0
NEGATIVE = -1e30
F32 = jnp.float32
BF16 = jnp.bfloat16


def inverse_root(values):
    return lax.rsqrt(jnp.mean(values * values, axis=-1, keepdims=True) + EPSILON)


def rope_tables(token_pos):
    half_width = HEAD_DIM // 2
    frequency = ROPE_BASE ** (-(jnp.arange(half_width, dtype=F32) * 2.0 / HEAD_DIM))
    angles = token_pos.astype(F32)[:, None] * frequency[None, :]
    cosine = jnp.cos(angles)
    sine = jnp.sin(angles)
    return (
        jnp.concatenate([cosine, cosine], axis=-1)[:, None, :],
        jnp.concatenate([sine, sine], axis=-1)[:, None, :],
    )


def rotate(values, cosine, sine):
    half_width = values.shape[-1] // 2
    turned = jnp.concatenate([-values[..., half_width:], values[..., :half_width]], axis=-1)
    return values * cosine + turned * sine


def rotate_back(grads, cosine, sine):
    half_width = grads.shape[-1] // 2
    scaled = grads * sine
    turned = jnp.concatenate([scaled[..., half_width:], -scaled[..., :half_width]], axis=-1)
    return grads * cosine + turned


def norm_back(grads, values, inverse, gain):
    scaled = grads * gain
    return inverse * scaled - values * inverse**3 * jnp.mean(
        scaled * values, axis=-1, keepdims=True
    )


def mul(eq, left, right):
    return jnp.einsum(eq, left, right, preferred_element_type=F32)


def sum_scatter(part, axis):
    return lax.psum_scatter(part.astype(BF16), axis, scatter_dimension=0, tiled=True).astype(F32)


def slice_weights(item, ways):
    rows = item.shape[0]
    return item.reshape(rows, ways, -1).transpose(1, 0, 2)


def plain_body(tokens, positions, g_in, g_post, g_query, g_key, w_query, w_key, w_value,
               w_out, w_gate, w_up, w_down, cotangent):
    ways = lax.axis_size("seq")
    heads, kv_heads = HEADS // ways, KV_HEADS // ways
    micro, rows, width = tokens.shape[0], tokens.shape[2], tokens.shape[3]
    length = positions.shape[2]
    everyone = ("seq", "fsdp")
    gains = [
        lax.all_gather(item, everyone, axis=0, tiled=True).astype(F32)
        for item in (g_in, g_post, g_query, g_key)
    ]
    gain_in, gain_post, gain_query, gain_key = gains

    def spread(*items):
        packed = jnp.concatenate([slice_weights(item, ways) for item in items], axis=2)
        packed = lax.all_to_all(packed, "seq", 0, 0, tiled=True)
        packed = lax.all_gather(packed, "fsdp", axis=1, tiled=True)
        packed = packed.reshape(-1, packed.shape[2])
        sizes = [item.shape[1] // ways for item in items]
        cuts = [sum(sizes[: at + 1]) for at in range(len(sizes) - 1)]
        return jnp.split(packed, cuts, axis=1)

    wq, wk, wv = spread(w_query, w_key, w_value)
    wo = lax.all_gather(w_out, "fsdp", axis=0, tiled=True)
    wg, wu = spread(w_gate, w_up)
    wd = lax.all_gather(w_down, "fsdp", axis=0, tiled=True)
    scale = HEAD_DIM ** (-0.5)

    def gather_rows(item):
        return lax.all_gather(item, "seq", axis=0, tiled=True)

    grads = None
    outs, token_grads = [], []
    for at in range(micro):
        inputs = tokens[at, 0].astype(F32)
        pos = positions[at, 0]
        cosine, sine = rope_tables(pos)
        allowed = pos[None, :] <= pos[:, None]
        inv_in = inverse_root(inputs)
        normed = gather_rows((inputs * inv_in * gain_in).astype(BF16))
        q_raw = mul("td,df->tf", normed, wq).reshape(length, heads, HEAD_DIM)
        k_raw = mul("td,df->tf", normed, wk).reshape(length, kv_heads, HEAD_DIM)
        value = mul("td,df->tf", normed, wv).astype(BF16).reshape(length, kv_heads, HEAD_DIM)
        inv_q, inv_k = inverse_root(q_raw), inverse_root(k_raw)
        query = rotate(q_raw * inv_q * gain_query, cosine, sine).astype(BF16)
        query = query.reshape(length, kv_heads, heads // kv_heads, HEAD_DIM)
        key = rotate(k_raw * inv_k * gain_key, cosine, sine).astype(BF16)
        scores = jnp.where(allowed, mul("qjgd,kjd->jgqk", query, key) * scale, NEGATIVE)
        soft = jax.nn.softmax(scores, axis=-1)
        soft_low = soft.astype(BF16)
        mixed = mul("jgqk,kjd->qjgd", soft_low, value).astype(BF16).reshape(length, -1)
        resid = inputs + sum_scatter(mul("th,hd->td", mixed, wo), "seq")
        inv_post = inverse_root(resid)
        post = gather_rows((resid * inv_post * gain_post).astype(BF16))
        gate = mul("td,df->tf", post, wg)
        upper = mul("td,df->tf", post, wu)
        sigma = jax.nn.sigmoid(gate)
        hidden = (gate * sigma * upper).astype(BF16)
        outs.append((resid + sum_scatter(mul("tf,fd->td", hidden, wd), "seq")).astype(BF16))
        back_low = cotangent[at, 0]
        back = gather_rows(back_low)
        g_down = mul("tf,td->fd", hidden, back)
        d_hidden = mul("td,fd->tf", back, wd)
        d_gate = (d_hidden * upper * sigma * (1.0 + gate * (1.0 - sigma))).astype(BF16)
        d_upper = (d_hidden * gate * sigma).astype(BF16)
        g_gate = mul("td,tf->df", post, d_gate)
        g_up = mul("td,tf->df", post, d_upper)
        d_post = sum_scatter(mul("tf,df->td", d_gate, wg) + mul("tf,df->td", d_upper, wu), "seq")
        post_grad = jnp.sum(d_post * resid * inv_post, axis=0)
        d_resid = back_low.astype(F32) + norm_back(d_post, resid, inv_post, gain_post)
        d_attn = gather_rows(d_resid.astype(BF16))
        g_out = mul("th,td->hd", mixed, d_attn)
        d_mixed = mul("td,hd->th", d_attn, wo).astype(BF16)
        d_mixed = d_mixed.reshape(length, kv_heads, heads // kv_heads, HEAD_DIM)
        d_soft = mul("qjgd,kjd->jgqk", d_mixed, value)
        d_scores = (soft * (d_soft - jnp.sum(d_soft * soft, axis=-1, keepdims=True))).astype(BF16)
        d_query = mul("jgqk,kjd->qjgd", d_scores, key) * scale
        d_key = mul("jgqk,qjgd->kjd", d_scores, query) * scale
        d_value = mul("jgqk,qjgd->kjd", soft_low, d_mixed).astype(BF16).reshape(length, -1)
        key_turn = rotate_back(d_key, cosine, sine)
        query_turn = rotate_back(d_query.reshape(length, heads, HEAD_DIM), cosine, sine)
        key_grad = jnp.sum(key_turn * k_raw * inv_k, axis=(0, 1))
        query_grad = jnp.sum(query_turn * q_raw * inv_q, axis=(0, 1))
        d_key = norm_back(key_turn, k_raw, inv_k, gain_key).astype(BF16).reshape(length, -1)
        d_query = norm_back(query_turn, q_raw, inv_q, gain_query).astype(BF16).reshape(length, -1)
        g_query_w = mul("td,tf->df", normed, d_query)
        g_key_w = mul("td,tf->df", normed, d_key)
        g_value_w = mul("td,tf->df", normed, d_value)
        d_normed = mul("tf,df->td", d_query, wq) + mul("tf,df->td", d_key, wk)
        d_normed = sum_scatter(d_normed + mul("tf,df->td", d_value, wv), "seq")
        in_grad = jnp.sum(d_normed * inputs * inv_in, axis=0)
        token_grads.append(d_resid + norm_back(d_normed, inputs, inv_in, gain_in))
        found = [in_grad, post_grad, query_grad, key_grad, g_query_w, g_key_w, g_value_w,
                 g_out, g_gate, g_up, g_down]
        grads = found if grads is None else [left + right for left, right in zip(grads, found)]

    small = [lax.psum_scatter(item, everyone, scatter_dimension=0, tiled=True) for item in grads[:4]]

    def columns_home(item):
        full, wide = item.shape
        item = item.reshape(ways, -1, wide).astype(BF16)
        item = lax.psum_scatter(item, "fsdp", scatter_dimension=1, tiled=True)
        item = lax.all_to_all(item, "seq", 0, 0, tiled=True)
        return item.transpose(1, 0, 2).reshape(item.shape[1], ways * wide).astype(F32)

    def rows_home(item):
        return sum_scatter(item, "fsdp")

    large = [columns_home(item) for item in grads[4:7]] + [rows_home(grads[7])]
    large += [columns_home(item) for item in grads[8:10]] + [rows_home(grads[10])]
    return (jnp.stack(outs)[:, None], jnp.stack(token_grads)[:, None], *small, *large)


def solution(mesh):
    both = ("seq", "fsdp")
    act = P(None, "fsdp", "seq", None)
    vec, mat = P(both), P(both, None)
    return jax.shard_map(
        plain_body,
        mesh=mesh,
        in_specs=(act, P(None, "fsdp", None), *[vec] * 4, *[mat] * 7, act),
        out_specs=(act, act, *[vec] * 4, *[mat] * 7),
        check_vma=False,
    )
```

```python
import functools

import jax
import jax.numpy as jnp
from jax import lax
from jax.experimental import pallas as pl
from jax.experimental.pallas import tpu as pltpu
from jax.sharding import PartitionSpec as P

HEADS = 16
KV_HEADS = 8
HEAD_DIM = 128
EPSILON = 1e-06
ROPE_BASE = 1000000.0
NEGATIVE = -1e30
F32 = jnp.float32
BF16 = jnp.bfloat16


def inverse_root(values):
    return lax.rsqrt(jnp.mean(values * values, axis=-1, keepdims=True) + EPSILON)


def rope_tables(token_pos):
    half_width = HEAD_DIM // 2
    frequency = ROPE_BASE ** (-(jnp.arange(half_width, dtype=F32) * 2.0 / HEAD_DIM))
    angles = token_pos.astype(F32)[:, None] * frequency[None, :]
    cosine = jnp.cos(angles)
    sine = jnp.sin(angles)
    return (
        jnp.concatenate([cosine, cosine], axis=-1)[:, None, :],
        jnp.concatenate([sine, sine], axis=-1)[:, None, :],
    )


def rotate(values, cosine, sine):
    half_width = values.shape[-1] // 2
    turned = jnp.concatenate([-values[..., half_width:], values[..., :half_width]], axis=-1)
    return values * cosine + turned * sine


def rotate_back(grads, cosine, sine):
    half_width = grads.shape[-1] // 2
    scaled = grads * sine
    turned = jnp.concatenate([scaled[..., half_width:], -scaled[..., :half_width]], axis=-1)
    return grads * cosine + turned


def norm_back(grads, values, inverse, gain):
    scaled = grads * gain
    return inverse * scaled - values * inverse**3 * jnp.mean(
        scaled * values, axis=-1, keepdims=True
    )


def mul(eq, left, right):
    return jnp.einsum(eq, left, right, preferred_element_type=F32)


def sum_scatter(part, axis):
    return lax.psum_scatter(part.astype(BF16), axis, scatter_dimension=0, tiled=True).astype(F32)


def slice_weights(item, ways):
    rows = item.shape[0]
    return item.reshape(rows, ways, -1).transpose(1, 0, 2)


def plain_body(tokens, positions, g_in, g_post, g_query, g_key, w_query, w_key, w_value,
               w_out, w_gate, w_up, w_down, cotangent):
    ways = lax.axis_size("seq")
    heads, kv_heads = HEADS // ways, KV_HEADS // ways
    micro, rows, width = tokens.shape[0], tokens.shape[2], tokens.shape[3]
    length = positions.shape[2]
    everyone = ("seq", "fsdp")
    gains = [
        lax.all_gather(item, everyone, axis=0, tiled=True).astype(F32)
        for item in (g_in, g_post, g_query, g_key)
    ]
    gain_in, gain_post, gain_query, gain_key = gains

    def spread(*items):
        packed = jnp.concatenate([slice_weights(item, ways) for item in items], axis=2)
        packed = lax.all_to_all(packed, "seq", 0, 0, tiled=True)
        packed = lax.all_gather(packed, "fsdp", axis=1, tiled=True)
        packed = packed.reshape(-1, packed.shape[2])
        sizes = [item.shape[1] // ways for item in items]
        cuts = [sum(sizes[: at + 1]) for at in range(len(sizes) - 1)]
        return jnp.split(packed, cuts, axis=1)

    wq, wk, wv = spread(w_query, w_key, w_value)
    wo = lax.all_gather(w_out, "fsdp", axis=0, tiled=True)
    wg, wu = spread(w_gate, w_up)
    wd = lax.all_gather(w_down, "fsdp", axis=0, tiled=True)
    scale = HEAD_DIM ** (-0.5)

    def gather_rows(item):
        return lax.all_gather(item, "seq", axis=0, tiled=True)

    grads = None
    outs, token_grads = [], []
    for at in range(micro):
        inputs = tokens[at, 0].astype(F32)
        pos = positions[at, 0]
        cosine, sine = rope_tables(pos)
        allowed = pos[None, :] <= pos[:, None]
        inv_in = inverse_root(inputs)
        normed = gather_rows((inputs * inv_in * gain_in).astype(BF16))
        q_raw = mul("td,df->tf", normed, wq).reshape(length, heads, HEAD_DIM)
        k_raw = mul("td,df->tf", normed, wk).reshape(length, kv_heads, HEAD_DIM)
        value = mul("td,df->tf", normed, wv).astype(BF16).reshape(length, kv_heads, HEAD_DIM)
        inv_q, inv_k = inverse_root(q_raw), inverse_root(k_raw)
        query = rotate(q_raw * inv_q * gain_query, cosine, sine).astype(BF16)
        query = query.reshape(length, kv_heads, heads // kv_heads, HEAD_DIM)
        key = rotate(k_raw * inv_k * gain_key, cosine, sine).astype(BF16)
        scores = jnp.where(allowed, mul("qjgd,kjd->jgqk", query, key) * scale, NEGATIVE)
        soft = jax.nn.softmax(scores, axis=-1)
        soft_low = soft.astype(BF16)
        mixed = mul("jgqk,kjd->qjgd", soft_low, value).astype(BF16).reshape(length, -1)
        resid = inputs + sum_scatter(mul("th,hd->td", mixed, wo), "seq")
        inv_post = inverse_root(resid)
        post = gather_rows((resid * inv_post * gain_post).astype(BF16))
        gate = mul("td,df->tf", post, wg)
        upper = mul("td,df->tf", post, wu)
        sigma = jax.nn.sigmoid(gate)
        hidden = (gate * sigma * upper).astype(BF16)
        outs.append((resid + sum_scatter(mul("tf,fd->td", hidden, wd), "seq")).astype(BF16))
        back_low = cotangent[at, 0]
        back = gather_rows(back_low)
        g_down = mul("tf,td->fd", hidden, back)
        d_hidden = mul("td,fd->tf", back, wd)
        d_gate = (d_hidden * upper * sigma * (1.0 + gate * (1.0 - sigma))).astype(BF16)
        d_upper = (d_hidden * gate * sigma).astype(BF16)
        g_gate = mul("td,tf->df", post, d_gate)
        g_up = mul("td,tf->df", post, d_upper)
        d_post = sum_scatter(mul("tf,df->td", d_gate, wg) + mul("tf,df->td", d_upper, wu), "seq")
        post_grad = jnp.sum(d_post * resid * inv_post, axis=0)
        d_resid = back_low.astype(F32) + norm_back(d_post, resid, inv_post, gain_post)
        d_attn = gather_rows(d_resid.astype(BF16))
        g_out = mul("th,td->hd", mixed, d_attn)
        d_mixed = mul("td,hd->th", d_attn, wo).astype(BF16)
        d_mixed = d_mixed.reshape(length, kv_heads, heads // kv_heads, HEAD_DIM)
        d_soft = mul("qjgd,kjd->jgqk", d_mixed, value)
        d_scores = (soft * (d_soft - jnp.sum(d_soft * soft, axis=-1, keepdims=True))).astype(BF16)
        d_query = mul("jgqk,kjd->qjgd", d_scores, key) * scale
        d_key = mul("jgqk,qjgd->kjd", d_scores, query) * scale
        d_value = mul("jgqk,qjgd->kjd", soft_low, d_mixed).astype(BF16).reshape(length, -1)
        key_turn = rotate_back(d_key, cosine, sine)
        query_turn = rotate_back(d_query.reshape(length, heads, HEAD_DIM), cosine, sine)
        key_grad = jnp.sum(key_turn * k_raw * inv_k, axis=(0, 1))
        query_grad = jnp.sum(query_turn * q_raw * inv_q, axis=(0, 1))
        d_key = norm_back(key_turn, k_raw, inv_k, gain_key).astype(BF16).reshape(length, -1)
        d_query = norm_back(query_turn, q_raw, inv_q, gain_query).astype(BF16).reshape(length, -1)
        g_query_w = mul("td,tf->df", normed, d_query)
        g_key_w = mul("td,tf->df", normed, d_key)
        g_value_w = mul("td,tf->df", normed, d_value)
        d_normed = mul("tf,df->td", d_query, wq) + mul("tf,df->td", d_key, wk)
        d_normed = sum_scatter(d_normed + mul("tf,df->td", d_value, wv), "seq")
        in_grad = jnp.sum(d_normed * inputs * inv_in, axis=0)
        token_grads.append(d_resid + norm_back(d_normed, inputs, inv_in, gain_in))
        found = [in_grad, post_grad, query_grad, key_grad, g_query_w, g_key_w, g_value_w,
                 g_out, g_gate, g_up, g_down]
        grads = found if grads is None else [left + right for left, right in zip(grads, found)]

    small = [lax.psum_scatter(item, everyone, scatter_dimension=0, tiled=True) for item in grads[:4]]

    def columns_home(item):
        full, wide = item.shape
        item = item.reshape(ways, -1, wide).astype(BF16)
        item = lax.psum_scatter(item, "fsdp", scatter_dimension=1, tiled=True)
        item = lax.all_to_all(item, "seq", 0, 0, tiled=True)
        return item.transpose(1, 0, 2).reshape(item.shape[1], ways * wide).astype(F32)

    def rows_home(item):
        return sum_scatter(item, "fsdp")

    large = [columns_home(item) for item in grads[4:7]] + [rows_home(grads[7])]
    large += [columns_home(item) for item in grads[8:10]] + [rows_home(grads[10])]
    return (jnp.stack(outs)[:, None], jnp.stack(token_grads)[:, None], *small, *large)


MESH = pl.DeviceIdType.MESH
ANY = pl.ANY
VMEM = pltpu.VMEM
RUN = 128
BLOCK = 256
NARROW = (((1,), (1,)), ((), ()))
TALL = (((0,), (0,)), ((), ()))
PLAIN = (((1,), (0,)), ((), ()))
LOG2E = 1.4426950408889634
SCALE = HEAD_DIM ** (-0.5)
VMEM_BYTES = 60 * 2**20


def dot(left, right, dims=PLAIN):
    return lax.dot_general(left, right, dims, preferred_element_type=F32)


class Place:
    def __init__(self, planes):
        self.planes = planes
        self.s = lax.axis_index("seq")
        self.f = lax.axis_index("fsdp")
        self.x, self.c = self.s // 2, self.s % 2
        self.z, self.y = self.f // 2, self.f % 2
        self.other_y = 1 - self.y
        self.core_dev = (self.x * 2 + 1 - self.c, self.f)
        self.x_dev = ((1 - self.x) * 2 + self.c, self.f)
        self.far_dev = ((1 - self.x) * 2 + 1 - self.c, self.f)
        self.y_dev = (self.s, self.z * 2 + self.other_y)

    def z_at(self, step):
        return lax.rem(self.z + step, self.planes)

    def z_dev(self, step):
        return (self.s, self.z_at(step) * 2 + self.y)

    def peers(self):
        return [self.core_dev, self.x_dev, self.far_dev, self.y_dev] + [
            self.z_dev(step) for step in range(1, self.planes)
        ]

    def meet(self):
        barrier = pltpu.get_barrier_semaphore()
        for peer in self.peers():
            pl.semaphore_signal(barrier, inc=1, device_id=peer, device_id_type=MESH)
        pl.semaphore_wait(barrier, 3 + self.planes)


def remote(src, dst, out_sem, in_sem, device):
    return pltpu.make_async_remote_copy(
        src_ref=src, dst_ref=dst, send_sem=out_sem, recv_sem=in_sem,
        device_id=device, device_id_type=MESH,
    )


class Wire:
    def __init__(self, out_sems, in_sems, own_sems):
        self.out_sems, self.in_sems, self.own_sems = out_sems, in_sems, own_sems
        self.sent, self.owned = [], 0

    def send(self, src, dst, device):
        at = len(self.sent)
        copy = remote(src, dst, self.out_sems.at[at], self.in_sems.at[at], device)
        copy.start()
        self.sent.append(copy)
        return copy

    def own(self, src, dst):
        copy = pltpu.make_async_copy(src, dst, self.own_sems.at[self.owned])
        copy.start()
        self.owned += 1
        return copy

    def close(self):
        for copy in self.sent:
            copy.wait_send()


def wire_scratch(copies, owns):
    return [
        pltpu.SemaphoreType.DMA((copies,)),
        pltpu.SemaphoreType.DMA((copies,)),
        pltpu.SemaphoreType.DMA((owns,)),
    ]


class Reducer:
    def __init__(self, place, part, core_out, core_in, x_out, x_in, keep, sems):
        self.place, self.part = place, part
        self.core_out, self.core_in = core_out, core_in
        self.x_out, self.x_in, self.keep = x_out, x_in, keep
        self.core_s, self.core_r, self.x_s, self.x_r = sems

    def block(self, step):
        p = self.place
        turn = step % 4
        x = jnp.where(turn % 2 == 0, 1 - p.x, p.x)
        c = jnp.where(turn < 2, 1 - p.c, p.c)
        return step // 4, x * 2 + c

    def core_copy(self, slot):
        return remote(self.core_out.at[slot], self.core_in.at[slot], self.core_s.at[slot],
                      self.core_r.at[slot], self.place.core_dev)

    def x_copy(self, micro):
        return remote(self.x_out.at[micro], self.x_in.at[micro], self.x_s.at[micro],
                      self.x_r.at[micro], self.place.x_dev)

    def take(self, step, send_x=True):
        micro, turn = step // 4, step % 4

        @pl.when(turn < 2)
        def _():
            slot = micro * 2 + turn
            self.core_out[slot] = self.part[...].astype(BF16)
            self.core_copy(slot).start()

        @pl.when(turn == 2)
        def _():
            slot = micro * 2
            self.core_copy(slot).wait_recv()
            self.x_out[micro] = (self.part[...] + self.core_in[slot].astype(F32)).astype(BF16)
            if send_x:
                self.x_copy(micro).start()

        @pl.when(turn == 3)
        def _():
            slot = micro * 2 + 1
            self.core_copy(slot).wait_recv()
            self.keep[micro] = self.part[...] + self.core_in[slot].astype(F32)

    def total(self, micro):
        self.x_copy(micro).wait_recv()
        return self.keep[micro] + self.x_in[micro].astype(F32)

    def close(self, send_x=True):
        for slot in range(4):
            self.core_copy(slot).wait_send()
        if send_x:
            for micro in range(2):
                self.x_copy(micro).wait_send()


def reducer_scratch(width):
    return [
        VMEM((4, BLOCK, width), BF16),
        VMEM((4, BLOCK, width), BF16),
        VMEM((2, BLOCK, width), BF16),
        VMEM((2, BLOCK, width), BF16),
        VMEM((2, BLOCK, width), F32),
        pltpu.SemaphoreType.DMA((4,)),
        pltpu.SemaphoreType.DMA((4,)),
        pltpu.SemaphoreType.DMA((2,)),
        pltpu.SemaphoreType.DMA((2,)),
    ]


def row_mean(values):
    return jnp.mean(values, axis=-1, keepdims=True)


def spread_gain(table, row, devices, width):
    per = width // devices
    lanes = lax.broadcasted_iota(jnp.int32, (RUN, width), 0)
    column = lax.broadcasted_iota(jnp.int32, (RUN, width), 1)
    pick = (lanes == lax.rem(column, per)).astype(BF16)
    picked = dot(table, pick)
    rows = lax.broadcasted_iota(jnp.int32, (devices * 8, width), 0)
    owner = lax.broadcasted_iota(jnp.int32, (devices * 8, width), 1) // per
    return jnp.sum(jnp.where(rows == owner * 8 + row, picked, 0.0), axis=0, keepdims=True)


def two_runs(ref, first, second):
    return jnp.concatenate([ref[first], ref[second]], axis=0)


def joined(value):
    return value.reshape(-1, value.shape[-1])


def flat(ref):
    return joined(ref[...])


def front_kernel(
    planes,
    order, rank, tokens, cotangent, gain_tile, cosine, sine,
    s_q, s_k, s_v, s_o, s_g, s_u, s_d,
    wq, wk, wv, wo, wg, wu, wd,
    normed, query, key, value, q_unit, k_unit, roots, mixed, lse,
    resid, post_full, back_full, gains,
    tok_full, gain_all, post_own, part,
    core_out, core_in, x_out, x_in, keep, core_s, core_r, x_s, x_r,
    out_sems, in_sems, own_sems,
):
    p = Place(planes)
    s, f = p.s, p.f
    devices = 8 * planes
    wire = Wire(out_sems, in_sems, own_sems)
    reducer = Reducer(p, part, core_out, core_in, x_out, x_in, keep, (core_s, core_r, x_s, x_r))
    rows = BLOCK
    mine = pl.ds(s * rows, rows)
    theirs = pl.ds(p.x_dev[0] * rows, rows)
    length = 4 * rows
    p.meet()

    gain_all[s, f] = gain_tile[...]
    gain_in = [wire.send(gain_all.at[s, f], gain_all.at[s, f], dev)
               for dev in (p.core_dev, p.x_dev, p.far_dev)]

    def spread_columns(item, full):
        wide = item.shape[1] // 4
        came = [wire.own(item.at[:, pl.ds(s * wide, wide)], full.at[s, f])]
        sent = []
        for dev in (p.core_dev, p.x_dev, p.far_dev):
            sent.append(wire.send(item.at[:, pl.ds(dev[0] * wide, wide)], full.at[s, f], dev))
        return came, sent

    first = [spread_columns(item, full) for item, full in ((s_q, wq), (s_k, wk), (s_v, wv))]
    tok_here, tok_x, tok_core = [], [], []
    for micro in range(2):
        to = tok_full.at[pl.ds(micro * (length // RUN) + s * 2, 2)]
        tok_here.append(wire.own(tokens.at[micro], to))
        tok_x.append(wire.send(tokens.at[micro], to, p.x_dev))
        tok_core.append(wire.send(tokens.at[micro], to, p.core_dev))
    second = [spread_columns(item, full) for item, full in ((s_g, wg), (s_u, wu))]

    def arrived(group):
        came, sent = group
        for copy in came:
            copy.wait()
        for copy in sent:
            copy.wait_recv()

    def blocks(full, at):
        return full.at[:, at] if len(full.shape) == 4 else full.at[at]

    def push_planes(full):
        here = blocks(full, f)
        far = [wire.send(here, here, p.z_dev(step)) for step in range(1, planes)]
        return far, [wire.send(here, here, p.y_dev)]

    def forward(full, state):
        far, side = state
        for step, copy in enumerate(far, 1):
            copy.wait_recv()
            there = blocks(full, p.z_at(planes - step) * 2 + p.y)
            side.append(wire.send(there, there, p.y_dev))

    def settle(state):
        for copy in state[1]:
            copy.wait_recv()

    def push_rows(item, full):
        kept = wire.own(item, full.at[f])
        far = [wire.send(item, full.at[f], p.z_dev(step)) for step in range(1, planes)]
        return kept, (far, [wire.send(item, full.at[f], p.y_dev)])

    for copy in gain_in:
        copy.wait_recv()
    gain_state = push_planes(gain_all)
    states = []
    for group, full in zip(first, (wq, wk, wv)):
        arrived(group)
        states.append(push_planes(full))
    forward(gain_all, gain_state)
    out_kept, out_state = push_rows(s_o, wo)
    tok_fwd = []
    for micro in range(2):
        tok_x[micro].wait_recv()
        block = tok_full.at[pl.ds(micro * (length // RUN) + p.x_dev[0] * 2, 2)]
        tok_fwd.append(wire.send(block, block, p.core_dev))
    for full, state in zip((wq, wk, wv), states):
        forward(full, state)
    back_x, back_core, back_kept = [], [], []
    for micro in range(2):
        to = back_full.at[micro, mine]
        back_x.append(wire.send(cotangent.at[micro], to, p.x_dev))
        back_kept.append(wire.own(cotangent.at[micro], to))
        back_core.append(wire.send(cotangent.at[micro], to, p.core_dev))
    wide_states = []
    for group, full in zip(second, (wg, wu)):
        arrived(group)
        wide_states.append(push_planes(full))
    down_kept, down_state = push_rows(s_d, wd)
    settle(gain_state)
    table = gain_all[...].reshape(devices * 8, RUN).astype(BF16)
    gain_first = spread_gain(table, 0, devices, 1024)
    gain_post = spread_gain(table, 1, devices, 1024)
    gain_query = spread_gain(table, 2, devices, RUN)
    gain_key = spread_gain(table, 3, devices, RUN)
    gains[...] = jnp.zeros_like(gains)
    gains[0:1] = gain_first
    gains[1:2] = gain_post
    gains[2:3, 0:RUN] = gain_query
    gains[3:4, 0:RUN] = gain_key
    for copy in tok_here:
        copy.wait()
    for copy in tok_core + tok_fwd:
        copy.wait_recv()
    for state in states:
        settle(state)

    def project(step, carry):
        here = pl.ds(pl.multiple_of(step * BLOCK, BLOCK), BLOCK)
        raw = two_runs(tok_full, order[step * 2], order[step * 2 + 1]).astype(F32)
        root = lax.rsqrt(row_mean(raw * raw) + EPSILON)
        low = (raw * root * gains[0:1]).astype(BF16)
        normed[here] = low
        turn = pl.ds(pl.multiple_of(lax.rem(step, length // BLOCK) * BLOCK, BLOCK), BLOCK)
        cos, sin = cosine[turn], sine[turn]
        found = []
        for weight, low_ref, unit_ref, row in ((wq, query, q_unit, 2), (wk, key, k_unit, 3)):
            product = dot(low, flat(weight))
            gain = gains[row : row + 1, 0:RUN]
            for head in range(low_ref.shape[1] // HEAD_DIM):
                at = slice(head * HEAD_DIM, (head + 1) * HEAD_DIM)
                one = product[:, at]
                inverse = lax.rsqrt(row_mean(one * one) + EPSILON)
                unit = one * inverse
                unit_ref[here, at] = unit.astype(BF16)
                scaled = unit * gain
                low_ref[here, at] = (scaled * cos + pltpu.roll(scaled, HEAD_DIM // 2, 1) * sin).astype(BF16)
                found.append(inverse)
        for at, inverse in enumerate(found):
            roots[here, at : at + 1] = inverse
        value[here] = dot(low, flat(wv)).astype(BF16)
        return carry

    lax.fori_loop(0, 2 * length // BLOCK, project, 0)
    for full, state in zip((wg, wu), wide_states):
        forward(full, state)

    def attend(step, carry):
        micro, head = step // 2, lax.rem(step, 2)
        keys_at = pl.ds(pl.multiple_of(head * HEAD_DIM, HEAD_DIM), HEAD_DIM)
        lanes = [pl.ds(pl.multiple_of(head * 2 * HEAD_DIM + g * HEAD_DIM, HEAD_DIM), HEAD_DIM) for g in range(2)]
        for block in range(length // BLOCK):
            here = pl.ds(pl.multiple_of(micro * length + block * BLOCK, BLOCK), BLOCK)
            seen = (block + 1) * BLOCK
            past = pl.ds(pl.multiple_of(micro * length, BLOCK), seen)
            asked = jnp.concatenate([query[here, lane] for lane in lanes], axis=0)
            scores = dot(asked, key[past, keys_at], NARROW)
            line = lax.broadcasted_iota(jnp.int32, (2 * BLOCK, seen), 0)
            line = jnp.where(line >= BLOCK, line - BLOCK, line) + block * BLOCK
            column = lax.broadcasted_iota(jnp.int32, (2 * BLOCK, seen), 1)
            scores = jnp.where(column <= line, scores, NEGATIVE)
            top = jnp.max(scores, axis=-1, keepdims=True)
            weight = jnp.exp2((scores - top) * (SCALE * LOG2E))
            total = jnp.sum(weight, axis=-1, keepdims=True)
            out = dot(weight.astype(BF16), value[past, keys_at]) * (1.0 / total)
            level = top * (SCALE * LOG2E) + jnp.log2(total)
            for g, lane in enumerate(lanes):
                half = slice(g * BLOCK, (g + 1) * BLOCK)
                pair = pl.ds(micro * (length // RUN) + block * 2, 2)
                mixed[pair, :, lane] = out[half].astype(BF16).reshape(2, RUN, HEAD_DIM)
                lse[step, pl.ds(block * BLOCK, BLOCK), g : g + 1] = level[half]
        return carry

    lax.fori_loop(0, 2, attend, 0)
    forward(wo, out_state)
    forward(wd, down_state)
    lax.fori_loop(2, 4, attend, 0)
    for micro in range(2):
        back_x[micro].wait_recv()
        block = back_full.at[micro, theirs]
        back_core.append(wire.send(block, block, p.core_dev))
    out_kept.wait()
    settle(out_state)

    def mix_out(step, carry):
        micro, block = reducer.block(step)
        at = micro * (length // RUN) + block * 2
        low = two_runs(mixed, rank[at], rank[at + 1])
        part[...] = dot(low, flat(wo))
        reducer.take(step)
        return carry

    lax.fori_loop(0, 8, mix_out, 0)
    posts = []
    for micro in range(2):
        total = reducer.total(micro)
        own = joined(tok_full[pl.ds(micro * (length // RUN) + s * 2, 2)]).astype(F32)
        total = own + total
        resid[micro] = total
        root = lax.rsqrt(row_mean(total * total) + EPSILON)
        post_own[micro] = (total * root * gains[1:2]).astype(BF16)
        to = post_full.at[micro, mine]
        posts.append((wire.send(post_own.at[micro], to, p.x_dev), wire.send(post_own.at[micro], to, p.core_dev),
                      wire.own(post_own.at[micro], to)))
    for micro in range(2):
        posts[micro][0].wait_recv()
        block = post_full.at[micro, theirs]
        wire.send(block, block, p.core_dev).wait_recv()
        posts[micro][1].wait_recv()
        posts[micro][2].wait()
    for copy in back_core:
        copy.wait_recv()
    for copy in back_kept:
        copy.wait()
    for state in wide_states + [down_state]:
        settle(state)
    down_kept.wait()
    reducer.close()
    wire.close()


def front(planes, order, rank, tokens, cotangent, gain_tile, cosine, sine, shards):
    nf = 2 * planes
    rows = tokens.shape[1]
    length = 4 * rows
    total = 2 * length
    tokens = tokens.reshape(2, 2, RUN, tokens.shape[2])
    quarter = [item.shape[1] // 4 for item in shards[:3]] + [None] + [item.shape[1] // 4 for item in shards[4:6]]
    def col(at):
        return jax.ShapeDtypeStruct((4, nf, shards[at].shape[0], quarter[at]), BF16)
    def row(at):
        return jax.ShapeDtypeStruct((nf, *shards[at].shape), BF16)
    def low(width):
        return jax.ShapeDtypeStruct((total, width), BF16)
    shapes = [col(0), col(1), col(2), row(3), col(4), col(5), row(6),
              low(1024), low(512), low(256), low(256), low(512), low(256),
              jax.ShapeDtypeStruct((total, 8), F32),
              jax.ShapeDtypeStruct((total // RUN, RUN, 512), BF16), jax.ShapeDtypeStruct((4, length, 2), F32),
              jax.ShapeDtypeStruct((2, rows, 1024), F32),
              jax.ShapeDtypeStruct((2, length, 1024), BF16), jax.ShapeDtypeStruct((2, length, 1024), BF16),
              jax.ShapeDtypeStruct((8, 1024), F32)]
    far = {4, 5, 6, 17, 18}
    vm = pl.BlockSpec(memory_space=VMEM)
    hb = pl.BlockSpec(memory_space=ANY)
    sm = pl.BlockSpec(memory_space=pltpu.SMEM)
    return pl.pallas_call(
        functools.partial(front_kernel, planes),
        out_shape=shapes,
        in_specs=[sm, sm, hb, hb, vm, vm, vm] + [hb] * 7,
        out_specs=[hb if at in far else vm for at in range(len(shapes))],
        scratch_shapes=[
            VMEM((total // RUN, RUN, 1024), BF16), VMEM((4, nf, 8, RUN), F32), VMEM((2, rows, 1024), BF16),
            VMEM((BLOCK, 1024), F32), *reducer_scratch(1024), *wire_scratch(120, 24),
        ],
        compiler_params=pltpu.CompilerParams(
            collective_id=0, has_side_effects=True, vmem_limit_bytes=VMEM_BYTES),
        name="front",
    )(order, rank, tokens, cotangent, gain_tile, cosine, sine, *shards)


def middle_kernel(
    planes,
    post, back, wg, wu, wd, resid, gains,
    grad_g, grad_u, grad_d, y_out, y_keep, d_resid, attn_full, sums,
    hidden, d_gate, d_up, part_y, part_p, attn_own,
    y_core_out, y_core_in,
    core_out, core_in, x_out, x_in, keep, core_s, core_r, x_s, x_r,
    y_core_s, y_core_r, out_sems, in_sems, own_sems,
):
    p = Place(planes)
    s = p.s
    wire = Wire(out_sems, in_sems, own_sems)
    into_post = Reducer(p, part_p, core_out, core_in, x_out, x_in, keep, (core_s, core_r, x_s, x_r))
    into_out = Reducer(p, part_y, y_core_out, y_core_in, y_out, None, y_keep, (y_core_s, y_core_r, None, None))
    rows = resid.shape[1]
    length = 4 * rows
    mine = pl.ds(s * rows, rows)
    theirs = pl.ds(p.x_dev[0] * rows, rows)
    p.meet()

    def feed(step, carry):
        micro, block = into_post.block(step)
        here = pl.ds(pl.multiple_of(micro * length + block * BLOCK, BLOCK), BLOCK)
        given, pulled = post[here, :], back[here, :]
        gate = dot(given, wg[...])
        upper = dot(given, wu[...])
        d_hidden = dot(pulled, wd[...], NARROW)
        sigma = 1.0 / (1.0 + jnp.exp(-gate))
        lit = gate * sigma
        low = (lit * upper).astype(BF16)
        gate_low = (d_hidden * upper * sigma * (1.0 + gate * (1.0 - sigma))).astype(BF16)
        up_low = (d_hidden * lit).astype(BF16)
        hidden[here] = low
        d_gate[here] = gate_low
        d_up[here] = up_low
        part_p[...] = dot(gate_low, wg[...], NARROW) + dot(up_low, wu[...], NARROW)
        into_post.take(step)
        part_y[...] = dot(low, wd[...])
        into_out.take(step, send_x=False)
        return carry

    lax.fori_loop(0, 8, feed, 0)

    def down_tile(at, carry):
        cut = pl.ds(pl.multiple_of(at * BLOCK, BLOCK), BLOCK)
        grad_d[cut] = dot(hidden[:, cut], back[...], TALL).astype(BF16)
        return carry

    def gate_tile(at, carry):
        cut = pl.ds(pl.multiple_of(at * BLOCK, BLOCK), BLOCK)
        grad_g[cut] = dot(post[:, cut], d_gate[...], TALL).astype(BF16)
        return carry

    def up_tile(at, carry):
        cut = pl.ds(pl.multiple_of(at * BLOCK, BLOCK), BLOCK)
        grad_u[cut] = dot(post[:, cut], d_up[...], TALL).astype(BF16)
        return carry

    gain = gains[1:2]
    sends = []
    sums[...] = jnp.zeros_like(sums)

    def settle(micro):
        grad = into_post.total(micro)
        held = resid[micro]
        root = lax.rsqrt(row_mean(held * held) + EPSILON)
        unit = held * root
        sums[0:1] += jnp.sum(grad * unit, axis=0, keepdims=True)
        scaled = grad * gain
        own = back[pl.ds(pl.multiple_of(micro * length + s * rows, rows), rows), :].astype(F32)
        whole = own + root * (scaled - unit * row_mean(scaled * unit))
        d_resid[micro] = whole
        attn_own[micro] = whole.astype(BF16)
        to = attn_full.at[micro, mine]
        sends.append((wire.send(attn_own.at[micro], to, p.x_dev), wire.send(attn_own.at[micro], to, p.core_dev),
                      wire.own(attn_own.at[micro], to)))
        y_keep[micro] = y_keep[micro] + held

    lax.fori_loop(0, 3, down_tile, 0)
    settle(0)
    lax.fori_loop(0, 4, gate_tile, 0)
    settle(1)
    lax.fori_loop(0, 4, up_tile, 0)
    for micro in range(2):
        sends[micro][0].wait_recv()
        block = attn_full.at[micro, theirs]
        wire.send(block, block, p.core_dev).wait_recv()
        sends[micro][1].wait_recv()
        sends[micro][2].wait()
    into_post.close()
    into_out.close(send_x=False)
    wire.close()


def middle(planes, post, back, wg, wu, wd, resid, gains):
    rows = resid.shape[1]
    total = 8 * rows
    wide = wg.shape[1]
    shapes = [
        jax.ShapeDtypeStruct((1024, wide), BF16), jax.ShapeDtypeStruct((1024, wide), BF16),
        jax.ShapeDtypeStruct((wide, 1024), BF16),
        jax.ShapeDtypeStruct((2, rows, 1024), BF16), jax.ShapeDtypeStruct((2, rows, 1024), F32),
        jax.ShapeDtypeStruct((2, rows, 1024), F32), jax.ShapeDtypeStruct((2, 4 * rows, 1024), BF16),
        jax.ShapeDtypeStruct((8, 1024), F32),
    ]
    vm = pl.BlockSpec(memory_space=VMEM)
    hb = pl.BlockSpec(memory_space=ANY)
    return pl.pallas_call(
        functools.partial(middle_kernel, planes),
        out_shape=shapes,
        in_specs=[vm] * 7,
        out_specs=[vm] * 6 + [hb, vm],
        scratch_shapes=[
            VMEM((total, wide), BF16), VMEM((total, wide), BF16), VMEM((total, wide), BF16),
            VMEM((BLOCK, 1024), F32), VMEM((BLOCK, 1024), F32), VMEM((2, rows, 1024), BF16),
            VMEM((4, BLOCK, 1024), BF16), VMEM((4, BLOCK, 1024), BF16),
            *reducer_scratch(1024),
            pltpu.SemaphoreType.DMA((4,)), pltpu.SemaphoreType.DMA((4,)),
            *wire_scratch(8, 4),
        ],
        compiler_params=pltpu.CompilerParams(
            collective_id=1, has_side_effects=True, vmem_limit_bytes=VMEM_BYTES),
        name="middle",
    )(post, back, wg, wu, wd, resid, gains)


class Homing:
    def __init__(self, place, wire, grad, came, sums, far, turned, home):
        self.p, self.wire, self.grad, self.came, self.sums = place, wire, grad, came, sums
        self.far, self.turned, self.home = far, turned, home
        self.by_columns = len(grad.shape) == 5

    def side(self, ref, y):
        return ref.at[:, :, y] if self.by_columns else ref.at[:, y]

    def start(self):
        self.kept = self.wire.own(self.side(self.grad, self.p.y), self.sums)
        self.sent = self.wire.send(self.side(self.grad, self.p.other_y), self.came, self.p.y_dev)

    def plane(self, ref, z):
        return ref.at[:, z] if self.by_columns else ref.at[z]

    def spread(self):
        self.kept.wait()
        self.sent.wait_recv()

        def add(z, carry):
            at = (slice(None), z) if self.by_columns else (z,)
            self.sums[at] = (self.sums[at].astype(F32) + self.came[at].astype(F32)).astype(BF16)
            return carry

        lax.fori_loop(0, self.p.planes, add, 0)
        self.out = [
            self.wire.send(self.plane(self.sums, self.p.z_at(step)), self.far.at[step - 1], self.p.z_dev(step))
            for step in range(1, self.p.planes)
        ]

    def gather(self):
        for copy in self.out:
            copy.wait_recv()
        at = (slice(None), self.p.z) if self.by_columns else (self.p.z,)
        total = self.sums[at].astype(F32)
        for step in range(1, self.p.planes):
            total = total + self.far[step - 1].astype(F32)
        if not self.by_columns:
            self.home[...] = total
            return
        leave, arrive, own = self.turned
        s = self.p.s
        leave[...] = total.astype(BF16)
        own[...] = total
        self.back = []
        for dev in (self.p.core_dev, self.p.x_dev, self.p.far_dev):
            self.back.append((dev[0], self.wire.send(leave.at[dev[0]], arrive.at[s], dev)))

    def finish(self):
        if not self.by_columns:
            return
        leave, arrive, own = self.turned
        width = own.shape[-1]
        s = self.p.s
        self.home[:, pl.ds(pl.multiple_of(s * width, RUN), width)] = own[s]
        for owner, copy in self.back:
            copy.wait_recv()
            self.home[:, pl.ds(pl.multiple_of(owner * width, RUN), width)] = arrive[owner].astype(F32)


def homing_scratch(planes, shape):
    kept = shape[:-3] + shape[-2:]
    once = shape[:-4] + shape[-2:]
    found = [VMEM(kept, BF16), VMEM(kept, BF16), VMEM((planes - 1, *once), BF16)]
    if len(shape) == 5:
        found += [VMEM(once, BF16), VMEM(once, BF16), VMEM(once, F32)]
    return found


def homing_of(place, wire, grad, home, refs):
    refs = list(refs)
    count = 6 if len(grad.shape) == 5 else 3
    mine, rest = refs[:count], refs[count:]
    return Homing(place, wire, grad, *mine[:3], mine[3:], home), rest


def turn_kernel(
    planes,
    order, attn, query, key, value, q_unit, k_unit, roots, mixed, lse, wo, cosine, sine, gains,
    y_out, y_keep, sums_in, grad_g, grad_u, grad_d,
    d_q, d_k, d_v, grad_o, sums, block_out, home_g, home_u, home_d,
    d_mixed, attn_sorted, keys_grad, values_grad, y_in, *rest,
):
    p = Place(planes)
    wire = Wire(*rest[-3:])
    refs = list(rest[:-3])
    rows = y_keep.shape[1]
    length = 4 * rows
    p.meet()
    homes = []
    for grad, home in ((grad_d, home_d), (grad_g, home_g), (grad_u, home_u)):
        one, refs = homing_of(p, wire, grad, home, refs)
        one.start()
        homes.append(one)
    y_sent = [wire.send(y_out.at[micro], y_in.at[micro], p.x_dev) for micro in range(2)]

    def draw(step, carry):
        here = pl.ds(pl.multiple_of(step * BLOCK, BLOCK), BLOCK)
        low = two_runs(attn, order[step * 2], order[step * 2 + 1])
        attn_sorted[here] = low
        d_mixed[here] = dot(low, wo[...], NARROW).astype(BF16)
        return carry

    lax.fori_loop(0, 2 * length // BLOCK, draw, 0)

    def out_tile(at, carry):
        cut = pl.ds(pl.multiple_of(at * BLOCK, BLOCK), BLOCK)
        grad_o[cut] = dot(mixed[:, cut], attn_sorted[...], TALL).astype(BF16)
        return carry

    lax.fori_loop(0, 2, out_tile, 0)
    sums[...] = sums_in[...]

    def lane_of(ref, here, lane):
        held = ref[here, :]
        lanes = lax.broadcasted_iota(jnp.int32, held.shape, 1)
        return jnp.sum(jnp.where(lanes == lane, held, 0.0), axis=1, keepdims=True)

    def norm_home(grad, cos, sin, unit, root, gain):
        turned = grad * cos - pltpu.roll(grad, HEAD_DIM // 2, 1) * sin
        scaled = turned * gain
        back = root * (scaled - unit * row_mean(scaled * unit))
        return back, jnp.sum(turned * unit, axis=0, keepdims=True)

    def attend_back(step, carry):
        micro, head = step // 2, lax.rem(step, 2)
        keys_at = pl.ds(pl.multiple_of(head * HEAD_DIM, HEAD_DIM), HEAD_DIM)
        lanes = [pl.ds(pl.multiple_of(head * 2 * HEAD_DIM + g * HEAD_DIM, HEAD_DIM), HEAD_DIM) for g in range(2)]
        q_gain, k_gain = gains[2:3, 0:RUN], gains[3:4, 0:RUN]
        keys_grad[...] = jnp.zeros_like(keys_grad)
        values_grad[...] = jnp.zeros_like(values_grad)
        for block in range(length // BLOCK):
            here = pl.ds(pl.multiple_of(micro * length + block * BLOCK, BLOCK), BLOCK)
            seen = (block + 1) * BLOCK
            past = pl.ds(pl.multiple_of(micro * length, BLOCK), seen)
            asked = jnp.concatenate([query[here, lane] for lane in lanes], axis=0)
            pulled = jnp.concatenate([d_mixed[here, lane] for lane in lanes], axis=0)
            given = jnp.concatenate([mixed[here, lane] for lane in lanes], axis=0)
            level = jnp.concatenate(
                [lse[step, pl.ds(block * BLOCK, BLOCK), g : g + 1] for g in range(2)], axis=0)
            delta = jnp.sum(pulled.astype(F32) * given.astype(F32), axis=1, keepdims=True)
            scores = dot(asked, key[past, keys_at], NARROW)
            line = lax.broadcasted_iota(jnp.int32, (2 * BLOCK, seen), 0)
            line = jnp.where(line >= BLOCK, line - BLOCK, line) + block * BLOCK
            column = lax.broadcasted_iota(jnp.int32, (2 * BLOCK, seen), 1)
            weight = jnp.exp2(scores * (SCALE * LOG2E) - level)
            weight = jnp.where(column <= line, weight, 0.0)
            d_soft = dot(pulled, value[past, keys_at], NARROW)
            d_scores = (weight * (d_soft - delta)).astype(BF16)
            values_grad[0:seen] += dot(weight.astype(BF16), pulled, TALL)
            keys_grad[0:seen] += dot(d_scores, asked, TALL)
            moved = dot(d_scores, key[past, keys_at]) * SCALE
            spin = slice(block * BLOCK, (block + 1) * BLOCK)
            for g, lane in enumerate(lanes):
                root = lane_of(roots, here, head * 2 + g)
                unit = q_unit[here, lane].astype(F32)
                back, gained = norm_home(
                    moved[g * BLOCK : (g + 1) * BLOCK], cosine[spin], sine[spin], unit, root, q_gain)
                d_q[here, lane] = back.astype(BF16)
                sums[1:2, 0:RUN] += gained
        everything = pl.ds(pl.multiple_of(micro * length, BLOCK), length)
        root = lane_of(roots, everything, head + 4)
        unit = k_unit[everything, keys_at].astype(F32)
        back, gained = norm_home(keys_grad[...] * SCALE, cosine[...], sine[...], unit, root, k_gain)
        d_k[everything, keys_at] = back.astype(BF16)
        sums[2:3, 0:RUN] += gained
        d_v[everything, keys_at] = values_grad[...].astype(BF16)
        return carry

    lax.fori_loop(0, 1, attend_back, 0)
    homes[0].spread()
    lax.fori_loop(1, 2, attend_back, 0)
    homes[1].spread()
    for micro in range(2):
        y_sent[micro].wait_recv()
        block_out[micro] = (y_keep[micro] + y_in[micro].astype(F32)).astype(BF16)
    lax.fori_loop(2, 4, attend_back, 0)
    homes[2].spread()
    for one in homes:
        one.gather()
    for one in homes:
        one.finish()
    wire.close()


def turn(planes, order, attn, query, key, value, q_unit, k_unit, roots, mixed, lse, wo, cosine, sine, gains,
         y_out, y_keep, sums, grad_g, grad_u, grad_d):
    rows = y_keep.shape[1]
    length = 4 * rows
    total = 2 * length
    shapes = [
        jax.ShapeDtypeStruct((total, 512), BF16), jax.ShapeDtypeStruct((total, 256), BF16),
        jax.ShapeDtypeStruct((total, 256), BF16), jax.ShapeDtypeStruct((512, 1024), BF16),
        jax.ShapeDtypeStruct((8, 1024), F32), jax.ShapeDtypeStruct((2, rows, 1024), BF16),
        jax.ShapeDtypeStruct((grad_g.shape[3], 4 * grad_g.shape[4]), F32),
        jax.ShapeDtypeStruct((grad_u.shape[3], 4 * grad_u.shape[4]), F32),
        jax.ShapeDtypeStruct(grad_d.shape[2:], F32),
    ]
    vm = pl.BlockSpec(memory_space=VMEM)
    hb = pl.BlockSpec(memory_space=ANY)
    sm = pl.BlockSpec(memory_space=pltpu.SMEM)
    return pl.pallas_call(
        functools.partial(turn_kernel, planes),
        out_shape=shapes,
        in_specs=[sm] + [vm] * 13 + [hb, vm, vm] + [hb] * 3,
        out_specs=[vm] * len(shapes),
        scratch_shapes=[
            VMEM((total, 512), BF16), VMEM((total, 1024), BF16), VMEM((length, HEAD_DIM), F32),
            VMEM((length, HEAD_DIM), F32), VMEM((2, rows, 1024), BF16),
            *homing_scratch(planes, grad_d.shape), *homing_scratch(planes, grad_g.shape),
            *homing_scratch(planes, grad_u.shape), *wire_scratch(24, 4),
        ],
        compiler_params=pltpu.CompilerParams(
            collective_id=2, has_side_effects=True, vmem_limit_bytes=VMEM_BYTES),
        name="turn",
    )(order, attn, query, key, value, q_unit, k_unit, roots, mixed, lse, wo, cosine, sine, gains,
      y_out, y_keep, sums, grad_g, grad_u, grad_d)


def last_kernel(
    planes,
    rank, normed, d_q, d_k, d_v, wq, wk, wv, tokens, d_resid, gains, sums_in, grad_o,
    token_grad, sums, home_q, home_k, home_v, home_o,
    grad_q, grad_k, grad_v, part, sums_out, sums_came,
    core_out, core_in, x_out, x_in, keep, core_s, core_r, x_s, x_r, *rest,
):
    p = Place(planes)
    s, f = p.s, p.f
    wire = Wire(*rest[-3:])
    refs = list(rest[:-3])
    reducer = Reducer(p, part, core_out, core_in, x_out, x_in, keep, (core_s, core_r, x_s, x_r))
    rows = tokens.shape[1]
    length = 4 * rows
    p.meet()
    out_home, refs = homing_of(p, wire, grad_o, home_o, refs)
    out_home.start()
    homes = []
    for grad, pulled, home in ((grad_q, d_q, home_q), (grad_k, d_k, home_k), (grad_v, d_v, home_v)):
        def tile(at, carry, grad=grad, pulled=pulled):
            cut = pl.ds(pl.multiple_of(at * BLOCK, BLOCK), BLOCK)
            found = dot(joined(normed[:, :, cut]), flat(pulled), TALL).astype(BF16)
            grad[at] = found.reshape(grad.shape[1:])
            return carry

        lax.fori_loop(0, 4, tile, 0)
        one, refs = homing_of(p, wire, grad, home, refs)
        one.start()
        homes.append(one)
    sums[...] = sums_in[...]

    def pull(step, carry):
        micro, block = reducer.block(step)
        at = micro * (length // RUN) + block * 2
        runs = (rank[at], rank[at + 1])
        found = dot(two_runs(d_q, *runs), wq[...], NARROW)
        found += dot(two_runs(d_k, *runs), wk[...], NARROW)
        found += dot(two_runs(d_v, *runs), wv[...], NARROW)
        part[...] = found
        sums[3:4] += jnp.sum(found * two_runs(normed, *runs).astype(F32), axis=0, keepdims=True)
        reducer.take(step)
        return carry

    lax.fori_loop(0, 8, pull, 0)
    out_home.spread()
    sums[3:4] = sums[3:4] / gains[0:1]

    def exchange(stage, devices, base):
        sums_out[stage] = sums[...]
        sent = [wire.send(sums_out.at[stage], sums_came.at[base + at], dev) for at, dev in enumerate(devices)]
        return base, sent

    def absorb(state):
        base, sent = state
        total = sums[...]
        for at, copy in enumerate(sent):
            copy.wait_recv()
            total = total + sums_came[base + at]
        sums[...] = total

    state = exchange(0, (p.core_dev, p.x_dev, p.far_dev), 0)
    for one in homes:
        one.spread()
    absorb(state)
    state = exchange(1, [p.z_dev(step) for step in range(1, planes)], 3)
    out_home.gather()
    absorb(state)
    state = exchange(2, [p.y_dev], 2 + planes)
    for micro in range(2):
        grad = reducer.total(micro)
        held = tokens[micro].astype(F32)
        root = lax.rsqrt(row_mean(held * held) + EPSILON)
        unit = held * root
        scaled = grad * gains[0:1]
        token_grad[micro] = d_resid[micro] + root * (scaled - unit * row_mean(scaled * unit))
    for one in homes:
        one.gather()
    absorb(state)
    for one in homes:
        one.finish()
    reducer.close()
    wire.close()


def last(planes, rank, normed, d_q, d_k, d_v, wq, wk, wv, tokens, d_resid, gains, sums, grad_o):
    nf = 2 * planes
    rows = tokens.shape[1]
    widths = [wq.shape[1], wk.shape[1], wv.shape[1]]
    deep = 1024 // (4 * nf)
    grads = [(4, planes, 2, deep, wide) for wide in widths]
    shapes = [
        jax.ShapeDtypeStruct((2, rows, 1024), F32), jax.ShapeDtypeStruct((8, 1024), F32),
        *[jax.ShapeDtypeStruct((deep, 4 * wide), F32) for wide in widths],
        jax.ShapeDtypeStruct(grad_o.shape[2:], F32),
    ]
    vm = pl.BlockSpec(memory_space=VMEM)
    hb = pl.BlockSpec(memory_space=ANY)
    sm = pl.BlockSpec(memory_space=pltpu.SMEM)
    scratch = [VMEM(shape, BF16) for shape in grads]
    scratch += [VMEM((BLOCK, 1024), F32), VMEM((3, 8, 1024), F32), VMEM((3 + planes, 8, 1024), F32)]
    scratch += [*reducer_scratch(1024), *homing_scratch(planes, grad_o.shape)]
    for shape in grads:
        scratch += homing_scratch(planes, shape)
    return pl.pallas_call(
        functools.partial(last_kernel, planes),
        out_shape=shapes,
        in_specs=[sm] + [vm] * 11 + [hb],
        out_specs=[vm] * len(shapes),
        scratch_shapes=scratch + wire_scratch(48, 4),
        compiler_params=pltpu.CompilerParams(
            collective_id=3, has_side_effects=True, vmem_limit_bytes=VMEM_BYTES),
        name="last",
    )(rank, normed, d_q, d_k, d_v, wq, wk, wv, tokens, d_resid, gains, sums, grad_o)


def run_tables(positions):
    runs = positions.shape[1] // RUN
    rank = positions[:, ::RUN] // RUN
    index = jnp.arange(runs, dtype=jnp.int32)
    order = jnp.sum(jnp.where(rank[:, :, None] == index, index[None, :, None], 0), axis=1)
    base = jnp.arange(positions.shape[0], dtype=jnp.int32)[:, None] * runs
    return (order + base).reshape(-1), (rank + base).reshape(-1)


def kernel_body(tokens, positions, g_in, g_post, g_query, g_key, w_query, w_key, w_value,
                w_out, w_gate, w_up, w_down, cotangent):
    planes = lax.axis_size("fsdp") // 2
    length = positions.shape[2]
    order, rank = run_tables(positions[:, 0])
    tile = jnp.stack(
        [jnp.pad(item.astype(F32), (0, RUN - item.shape[0])) for item in (g_in, g_post, g_query, g_key)])
    tile = jnp.pad(tile, ((0, 4), (0, 0)))
    cosine, sine = rope_tables(jnp.arange(length))
    cosine, sine = cosine[:, 0], sine[:, 0]
    half = HEAD_DIM // 2
    sine = jnp.concatenate([-sine[:, :half], sine[:, half:]], axis=1)
    near = tokens[:, 0]
    shards = (w_query, w_key, w_value, w_out, w_gate, w_up, w_down)
    (wq, wk, wv, wo, wg, wu, wd, normed, query, key, value, q_unit, k_unit, roots, mixed, lse,
     resid, post, back, gains) = front(
        planes, order, rank, near, cotangent[:, 0], tile, cosine, sine, shards)
    wq, wk, wv, wo, wg, wu, wd = [
        item.reshape(-1, item.shape[-1]) for item in (wq, wk, wv, wo, wg, wu, wd)]
    post, back = post.reshape(-1, post.shape[-1]), back.reshape(-1, back.shape[-1])
    grad_g, grad_u, grad_d, y_out, y_keep, d_resid, attn, sums = middle(
        planes, post, back, wg, wu, wd, resid, gains)
    apart = lambda item: item.reshape(-1, RUN, item.shape[-1])
    columns = lambda item: item.reshape(4, planes, 2, -1, item.shape[-1])
    lines = lambda item: item.reshape(planes, 2, -1, item.shape[-1])
    d_q, d_k, d_v, grad_o, sums, block_out, home_g, home_u, home_d = turn(
        planes, order, apart(attn), query, key, value, q_unit, k_unit, roots,
        mixed.reshape(-1, mixed.shape[-1]), lse,
        wo, cosine, sine, gains, y_out, y_keep, sums, columns(grad_g), columns(grad_u), lines(grad_d))
    token_grad, sums, home_q, home_k, home_v, home_o = last(
        planes, rank, apart(normed), apart(d_q), apart(d_k), apart(d_v), wq, wk, wv, near, d_resid, gains, sums, lines(grad_o))
    me = lax.axis_index("seq") * (2 * planes) + lax.axis_index("fsdp")
    small = [
        lax.dynamic_slice(sums, (row, me * item.shape[0]), (1, item.shape[0]))[0]
        for row, item in ((3, g_in), (0, g_post), (1, g_query), (2, g_key))
    ]
    return (block_out[:, None], token_grad[:, None], *small, home_q, home_k, home_v, home_o,
            home_g, home_u, home_d)


def solution(mesh):
    both = ("seq", "fsdp")
    act = P(None, "fsdp", "seq", None)
    vec, mat = P(both), P(both, None)

    def body(*args):
        rows = args[6].shape[0]
        fits = mesh.shape["seq"] == 4 and mesh.shape["fsdp"] % 2 == 0 and rows % 16 == 0
        return (kernel_body if fits else plain_body)(*args)

    return jax.shard_map(
        body,
        mesh=mesh,
        in_specs=(act, P(None, "fsdp", None), *[vec] * 4, *[mat] * 7, act),
        out_specs=(act, act, *[vec] * 4, *[mat] * 7),
        check_vma=False,
    )
```

```python
import functools

import jax
import jax.numpy as jnp
from jax import lax
from jax.experimental import pallas as pl
from jax.experimental.pallas import tpu as pltpu
from jax.sharding import PartitionSpec as P

HEADS = 16
KV_HEADS = 8
HEAD_DIM = 128
EPSILON = 1e-06
ROPE_BASE = 1000000.0
NEGATIVE = -1e30
F32 = jnp.float32
BF16 = jnp.bfloat16


def inverse_root(values):
    return lax.rsqrt(jnp.mean(values * values, axis=-1, keepdims=True) + EPSILON)


def rope_tables(token_pos):
    half_width = HEAD_DIM // 2
    frequency = ROPE_BASE ** (-(jnp.arange(half_width, dtype=F32) * 2.0 / HEAD_DIM))
    angles = token_pos.astype(F32)[:, None] * frequency[None, :]
    cosine = jnp.cos(angles)
    sine = jnp.sin(angles)
    return (
        jnp.concatenate([cosine, cosine], axis=-1)[:, None, :],
        jnp.concatenate([sine, sine], axis=-1)[:, None, :],
    )


def rotate(values, cosine, sine):
    half_width = values.shape[-1] // 2
    turned = jnp.concatenate([-values[..., half_width:], values[..., :half_width]], axis=-1)
    return values * cosine + turned * sine


def rotate_back(grads, cosine, sine):
    half_width = grads.shape[-1] // 2
    scaled = grads * sine
    turned = jnp.concatenate([scaled[..., half_width:], -scaled[..., :half_width]], axis=-1)
    return grads * cosine + turned


def norm_back(grads, values, inverse, gain):
    scaled = grads * gain
    return inverse * scaled - values * inverse**3 * jnp.mean(
        scaled * values, axis=-1, keepdims=True
    )


def mul(eq, left, right):
    return jnp.einsum(eq, left, right, preferred_element_type=F32)


def sum_scatter(part, axis):
    return lax.psum_scatter(part.astype(BF16), axis, scatter_dimension=0, tiled=True).astype(F32)


def slice_weights(item, ways):
    rows = item.shape[0]
    return item.reshape(rows, ways, -1).transpose(1, 0, 2)


def plain_body(tokens, positions, g_in, g_post, g_query, g_key, w_query, w_key, w_value,
               w_out, w_gate, w_up, w_down, cotangent):
    ways = lax.axis_size("seq")
    heads, kv_heads = HEADS // ways, KV_HEADS // ways
    micro, rows, width = tokens.shape[0], tokens.shape[2], tokens.shape[3]
    length = positions.shape[2]
    everyone = ("seq", "fsdp")
    gains = [
        lax.all_gather(item, everyone, axis=0, tiled=True).astype(F32)
        for item in (g_in, g_post, g_query, g_key)
    ]
    gain_in, gain_post, gain_query, gain_key = gains

    def spread(*items):
        packed = jnp.concatenate([slice_weights(item, ways) for item in items], axis=2)
        packed = lax.all_to_all(packed, "seq", 0, 0, tiled=True)
        packed = lax.all_gather(packed, "fsdp", axis=1, tiled=True)
        packed = packed.reshape(-1, packed.shape[2])
        sizes = [item.shape[1] // ways for item in items]
        cuts = [sum(sizes[: at + 1]) for at in range(len(sizes) - 1)]
        return jnp.split(packed, cuts, axis=1)

    wq, wk, wv = spread(w_query, w_key, w_value)
    wo = lax.all_gather(w_out, "fsdp", axis=0, tiled=True)
    wg, wu = spread(w_gate, w_up)
    wd = lax.all_gather(w_down, "fsdp", axis=0, tiled=True)
    scale = HEAD_DIM ** (-0.5)

    def gather_rows(item):
        return lax.all_gather(item, "seq", axis=0, tiled=True)

    grads = None
    outs, token_grads = [], []
    for at in range(micro):
        inputs = tokens[at, 0].astype(F32)
        pos = positions[at, 0]
        cosine, sine = rope_tables(pos)
        allowed = pos[None, :] <= pos[:, None]
        inv_in = inverse_root(inputs)
        normed = gather_rows((inputs * inv_in * gain_in).astype(BF16))
        q_raw = mul("td,df->tf", normed, wq).reshape(length, heads, HEAD_DIM)
        k_raw = mul("td,df->tf", normed, wk).reshape(length, kv_heads, HEAD_DIM)
        value = mul("td,df->tf", normed, wv).astype(BF16).reshape(length, kv_heads, HEAD_DIM)
        inv_q, inv_k = inverse_root(q_raw), inverse_root(k_raw)
        query = rotate(q_raw * inv_q * gain_query, cosine, sine).astype(BF16)
        query = query.reshape(length, kv_heads, heads // kv_heads, HEAD_DIM)
        key = rotate(k_raw * inv_k * gain_key, cosine, sine).astype(BF16)
        scores = jnp.where(allowed, mul("qjgd,kjd->jgqk", query, key) * scale, NEGATIVE)
        soft = jax.nn.softmax(scores, axis=-1)
        soft_low = soft.astype(BF16)
        mixed = mul("jgqk,kjd->qjgd", soft_low, value).astype(BF16).reshape(length, -1)
        resid = inputs + sum_scatter(mul("th,hd->td", mixed, wo), "seq")
        inv_post = inverse_root(resid)
        post = gather_rows((resid * inv_post * gain_post).astype(BF16))
        gate = mul("td,df->tf", post, wg)
        upper = mul("td,df->tf", post, wu)
        sigma = jax.nn.sigmoid(gate)
        hidden = (gate * sigma * upper).astype(BF16)
        outs.append((resid + sum_scatter(mul("tf,fd->td", hidden, wd), "seq")).astype(BF16))
        back_low = cotangent[at, 0]
        back = gather_rows(back_low)
        g_down = mul("tf,td->fd", hidden, back)
        d_hidden = mul("td,fd->tf", back, wd)
        d_gate = (d_hidden * upper * sigma * (1.0 + gate * (1.0 - sigma))).astype(BF16)
        d_upper = (d_hidden * gate * sigma).astype(BF16)
        g_gate = mul("td,tf->df", post, d_gate)
        g_up = mul("td,tf->df", post, d_upper)
        d_post = sum_scatter(mul("tf,df->td", d_gate, wg) + mul("tf,df->td", d_upper, wu), "seq")
        post_grad = jnp.sum(d_post * resid * inv_post, axis=0)
        d_resid = back_low.astype(F32) + norm_back(d_post, resid, inv_post, gain_post)
        d_attn = gather_rows(d_resid.astype(BF16))
        g_out = mul("th,td->hd", mixed, d_attn)
        d_mixed = mul("td,hd->th", d_attn, wo).astype(BF16)
        d_mixed = d_mixed.reshape(length, kv_heads, heads // kv_heads, HEAD_DIM)
        d_soft = mul("qjgd,kjd->jgqk", d_mixed, value)
        d_scores = (soft * (d_soft - jnp.sum(d_soft * soft, axis=-1, keepdims=True))).astype(BF16)
        d_query = mul("jgqk,kjd->qjgd", d_scores, key) * scale
        d_key = mul("jgqk,qjgd->kjd", d_scores, query) * scale
        d_value = mul("jgqk,qjgd->kjd", soft_low, d_mixed).astype(BF16).reshape(length, -1)
        key_turn = rotate_back(d_key, cosine, sine)
        query_turn = rotate_back(d_query.reshape(length, heads, HEAD_DIM), cosine, sine)
        key_grad = jnp.sum(key_turn * k_raw * inv_k, axis=(0, 1))
        query_grad = jnp.sum(query_turn * q_raw * inv_q, axis=(0, 1))
        d_key = norm_back(key_turn, k_raw, inv_k, gain_key).astype(BF16).reshape(length, -1)
        d_query = norm_back(query_turn, q_raw, inv_q, gain_query).astype(BF16).reshape(length, -1)
        g_query_w = mul("td,tf->df", normed, d_query)
        g_key_w = mul("td,tf->df", normed, d_key)
        g_value_w = mul("td,tf->df", normed, d_value)
        d_normed = mul("tf,df->td", d_query, wq) + mul("tf,df->td", d_key, wk)
        d_normed = sum_scatter(d_normed + mul("tf,df->td", d_value, wv), "seq")
        in_grad = jnp.sum(d_normed * inputs * inv_in, axis=0)
        token_grads.append(d_resid + norm_back(d_normed, inputs, inv_in, gain_in))
        found = [in_grad, post_grad, query_grad, key_grad, g_query_w, g_key_w, g_value_w,
                 g_out, g_gate, g_up, g_down]
        grads = found if grads is None else [left + right for left, right in zip(grads, found)]

    small = [lax.psum_scatter(item, everyone, scatter_dimension=0, tiled=True) for item in grads[:4]]

    def columns_home(item):
        full, wide = item.shape
        item = item.reshape(ways, -1, wide).astype(BF16)
        item = lax.psum_scatter(item, "fsdp", scatter_dimension=1, tiled=True)
        item = lax.all_to_all(item, "seq", 0, 0, tiled=True)
        return item.transpose(1, 0, 2).reshape(item.shape[1], ways * wide).astype(F32)

    def rows_home(item):
        return sum_scatter(item, "fsdp")

    large = [columns_home(item) for item in grads[4:7]] + [rows_home(grads[7])]
    large += [columns_home(item) for item in grads[8:10]] + [rows_home(grads[10])]
    return (jnp.stack(outs)[:, None], jnp.stack(token_grads)[:, None], *small, *large)


MESH = pl.DeviceIdType.MESH
ANY = pl.ANY
VMEM = pltpu.VMEM
RUN = 128
BLOCK = 256
NARROW = (((1,), (1,)), ((), ()))
TALL = (((0,), (0,)), ((), ()))
PLAIN = (((1,), (0,)), ((), ()))
LOG2E = 1.4426950408889634
SCALE = HEAD_DIM ** (-0.5)
VMEM_BYTES = 63 * 2**20


def dot(left, right, dims=PLAIN):
    return lax.dot_general(left, right, dims, preferred_element_type=F32)


class Place:
    def __init__(self, planes):
        self.planes = planes
        self.s = lax.axis_index("seq")
        self.f = lax.axis_index("fsdp")
        self.x, self.c = self.s // 2, self.s % 2
        self.z, self.y = self.f // 2, self.f % 2
        self.other_y = 1 - self.y
        self.core_dev = (self.x * 2 + 1 - self.c, self.f)
        self.x_dev = ((1 - self.x) * 2 + self.c, self.f)
        self.far_dev = ((1 - self.x) * 2 + 1 - self.c, self.f)
        self.y_dev = (self.s, self.z * 2 + self.other_y)

    def z_at(self, step):
        return lax.rem(self.z + step, self.planes)

    def z_dev(self, step):
        return (self.s, self.z_at(step) * 2 + self.y)

    def peers(self):
        return [self.core_dev, self.x_dev, self.far_dev, self.y_dev] + [
            self.z_dev(step) for step in range(1, self.planes)
        ]

    def meet(self):
        barrier = pltpu.get_barrier_semaphore()
        for peer in self.peers():
            pl.semaphore_signal(barrier, inc=1, device_id=peer, device_id_type=MESH)
        pl.semaphore_wait(barrier, 3 + self.planes)


def remote(src, dst, out_sem, in_sem, device):
    return pltpu.make_async_remote_copy(
        src_ref=src, dst_ref=dst, send_sem=out_sem, recv_sem=in_sem,
        device_id=device, device_id_type=MESH,
    )


class Wire:
    def __init__(self, out_sems, in_sems, own_sems):
        self.out_sems, self.in_sems, self.own_sems = out_sems, in_sems, own_sems
        self.sent, self.owned = [], 0

    def send(self, src, dst, device):
        at = len(self.sent)
        copy = remote(src, dst, self.out_sems.at[at], self.in_sems.at[at], device)
        copy.start()
        self.sent.append(copy)
        return copy

    def own(self, src, dst):
        copy = pltpu.make_async_copy(src, dst, self.own_sems.at[self.owned])
        copy.start()
        self.owned += 1
        return copy

    def close(self):
        for copy in self.sent:
            copy.wait_send()


def wire_scratch(copies, owns):
    return [
        pltpu.SemaphoreType.DMA((copies,)),
        pltpu.SemaphoreType.DMA((copies,)),
        pltpu.SemaphoreType.DMA((owns,)),
    ]


class Reducer:
    def __init__(self, place, part, core_out, core_in, x_out, x_in, keep, sems):
        self.place, self.part = place, part
        self.core_out, self.core_in = core_out, core_in
        self.x_out, self.x_in, self.keep = x_out, x_in, keep
        self.core_s, self.core_r, self.x_s, self.x_r = sems

    def block(self, step):
        p = self.place
        turn = step % 4
        x = jnp.where(turn < 2, 1 - p.x, p.x)
        c = jnp.where(turn % 2 == 0, 1 - p.c, p.c)
        return step // 4, x * 2 + c

    def core_copy(self, slot):
        return remote(self.core_out.at[slot], self.core_in.at[slot], self.core_s.at[slot],
                      self.core_r.at[slot], self.place.core_dev)

    def x_copy(self, micro):
        return remote(self.x_out.at[micro], self.x_in.at[micro], self.x_s.at[micro],
                      self.x_r.at[micro], self.place.x_dev)

    def take(self, step, send_x=True):
        micro, turn = step // 4, step % 4

        @pl.when(turn % 2 == 0)
        def _():
            slot = micro * 2 + turn // 2
            self.core_out[slot] = self.part[...].astype(BF16)
            self.core_copy(slot).start()

        @pl.when(turn == 1)
        def _():
            slot = micro * 2
            self.core_copy(slot).wait_recv()
            self.x_out[micro] = (self.part[...] + self.core_in[slot].astype(F32)).astype(BF16)
            if send_x:
                self.x_copy(micro).start()

        @pl.when(turn == 3)
        def _():
            slot = micro * 2 + 1
            self.core_copy(slot).wait_recv()
            self.keep[micro] = self.part[...] + self.core_in[slot].astype(F32)

    def total(self, micro):
        self.x_copy(micro).wait_recv()
        return self.keep[micro] + self.x_in[micro].astype(F32)

    def close(self, send_x=True):
        for slot in range(4):
            self.core_copy(slot).wait_send()
        if send_x:
            for micro in range(2):
                self.x_copy(micro).wait_send()


def reducer_scratch(width):
    return [
        VMEM((4, BLOCK, width), BF16),
        VMEM((4, BLOCK, width), BF16),
        VMEM((2, BLOCK, width), BF16),
        VMEM((2, BLOCK, width), BF16),
        VMEM((2, BLOCK, width), F32),
        pltpu.SemaphoreType.DMA((4,)),
        pltpu.SemaphoreType.DMA((4,)),
        pltpu.SemaphoreType.DMA((2,)),
        pltpu.SemaphoreType.DMA((2,)),
    ]


def row_mean(values):
    return jnp.mean(values, axis=-1, keepdims=True)


def spread_gain(table, row, devices, width):
    per = width // devices
    lanes = lax.broadcasted_iota(jnp.int32, (RUN, width), 0)
    column = lax.broadcasted_iota(jnp.int32, (RUN, width), 1)
    pick = (lanes == lax.rem(column, per)).astype(BF16)
    picked = dot(table, pick)
    rows = lax.broadcasted_iota(jnp.int32, (devices * 8, width), 0)
    owner = lax.broadcasted_iota(jnp.int32, (devices * 8, width), 1) // per
    return jnp.sum(jnp.where(rows == owner * 8 + row, picked, 0.0), axis=0, keepdims=True)


def two_runs(ref, first, second):
    return jnp.concatenate([ref[first], ref[second]], axis=0)


def joined(value):
    return value.reshape(-1, value.shape[-1])


def flat(ref):
    return joined(ref[...])


def front_kernel(
    planes,
    order, rank, tokens, cotangent, gain_tile, cosine, sine,
    s_q, s_k, s_v, s_o, s_g, s_u, s_d,
    wq_out, wk_out, wv_out, wo_out, wg, wu, wd,
    normed_out, query_out, key_out, value_out, q_unit_out, k_unit_out, roots_out, mixed_out, lse_out,
    resid_out, post_full, back_full, gains,
    wq, wk, wv, wo, normed, query, key, value, q_unit, k_unit, roots, mixed, lse, resid,
    tok_full, gain_all, post_own, part,
    core_out, core_in, x_out, x_in, keep, core_s, core_r, x_s, x_r,
    out_sems, in_sems, own_sems,
):
    p = Place(planes)
    s, f = p.s, p.f
    devices = 8 * planes
    wire = Wire(out_sems, in_sems, own_sems)
    reducer = Reducer(p, part, core_out, core_in, x_out, x_in, keep, (core_s, core_r, x_s, x_r))
    rows = BLOCK
    mine = pl.ds(s * rows, rows)
    theirs = pl.ds(p.x_dev[0] * rows, rows)
    length = 4 * rows
    p.meet()

    gain_all[s, f] = gain_tile[...]
    gain_in = [wire.send(gain_all.at[s, f], gain_all.at[s, f], dev)
               for dev in (p.core_dev, p.x_dev, p.far_dev)]

    def spread_columns(item, full):
        wide = item.shape[1] // 4
        came = [wire.own(item.at[:, pl.ds(s * wide, wide)], full.at[s, f])]
        sent = []
        for dev in (p.core_dev, p.x_dev, p.far_dev):
            sent.append(wire.send(item.at[:, pl.ds(dev[0] * wide, wide)], full.at[s, f], dev))
        return came, sent

    first = [spread_columns(item, full) for item, full in ((s_q, wq), (s_k, wk), (s_v, wv))]
    tok_here, tok_x, tok_core = [], [], []
    for micro in range(2):
        to = tok_full.at[pl.ds(micro * (length // RUN) + s * 2, 2)]
        tok_here.append(wire.own(tokens.at[micro], to))
        tok_x.append(wire.send(tokens.at[micro], to, p.x_dev))
        tok_core.append(wire.send(tokens.at[micro], to, p.core_dev))
    second = [spread_columns(item, full) for item, full in ((s_g, wg), (s_u, wu))]

    def arrived(group):
        came, sent = group
        for copy in came:
            copy.wait()
        for copy in sent:
            copy.wait_recv()

    def blocks(full, at):
        return full.at[:, at] if len(full.shape) == 4 else full.at[at]

    def push_planes(full, side=True):
        here = blocks(full, f)
        far = [wire.send(here, here, p.z_dev(step)) for step in range(1, planes)]
        return far, [wire.send(here, here, p.y_dev)] if side else []

    def forward(full, state):
        far, side = state
        for step, copy in enumerate(far, 1):
            copy.wait_recv()
            there = blocks(full, p.z_at(planes - step) * 2 + p.y)
            side.append(wire.send(there, there, p.y_dev))

    def settle(state):
        for copy in state[1]:
            copy.wait_recv()

    def push_rows(item, full, side=True):
        kept = wire.own(item, full.at[f])
        far = [wire.send(item, full.at[f], p.z_dev(step)) for step in range(1, planes)]
        return kept, (far, [wire.send(item, full.at[f], p.y_dev)] if side else [])

    for copy in gain_in:
        copy.wait_recv()
    gain_state = push_planes(gain_all)
    states = []
    for group, full in zip(first, (wq, wk, wv)):
        arrived(group)
        states.append(push_planes(full))
    forward(gain_all, gain_state)
    for full, state in zip((wq, wk, wv), states):
        forward(full, state)
    tok_fwd = []
    for micro in range(2):
        tok_x[micro].wait_recv()
        block = tok_full.at[pl.ds(micro * (length // RUN) + p.x_dev[0] * 2, 2)]
        tok_fwd.append(wire.send(block, block, p.core_dev))
    out_kept, out_state = push_rows(s_o, wo, side=False)
    wide_states = []
    for group, full in zip(second, (wg, wu)):
        arrived(group)
        wide_states.append(push_planes(full, side=False))
    settle(gain_state)
    table = gain_all[...].reshape(devices * 8, RUN).astype(BF16)
    gain_first = spread_gain(table, 0, devices, 1024)
    gain_post = spread_gain(table, 1, devices, 1024)
    gain_query = spread_gain(table, 2, devices, RUN)
    gain_key = spread_gain(table, 3, devices, RUN)
    gains[...] = jnp.zeros_like(gains)
    gains[0:1] = gain_first
    gains[1:2] = gain_post
    gains[2:3, 0:RUN] = gain_query
    gains[3:4, 0:RUN] = gain_key
    for state in states:
        settle(state)
    saved = [wire.own(here, there) for here, there in ((wq, wq_out), (wk, wk_out), (wv, wv_out))]
    out_state[1].append(wire.send(s_o, wo.at[f], p.y_dev))
    for full, state in zip((wg, wu), wide_states):
        state[1].append(wire.send(blocks(full, f), blocks(full, f), p.y_dev))
    down_kept, down_state = push_rows(s_d, wd)
    back_x, back_core, back_kept = [], [], []
    for micro in range(2):
        to = back_full.at[micro, mine]
        back_x.append(wire.send(cotangent.at[micro], to, p.x_dev))
        back_kept.append(wire.own(cotangent.at[micro], to))
        back_core.append(wire.send(cotangent.at[micro], to, p.core_dev))
    for copy in tok_here:
        copy.wait()
    for copy in tok_core + tok_fwd:
        copy.wait_recv()

    def project(step, carry):
        here = pl.ds(pl.multiple_of(step * BLOCK, BLOCK), BLOCK)
        raw = two_runs(tok_full, order[step * 2], order[step * 2 + 1]).astype(F32)
        root = lax.rsqrt(row_mean(raw * raw) + EPSILON)
        low = (raw * root * gains[0:1]).astype(BF16)
        normed[here] = low
        turn = pl.ds(pl.multiple_of(lax.rem(step, length // BLOCK) * BLOCK, BLOCK), BLOCK)
        cos, sin = cosine[turn], sine[turn]
        found = []
        for weight, low_ref, unit_ref, row in ((wq, query, q_unit, 2), (wk, key, k_unit, 3)):
            product = dot(low, flat(weight))
            gain = gains[row : row + 1, 0:RUN]
            for head in range(low_ref.shape[1] // HEAD_DIM):
                at = slice(head * HEAD_DIM, (head + 1) * HEAD_DIM)
                one = product[:, at]
                inverse = lax.rsqrt(row_mean(one * one) + EPSILON)
                unit = one * inverse
                unit_ref[here, at] = unit.astype(BF16)
                scaled = unit * gain
                low_ref[here, at] = (scaled * cos + pltpu.roll(scaled, HEAD_DIM // 2, 1) * sin).astype(BF16)
                found.append(inverse)
        for at, inverse in enumerate(found):
            roots[here, at : at + 1] = inverse
        value[here] = dot(low, flat(wv)).astype(BF16)
        return carry

    lax.fori_loop(0, length // BLOCK, project, 0)
    forward(wo, out_state)
    lax.fori_loop(length // BLOCK, 2 * length // BLOCK, project, 0)
    saved += [wire.own(here, there) for here, there in (
        (normed, normed_out), (query, query_out), (key, key_out), (value, value_out),
        (q_unit, q_unit_out), (k_unit, k_unit_out), (roots, roots_out))]

    def attend(step, carry):
        micro, head = step // 2, lax.rem(step, 2)
        keys_at = pl.ds(pl.multiple_of(head * HEAD_DIM, HEAD_DIM), HEAD_DIM)
        lanes = [pl.ds(pl.multiple_of(head * 2 * HEAD_DIM + g * HEAD_DIM, HEAD_DIM), HEAD_DIM) for g in range(2)]
        for block in range(length // BLOCK):
            here = pl.ds(pl.multiple_of(micro * length + block * BLOCK, BLOCK), BLOCK)
            seen = (block + 1) * BLOCK
            past = pl.ds(pl.multiple_of(micro * length, BLOCK), seen)
            asked = jnp.concatenate([query[here, lane] for lane in lanes], axis=0)
            scores = dot(asked, key[past, keys_at], NARROW)
            line = lax.broadcasted_iota(jnp.int32, (2 * BLOCK, seen), 0)
            line = jnp.where(line >= BLOCK, line - BLOCK, line) + block * BLOCK
            column = lax.broadcasted_iota(jnp.int32, (2 * BLOCK, seen), 1)
            scores = jnp.where(column <= line, scores, NEGATIVE)
            top = jnp.max(scores, axis=-1, keepdims=True)
            weight = jnp.exp2((scores - top) * (SCALE * LOG2E))
            total = jnp.sum(weight, axis=-1, keepdims=True)
            out = dot(weight.astype(BF16), value[past, keys_at]) * (1.0 / total)
            level = top * (SCALE * LOG2E) + jnp.log2(total)
            for g, lane in enumerate(lanes):
                half = slice(g * BLOCK, (g + 1) * BLOCK)
                pair = pl.ds(micro * (length // RUN) + block * 2, 2)
                mixed[pair, :, lane] = out[half].astype(BF16).reshape(2, RUN, HEAD_DIM)
                lse[step, pl.ds(block * BLOCK, BLOCK), g : g + 1] = level[half]
        return carry

    def mix_out(step, carry):
        micro, block = reducer.block(step)
        at = micro * (length // RUN) + block * 2
        low = two_runs(mixed, rank[at], rank[at + 1])
        part[...] = dot(low, flat(wo))
        reducer.take(step)
        return carry

    lax.fori_loop(0, 2, attend, 0)
    out_kept.wait()
    settle(out_state)
    lax.fori_loop(0, 4, mix_out, 0)
    forward(wg, wide_states[0])
    lax.fori_loop(2, 4, attend, 0)
    saved += [wire.own(mixed, mixed_out), wire.own(lse, lse_out), wire.own(wo, wo_out)]
    lax.fori_loop(4, 8, mix_out, 0)
    forward(wu, wide_states[1])
    for micro in range(2):
        back_x[micro].wait_recv()
        block = back_full.at[micro, theirs]
        back_core.append(wire.send(block, block, p.core_dev))
    posts = []
    for micro in range(2):
        total = reducer.total(micro)
        own = joined(tok_full[pl.ds(micro * (length // RUN) + s * 2, 2)]).astype(F32)
        total = own + total
        resid[micro] = total
        root = lax.rsqrt(row_mean(total * total) + EPSILON)
        post_own[micro] = (total * root * gains[1:2]).astype(BF16)
        to = post_full.at[micro, mine]
        posts.append((wire.send(post_own.at[micro], to, p.x_dev), wire.send(post_own.at[micro], to, p.core_dev),
                      wire.own(post_own.at[micro], to)))
        saved.append(wire.own(resid.at[micro], resid_out.at[micro]))
    forward(wd, down_state)
    for micro in range(2):
        posts[micro][0].wait_recv()
        block = post_full.at[micro, theirs]
        wire.send(block, block, p.core_dev).wait_recv()
        posts[micro][1].wait_recv()
        posts[micro][2].wait()
    for copy in back_core:
        copy.wait_recv()
    for copy in back_kept:
        copy.wait()
    for state in wide_states + [down_state]:
        settle(state)
    down_kept.wait()
    for copy in saved:
        copy.wait()
    reducer.close()
    wire.close()


def front(planes, order, rank, tokens, cotangent, gain_tile, cosine, sine, shards):
    nf = 2 * planes
    rows = tokens.shape[1]
    length = 4 * rows
    total = 2 * length
    tokens = tokens.reshape(2, 2, RUN, tokens.shape[2])
    quarter = [item.shape[1] // 4 for item in shards[:3]] + [None] + [item.shape[1] // 4 for item in shards[4:6]]
    def col(at):
        return jax.ShapeDtypeStruct((4, nf, shards[at].shape[0], quarter[at]), BF16)
    def row(at):
        return jax.ShapeDtypeStruct((nf, *shards[at].shape), BF16)
    def low(width):
        return jax.ShapeDtypeStruct((total, width), BF16)
    shapes = [col(0), col(1), col(2), row(3), col(4), col(5), row(6),
              low(1024), low(512), low(256), low(256), low(512), low(256),
              jax.ShapeDtypeStruct((total, 8), F32),
              jax.ShapeDtypeStruct((total // RUN, RUN, 512), BF16), jax.ShapeDtypeStruct((4, length, 2), F32),
              jax.ShapeDtypeStruct((2, rows, 1024), F32),
              jax.ShapeDtypeStruct((2, length, 1024), BF16), jax.ShapeDtypeStruct((2, length, 1024), BF16),
              jax.ShapeDtypeStruct((8, 1024), F32)]
    near = {19}
    held = [shapes[at] for at in (0, 1, 2, 3, 7, 8, 9, 10, 11, 12, 13, 14, 15, 16)]
    vm = pl.BlockSpec(memory_space=VMEM)
    hb = pl.BlockSpec(memory_space=ANY)
    sm = pl.BlockSpec(memory_space=pltpu.SMEM)
    return pl.pallas_call(
        functools.partial(front_kernel, planes),
        out_shape=shapes,
        in_specs=[sm, sm] + [vm] * 12,
        out_specs=[vm if at in near else hb for at in range(len(shapes))],
        scratch_shapes=[
            *[VMEM(item.shape, item.dtype) for item in held],
            VMEM((total // RUN, RUN, 1024), BF16), VMEM((4, nf, 8, RUN), F32), VMEM((2, rows, 1024), BF16),
            VMEM((BLOCK, 1024), F32), *reducer_scratch(1024), *wire_scratch(120, 48),
        ],
        compiler_params=pltpu.CompilerParams(
            collective_id=0, has_side_effects=True, vmem_limit_bytes=VMEM_BYTES),
        name="front",
    )(order, rank, tokens, cotangent, gain_tile, cosine, sine, *shards)


class Homing:
    def __init__(self, place, wire, by_columns, came=None, sums=None, far=None, turned=None, home=None):
        self.p, self.wire, self.by_columns = place, wire, by_columns
        self.came, self.sums, self.far, self.turned, self.home = came, sums, far, turned, home

    def side(self, ref, y):
        return ref.at[:, :, y] if self.by_columns else ref.at[:, y]

    def plane(self, ref, z):
        return ref.at[:, z] if self.by_columns else ref.at[z]

    def start(self, grad):
        self.kept = self.wire.own(self.side(grad, self.p.y), self.sums)
        self.sent = self.wire.send(self.side(grad, self.p.other_y), self.came, self.p.y_dev)

    def add(self):
        self.kept.wait()
        self.sent.wait_recv()

        def add(z, carry):
            at = (slice(None), z) if self.by_columns else (z,)
            self.sums[at] = (self.sums[at].astype(F32) + self.came[at].astype(F32)).astype(BF16)
            return carry

        lax.fori_loop(0, self.p.planes, add, 0)

    def push(self):
        self.out = [
            self.wire.send(self.plane(self.sums, self.p.z_at(step)), self.far.at[step - 1], self.p.z_dev(step))
            for step in range(1, self.p.planes)
        ]

    def gather(self):
        for copy in self.out:
            copy.wait_recv()
        at = (slice(None), self.p.z) if self.by_columns else (self.p.z,)
        total = self.sums[at].astype(F32)
        for step in range(1, self.p.planes):
            total = total + self.far[step - 1].astype(F32)
        if not self.by_columns:
            self.home[...] = total
            return
        leave, arrive, own = self.turned
        s = self.p.s
        leave[...] = total.astype(BF16)
        own[...] = total
        self.back = []
        for dev in (self.p.core_dev, self.p.x_dev, self.p.far_dev):
            self.back.append((dev[0], self.wire.send(leave.at[dev[0]], arrive.at[s], dev)))

    def finish(self):
        if not self.by_columns:
            return
        leave, arrive, own = self.turned
        width = own.shape[-1]
        s = self.p.s
        self.home[:, pl.ds(pl.multiple_of(s * width, RUN), width)] = own[s]
        for owner, copy in self.back:
            copy.wait_recv()
            self.home[:, pl.ds(pl.multiple_of(owner * width, RUN), width)] = arrive[owner].astype(F32)


def kept_shape(shape):
    return shape[:-3] + shape[-2:]


def once_shape(shape):
    return shape[:-4] + shape[-2:]


def y_scratch(shape):
    return [VMEM(kept_shape(shape), BF16), VMEM(kept_shape(shape), BF16)]


def z_scratch(planes, shape):
    once = once_shape(shape)
    found = [VMEM((planes - 1, *once), BF16)]
    if len(shape) == 5:
        found += [VMEM(once, BF16), VMEM(once, BF16), VMEM(once, F32)]
    return found


def middle_kernel(
    planes,
    post_in, back_in, wg_in, wu_in, wd_in, resid_in, gains,
    gate_sums, grad_u, d_sums, y_out, y_keep, d_resid, attn_full, sums,
    post, back, wg, wu, wd, resid, load_sems,
    grad_g, grad_d, g_came, d_came, hidden, d_gate, d_up, part_y, part_p, attn_own,
    y_core_out, y_core_in,
    core_out, core_in, x_out, x_in, keep, core_s, core_r, x_s, x_r,
    y_core_s, y_core_r, out_sems, in_sems, own_sems,
):
    p = Place(planes)
    s = p.s
    wire = Wire(out_sems, in_sems, own_sems)
    into_post = Reducer(p, part_p, core_out, core_in, x_out, x_in, keep, (core_s, core_r, x_s, x_r))
    into_out = Reducer(p, part_y, y_core_out, y_core_in, y_out, None, y_keep, (y_core_s, y_core_r, None, None))
    rows = resid.shape[1]
    length = 4 * rows
    mine = pl.ds(s * rows, rows)
    theirs = pl.ds(p.x_dev[0] * rows, rows)
    loads = [wire.own(wg_in, wg), wire.own(wu_in, wu), wire.own(wd_in, wd), wire.own(resid_in, resid)]

    def chunk(step):
        micro, block = into_post.block(step)
        here = pl.ds(pl.multiple_of(micro * length + block * BLOCK, BLOCK), BLOCK)
        return [pltpu.make_async_copy(far.at[here], near.at[here], load_sems.at[at, step])
                for at, (far, near) in enumerate(((post_in, post), (back_in, back)))]

    for step in range(8):
        for copy in chunk(step):
            copy.start()
    p.meet()
    for copy in loads:
        copy.wait()

    def feed(step, carry):
        micro, block = into_post.block(step)
        here = pl.ds(pl.multiple_of(micro * length + block * BLOCK, BLOCK), BLOCK)
        for copy in chunk(step):
            copy.wait()
        given, pulled = post[here, :], back[here, :]
        gate = dot(given, wg[...])
        upper = dot(given, wu[...])
        d_hidden = dot(pulled, wd[...], NARROW)
        sigma = 1.0 / (1.0 + jnp.exp(-gate))
        lit = gate * sigma
        low = (lit * upper).astype(BF16)
        gate_low = (d_hidden * upper * sigma * (1.0 + gate * (1.0 - sigma))).astype(BF16)
        up_low = (d_hidden * lit).astype(BF16)
        hidden[here] = low
        d_gate[here] = gate_low
        d_up[here] = up_low
        part_p[...] = dot(gate_low, wg[...], NARROW) + dot(up_low, wu[...], NARROW)
        into_post.take(step)
        part_y[...] = dot(low, wd[...])
        into_out.take(step, send_x=False)
        return carry

    down = Homing(p, wire, False, d_came, d_sums)
    gate_home = Homing(p, wire, True, g_came, gate_sums)

    def down_tile(at, carry):
        tall = hidden.shape[1] // 2
        cut = pl.ds(pl.multiple_of(at * tall, RUN), tall)
        found = dot(hidden[:, cut], back[...], TALL).astype(BF16)
        grad_d[pl.ds(at * (planes // 2), planes // 2)] = found.reshape(planes // 2, *grad_d.shape[1:])
        return carry

    def gate_tile(at, carry):
        cut = pl.ds(pl.multiple_of(at * BLOCK, BLOCK), BLOCK)
        grad_g[at] = dot(post[:, cut], d_gate[...], TALL).astype(BF16).reshape(grad_g.shape[1:])
        return carry

    def up_tile(at, carry):
        cut = pl.ds(pl.multiple_of(at * BLOCK, BLOCK), BLOCK)
        grad_u[at] = dot(post[:, cut], d_up[...], TALL).astype(BF16).reshape(grad_u.shape[1:])
        return carry

    gain = gains[1:2]
    sends = []
    sums[...] = jnp.zeros_like(sums)

    def settle(micro):
        grad = into_post.total(micro)
        held = resid[micro]
        root = lax.rsqrt(row_mean(held * held) + EPSILON)
        unit = held * root
        sums[0:1] += jnp.sum(grad * unit, axis=0, keepdims=True)
        scaled = grad * gain
        own = back[pl.ds(pl.multiple_of(micro * length + s * rows, rows), rows), :].astype(F32)
        whole = own + root * (scaled - unit * row_mean(scaled * unit))
        d_resid[micro] = whole
        attn_own[micro] = whole.astype(BF16)
        to = attn_full.at[micro, mine]
        sends.append((wire.send(attn_own.at[micro], to, p.x_dev), wire.send(attn_own.at[micro], to, p.core_dev),
                      wire.own(attn_own.at[micro], to)))
        y_keep[micro] = y_keep[micro] + held

    lax.fori_loop(0, 7, feed, 0)
    settle(0)
    lax.fori_loop(7, 8, feed, 0)
    lax.fori_loop(0, 2, down_tile, 0)
    down.start(grad_d)
    lax.fori_loop(0, 4, gate_tile, 0)
    gate_home.start(grad_g)
    settle(1)
    lax.fori_loop(0, 4, up_tile, 0)
    down.add()
    forwards = []
    for micro in range(2):
        sends[micro][0].wait_recv()
        block = attn_full.at[micro, theirs]
        forwards.append(wire.send(block, block, p.core_dev))
    gate_home.add()
    for micro in range(2):
        forwards[micro].wait_recv()
        sends[micro][1].wait_recv()
        sends[micro][2].wait()
    into_post.close()
    into_out.close(send_x=False)
    wire.close()


def middle(planes, post, back, wg, wu, wd, resid, gains):
    rows = resid.shape[1]
    total = 8 * rows
    wide = wg.shape[1]
    tall = (4, planes, 2, 1024 // (8 * planes), wide)
    flat_shape = (planes, 2, wide // (2 * planes), 1024)
    shapes = [
        jax.ShapeDtypeStruct(kept_shape(tall), BF16), jax.ShapeDtypeStruct(tall, BF16),
        jax.ShapeDtypeStruct(kept_shape(flat_shape), BF16),
        jax.ShapeDtypeStruct((2, rows, 1024), BF16), jax.ShapeDtypeStruct((2, rows, 1024), F32),
        jax.ShapeDtypeStruct((2, rows, 1024), F32), jax.ShapeDtypeStruct((2, 4 * rows, 1024), BF16),
        jax.ShapeDtypeStruct((8, 1024), F32),
    ]
    vm = pl.BlockSpec(memory_space=VMEM)
    hb = pl.BlockSpec(memory_space=ANY)
    return pl.pallas_call(
        functools.partial(middle_kernel, planes),
        out_shape=shapes,
        in_specs=[hb] * 6 + [vm],
        out_specs=[vm] * 6 + [hb, vm],
        scratch_shapes=[
            *[VMEM(item.shape, item.dtype) for item in (post, back, wg, wu, wd, resid)],
            pltpu.SemaphoreType.DMA((2, 8)),
            VMEM(tall, BF16), VMEM(flat_shape, BF16), VMEM(kept_shape(tall), BF16),
            VMEM(kept_shape(flat_shape), BF16),
            VMEM((total, wide), BF16), VMEM((total, wide), BF16), VMEM((total, wide), BF16),
            VMEM((BLOCK, 1024), F32), VMEM((BLOCK, 1024), F32), VMEM((2, rows, 1024), BF16),
            VMEM((4, BLOCK, 1024), BF16), VMEM((4, BLOCK, 1024), BF16),
            *reducer_scratch(1024),
            pltpu.SemaphoreType.DMA((4,)), pltpu.SemaphoreType.DMA((4,)),
            *wire_scratch(16, 10),
        ],
        compiler_params=pltpu.CompilerParams(
            collective_id=1, has_side_effects=True, vmem_limit_bytes=VMEM_BYTES),
        name="middle",
    )(post, back, wg, wu, wd, resid, gains)


def turn_kernel(
    planes,
    order, attn_in, query_in, key_in, value_in, q_unit_in, k_unit_in, roots_in, mixed_in, lse_in, wo_in,
    cosine, sine, gains, y_out, y_keep_in, sums_in, gate_sums, down_sums, grad_u,
    d_q_out, d_k_out, d_v_out, sums, block_out, home_g, home_u, home_d, home_o,
    attn, query, key, value, q_unit, k_unit, roots, mixed, lse, wo, y_keep, d_q, d_k, d_v, d_far,
    d_mixed, attn_sorted, keys_grad, values_grad, y_in, grad_o,
    g_far, g_leave, g_arrive, g_own, u_came, u_sums, u_far, u_leave, u_arrive, u_own, o_came, o_sums, o_far,
    out_sems, in_sems, own_sems,
):
    p = Place(planes)
    wire = Wire(out_sems, in_sems, own_sems)
    rows = y_keep.shape[1]
    length = 4 * rows
    loads = [wire.own(far, near) for far, near in (
        (attn_in, attn), (wo_in, wo), (mixed_in, mixed), (query_in, query), (key_in, key), (value_in, value),
        (q_unit_in, q_unit), (k_unit_in, k_unit), (roots_in, roots), (lse_in, lse), (y_keep_in, y_keep))]
    p.meet()
    down = Homing(p, wire, False, None, down_sums, d_far, None, home_d)
    gate = Homing(p, wire, True, None, gate_sums, g_far, (g_leave, g_arrive, g_own), home_g)
    upper = Homing(p, wire, True, u_came, u_sums, u_far, (u_leave, u_arrive, u_own), home_u)
    outer = Homing(p, wire, False, o_came, o_sums, o_far, None, home_o)
    upper.start(grad_u)
    down.push()
    gate.push()
    loads[0].wait()
    loads[1].wait()
    y_sent = [wire.send(y_out.at[micro], y_in.at[micro], p.x_dev) for micro in range(2)]

    def draw(step, carry):
        here = pl.ds(pl.multiple_of(step * BLOCK, BLOCK), BLOCK)
        low = two_runs(attn, order[step * 2], order[step * 2 + 1])
        attn_sorted[here] = low
        d_mixed[here] = dot(low, wo[...], NARROW).astype(BF16)
        return carry

    lax.fori_loop(0, 2 * length // BLOCK, draw, 0)

    def out_tile(at, carry):
        cut = pl.ds(pl.multiple_of(at * BLOCK, BLOCK), BLOCK)
        found = dot(mixed[:, cut], attn_sorted[...], TALL).astype(BF16)
        grad_o[pl.ds(at * (planes // 2), planes // 2)] = found.reshape(planes // 2, *grad_o.shape[1:])
        return carry

    loads[2].wait()
    lax.fori_loop(0, 2, out_tile, 0)
    outer.start(grad_o)
    sums[...] = sums_in[...]

    def lane_of(ref, here, lane):
        held = ref[here, :]
        lanes = lax.broadcasted_iota(jnp.int32, held.shape, 1)
        return jnp.sum(jnp.where(lanes == lane, held, 0.0), axis=1, keepdims=True)

    def norm_home(grad, cos, sin, unit, root, gain):
        turned = grad * cos - pltpu.roll(grad, HEAD_DIM // 2, 1) * sin
        scaled = turned * gain
        back = root * (scaled - unit * row_mean(scaled * unit))
        return back, jnp.sum(turned * unit, axis=0, keepdims=True)

    def attend_back(step, carry):
        micro, head = step // 2, lax.rem(step, 2)
        keys_at = pl.ds(pl.multiple_of(head * HEAD_DIM, HEAD_DIM), HEAD_DIM)
        lanes = [pl.ds(pl.multiple_of(head * 2 * HEAD_DIM + g * HEAD_DIM, HEAD_DIM), HEAD_DIM) for g in range(2)]
        q_gain, k_gain = gains[2:3, 0:RUN], gains[3:4, 0:RUN]
        keys_grad[...] = jnp.zeros_like(keys_grad)
        values_grad[...] = jnp.zeros_like(values_grad)
        for block in range(length // BLOCK):
            here = pl.ds(pl.multiple_of(micro * length + block * BLOCK, BLOCK), BLOCK)
            seen = (block + 1) * BLOCK
            past = pl.ds(pl.multiple_of(micro * length, BLOCK), seen)
            asked = jnp.concatenate([query[here, lane] for lane in lanes], axis=0)
            pulled = jnp.concatenate([d_mixed[here, lane] for lane in lanes], axis=0)
            given = jnp.concatenate([mixed[here, lane] for lane in lanes], axis=0)
            level = jnp.concatenate(
                [lse[step, pl.ds(block * BLOCK, BLOCK), g : g + 1] for g in range(2)], axis=0)
            delta = jnp.sum(pulled.astype(F32) * given.astype(F32), axis=1, keepdims=True)
            scores = dot(asked, key[past, keys_at], NARROW)
            line = lax.broadcasted_iota(jnp.int32, (2 * BLOCK, seen), 0)
            line = jnp.where(line >= BLOCK, line - BLOCK, line) + block * BLOCK
            column = lax.broadcasted_iota(jnp.int32, (2 * BLOCK, seen), 1)
            weight = jnp.exp2(scores * (SCALE * LOG2E) - level)
            weight = jnp.where(column <= line, weight, 0.0)
            d_soft = dot(pulled, value[past, keys_at], NARROW)
            d_scores = (weight * (d_soft - delta)).astype(BF16)
            values_grad[0:seen] += dot(weight.astype(BF16), pulled, TALL)
            keys_grad[0:seen] += dot(d_scores, asked, TALL)
            moved = dot(d_scores, key[past, keys_at]) * SCALE
            spin = slice(block * BLOCK, (block + 1) * BLOCK)
            for g, lane in enumerate(lanes):
                root = lane_of(roots, here, head * 2 + g)
                unit = q_unit[here, lane].astype(F32)
                back, gained = norm_home(
                    moved[g * BLOCK : (g + 1) * BLOCK], cosine[spin], sine[spin], unit, root, q_gain)
                d_q[here, lane] = back.astype(BF16)
                sums[1:2, 0:RUN] += gained
        everything = pl.ds(pl.multiple_of(micro * length, BLOCK), length)
        root = lane_of(roots, everything, head + 4)
        unit = k_unit[everything, keys_at].astype(F32)
        back, gained = norm_home(keys_grad[...] * SCALE, cosine[...], sine[...], unit, root, k_gain)
        d_k[everything, keys_at] = back.astype(BF16)
        sums[2:3, 0:RUN] += gained
        d_v[everything, keys_at] = values_grad[...].astype(BF16)
        return carry

    for copy in loads[3:]:
        copy.wait()
    lax.fori_loop(0, 1, attend_back, 0)
    upper.add()
    upper.push()
    lax.fori_loop(1, 2, attend_back, 0)
    outer.add()
    outer.push()
    for micro in range(2):
        y_sent[micro].wait_recv()
        block_out[micro] = (y_keep[micro] + y_in[micro].astype(F32)).astype(BF16)
    def save(micro):
        half = pl.ds(micro * length, length)
        return [wire.own(near.at[half], far.at[half]) for near, far in (
            (d_q, d_q_out), (d_k, d_k_out), (d_v, d_v_out))]

    saved = save(0)
    lax.fori_loop(2, 3, attend_back, 0)
    down.gather()
    gate.gather()
    lax.fori_loop(3, 4, attend_back, 0)
    saved += save(1)
    upper.gather()
    outer.gather()
    gate.finish()
    upper.finish()
    for copy in saved:
        copy.wait()
    wire.close()


def turn(planes, order, attn, query, key, value, q_unit, k_unit, roots, mixed, lse, wo, cosine, sine, gains,
         y_out, y_keep, sums, gate_sums, down_sums, grad_u):
    rows = y_keep.shape[1]
    length = 4 * rows
    total = 2 * length
    out_shape = (planes, 2, 512 // (2 * planes), 1024)
    shapes = [
        jax.ShapeDtypeStruct((total, 512), BF16), jax.ShapeDtypeStruct((total, 256), BF16),
        jax.ShapeDtypeStruct((total, 256), BF16),
        jax.ShapeDtypeStruct((8, 1024), F32), jax.ShapeDtypeStruct((2, rows, 1024), BF16),
        jax.ShapeDtypeStruct((grad_u.shape[3], 4 * grad_u.shape[4]), F32),
        jax.ShapeDtypeStruct((grad_u.shape[3], 4 * grad_u.shape[4]), F32),
        jax.ShapeDtypeStruct(down_sums.shape[1:], F32), jax.ShapeDtypeStruct(out_shape[2:], F32),
    ]
    held = (attn, query, key, value, q_unit, k_unit, roots, mixed, lse, wo, y_keep, *shapes[:3])
    vm = pl.BlockSpec(memory_space=VMEM)
    hb = pl.BlockSpec(memory_space=ANY)
    sm = pl.BlockSpec(memory_space=pltpu.SMEM)
    return pl.pallas_call(
        functools.partial(turn_kernel, planes),
        out_shape=shapes,
        in_specs=[sm] + [hb] * 10 + [vm] * 3 + [hb, hb, vm, vm, vm, hb],
        out_specs=[hb] * 3 + [vm] * (len(shapes) - 3),
        scratch_shapes=[
            *[VMEM(item.shape, item.dtype) for item in held], VMEM((planes - 1, *down_sums.shape[1:]), BF16),
            VMEM((total, 512), BF16), VMEM((total, 1024), BF16), VMEM((length, HEAD_DIM), F32),
            VMEM((length, HEAD_DIM), F32), VMEM((2, rows, 1024), BF16), VMEM(out_shape, BF16),
            *z_scratch(planes, grad_u.shape), *y_scratch(grad_u.shape), *z_scratch(planes, grad_u.shape),
            *y_scratch(out_shape), *z_scratch(planes, out_shape), *wire_scratch(32, 24),
        ],
        compiler_params=pltpu.CompilerParams(
            collective_id=2, has_side_effects=True, vmem_limit_bytes=VMEM_BYTES),
        name="turn",
    )(order, attn, query, key, value, q_unit, k_unit, roots, mixed, lse, wo, cosine, sine, gains,
      y_out, y_keep, sums, gate_sums, down_sums, grad_u)


def last_kernel(
    planes,
    rank, normed_in, d_q_in, d_k_in, d_v_in, wq_in, wk_in, wv_in, tokens, d_resid_in, gains, sums_in,
    token_grad, sums, home_q, home_k, home_v,
    normed, d_q, d_k, d_v, wq, wk, wv, d_resid,
    grad_q, grad_k, grad_v, part, sums_out, sums_came,
    core_out, core_in, x_out, x_in, keep, core_s, core_r, x_s, x_r, *rest,
):
    p = Place(planes)
    s, f = p.s, p.f
    wire = Wire(*rest[-3:])
    refs = list(rest[:-3])
    reducer = Reducer(p, part, core_out, core_in, x_out, x_in, keep, (core_s, core_r, x_s, x_r))
    rows = tokens.shape[1]
    length = 4 * rows
    loads = [wire.own(far, near) for far, near in (
        (normed_in, normed), (d_q_in, d_q), (d_k_in, d_k), (d_v_in, d_v), (wq_in, wq), (wk_in, wk), (wv_in, wv),
        (d_resid_in, d_resid))]
    p.meet()
    loads[0].wait()
    homes = []
    for grad, pulled, home, load in (
            (grad_q, d_q, home_q, 1), (grad_k, d_k, home_k, 2), (grad_v, d_v, home_v, 3)):
        loads[load].wait()

        def tile(at, carry, grad=grad, pulled=pulled):
            cut = pl.ds(pl.multiple_of(at * BLOCK, BLOCK), BLOCK)
            found = dot(joined(normed[:, :, cut]), flat(pulled), TALL).astype(BF16)
            grad[at] = found.reshape(grad.shape[1:])
            return carry

        lax.fori_loop(0, 4, tile, 0)
        came, kept, far, *turned = refs[:6]
        refs = refs[6:]
        one = Homing(p, wire, True, came, kept, far, turned, home)
        one.start(grad)
        homes.append(one)
    for copy in loads[4:]:
        copy.wait()
    sums[...] = sums_in[...]

    def pull(step, carry):
        micro, block = reducer.block(step)
        at = micro * (length // RUN) + block * 2
        runs = (rank[at], rank[at + 1])
        found = dot(two_runs(d_q, *runs), wq[...], NARROW)
        found += dot(two_runs(d_k, *runs), wk[...], NARROW)
        found += dot(two_runs(d_v, *runs), wv[...], NARROW)
        part[...] = found
        sums[3:4] += jnp.sum(found * two_runs(normed, *runs).astype(F32), axis=0, keepdims=True)
        reducer.take(step)
        return carry

    lax.fori_loop(0, 8, pull, 0)
    sums[3:4] = sums[3:4] / gains[0:1]

    def exchange(stage, devices, base):
        sums_out[stage] = sums[...]
        sent = [wire.send(sums_out.at[stage], sums_came.at[base + at], dev) for at, dev in enumerate(devices)]
        return base, sent

    def absorb(state):
        base, sent = state
        total = sums[...]
        for at, copy in enumerate(sent):
            copy.wait_recv()
            total = total + sums_came[base + at]
        sums[...] = total

    state = exchange(0, (p.core_dev, p.x_dev, p.far_dev), 0)
    for one in homes:
        one.add()
        one.push()
    absorb(state)
    state = exchange(1, [p.z_dev(step) for step in range(1, planes)], 3)
    absorb(state)
    state = exchange(2, [p.y_dev], 2 + planes)
    for micro in range(2):
        grad = reducer.total(micro)
        held = tokens[micro].astype(F32)
        root = lax.rsqrt(row_mean(held * held) + EPSILON)
        unit = held * root
        scaled = grad * gains[0:1]
        token_grad[micro] = d_resid[micro] + root * (scaled - unit * row_mean(scaled * unit))
    for one in homes:
        one.gather()
    absorb(state)
    for one in homes:
        one.finish()
    reducer.close()
    wire.close()


def last(planes, rank, normed, d_q, d_k, d_v, wq, wk, wv, tokens, d_resid, gains, sums):
    nf = 2 * planes
    rows = tokens.shape[1]
    widths = [wq.shape[1], wk.shape[1], wv.shape[1]]
    deep = 1024 // (4 * nf)
    grads = [(4, planes, 2, deep, wide) for wide in widths]
    shapes = [
        jax.ShapeDtypeStruct((2, rows, 1024), F32), jax.ShapeDtypeStruct((8, 1024), F32),
        *[jax.ShapeDtypeStruct((deep, 4 * wide), F32) for wide in widths],
    ]
    vm = pl.BlockSpec(memory_space=VMEM)
    sm = pl.BlockSpec(memory_space=pltpu.SMEM)
    held = (normed, d_q, d_k, d_v, wq, wk, wv, d_resid)
    scratch = [VMEM(item.shape, item.dtype) for item in held] + [VMEM(shape, BF16) for shape in grads]
    hb = pl.BlockSpec(memory_space=ANY)
    scratch += [VMEM((BLOCK, 1024), F32), VMEM((3, 8, 1024), F32), VMEM((3 + planes, 8, 1024), F32)]
    scratch += reducer_scratch(1024)
    for shape in grads:
        scratch += y_scratch(shape) + z_scratch(planes, shape)
    return pl.pallas_call(
        functools.partial(last_kernel, planes),
        out_shape=shapes,
        in_specs=[sm] + [hb] * 7 + [vm, hb, vm, vm],
        out_specs=[vm] * len(shapes),
        scratch_shapes=scratch + wire_scratch(48, 16),
        compiler_params=pltpu.CompilerParams(
            collective_id=3, has_side_effects=True, vmem_limit_bytes=VMEM_BYTES),
        name="last",
    )(rank, normed, d_q, d_k, d_v, wq, wk, wv, tokens, d_resid, gains, sums)


def run_tables(positions):
    runs = positions.shape[1] // RUN
    rank = positions[:, ::RUN] // RUN
    index = jnp.arange(runs, dtype=jnp.int32)
    order = jnp.sum(jnp.where(rank[:, :, None] == index, index[None, :, None], 0), axis=1)
    base = jnp.arange(positions.shape[0], dtype=jnp.int32)[:, None] * runs
    return (order + base).reshape(-1), (rank + base).reshape(-1)


def kernel_body(tokens, positions, g_in, g_post, g_query, g_key, w_query, w_key, w_value,
                w_out, w_gate, w_up, w_down, cotangent):
    planes = lax.axis_size("fsdp") // 2
    length = positions.shape[2]
    order, rank = run_tables(positions[:, 0])
    tile = jnp.stack(
        [jnp.pad(item.astype(F32), (0, RUN - item.shape[0])) for item in (g_in, g_post, g_query, g_key)])
    tile = jnp.pad(tile, ((0, 4), (0, 0)))
    cosine, sine = rope_tables(jnp.arange(length))
    cosine, sine = cosine[:, 0], sine[:, 0]
    half = HEAD_DIM // 2
    sine = jnp.concatenate([-sine[:, :half], sine[:, half:]], axis=1)
    near = tokens[:, 0]
    shards = (w_query, w_key, w_value, w_out, w_gate, w_up, w_down)
    (wq, wk, wv, wo, wg, wu, wd, normed, query, key, value, q_unit, k_unit, roots, mixed, lse,
     resid, post, back, gains) = front(
        planes, order, rank, near, cotangent[:, 0], tile, cosine, sine, shards)
    wq, wk, wv, wo, wg, wu, wd = [
        item.reshape(-1, item.shape[-1]) for item in (wq, wk, wv, wo, wg, wu, wd)]
    post, back = post.reshape(-1, post.shape[-1]), back.reshape(-1, back.shape[-1])
    gate_sums, grad_u, down_sums, y_out, y_keep, d_resid, attn, sums = middle(
        planes, post, back, wg, wu, wd, resid, gains)
    apart = lambda item: item.reshape(-1, RUN, item.shape[-1])
    d_q, d_k, d_v, sums, block_out, home_g, home_u, home_d, home_o = turn(
        planes, order, apart(attn), query, key, value, q_unit, k_unit, roots,
        mixed.reshape(-1, mixed.shape[-1]), lse,
        wo, cosine, sine, gains, y_out, y_keep, sums, gate_sums,
        down_sums, grad_u)
    token_grad, sums, home_q, home_k, home_v = last(
        planes, rank, apart(normed), apart(d_q), apart(d_k), apart(d_v), wq, wk, wv, near, d_resid, gains, sums)
    me = lax.axis_index("seq") * (2 * planes) + lax.axis_index("fsdp")
    small = [
        lax.dynamic_slice(sums, (row, me * item.shape[0]), (1, item.shape[0]))[0]
        for row, item in ((3, g_in), (0, g_post), (1, g_query), (2, g_key))
    ]
    return (block_out[:, None], token_grad[:, None], *small, home_q, home_k, home_v, home_o,
            home_g, home_u, home_d)


def solution(mesh):
    both = ("seq", "fsdp")
    act = P(None, "fsdp", "seq", None)
    vec, mat = P(both), P(both, None)

    def body(*args):
        rows = args[6].shape[0]
        fits = mesh.shape["seq"] == 4 and mesh.shape["fsdp"] % 2 == 0 and rows % 16 == 0
        return (kernel_body if fits else plain_body)(*args)

    return jax.shard_map(
        body,
        mesh=mesh,
        in_specs=(act, P(None, "fsdp", None), *[vec] * 4, *[mat] * 7, act),
        out_specs=(act, act, *[vec] * 4, *[mat] * 7),
        check_vma=False,
    )
```

```python
import functools

import jax
import jax.numpy as jnp
import numpy as np
from jax import lax
from jax.experimental import pallas as pl
from jax.experimental.pallas import tpu as pltpu
from jax.sharding import PartitionSpec as P

HEADS = 16
KV_HEADS = 8
HEAD_DIM = 128
EPSILON = 1e-06
ROPE_BASE = 1000000.0
NEGATIVE = -1e30
F32 = jnp.float32
BF16 = jnp.bfloat16


def inverse_root(values):
    return lax.rsqrt(jnp.mean(values * values, axis=-1, keepdims=True) + EPSILON)


def rope_tables(token_pos):
    half_width = HEAD_DIM // 2
    frequency = ROPE_BASE ** (-(jnp.arange(half_width, dtype=F32) * 2.0 / HEAD_DIM))
    angles = token_pos.astype(F32)[:, None] * frequency[None, :]
    cosine = jnp.cos(angles)
    sine = jnp.sin(angles)
    return (
        jnp.concatenate([cosine, cosine], axis=-1)[:, None, :],
        jnp.concatenate([sine, sine], axis=-1)[:, None, :],
    )


def rotate(values, cosine, sine):
    half_width = values.shape[-1] // 2
    turned = jnp.concatenate([-values[..., half_width:], values[..., :half_width]], axis=-1)
    return values * cosine + turned * sine


def rotate_back(grads, cosine, sine):
    half_width = grads.shape[-1] // 2
    scaled = grads * sine
    turned = jnp.concatenate([scaled[..., half_width:], -scaled[..., :half_width]], axis=-1)
    return grads * cosine + turned


def norm_back(grads, values, inverse, gain):
    scaled = grads * gain
    return inverse * scaled - values * inverse**3 * jnp.mean(
        scaled * values, axis=-1, keepdims=True
    )


def mul(eq, left, right):
    return jnp.einsum(eq, left, right, preferred_element_type=F32)


def sum_scatter(part, axis):
    return lax.psum_scatter(part.astype(BF16), axis, scatter_dimension=0, tiled=True).astype(F32)


def slice_weights(item, ways):
    rows = item.shape[0]
    return item.reshape(rows, ways, -1).transpose(1, 0, 2)


def plain_body(tokens, positions, g_in, g_post, g_query, g_key, w_query, w_key, w_value,
               w_out, w_gate, w_up, w_down, cotangent):
    ways = lax.axis_size("seq")
    heads, kv_heads = HEADS // ways, KV_HEADS // ways
    micro, rows, width = tokens.shape[0], tokens.shape[2], tokens.shape[3]
    length = positions.shape[2]
    everyone = ("seq", "fsdp")
    gains = [
        lax.all_gather(item, everyone, axis=0, tiled=True).astype(F32)
        for item in (g_in, g_post, g_query, g_key)
    ]
    gain_in, gain_post, gain_query, gain_key = gains

    def spread(*items):
        packed = jnp.concatenate([slice_weights(item, ways) for item in items], axis=2)
        packed = lax.all_to_all(packed, "seq", 0, 0, tiled=True)
        packed = lax.all_gather(packed, "fsdp", axis=1, tiled=True)
        packed = packed.reshape(-1, packed.shape[2])
        sizes = [item.shape[1] // ways for item in items]
        cuts = [sum(sizes[: at + 1]) for at in range(len(sizes) - 1)]
        return jnp.split(packed, cuts, axis=1)

    wq, wk, wv = spread(w_query, w_key, w_value)
    wo = lax.all_gather(w_out, "fsdp", axis=0, tiled=True)
    wg, wu = spread(w_gate, w_up)
    wd = lax.all_gather(w_down, "fsdp", axis=0, tiled=True)
    scale = HEAD_DIM ** (-0.5)

    def gather_rows(item):
        return lax.all_gather(item, "seq", axis=0, tiled=True)

    grads = None
    outs, token_grads = [], []
    for at in range(micro):
        inputs = tokens[at, 0].astype(F32)
        pos = positions[at, 0]
        cosine, sine = rope_tables(pos)
        allowed = pos[None, :] <= pos[:, None]
        inv_in = inverse_root(inputs)
        normed = gather_rows((inputs * inv_in * gain_in).astype(BF16))
        q_raw = mul("td,df->tf", normed, wq).reshape(length, heads, HEAD_DIM)
        k_raw = mul("td,df->tf", normed, wk).reshape(length, kv_heads, HEAD_DIM)
        value = mul("td,df->tf", normed, wv).astype(BF16).reshape(length, kv_heads, HEAD_DIM)
        inv_q, inv_k = inverse_root(q_raw), inverse_root(k_raw)
        query = rotate(q_raw * inv_q * gain_query, cosine, sine).astype(BF16)
        query = query.reshape(length, kv_heads, heads // kv_heads, HEAD_DIM)
        key = rotate(k_raw * inv_k * gain_key, cosine, sine).astype(BF16)
        scores = jnp.where(allowed, mul("qjgd,kjd->jgqk", query, key) * scale, NEGATIVE)
        soft = jax.nn.softmax(scores, axis=-1)
        soft_low = soft.astype(BF16)
        mixed = mul("jgqk,kjd->qjgd", soft_low, value).astype(BF16).reshape(length, -1)
        resid = inputs + sum_scatter(mul("th,hd->td", mixed, wo), "seq")
        inv_post = inverse_root(resid)
        post = gather_rows((resid * inv_post * gain_post).astype(BF16))
        gate = mul("td,df->tf", post, wg)
        upper = mul("td,df->tf", post, wu)
        sigma = jax.nn.sigmoid(gate)
        hidden = (gate * sigma * upper).astype(BF16)
        outs.append((resid + sum_scatter(mul("tf,fd->td", hidden, wd), "seq")).astype(BF16))
        back_low = cotangent[at, 0]
        back = gather_rows(back_low)
        g_down = mul("tf,td->fd", hidden, back)
        d_hidden = mul("td,fd->tf", back, wd)
        d_gate = (d_hidden * upper * sigma * (1.0 + gate * (1.0 - sigma))).astype(BF16)
        d_upper = (d_hidden * gate * sigma).astype(BF16)
        g_gate = mul("td,tf->df", post, d_gate)
        g_up = mul("td,tf->df", post, d_upper)
        d_post = sum_scatter(mul("tf,df->td", d_gate, wg) + mul("tf,df->td", d_upper, wu), "seq")
        post_grad = jnp.sum(d_post * resid * inv_post, axis=0)
        d_resid = back_low.astype(F32) + norm_back(d_post, resid, inv_post, gain_post)
        d_attn = gather_rows(d_resid.astype(BF16))
        g_out = mul("th,td->hd", mixed, d_attn)
        d_mixed = mul("td,hd->th", d_attn, wo).astype(BF16)
        d_mixed = d_mixed.reshape(length, kv_heads, heads // kv_heads, HEAD_DIM)
        d_soft = mul("qjgd,kjd->jgqk", d_mixed, value)
        d_scores = (soft * (d_soft - jnp.sum(d_soft * soft, axis=-1, keepdims=True))).astype(BF16)
        d_query = mul("jgqk,kjd->qjgd", d_scores, key) * scale
        d_key = mul("jgqk,qjgd->kjd", d_scores, query) * scale
        d_value = mul("jgqk,qjgd->kjd", soft_low, d_mixed).astype(BF16).reshape(length, -1)
        key_turn = rotate_back(d_key, cosine, sine)
        query_turn = rotate_back(d_query.reshape(length, heads, HEAD_DIM), cosine, sine)
        key_grad = jnp.sum(key_turn * k_raw * inv_k, axis=(0, 1))
        query_grad = jnp.sum(query_turn * q_raw * inv_q, axis=(0, 1))
        d_key = norm_back(key_turn, k_raw, inv_k, gain_key).astype(BF16).reshape(length, -1)
        d_query = norm_back(query_turn, q_raw, inv_q, gain_query).astype(BF16).reshape(length, -1)
        g_query_w = mul("td,tf->df", normed, d_query)
        g_key_w = mul("td,tf->df", normed, d_key)
        g_value_w = mul("td,tf->df", normed, d_value)
        d_normed = mul("tf,df->td", d_query, wq) + mul("tf,df->td", d_key, wk)
        d_normed = sum_scatter(d_normed + mul("tf,df->td", d_value, wv), "seq")
        in_grad = jnp.sum(d_normed * inputs * inv_in, axis=0)
        token_grads.append(d_resid + norm_back(d_normed, inputs, inv_in, gain_in))
        found = [in_grad, post_grad, query_grad, key_grad, g_query_w, g_key_w, g_value_w,
                 g_out, g_gate, g_up, g_down]
        grads = found if grads is None else [left + right for left, right in zip(grads, found)]

    small = [lax.psum_scatter(item, everyone, scatter_dimension=0, tiled=True) for item in grads[:4]]

    def columns_home(item):
        full, wide = item.shape
        item = item.reshape(ways, -1, wide).astype(BF16)
        item = lax.psum_scatter(item, "fsdp", scatter_dimension=1, tiled=True)
        item = lax.all_to_all(item, "seq", 0, 0, tiled=True)
        return item.transpose(1, 0, 2).reshape(item.shape[1], ways * wide).astype(F32)

    def rows_home(item):
        return sum_scatter(item, "fsdp")

    large = [columns_home(item) for item in grads[4:7]] + [rows_home(grads[7])]
    large += [columns_home(item) for item in grads[8:10]] + [rows_home(grads[10])]
    return (jnp.stack(outs)[:, None], jnp.stack(token_grads)[:, None], *small, *large)


MESH = pl.DeviceIdType.MESH
ANY = pl.ANY
VMEM = pltpu.VMEM
RUN = 128
BLOCK = 256
NARROW = (((1,), (1,)), ((), ()))
TALL = (((0,), (0,)), ((), ()))
PLAIN = (((1,), (0,)), ((), ()))
LOG2E = 1.4426950408889634
SCALE = HEAD_DIM ** (-0.5)
VMEM_BYTES = 63 * 2**20


def dot(left, right, dims=PLAIN):
    return lax.dot_general(left, right, dims, preferred_element_type=F32)


class Place:
    def __init__(self, planes):
        self.planes = planes
        self.s = lax.axis_index("seq")
        self.f = lax.axis_index("fsdp")
        self.x, self.c = self.s // 2, self.s % 2
        self.z, self.y = self.f // 2, self.f % 2
        self.other_y = 1 - self.y
        self.core_dev = (self.x * 2 + 1 - self.c, self.f)
        self.x_dev = ((1 - self.x) * 2 + self.c, self.f)
        self.far_dev = ((1 - self.x) * 2 + 1 - self.c, self.f)
        self.y_dev = (self.s, self.z * 2 + self.other_y)
        self.seq_dev = [(self.s, self.f), self.core_dev, self.x_dev, self.far_dev]

    def z_at(self, step):
        return lax.rem(self.z + step, self.planes)

    def z_dev(self, step):
        return (self.s, self.z_at(step) * 2 + self.y)

    def peers(self):
        return [self.core_dev, self.x_dev, self.far_dev, self.y_dev] + [
            self.z_dev(step) for step in range(1, self.planes)
        ]

    def meet(self):
        barrier = pltpu.get_barrier_semaphore()
        for peer in self.peers():
            pl.semaphore_signal(barrier, inc=1, device_id=peer, device_id_type=MESH)
        pl.semaphore_wait(barrier, 3 + self.planes)


def remote(src, dst, out_sem, in_sem, device):
    return pltpu.make_async_remote_copy(
        src_ref=src, dst_ref=dst, send_sem=out_sem, recv_sem=in_sem,
        device_id=device, device_id_type=MESH,
    )


class Wire:
    def __init__(self, out_sems, in_sems, own_sems):
        self.out_sems, self.in_sems, self.own_sems = out_sems, in_sems, own_sems
        self.sent, self.owned = [], 0

    def send(self, src, dst, device, start=True):
        at = len(self.sent)
        copy = remote(src, dst, self.out_sems.at[at], self.in_sems.at[at], device)
        if start:
            copy.start()
        self.sent.append(copy)
        return copy

    def own(self, src, dst):
        copy = pltpu.make_async_copy(src, dst, self.own_sems.at[self.owned])
        copy.start()
        self.owned += 1
        return copy

    def close(self):
        for copy in self.sent:
            copy.wait_send()


def wire_scratch(copies, owns):
    return [
        pltpu.SemaphoreType.DMA((copies,)),
        pltpu.SemaphoreType.DMA((copies,)),
        pltpu.SemaphoreType.DMA((owns,)),
    ]


class Reducer:
    def __init__(self, place, part, core_out, core_in, x_out, x_in, keep, sems):
        self.place, self.part = place, part
        self.core_out, self.core_in = core_out, core_in
        self.x_out, self.x_in, self.keep = x_out, x_in, keep
        self.core_s, self.core_r, self.x_s, self.x_r = sems

    def block(self, step):
        p = self.place
        turn = step % 4
        x = jnp.where(turn < 2, 1 - p.x, p.x)
        c = jnp.where(turn % 2 == 0, 1 - p.c, p.c)
        return step // 4, x * 2 + c

    def core_copy(self, slot):
        return remote(self.core_out.at[slot], self.core_in.at[slot], self.core_s.at[slot],
                      self.core_r.at[slot], self.place.core_dev)

    def x_copy(self, micro):
        return remote(self.x_out.at[micro], self.x_in.at[micro], self.x_s.at[micro],
                      self.x_r.at[micro], self.place.x_dev)

    def take(self, step, send_x=True):
        micro, turn = step // 4, step % 4

        @pl.when(turn % 2 == 0)
        def _():
            slot = micro * 2 + turn // 2
            self.core_out[slot] = self.part[...].astype(BF16)
            self.core_copy(slot).start()

        @pl.when(turn == 1)
        def _():
            slot = micro * 2
            self.core_copy(slot).wait_recv()
            self.x_out[micro] = (self.part[...] + self.core_in[slot].astype(F32)).astype(BF16)
            if send_x:
                self.x_copy(micro).start()

        @pl.when(turn == 3)
        def _():
            slot = micro * 2 + 1
            self.core_copy(slot).wait_recv()
            self.keep[micro] = self.part[...] + self.core_in[slot].astype(F32)

    def total(self, micro):
        self.x_copy(micro).wait_recv()
        return self.keep[micro] + self.x_in[micro].astype(F32)

    def close(self, send_x=True):
        for slot in range(4):
            self.core_copy(slot).wait_send()
        if send_x:
            for micro in range(2):
                self.x_copy(micro).wait_send()


def reducer_scratch(width):
    return [
        VMEM((4, BLOCK, width), BF16),
        VMEM((4, BLOCK, width), BF16),
        VMEM((2, BLOCK, width), BF16),
        VMEM((2, BLOCK, width), BF16),
        VMEM((2, BLOCK, width), F32),
        pltpu.SemaphoreType.DMA((4,)),
        pltpu.SemaphoreType.DMA((4,)),
        pltpu.SemaphoreType.DMA((2,)),
        pltpu.SemaphoreType.DMA((2,)),
    ]


def row_mean(values):
    return jnp.mean(values, axis=-1, keepdims=True)


def spread_gain(table, row, devices, width):
    per = width // devices
    lanes = lax.broadcasted_iota(jnp.int32, (RUN, width), 0)
    column = lax.broadcasted_iota(jnp.int32, (RUN, width), 1)
    pick = (lanes == lax.rem(column, per)).astype(BF16)
    picked = dot(table, pick)
    rows = lax.broadcasted_iota(jnp.int32, (devices * 8, width), 0)
    owner = lax.broadcasted_iota(jnp.int32, (devices * 8, width), 1) // per
    return jnp.sum(jnp.where(rows == owner * 8 + row, picked, 0.0), axis=0, keepdims=True)


def two_runs(ref, first, second):
    return jnp.concatenate([ref[first], ref[second]], axis=0)


def joined(value):
    return value.reshape(-1, value.shape[-1])


def flat(ref):
    return joined(ref[...])


def front_kernel(
    planes,
    order, rank, tokens, cotangent, gain_tile, cosine_in, sine_in,
    s_q, s_k, s_v, s_o, s_g, s_u, s_d,
    win_out, wo_out, wgu, wd,
    normed_out, query_out, key_out, value_out, q_unit_out, k_unit_out, roots_out, mixed_out, lse_out,
    resid_out, post_full, back_full, gains,
    win, wo, normed, query, key, value, q_unit, k_unit, roots, mixed, lse, resid,
    tok_full, gain_all, post_own, back_own, cosine, sine, part,
    core_out, core_in, x_out, x_in, keep, core_s, core_r, x_s, x_r,
    out_sems, in_sems, own_sems,
):
    p = Place(planes)
    s, f = p.s, p.f
    devices = 8 * planes
    wire = Wire(out_sems, in_sems, own_sems)
    reducer = Reducer(p, part, core_out, core_in, x_out, x_in, keep, (core_s, core_r, x_s, x_r))
    rows = BLOCK
    mine = pl.ds(s * rows, rows)
    theirs = pl.ds(p.x_dev[0] * rows, rows)
    length = 4 * rows
    runs = length // RUN
    p.meet()

    def spread_columns(items, full):
        came = [[] for _ in range(4)]
        for at in (0, 2, 3, 1):
            first = 0
            for item in items:
                wide = item.shape[1] // 4
                src = item.at[:, pl.ds(pl.multiple_of(p.seq_dev[at][0] * wide, RUN), wide)]
                dst = full.at[s, f, :, pl.ds(first, wide)]
                came[at].append(wire.send(src, dst, p.seq_dev[at]) if at else wire.own(src, dst))
                first += wide
        return came

    def arrived(copies, at):
        for copy in copies[at]:
            copy.wait_recv() if at else copy.wait()

    def side(here):
        return [wire.send(here, here, p.y_dev)]

    def push(here):
        return [wire.send(here, here, p.z_dev(step)) for step in range(1, planes)]

    def forward(view, far, near):
        for step, copy in enumerate(far, 1):
            copy.wait_recv()
            near += side(view(p.z_at(planes - step) * 2 + p.y))

    def settle(near):
        for copy in near:
            copy.wait_recv()

    gain_all[s, f] = gain_tile[...]
    gain_in = [wire.send(gain_all.at[s, f], gain_all.at[s, f], dev) for dev in p.seq_dev[1:]]
    first = spread_columns((s_q, s_k, s_v), win)
    out_near = [wire.send(s_o, wo.at[f], p.y_dev)]
    down_near = [wire.send(s_d, wd.at[f], p.y_dev)]
    tok_here, tok_x, tok_core = [], [], []
    for micro in range(2):
        to = tok_full.at[pl.ds(micro * runs + s * 2, 2)]
        tok_here.append(wire.own(tokens.at[micro], to))
        tok_core.append(wire.send(tokens.at[micro], to, p.core_dev))
    out_kept = wire.own(s_o, wo.at[f])
    down_kept = wire.own(s_d, wd.at[f])
    staged = [wire.own(cosine_in, cosine), wire.own(sine_in, sine), wire.own(cotangent, back_own)]

    def in_view(at):
        return lambda owner: win.at[p.seq_dev[at][0], owner]

    def wide_view(at):
        return lambda owner: wgu.at[p.seq_dev[at][0], owner]

    in_far, in_near, wide_far, wide_near = {}, [], {}, []
    arrived(first, 0)
    in_far[0] = push(in_view(0)(f))
    in_near += side(in_view(0)(f))
    for copy in gain_in:
        copy.wait_recv()
    gain_far = push(gain_all.at[:, f])
    gain_near = side(gain_all.at[:, f])
    for at in (1, 2, 3):
        arrived(first, at)
        in_near += side(in_view(at)(f))
        if at == 1:
            in_far[1] = push(in_view(1)(f))
    for micro in range(2):
        to = tok_full.at[pl.ds(micro * runs + s * 2, 2)]
        tok_x.append(wire.send(tokens.at[micro], to, p.x_dev))
    second = spread_columns((s_g, s_u), wgu)
    forward(lambda owner: gain_all.at[:, owner], gain_far, gain_near)
    forward(in_view(0), in_far[0], in_near)
    in_far[2] = push(in_view(2)(f))
    forward(in_view(1), in_far[1], in_near)
    in_far[3] = push(in_view(3)(f))
    settle(gain_near)
    table = gain_all[...].reshape(devices * 8, RUN).astype(BF16)
    gain_first = spread_gain(table, 0, devices, 1024)
    gain_post = spread_gain(table, 1, devices, 1024)
    gain_query = spread_gain(table, 2, devices, RUN)
    gain_key = spread_gain(table, 3, devices, RUN)
    gains[...] = jnp.zeros_like(gains)
    gains[0:1] = gain_first
    gains[1:2] = gain_post
    gains[2:3, 0:RUN] = gain_query
    gains[3:4, 0:RUN] = gain_key
    forward(in_view(2), in_far[2], in_near)
    out_far = [wire.send(s_o, wo.at[f], p.z_dev(step)) for step in range(1, planes)]
    forward(in_view(3), in_far[3], in_near)
    tok_fwd = []
    for micro in range(2):
        tok_x[micro].wait_recv()
        block = tok_full.at[pl.ds(micro * runs + p.x_dev[0] * 2, 2)]
        tok_fwd.append(wire.send(block, block, p.core_dev))
    for at in range(4):
        arrived(second, at)
        wide_near += side(wide_view(at)(f))
    for copy in staged:
        copy.wait()
    back_x, back_core, back_kept = [], [], []
    for micro in range(2):
        to = back_full.at[micro, mine]
        back_x.append(wire.send(cotangent.at[micro], to, p.x_dev))
        back_kept.append(wire.own(back_own.at[micro], to))
        back_core.append(wire.send(cotangent.at[micro], to, p.core_dev))
    wide_far[0] = push(wide_view(0)(f))
    down_far = [wire.send(s_d, wd.at[f], p.z_dev(step)) for step in range(1, planes)]
    settle(in_near)
    saved = [wire.own(win, win_out)]
    for copy in tok_here:
        copy.wait()
    for copy in tok_core + tok_fwd:
        copy.wait_recv()

    def project(step, carry):
        here = pl.ds(pl.multiple_of(step * BLOCK, BLOCK), BLOCK)
        raw = two_runs(tok_full, order[step * 2], order[step * 2 + 1]).astype(F32)
        root = lax.rsqrt(row_mean(raw * raw) + EPSILON)
        low = (raw * root * gains[0:1]).astype(BF16)
        normed[here] = low
        turn = pl.ds(pl.multiple_of(lax.rem(step, length // BLOCK) * BLOCK, BLOCK), BLOCK)
        cos, sin = cosine[turn], sine[turn]
        product = dot(low, flat(win))
        found, start = [], 0
        for low_ref, unit_ref, row in ((query, q_unit, 2), (key, k_unit, 3)):
            gain = gains[row : row + 1, 0:RUN]
            for head in range(low_ref.shape[1] // HEAD_DIM):
                at = slice(head * HEAD_DIM, (head + 1) * HEAD_DIM)
                one = product[:, start : start + HEAD_DIM]
                inverse = lax.rsqrt(row_mean(one * one) + EPSILON)
                unit = one * inverse
                unit_ref[here, at] = unit.astype(BF16)
                scaled = unit * gain
                low_ref[here, at] = (scaled * cos + pltpu.roll(scaled, HEAD_DIM // 2, 1) * sin).astype(BF16)
                found.append(inverse)
                start += HEAD_DIM
        for at, inverse in enumerate(found):
            roots[here, at : at + 1] = inverse
        value[here] = product[:, start:].astype(BF16)
        return carry

    def attend(step, carry):
        micro, head = step // 2, lax.rem(step, 2)
        keys_at = pl.ds(pl.multiple_of(head * HEAD_DIM, HEAD_DIM), HEAD_DIM)
        lanes = [pl.ds(pl.multiple_of(head * 2 * HEAD_DIM + g * HEAD_DIM, HEAD_DIM), HEAD_DIM) for g in range(2)]
        for block in range(length // BLOCK):
            here = pl.ds(pl.multiple_of(micro * length + block * BLOCK, BLOCK), BLOCK)
            seen = (block + 1) * BLOCK
            past = pl.ds(pl.multiple_of(micro * length, BLOCK), seen)
            asked = jnp.concatenate([query[here, lane] for lane in lanes], axis=0)
            scores = dot(asked, key[past, keys_at], NARROW)
            line = lax.broadcasted_iota(jnp.int32, (2 * BLOCK, seen), 0)
            line = jnp.where(line >= BLOCK, line - BLOCK, line) + block * BLOCK
            column = lax.broadcasted_iota(jnp.int32, (2 * BLOCK, seen), 1)
            scores = jnp.where(column <= line, scores, NEGATIVE)
            top = jnp.max(scores, axis=-1, keepdims=True)
            weight = jnp.exp2((scores - top) * (SCALE * LOG2E))
            total = jnp.sum(weight, axis=-1, keepdims=True)
            out = dot(weight.astype(BF16), value[past, keys_at]) * (1.0 / total)
            level = top * (SCALE * LOG2E) + jnp.log2(total)
            pair = pl.ds(micro * runs + block * 2, 2)
            for g, lane in enumerate(lanes):
                half = slice(g * BLOCK, (g + 1) * BLOCK)
                mixed[pair, :, lane] = out[half].astype(BF16).reshape(2, RUN, HEAD_DIM)
                lse[step, pl.ds(block * BLOCK, BLOCK), g : g + 1] = level[half]
        return carry

    def mix_out(step, carry):
        micro, block = reducer.block(step)
        at = micro * runs + block * 2
        low = two_runs(mixed, rank[at], rank[at + 1])
        part[...] = dot(low, flat(wo))
        reducer.take(step)
        return carry

    posts = []

    def finish(micro):
        own = joined(tok_full[pl.ds(micro * runs + s * 2, 2)]).astype(F32)
        total = own + reducer.total(micro)
        resid[micro] = total
        root = lax.rsqrt(row_mean(total * total) + EPSILON)
        post_own[micro] = (total * root * gains[1:2]).astype(BF16)
        to = post_full.at[micro, mine]
        posts.append((wire.send(post_own.at[micro], to, p.x_dev), wire.send(post_own.at[micro], to, p.core_dev),
                      wire.own(post_own.at[micro], to)))
        saved.append(wire.own(resid.at[micro], resid_out.at[micro]))

    steps = length // BLOCK
    lax.fori_loop(0, steps, project, 0)
    forward(lambda owner: wo.at[owner], out_far, out_near)
    wide_far[1] = push(wide_view(1)(f))
    lax.fori_loop(0, 2, attend, 0)
    lax.fori_loop(steps, 2 * steps, project, 0)
    saved += [wire.own(here, there) for here, there in (
        (normed, normed_out), (query, query_out), (key, key_out), (value, value_out),
        (q_unit, q_unit_out), (k_unit, k_unit_out), (roots, roots_out))]
    out_kept.wait()
    settle(out_near)
    lax.fori_loop(0, 4, mix_out, 0)
    forward(wide_view(0), wide_far[0], wide_near)
    wide_far[2] = push(wide_view(2)(f))
    lax.fori_loop(2, 4, attend, 0)
    lax.fori_loop(4, 8, mix_out, 0)
    saved += [wire.own(mixed, mixed_out), wire.own(lse, lse_out), wire.own(wo, wo_out)]
    wide_far[3] = push(wide_view(3)(f))
    finish(0)
    forward(lambda owner: wd.at[owner], down_far, down_near)
    forward(wide_view(1), wide_far[1], wide_near)
    for micro in range(2):
        back_x[micro].wait_recv()
        block = back_full.at[micro, theirs]
        back_core.append(wire.send(block, block, p.core_dev))
    finish(1)
    forward(wide_view(2), wide_far[2], wide_near)
    forward(wide_view(3), wide_far[3], wide_near)
    last = []
    for micro in range(2):
        posts[micro][0].wait_recv()
        block = post_full.at[micro, theirs]
        last.append(wire.send(block, block, p.core_dev))
    for micro in range(2):
        last[micro].wait_recv()
        posts[micro][1].wait_recv()
        posts[micro][2].wait()
    for copy in back_core:
        copy.wait_recv()
    for copy in back_kept + saved + [down_kept]:
        copy.wait()
    settle(wide_near)
    settle(down_near)
    reducer.close()
    wire.close()


def front(planes, order, rank, tokens, cotangent, gain_tile, cosine, sine, shards):
    nf = 2 * planes
    rows = tokens.shape[1]
    length = 4 * rows
    total = 2 * length
    tokens = tokens.reshape(2, 2, RUN, tokens.shape[2])
    deep = shards[0].shape[0]

    def low(width):
        return jax.ShapeDtypeStruct((total, width), BF16)

    shapes = [
        jax.ShapeDtypeStruct((4, nf, deep, 1024), BF16), jax.ShapeDtypeStruct((nf, *shards[3].shape), BF16),
        jax.ShapeDtypeStruct((4, nf, deep, 2 * (shards[4].shape[1] // 4)), BF16),
        jax.ShapeDtypeStruct((nf, *shards[6].shape), BF16),
        low(1024), low(512), low(256), low(256), low(512), low(256),
        jax.ShapeDtypeStruct((total, 8), F32), jax.ShapeDtypeStruct((total // RUN, RUN, 512), BF16),
        jax.ShapeDtypeStruct((4, length, 2), F32), jax.ShapeDtypeStruct((2, rows, 1024), F32),
        jax.ShapeDtypeStruct((2, length, 1024), BF16), jax.ShapeDtypeStruct((2, length, 1024), BF16),
        jax.ShapeDtypeStruct((8, 1024), F32)]
    held = [shapes[at] for at in (0, 1, *range(4, 14))]
    vm = pl.BlockSpec(memory_space=VMEM)
    hb = pl.BlockSpec(memory_space=ANY)
    sm = pl.BlockSpec(memory_space=pltpu.SMEM)
    return pl.pallas_call(
        functools.partial(front_kernel, planes),
        out_shape=shapes,
        in_specs=[sm, sm, hb, hb, vm, hb, hb, hb, hb, hb, hb, vm, vm, vm],
        out_specs=[hb] * (len(shapes) - 1) + [vm],
        scratch_shapes=[
            *[VMEM(item.shape, item.dtype) for item in held],
            VMEM((total // RUN, RUN, 1024), BF16), VMEM((4, nf, 8, RUN), F32), VMEM((2, rows, 1024), BF16),
            VMEM((2, rows, 1024), BF16), VMEM(cosine.shape, F32), VMEM(sine.shape, F32),
            VMEM((BLOCK, 1024), F32), *reducer_scratch(1024), *wire_scratch(130, 40),
        ],
        compiler_params=pltpu.CompilerParams(
            collective_id=0, has_side_effects=True, vmem_limit_bytes=VMEM_BYTES),
        name="front",
    )(order, rank, tokens, cotangent, gain_tile, cosine, sine, *shards)


GROUPS = (2, 3, 1, 0)


class RowHoming:
    def __init__(self, place, wire, grad, came, sums, far, home):
        self.p, self.wire, self.grad = place, wire, grad
        self.came, self.sums, self.far, self.home = came, sums, far, home

    def half(self, ref, at):
        return ref.at[pl.ds(at * (self.p.planes // 2), self.p.planes // 2)]

    def start(self):
        p = self.p
        self.kept = self.wire.own(self.grad.at[:, p.y], self.sums)
        self.sent = [
            self.wire.send(self.half(self.grad, at).at[:, p.other_y], self.half(self.came, at), p.y_dev)
            for at in range(2)
        ]
        self.out = [
            self.wire.send(self.sums.at[p.z_at(step)], self.far.at[step - 1], p.z_dev(step), start=False)
            for step in range(1, p.planes)
        ]

    def push(self, at):
        if at == 0:
            self.kept.wait()
        self.sent[at].wait_recv()
        share = self.p.planes // 2

        def add(z, carry):
            self.sums[z] = (self.sums[z].astype(F32) + self.came[z].astype(F32)).astype(BF16)
            return carry

        lax.fori_loop(at * share, (at + 1) * share, add, 0)
        for step, copy in enumerate(self.out, 1):
            @pl.when(self.p.z_at(step) // share == at)
            def _(copy=copy):
                copy.start()

    def gather(self):
        for copy in self.out:
            copy.wait_recv()
        total = self.sums[self.p.z].astype(F32)
        for step in range(1, self.p.planes):
            total = total + self.far[step - 1].astype(F32)
        self.home[...] = total


class ColumnHoming:
    def __init__(self, place, wire, came, sums, far, leave=None, arrive=None, homes=()):
        self.p, self.wire, self.came, self.sums, self.far = place, wire, came, sums, far
        self.leave, self.arrive, self.homes = leave, arrive, homes
        self.kept, self.sent, self.out, self.back = {}, {}, {}, {}

    def start(self, at, grad):
        self.kept[at] = self.wire.own(grad.at[:, self.p.y], self.sums.at[at])
        self.sent[at] = self.wire.send(grad.at[:, self.p.other_y], self.came.at[at], self.p.y_dev)

    def add(self, at):
        self.kept[at].wait()
        self.sent[at].wait_recv()

        def add(z, carry):
            self.sums[at, z] = (self.sums[at, z].astype(F32) + self.came[at, z].astype(F32)).astype(BF16)
            return carry

        lax.fori_loop(0, self.p.planes, add, 0)

    def push(self, at):
        self.out[at] = [
            self.wire.send(self.sums.at[at, self.p.z_at(step)], self.far.at[at, step - 1], self.p.z_dev(step))
            for step in range(1, self.p.planes)
        ]

    def put(self, owner, value):
        first = 0
        for home in self.homes:
            width = home.shape[1] // 4
            home[:, pl.ds(pl.multiple_of(owner * width, RUN), width)] = value[:, first : first + width]
            first += width

    def gather(self, at):
        for copy in self.out[at]:
            copy.wait_recv()
        total = self.sums[at, self.p.z].astype(F32)
        for step in range(1, self.p.planes):
            total = total + self.far[at, step - 1].astype(F32)
        if GROUPS[at] == 0:
            self.put(self.p.s, total)
            return
        self.leave[at] = total.astype(BF16)
        self.back[at] = self.wire.send(self.leave.at[at], self.arrive.at[at], self.p.seq_dev[GROUPS[at]])

    def finish(self):
        for at, copy in self.back.items():
            copy.wait_recv()
            self.put(self.p.seq_dev[GROUPS[at]][0], self.arrive[at].astype(F32))


def group_rows(place, at):
    owner = place.seq_dev[GROUPS[at]][0]
    return pl.ds(pl.multiple_of(owner * BLOCK, BLOCK), BLOCK)


def column_scratch(planes, deep, width, groups=4):
    return [
        VMEM((groups, planes, deep, width), BF16), VMEM((groups, planes, deep, width), BF16),
        VMEM((4, planes - 1, deep, width), BF16), VMEM((3, deep, width), BF16), VMEM((3, deep, width), BF16),
    ]


def row_scratch(planes, deep, width):
    return [VMEM((planes, deep, width), BF16), VMEM((planes, deep, width), BF16),
            VMEM((planes - 1, deep, width), BF16)]


def middle_kernel(
    planes,
    post_in, back_in, wgu_in, wd_in, resid_in, gains,
    ready, grad_rest, home_d, y_out, y_keep, d_resid, attn_full, sums,
    post, back, wgu, wd, resid, load_sems,
    grad_first, g_came, grad_d, d_came, d_sums, d_far, hidden, d_gu, part, attn_own,
    y_core_out, y_core_in,
    core_out, core_in, x_out, x_in, keep, core_s, core_r, x_s, x_r,
    y_core_s, y_core_r, out_sems, in_sems, own_sems,
):
    p = Place(planes)
    s = p.s
    wire = Wire(out_sems, in_sems, own_sems)
    into_post = Reducer(p, part, core_out, core_in, x_out, x_in, keep, (core_s, core_r, x_s, x_r))
    into_out = Reducer(p, part, y_core_out, y_core_in, y_out, None, y_keep, (y_core_s, y_core_r, None, None))
    rows = resid.shape[1]
    length = 4 * rows
    wide = hidden.shape[1]
    mine = pl.ds(s * rows, rows)
    theirs = pl.ds(p.x_dev[0] * rows, rows)
    loads = [wire.own(wgu_in, wgu), wire.own(wd_in, wd), wire.own(resid_in, resid)]

    def chunk(step):
        micro, block = into_post.block(step)
        here = pl.ds(pl.multiple_of(micro * length + block * BLOCK, BLOCK), BLOCK)
        return [pltpu.make_async_copy(far.at[here], near.at[here], load_sems.at[at, step])
                for at, (far, near) in enumerate(((post_in, post), (back_in, back)))]

    for step in range(8):
        for copy in chunk(step):
            copy.start()
    p.meet()
    for copy in loads:
        copy.wait()

    def feed(step, carry):
        micro, block = into_post.block(step)
        here = pl.ds(pl.multiple_of(micro * length + block * BLOCK, BLOCK), BLOCK)
        for copy in chunk(step):
            copy.wait()
        both = dot(post[here, :], wgu[...])
        d_hidden = dot(back[here, :], wd[...], NARROW)
        gate, upper = both[:, :wide], both[:, wide:]
        sigma = 1.0 / (1.0 + jnp.exp(-gate))
        lit = gate * sigma
        hidden[here] = (lit * upper).astype(BF16)
        d_gu[here, :wide] = (d_hidden * upper * (sigma + lit * (1.0 - sigma))).astype(BF16)
        d_gu[here, wide:] = (d_hidden * lit).astype(BF16)
        part[...] = dot(d_gu[here, :], wgu[...], NARROW)
        into_post.take(step)
        part[...] = dot(hidden[here, :], wd[...])
        into_out.take(step, send_x=False)
        return carry

    down = RowHoming(p, wire, grad_d, d_came, d_sums, d_far, home_d)
    columns = ColumnHoming(p, wire, g_came, ready, None)

    def down_tile(at, carry):
        tall = wide // 2
        cut = pl.ds(pl.multiple_of(at * tall, RUN), tall)
        found = dot(hidden[:, cut], back[...], TALL).astype(BF16)
        grad_d[pl.ds(at * (planes // 2), planes // 2)] = found.reshape(planes // 2, *grad_d.shape[1:])
        return carry

    def wide_tile(at):
        found = dot(post[:, group_rows(p, at)], d_gu[...], TALL).astype(BF16)
        return found.reshape(grad_first.shape)

    gain = gains[1:2]
    sends = []
    sums[...] = jnp.zeros_like(sums)

    def settle(micro):
        grad = into_post.total(micro)
        held = resid[micro]
        root = lax.rsqrt(row_mean(held * held) + EPSILON)
        unit = held * root
        sums[0:1] += jnp.sum(grad * unit, axis=0, keepdims=True)
        scaled = grad * gain
        own = back[pl.ds(pl.multiple_of(micro * length + s * rows, rows), rows), :].astype(F32)
        whole = own + root * (scaled - unit * row_mean(scaled * unit))
        d_resid[micro] = whole
        attn_own[micro] = whole.astype(BF16)
        to = attn_full.at[micro, mine]
        sends.append((wire.send(attn_own.at[micro], to, p.x_dev), wire.send(attn_own.at[micro], to, p.core_dev),
                      wire.own(attn_own.at[micro], to)))
        y_keep[micro] = y_keep[micro] + held

    lax.fori_loop(0, 7, feed, 0)
    settle(0)
    lax.fori_loop(7, 8, feed, 0)
    lax.fori_loop(0, 2, down_tile, 0)
    down.start()
    grad_first[...] = wide_tile(0)
    columns.start(0, grad_first)
    settle(1)
    grad_rest[0] = wide_tile(1)
    down.push(0)
    grad_rest[1] = wide_tile(2)
    grad_rest[2] = wide_tile(3)
    down.push(1)
    forwards = []
    for micro in range(2):
        sends[micro][0].wait_recv()
        block = attn_full.at[micro, theirs]
        forwards.append(wire.send(block, block, p.core_dev))
    columns.add(0)
    for micro in range(2):
        forwards[micro].wait_recv()
        sends[micro][1].wait_recv()
        sends[micro][2].wait()
    down.gather()
    into_post.close()
    into_out.close(send_x=False)
    wire.close()


def middle(planes, post, back, wgu, wd, resid, gains):
    rows = resid.shape[1]
    total = 8 * rows
    wide = wd.shape[0]
    deep = 1024 // (8 * planes)
    once = (planes, 2, deep, 2 * wide)
    slim = (planes, 2, wide // (2 * planes), 1024)
    shapes = [
        jax.ShapeDtypeStruct((1, planes, deep, 2 * wide), BF16), jax.ShapeDtypeStruct((3, *once), BF16),
        jax.ShapeDtypeStruct(slim[2:], F32),
        jax.ShapeDtypeStruct((2, rows, 1024), BF16), jax.ShapeDtypeStruct((2, rows, 1024), F32),
        jax.ShapeDtypeStruct((2, rows, 1024), F32), jax.ShapeDtypeStruct((2, 4 * rows, 1024), BF16),
        jax.ShapeDtypeStruct((8, 1024), F32),
    ]
    vm = pl.BlockSpec(memory_space=VMEM)
    hb = pl.BlockSpec(memory_space=ANY)
    return pl.pallas_call(
        functools.partial(middle_kernel, planes),
        out_shape=shapes,
        in_specs=[hb] * 5 + [vm],
        out_specs=[vm] * 6 + [hb, vm],
        scratch_shapes=[
            *[VMEM(item.shape, item.dtype) for item in (post, back, wgu, wd, resid)],
            pltpu.SemaphoreType.DMA((2, 8)),
            VMEM(once, BF16), VMEM((1, planes, deep, 2 * wide), BF16), VMEM(slim, BF16),
            *row_scratch(planes, *slim[2:]),
            VMEM((total, wide), BF16), VMEM((total, 2 * wide), BF16),
            VMEM((BLOCK, 1024), F32), VMEM((2, rows, 1024), BF16),
            VMEM((4, BLOCK, 1024), BF16), VMEM((4, BLOCK, 1024), BF16),
            *reducer_scratch(1024),
            pltpu.SemaphoreType.DMA((4,)), pltpu.SemaphoreType.DMA((4,)),
            *wire_scratch(16, 10),
        ],
        compiler_params=pltpu.CompilerParams(
            collective_id=1, has_side_effects=True, vmem_limit_bytes=VMEM_BYTES),
        name="middle",
    )(post, back, wgu, wd, resid, gains)


def turn_kernel(
    planes,
    order, attn_in, query_in, key_in, value_in, q_unit_in, k_unit_in, roots_in, mixed_in, lse_in, wo_in,
    cosine, sine, gains, y_out, y_keep_in, sums_in, ready, grad_rest,
    d_in_out, sums, block_out, home_g, home_u, home_o,
    attn, query, key, value, q_unit, k_unit, roots, mixed, lse, wo, y_keep, d_in,
    d_mixed, attn_sorted, keys_grad, values_grad, y_in, grad_o,
    g_came, g_sums, g_far, g_leave, g_arrive, o_came, o_sums, o_far,
    out_sems, in_sems, own_sems,
):
    p = Place(planes)
    wire = Wire(out_sems, in_sems, own_sems)
    rows = y_keep.shape[1]
    length = 4 * rows
    loads = [wire.own(far, near) for far, near in (
        (attn_in, attn), (wo_in, wo), (mixed_in, mixed), (query_in, query), (key_in, key), (value_in, value),
        (q_unit_in, q_unit), (k_unit_in, k_unit), (roots_in, roots), (lse_in, lse), (y_keep_in, y_keep))]
    p.meet()
    wide = ColumnHoming(p, wire, g_came, g_sums, g_far, g_leave, g_arrive, (home_g, home_u))
    outer = RowHoming(p, wire, grad_o, o_came, o_sums, o_far, home_o)
    wide.start(1, grad_rest.at[0])
    g_sums[0] = ready[0]
    wide.push(0)
    y_sent = [wire.send(y_out.at[micro], y_in.at[micro], p.x_dev) for micro in range(2)]
    loads[0].wait()
    loads[1].wait()

    def draw(step, carry):
        here = pl.ds(pl.multiple_of(step * BLOCK, BLOCK), BLOCK)
        low = two_runs(attn, order[step * 2], order[step * 2 + 1])
        attn_sorted[here] = low
        d_mixed[here] = dot(low, wo[...], NARROW).astype(BF16)
        return carry

    lax.fori_loop(0, 2 * length // BLOCK, draw, 0)

    def out_tile(at, carry):
        cut = pl.ds(pl.multiple_of(at * BLOCK, BLOCK), BLOCK)
        found = dot(mixed[:, cut], attn_sorted[...], TALL).astype(BF16)
        grad_o[pl.ds(at * (planes // 2), planes // 2)] = found.reshape(planes // 2, *grad_o.shape[1:])
        return carry

    loads[2].wait()
    lax.fori_loop(0, 2, out_tile, 0)
    wide.start(2, grad_rest.at[1])
    wide.add(1)
    wide.push(1)
    sums[...] = sums_in[...]

    def lane_of(ref, here, lane):
        held = ref[here, :]
        lanes = lax.broadcasted_iota(jnp.int32, held.shape, 1)
        return jnp.sum(jnp.where(lanes == lane, held, 0.0), axis=1, keepdims=True)

    def norm_home(grad, cos, sin, unit, root, gain):
        turned = grad * cos - pltpu.roll(grad, HEAD_DIM // 2, 1) * sin
        scaled = turned * gain
        back = root * (scaled - unit * row_mean(scaled * unit))
        return back, jnp.sum(turned * unit, axis=0, keepdims=True)

    def attend_back(step, carry):
        micro, head = step // 2, lax.rem(step, 2)
        keys_at = pl.ds(pl.multiple_of(head * HEAD_DIM, HEAD_DIM), HEAD_DIM)
        lanes = [pl.ds(pl.multiple_of(head * 2 * HEAD_DIM + g * HEAD_DIM, HEAD_DIM), HEAD_DIM) for g in range(2)]
        q_gain, k_gain = gains[2:3, 0:RUN], gains[3:4, 0:RUN]
        keys_grad[...] = jnp.zeros_like(keys_grad)
        values_grad[...] = jnp.zeros_like(values_grad)
        for block in range(length // BLOCK):
            here = pl.ds(pl.multiple_of(micro * length + block * BLOCK, BLOCK), BLOCK)
            seen = (block + 1) * BLOCK
            past = pl.ds(pl.multiple_of(micro * length, BLOCK), seen)
            asked = jnp.concatenate([query[here, lane] for lane in lanes], axis=0)
            pulled = jnp.concatenate([d_mixed[here, lane] for lane in lanes], axis=0)
            given = jnp.concatenate([mixed[here, lane] for lane in lanes], axis=0)
            level = jnp.concatenate(
                [lse[step, pl.ds(block * BLOCK, BLOCK), g : g + 1] for g in range(2)], axis=0)
            delta = jnp.sum(pulled.astype(F32) * given.astype(F32), axis=1, keepdims=True)
            scores = dot(asked, key[past, keys_at], NARROW)
            line = lax.broadcasted_iota(jnp.int32, (2 * BLOCK, seen), 0)
            line = jnp.where(line >= BLOCK, line - BLOCK, line) + block * BLOCK
            column = lax.broadcasted_iota(jnp.int32, (2 * BLOCK, seen), 1)
            weight = jnp.exp2(scores * (SCALE * LOG2E) - level)
            weight = jnp.where(column <= line, weight, 0.0)
            d_soft = dot(pulled, value[past, keys_at], NARROW)
            d_scores = (weight * (d_soft - delta)).astype(BF16)
            values_grad[0:seen] += dot(weight.astype(BF16), pulled, TALL)
            keys_grad[0:seen] += dot(d_scores, asked, TALL)
            moved = dot(d_scores, key[past, keys_at]) * SCALE
            spin = slice(block * BLOCK, (block + 1) * BLOCK)
            for g, lane in enumerate(lanes):
                root = lane_of(roots, here, head * 2 + g)
                unit = q_unit[here, lane].astype(F32)
                back, gained = norm_home(
                    moved[g * BLOCK : (g + 1) * BLOCK], cosine[spin], sine[spin], unit, root, q_gain)
                d_in[here, lane] = back.astype(BF16)
                sums[1:2, 0:RUN] += gained
        everything = pl.ds(pl.multiple_of(micro * length, BLOCK), length)
        root = lane_of(roots, everything, head + 4)
        unit = k_unit[everything, keys_at].astype(F32)
        back, gained = norm_home(keys_grad[...] * SCALE, cosine[...], sine[...], unit, root, k_gain)
        at = head * HEAD_DIM
        d_in[everything, pl.ds(pl.multiple_of(512 + at, HEAD_DIM), HEAD_DIM)] = back.astype(BF16)
        sums[2:3, 0:RUN] += gained
        d_in[everything, pl.ds(pl.multiple_of(768 + at, HEAD_DIM), HEAD_DIM)] = values_grad[...].astype(BF16)
        return carry

    for copy in loads[3:]:
        copy.wait()
    lax.fori_loop(0, 1, attend_back, 0)
    wide.start(3, grad_rest.at[2])
    wide.add(2)
    wide.push(2)
    lax.fori_loop(1, 2, attend_back, 0)
    outer.start()
    wide.add(3)
    wide.push(3)
    wide.gather(0)

    def save(micro):
        half = pl.ds(micro * length, length)
        return wire.own(d_in.at[half], d_in_out.at[half])

    saved = [save(0)]
    for micro in range(2):
        y_sent[micro].wait_recv()
        block_out[micro] = (y_keep[micro] + y_in[micro].astype(F32)).astype(BF16)
    lax.fori_loop(2, 3, attend_back, 0)
    outer.push(0)
    outer.push(1)
    wide.gather(1)
    lax.fori_loop(3, 4, attend_back, 0)
    saved.append(save(1))
    wide.gather(2)
    wide.gather(3)
    outer.gather()
    wide.finish()
    for copy in saved:
        copy.wait()
    wire.close()


def turn(planes, order, attn, query, key, value, q_unit, k_unit, roots, mixed, lse, wo, cosine, sine, gains,
         y_out, y_keep, sums, ready, grad_rest):
    rows = y_keep.shape[1]
    length = 4 * rows
    total = 2 * length
    deep, wide = grad_rest.shape[3:]
    slim = (planes, 2, 512 // (2 * planes), 1024)
    shapes = [
        jax.ShapeDtypeStruct((total, 1024), BF16),
        jax.ShapeDtypeStruct((8, 1024), F32), jax.ShapeDtypeStruct((2, rows, 1024), BF16),
        jax.ShapeDtypeStruct((deep, 2 * wide), F32), jax.ShapeDtypeStruct((deep, 2 * wide), F32),
        jax.ShapeDtypeStruct(slim[2:], F32),
    ]
    held = (attn, query, key, value, q_unit, k_unit, roots, mixed, lse, wo, y_keep, shapes[0])
    vm = pl.BlockSpec(memory_space=VMEM)
    hb = pl.BlockSpec(memory_space=ANY)
    sm = pl.BlockSpec(memory_space=pltpu.SMEM)
    return pl.pallas_call(
        functools.partial(turn_kernel, planes),
        out_shape=shapes,
        in_specs=[sm] + [hb] * 10 + [vm] * 3 + [hb, hb, vm, vm, hb],
        out_specs=[hb] + [vm] * (len(shapes) - 1),
        scratch_shapes=[
            *[VMEM(item.shape, item.dtype) for item in held],
            VMEM((total, 512), BF16), VMEM((total, 1024), BF16), VMEM((length, HEAD_DIM), F32),
            VMEM((length, HEAD_DIM), F32), VMEM((2, rows, 1024), BF16), VMEM(slim, BF16),
            *column_scratch(planes, deep, wide), *row_scratch(planes, *slim[2:]), *wire_scratch(32, 24),
        ],
        compiler_params=pltpu.CompilerParams(
            collective_id=2, has_side_effects=True, vmem_limit_bytes=VMEM_BYTES),
        name="turn",
    )(order, attn, query, key, value, q_unit, k_unit, roots, mixed, lse, wo, cosine, sine, gains,
      y_out, y_keep, sums, ready, grad_rest)


def last_kernel(
    planes,
    rank, normed_in, d_in_in, win_in, tokens, d_resid_in, gains, sums_in,
    token_grad, sums, home_q, home_k, home_v,
    normed, d_in, win, d_resid, grad,
    part, sums_out, sums_came,
    core_out, core_in, x_out, x_in, keep, core_s, core_r, x_s, x_r,
    came, held_sums, far, leave, arrive, out_sems, in_sems, own_sems,
):
    p = Place(planes)
    wire = Wire(out_sems, in_sems, own_sems)
    reducer = Reducer(p, part, core_out, core_in, x_out, x_in, keep, (core_s, core_r, x_s, x_r))
    rows = tokens.shape[1]
    length = 4 * rows
    loads = [wire.own(far_ref, near) for far_ref, near in (
        (d_in_in, d_in), (normed_in, normed), (win_in, win), (d_resid_in, d_resid))]
    p.meet()
    home = ColumnHoming(p, wire, came, held_sums, far, leave, arrive, (home_q, home_k, home_v))
    loads[0].wait()
    loads[1].wait()

    def tile(at):
        found = dot(joined(normed[:, :, group_rows(p, at)]), flat(d_in), TALL).astype(BF16)
        grad[at] = found.reshape(grad.shape[1:])

    tile(0)
    home.start(0, grad.at[0])
    tile(1)
    tile(2)
    tile(3)
    home.start(1, grad.at[1])
    for copy in loads[2:]:
        copy.wait()
    sums[...] = sums_in[...]

    def pull(step, carry):
        micro, block = reducer.block(step)
        at = micro * (length // RUN) + block * 2
        runs = (rank[at], rank[at + 1])
        found = dot(two_runs(d_in, *runs), win[...], NARROW)
        part[...] = found
        sums[3:4] += jnp.sum(found * two_runs(normed, *runs).astype(F32), axis=0, keepdims=True)
        reducer.take(step)
        return carry

    lax.fori_loop(0, 4, pull, 0)
    home.add(0)
    home.push(0)
    home.start(2, grad.at[2])
    lax.fori_loop(4, 8, pull, 0)
    home.add(1)
    home.push(1)
    home.start(3, grad.at[3])
    sums[3:4] = sums[3:4] / gains[0:1]

    def exchange(stage, devices, base):
        sums_out[stage] = sums[...]
        sent = [wire.send(sums_out.at[stage], sums_came.at[base + at], dev) for at, dev in enumerate(devices)]
        return base, sent

    def absorb(state):
        base, sent = state
        total = sums[...]
        for at, copy in enumerate(sent):
            copy.wait_recv()
            total = total + sums_came[base + at]
        sums[...] = total

    state = exchange(0, p.seq_dev[1:], 0)
    absorb(state)
    state = exchange(1, [p.z_dev(step) for step in range(1, planes)], 3)
    home.add(2)
    home.push(2)
    home.gather(0)
    absorb(state)
    state = exchange(2, [p.y_dev], 2 + planes)
    home.add(3)
    home.push(3)
    home.gather(1)
    for micro in range(2):
        grad_rows = reducer.total(micro)
        raw = tokens[micro].astype(F32)
        root = lax.rsqrt(row_mean(raw * raw) + EPSILON)
        unit = raw * root
        scaled = grad_rows * gains[0:1]
        token_grad[micro] = d_resid[micro] + root * (scaled - unit * row_mean(scaled * unit))
    absorb(state)
    home.gather(2)
    home.gather(3)
    home.finish()
    reducer.close()
    wire.close()


def last(planes, rank, normed, d_in, win, tokens, d_resid, gains, sums):
    rows = tokens.shape[1]
    deep = 1024 // (8 * planes)
    shapes = [
        jax.ShapeDtypeStruct((2, rows, 1024), F32), jax.ShapeDtypeStruct((8, 1024), F32),
        jax.ShapeDtypeStruct((deep, 2048), F32), jax.ShapeDtypeStruct((deep, 1024), F32),
        jax.ShapeDtypeStruct((deep, 1024), F32),
    ]
    vm = pl.BlockSpec(memory_space=VMEM)
    hb = pl.BlockSpec(memory_space=ANY)
    sm = pl.BlockSpec(memory_space=pltpu.SMEM)
    held = (normed, d_in, win, d_resid)
    return pl.pallas_call(
        functools.partial(last_kernel, planes),
        out_shape=shapes,
        in_specs=[sm] + [hb] * 3 + [vm, hb, vm, vm],
        out_specs=[vm] * len(shapes),
        scratch_shapes=[
            *[VMEM(item.shape, item.dtype) for item in held], VMEM((4, planes, 2, deep, 1024), BF16),
            VMEM((BLOCK, 1024), F32), VMEM((3, 8, 1024), F32), VMEM((3 + planes, 8, 1024), F32),
            *reducer_scratch(1024), *column_scratch(planes, deep, 1024), *wire_scratch(48, 16),
        ],
        compiler_params=pltpu.CompilerParams(
            collective_id=3, has_side_effects=True, vmem_limit_bytes=VMEM_BYTES),
        name="last",
    )(rank, normed, d_in, win, tokens, d_resid, gains, sums)


def deliver_kernel(count, *refs):
    given, made, held, sems = refs[:count], refs[count : 2 * count], refs[2 * count : 3 * count], refs[3 * count]
    came = [pltpu.make_async_copy(src, mid, sems.at[0, at]) for at, (src, mid) in enumerate(zip(given, held))]
    gone = [pltpu.make_async_copy(mid, dst, sems.at[1, at]) for at, (mid, dst) in enumerate(zip(held, made))]
    for copy in came:
        copy.start()
    for first, second in zip(came, gone):
        first.wait()
        second.start()
    for copy in gone:
        copy.wait()


def deliver(*items):
    count = len(items)
    return pl.pallas_call(
        functools.partial(deliver_kernel, count),
        out_shape=[jax.ShapeDtypeStruct(item.shape, item.dtype) for item in items],
        in_specs=[pl.BlockSpec(memory_space=ANY)] * count,
        out_specs=[pl.BlockSpec(memory_space=ANY)] * count,
        scratch_shapes=[*[VMEM(item.shape, item.dtype) for item in items], pltpu.SemaphoreType.DMA((2, count))],
        compiler_params=pltpu.CompilerParams(vmem_limit_bytes=VMEM_BYTES),
        name="deliver",
    )(*items)


def run_tables(positions):
    runs = positions.shape[1] // RUN
    rank = positions[:, ::RUN] // RUN
    index = jnp.arange(runs, dtype=jnp.int32)
    order = jnp.sum(jnp.where(rank[:, :, None] == index, index[None, :, None], 0), axis=1)
    base = jnp.arange(positions.shape[0], dtype=jnp.int32)[:, None] * runs
    return (order + base).reshape(-1), (rank + base).reshape(-1)


def turn_tables(length):
    half = HEAD_DIM // 2
    frequency = (ROPE_BASE ** (-np.arange(half) * 2.0 / HEAD_DIM)).astype(np.float32)
    angles = (np.arange(length, dtype=np.float32)[:, None] * frequency[None, :]).astype(np.float64)
    cosine, sine = np.cos(angles), np.sin(angles)
    return (jnp.asarray(np.concatenate([cosine, cosine], axis=1).astype(np.float32)),
            jnp.asarray(np.concatenate([-sine, sine], axis=1).astype(np.float32)))


def kernel_body(tokens, positions, g_in, g_post, g_query, g_key, w_query, w_key, w_value,
                w_out, w_gate, w_up, w_down, cotangent):
    planes = lax.axis_size("fsdp") // 2
    length = positions.shape[2]
    order, rank = run_tables(positions[:, 0])
    tile = jnp.stack(
        [jnp.pad(item.astype(F32), (0, RUN - item.shape[0])) for item in (g_in, g_post, g_query, g_key)])
    tile = jnp.pad(tile, ((0, 4), (0, 0)))
    cosine, sine = turn_tables(length)
    near = tokens[:, 0]
    shards = (w_query, w_key, w_value, w_out, w_gate, w_up, w_down)
    (win, wo, wgu, wd, normed, query, key, value, q_unit, k_unit, roots, mixed, lse,
     resid, post, back, gains) = front(
        planes, order, rank, near, cotangent[:, 0], tile, cosine, sine, shards)
    plain = lambda item: item.reshape(-1, item.shape[-1])
    apart = lambda item: item.reshape(-1, RUN, item.shape[-1])
    win, wo, wgu, wd, post, back = [plain(item) for item in (win, wo, wgu, wd, post, back)]
    ready, grad_rest, home_d, y_out, y_keep, d_resid, attn, sums = middle(
        planes, post, back, wgu, wd, resid, gains)
    d_in, sums, block_out, home_g, home_u, home_o = turn(
        planes, order, apart(attn), query, key, value, q_unit, k_unit, roots, plain(mixed), lse,
        wo, cosine, sine, gains, y_out, y_keep, sums, ready, grad_rest)
    token_grad, sums, home_q, home_k, home_v = last(
        planes, rank, apart(normed), apart(d_in), win, near, d_resid, gains, sums)
    me = lax.axis_index("seq") * (2 * planes) + lax.axis_index("fsdp")
    small = [
        lax.dynamic_slice(sums, (row, me * item.shape[0]), (1, item.shape[0]))[0]
        for row, item in ((3, g_in), (0, g_post), (1, g_query), (2, g_key))
    ]
    token_grad, block_out, *homes = deliver(
        token_grad, block_out, home_d, home_g, home_u, home_o, home_q, home_k, home_v)
    home_d, home_g, home_u, home_o, home_q, home_k, home_v = homes
    return (block_out[:, None], token_grad[:, None], *small, home_q, home_k, home_v, home_o,
            home_g, home_u, home_d)


def solution(mesh):
    both = ("seq", "fsdp")
    act = P(None, "fsdp", "seq", None)
    vec, mat = P(both), P(both, None)

    def body(*args):
        rows = args[6].shape[0]
        fits = mesh.shape["seq"] == 4 and mesh.shape["fsdp"] % 2 == 0 and rows % 16 == 0
        return (kernel_body if fits else plain_body)(*args)

    return jax.shard_map(
        body,
        mesh=mesh,
        in_specs=(act, P(None, "fsdp", None), *[vec] * 4, *[mat] * 7, act),
        out_specs=(act, act, *[vec] * 4, *[mat] * 7),
        check_vma=False,
    )
```

```python
import functools

import jax
import jax.numpy as jnp
import numpy as np
from jax import lax
from jax.experimental import pallas as pl
from jax.experimental.pallas import tpu as pltpu
from jax.sharding import PartitionSpec as P

HEADS = 16
KV_HEADS = 8
HEAD_DIM = 128
EPSILON = 1e-06
ROPE_BASE = 1000000.0
NEGATIVE = -1e30
F32 = jnp.float32
BF16 = jnp.bfloat16


def inverse_root(values):
    return lax.rsqrt(jnp.mean(values * values, axis=-1, keepdims=True) + EPSILON)


def rope_tables(token_pos):
    half_width = HEAD_DIM // 2
    frequency = ROPE_BASE ** (-(jnp.arange(half_width, dtype=F32) * 2.0 / HEAD_DIM))
    angles = token_pos.astype(F32)[:, None] * frequency[None, :]
    cosine = jnp.cos(angles)
    sine = jnp.sin(angles)
    return (
        jnp.concatenate([cosine, cosine], axis=-1)[:, None, :],
        jnp.concatenate([sine, sine], axis=-1)[:, None, :],
    )


def rotate(values, cosine, sine):
    half_width = values.shape[-1] // 2
    turned = jnp.concatenate([-values[..., half_width:], values[..., :half_width]], axis=-1)
    return values * cosine + turned * sine


def rotate_back(grads, cosine, sine):
    half_width = grads.shape[-1] // 2
    scaled = grads * sine
    turned = jnp.concatenate([scaled[..., half_width:], -scaled[..., :half_width]], axis=-1)
    return grads * cosine + turned


def norm_back(grads, values, inverse, gain):
    scaled = grads * gain
    return inverse * scaled - values * inverse**3 * jnp.mean(
        scaled * values, axis=-1, keepdims=True
    )


def mul(eq, left, right):
    return jnp.einsum(eq, left, right, preferred_element_type=F32)


def sum_scatter(part, axis):
    return lax.psum_scatter(part.astype(BF16), axis, scatter_dimension=0, tiled=True).astype(F32)


def slice_weights(item, ways):
    rows = item.shape[0]
    return item.reshape(rows, ways, -1).transpose(1, 0, 2)


def plain_body(tokens, positions, g_in, g_post, g_query, g_key, w_query, w_key, w_value,
               w_out, w_gate, w_up, w_down, cotangent):
    ways = lax.axis_size("seq")
    heads, kv_heads = HEADS // ways, KV_HEADS // ways
    micro, rows, width = tokens.shape[0], tokens.shape[2], tokens.shape[3]
    length = positions.shape[2]
    everyone = ("seq", "fsdp")
    gains = [
        lax.all_gather(item, everyone, axis=0, tiled=True).astype(F32)
        for item in (g_in, g_post, g_query, g_key)
    ]
    gain_in, gain_post, gain_query, gain_key = gains

    def spread(*items):
        packed = jnp.concatenate([slice_weights(item, ways) for item in items], axis=2)
        packed = lax.all_to_all(packed, "seq", 0, 0, tiled=True)
        packed = lax.all_gather(packed, "fsdp", axis=1, tiled=True)
        packed = packed.reshape(-1, packed.shape[2])
        sizes = [item.shape[1] // ways for item in items]
        cuts = [sum(sizes[: at + 1]) for at in range(len(sizes) - 1)]
        return jnp.split(packed, cuts, axis=1)

    wq, wk, wv = spread(w_query, w_key, w_value)
    wo = lax.all_gather(w_out, "fsdp", axis=0, tiled=True)
    wg, wu = spread(w_gate, w_up)
    wd = lax.all_gather(w_down, "fsdp", axis=0, tiled=True)
    scale = HEAD_DIM ** (-0.5)

    def gather_rows(item):
        return lax.all_gather(item, "seq", axis=0, tiled=True)

    grads = None
    outs, token_grads = [], []
    for at in range(micro):
        inputs = tokens[at, 0].astype(F32)
        pos = positions[at, 0]
        cosine, sine = rope_tables(pos)
        allowed = pos[None, :] <= pos[:, None]
        inv_in = inverse_root(inputs)
        normed = gather_rows((inputs * inv_in * gain_in).astype(BF16))
        q_raw = mul("td,df->tf", normed, wq).reshape(length, heads, HEAD_DIM)
        k_raw = mul("td,df->tf", normed, wk).reshape(length, kv_heads, HEAD_DIM)
        value = mul("td,df->tf", normed, wv).astype(BF16).reshape(length, kv_heads, HEAD_DIM)
        inv_q, inv_k = inverse_root(q_raw), inverse_root(k_raw)
        query = rotate(q_raw * inv_q * gain_query, cosine, sine).astype(BF16)
        query = query.reshape(length, kv_heads, heads // kv_heads, HEAD_DIM)
        key = rotate(k_raw * inv_k * gain_key, cosine, sine).astype(BF16)
        scores = jnp.where(allowed, mul("qjgd,kjd->jgqk", query, key) * scale, NEGATIVE)
        soft = jax.nn.softmax(scores, axis=-1)
        soft_low = soft.astype(BF16)
        mixed = mul("jgqk,kjd->qjgd", soft_low, value).astype(BF16).reshape(length, -1)
        resid = inputs + sum_scatter(mul("th,hd->td", mixed, wo), "seq")
        inv_post = inverse_root(resid)
        post = gather_rows((resid * inv_post * gain_post).astype(BF16))
        gate = mul("td,df->tf", post, wg)
        upper = mul("td,df->tf", post, wu)
        sigma = jax.nn.sigmoid(gate)
        hidden = (gate * sigma * upper).astype(BF16)
        outs.append((resid + sum_scatter(mul("tf,fd->td", hidden, wd), "seq")).astype(BF16))
        back_low = cotangent[at, 0]
        back = gather_rows(back_low)
        g_down = mul("tf,td->fd", hidden, back)
        d_hidden = mul("td,fd->tf", back, wd)
        d_gate = (d_hidden * upper * sigma * (1.0 + gate * (1.0 - sigma))).astype(BF16)
        d_upper = (d_hidden * gate * sigma).astype(BF16)
        g_gate = mul("td,tf->df", post, d_gate)
        g_up = mul("td,tf->df", post, d_upper)
        d_post = sum_scatter(mul("tf,df->td", d_gate, wg) + mul("tf,df->td", d_upper, wu), "seq")
        post_grad = jnp.sum(d_post * resid * inv_post, axis=0)
        d_resid = back_low.astype(F32) + norm_back(d_post, resid, inv_post, gain_post)
        d_attn = gather_rows(d_resid.astype(BF16))
        g_out = mul("th,td->hd", mixed, d_attn)
        d_mixed = mul("td,hd->th", d_attn, wo).astype(BF16)
        d_mixed = d_mixed.reshape(length, kv_heads, heads // kv_heads, HEAD_DIM)
        d_soft = mul("qjgd,kjd->jgqk", d_mixed, value)
        d_scores = (soft * (d_soft - jnp.sum(d_soft * soft, axis=-1, keepdims=True))).astype(BF16)
        d_query = mul("jgqk,kjd->qjgd", d_scores, key) * scale
        d_key = mul("jgqk,qjgd->kjd", d_scores, query) * scale
        d_value = mul("jgqk,qjgd->kjd", soft_low, d_mixed).astype(BF16).reshape(length, -1)
        key_turn = rotate_back(d_key, cosine, sine)
        query_turn = rotate_back(d_query.reshape(length, heads, HEAD_DIM), cosine, sine)
        key_grad = jnp.sum(key_turn * k_raw * inv_k, axis=(0, 1))
        query_grad = jnp.sum(query_turn * q_raw * inv_q, axis=(0, 1))
        d_key = norm_back(key_turn, k_raw, inv_k, gain_key).astype(BF16).reshape(length, -1)
        d_query = norm_back(query_turn, q_raw, inv_q, gain_query).astype(BF16).reshape(length, -1)
        g_query_w = mul("td,tf->df", normed, d_query)
        g_key_w = mul("td,tf->df", normed, d_key)
        g_value_w = mul("td,tf->df", normed, d_value)
        d_normed = mul("tf,df->td", d_query, wq) + mul("tf,df->td", d_key, wk)
        d_normed = sum_scatter(d_normed + mul("tf,df->td", d_value, wv), "seq")
        in_grad = jnp.sum(d_normed * inputs * inv_in, axis=0)
        token_grads.append(d_resid + norm_back(d_normed, inputs, inv_in, gain_in))
        found = [in_grad, post_grad, query_grad, key_grad, g_query_w, g_key_w, g_value_w,
                 g_out, g_gate, g_up, g_down]
        grads = found if grads is None else [left + right for left, right in zip(grads, found)]

    small = [lax.psum_scatter(item, everyone, scatter_dimension=0, tiled=True) for item in grads[:4]]

    def columns_home(item):
        full, wide = item.shape
        item = item.reshape(ways, -1, wide).astype(BF16)
        item = lax.psum_scatter(item, "fsdp", scatter_dimension=1, tiled=True)
        item = lax.all_to_all(item, "seq", 0, 0, tiled=True)
        return item.transpose(1, 0, 2).reshape(item.shape[1], ways * wide).astype(F32)

    def rows_home(item):
        return sum_scatter(item, "fsdp")

    large = [columns_home(item) for item in grads[4:7]] + [rows_home(grads[7])]
    large += [columns_home(item) for item in grads[8:10]] + [rows_home(grads[10])]
    return (jnp.stack(outs)[:, None], jnp.stack(token_grads)[:, None], *small, *large)


MESH = pl.DeviceIdType.MESH
ANY = pl.ANY
VMEM = pltpu.VMEM
RUN = 128
BLOCK = 256
NARROW = (((1,), (1,)), ((), ()))
TALL = (((0,), (0,)), ((), ()))
PLAIN = (((1,), (0,)), ((), ()))
LOG2E = 1.4426950408889634
SCALE = HEAD_DIM ** (-0.5)
LEVEL = 8
VMEM_BYTES = 63 * 2**20


def dot(left, right, dims=PLAIN):
    return lax.dot_general(left, right, dims, preferred_element_type=F32)


class Place:
    def __init__(self, planes):
        self.planes = planes
        self.s = lax.axis_index("seq")
        self.f = lax.axis_index("fsdp")
        self.x, self.c = self.s // 2, self.s % 2
        self.z, self.y = self.f // 2, self.f % 2
        self.other_y = 1 - self.y
        self.core_dev = (self.x * 2 + 1 - self.c, self.f)
        self.x_dev = ((1 - self.x) * 2 + self.c, self.f)
        self.far_dev = ((1 - self.x) * 2 + 1 - self.c, self.f)
        self.y_dev = (self.s, self.z * 2 + self.other_y)
        self.seq_dev = [(self.s, self.f), self.core_dev, self.x_dev, self.far_dev]

    def z_at(self, step):
        return lax.rem(self.z + step, self.planes)

    def z_dev(self, step):
        return (self.s, self.z_at(step) * 2 + self.y)

    def peers(self):
        return [self.core_dev, self.x_dev, self.far_dev, self.y_dev] + [
            self.z_dev(step) for step in range(1, self.planes)
        ]

    def meet(self):
        barrier = pltpu.get_barrier_semaphore()
        for peer in self.peers():
            pl.semaphore_signal(barrier, inc=1, device_id=peer, device_id_type=MESH)
        pl.semaphore_wait(barrier, 3 + self.planes)


def remote(src, dst, out_sem, in_sem, device):
    return pltpu.make_async_remote_copy(
        src_ref=src, dst_ref=dst, send_sem=out_sem, recv_sem=in_sem,
        device_id=device, device_id_type=MESH,
    )


class Wire:
    def __init__(self, out_sems, in_sems, own_sems):
        self.out_sems, self.in_sems, self.own_sems = out_sems, in_sems, own_sems
        self.sent, self.owned = [], 0

    def send(self, src, dst, device, start=True):
        at = len(self.sent)
        copy = remote(src, dst, self.out_sems.at[at], self.in_sems.at[at], device)
        if start:
            copy.start()
        self.sent.append(copy)
        return copy

    def own(self, src, dst):
        copy = pltpu.make_async_copy(src, dst, self.own_sems.at[self.owned])
        copy.start()
        self.owned += 1
        return copy

    def close(self):
        for copy in self.sent:
            copy.wait_send()


def wire_scratch(copies, owns):
    return [
        pltpu.SemaphoreType.DMA((copies,)),
        pltpu.SemaphoreType.DMA((copies,)),
        pltpu.SemaphoreType.DMA((owns,)),
    ]


class Reducer:
    def __init__(self, place, part, core_out, core_in, x_out, x_in, keep, sems):
        self.place, self.part = place, part
        self.core_out, self.core_in = core_out, core_in
        self.x_out, self.x_in, self.keep = x_out, x_in, keep
        self.core_s, self.core_r, self.x_s, self.x_r = sems

    def block(self, step):
        p = self.place
        turn = step % 4
        x = jnp.where(turn < 2, 1 - p.x, p.x)
        c = jnp.where(turn % 2 == 0, 1 - p.c, p.c)
        return step // 4, x * 2 + c

    def core_copy(self, slot):
        return remote(self.core_out.at[slot], self.core_in.at[slot], self.core_s.at[slot],
                      self.core_r.at[slot], self.place.core_dev)

    def x_copy(self, micro):
        return remote(self.x_out.at[micro], self.x_in.at[micro], self.x_s.at[micro],
                      self.x_r.at[micro], self.place.x_dev)

    def take(self, step, send_x=True):
        micro, turn = step // 4, step % 4

        @pl.when(turn % 2 == 0)
        def _():
            slot = micro * 2 + turn // 2
            self.core_out[slot] = self.part[...].astype(BF16)
            self.core_copy(slot).start()

        @pl.when(turn == 1)
        def _():
            slot = micro * 2
            self.core_copy(slot).wait_recv()
            self.x_out[micro] = (self.part[...] + self.core_in[slot].astype(F32)).astype(BF16)
            if send_x:
                self.x_copy(micro).start()

        @pl.when(turn == 3)
        def _():
            slot = micro * 2 + 1
            self.core_copy(slot).wait_recv()
            self.keep[micro] = self.part[...] + self.core_in[slot].astype(F32)

    def total(self, micro):
        self.x_copy(micro).wait_recv()
        return self.keep[micro] + self.x_in[micro].astype(F32)

    def close(self, send_x=True):
        for slot in range(4):
            self.core_copy(slot).wait_send()
        if send_x:
            for micro in range(2):
                self.x_copy(micro).wait_send()


def reducer_scratch(width):
    return [
        VMEM((4, BLOCK, width), BF16),
        VMEM((4, BLOCK, width), BF16),
        VMEM((2, BLOCK, width), BF16),
        VMEM((2, BLOCK, width), BF16),
        VMEM((2, BLOCK, width), F32),
        pltpu.SemaphoreType.DMA((4,)),
        pltpu.SemaphoreType.DMA((4,)),
        pltpu.SemaphoreType.DMA((2,)),
        pltpu.SemaphoreType.DMA((2,)),
    ]


def row_mean(values):
    return jnp.mean(values, axis=-1, keepdims=True)


def spread_gain(table, row, devices, width):
    per = width // devices
    lanes = lax.broadcasted_iota(jnp.int32, (RUN, width), 0)
    column = lax.broadcasted_iota(jnp.int32, (RUN, width), 1)
    pick = (lanes == lax.rem(column, per)).astype(BF16)
    picked = dot(table, pick)
    rows = lax.broadcasted_iota(jnp.int32, (devices * 8, width), 0)
    owner = lax.broadcasted_iota(jnp.int32, (devices * 8, width), 1) // per
    return jnp.sum(jnp.where(rows == owner * 8 + row, picked, 0.0), axis=0, keepdims=True)


def two_runs(ref, first, second):
    return jnp.concatenate([ref[first], ref[second]], axis=0)


def joined(value):
    return value.reshape(-1, value.shape[-1])


def flat(ref):
    return joined(ref[...])


def front_kernel(
    planes,
    order, rank, tokens, cotangent, gain_tile, cosine_in, sine_in,
    s_q, s_k, s_v, s_o, s_g, s_u, s_d,
    win_out, wo_out, wgu, wd,
    normed_out, query_out, key_out, value_out, q_unit_out, k_unit_out, roots_out, mixed_out,
    resid_out, post_full, back_full, gains,
    win, wo, normed, query, key, value, q_unit, k_unit, roots, mixed, resid,
    tok_full, gain_all, post_own, back_own, cosine, sine, part,
    core_out, core_in, x_out, x_in, keep, core_s, core_r, x_s, x_r,
    out_sems, in_sems, own_sems,
):
    p = Place(planes)
    s, f = p.s, p.f
    devices = 8 * planes
    wire = Wire(out_sems, in_sems, own_sems)
    reducer = Reducer(p, part, core_out, core_in, x_out, x_in, keep, (core_s, core_r, x_s, x_r))
    rows = BLOCK
    mine = pl.ds(s * rows, rows)
    theirs = pl.ds(p.x_dev[0] * rows, rows)
    length = 4 * rows
    runs = length // RUN
    p.meet()

    def spread_columns(items, full):
        came = [[] for _ in range(4)]
        for at in (0, 2, 3, 1):
            first = 0
            for item in items:
                wide = item.shape[1] // 4
                src = item.at[:, pl.ds(pl.multiple_of(p.seq_dev[at][0] * wide, RUN), wide)]
                dst = full.at[s, f, :, pl.ds(first, wide)]
                came[at].append(wire.send(src, dst, p.seq_dev[at]) if at else wire.own(src, dst))
                first += wide
        return came

    def arrived(copies, at):
        for copy in copies[at]:
            copy.wait_recv() if at else copy.wait()

    def side(here):
        return [wire.send(here, here, p.y_dev)]

    def push(here):
        return [wire.send(here, here, p.z_dev(step)) for step in range(1, planes)]

    def forward(view, far, near):
        for step, copy in enumerate(far, 1):
            copy.wait_recv()
            near += side(view(p.z_at(planes - step) * 2 + p.y))

    def settle(near):
        for copy in near:
            copy.wait_recv()

    gain_all[s, f] = gain_tile[...]
    gain_in = [wire.send(gain_all.at[s, f], gain_all.at[s, f], dev) for dev in p.seq_dev[1:]]
    first = spread_columns((s_q, s_k, s_v), win)
    out_near = [wire.send(s_o, wo.at[f], p.y_dev)]
    down_near = [wire.send(s_d, wd.at[f], p.y_dev)]
    tok_here, tok_x, tok_core = [], [], []
    for micro in range(2):
        to = tok_full.at[pl.ds(micro * runs + s * 2, 2)]
        tok_here.append(wire.own(tokens.at[micro], to))
        tok_core.append(wire.send(tokens.at[micro], to, p.core_dev))
    out_kept = wire.own(s_o, wo.at[f])
    down_kept = wire.own(s_d, wd.at[f])
    staged = [wire.own(cosine_in, cosine), wire.own(sine_in, sine), wire.own(cotangent, back_own)]

    def in_view(at):
        return lambda owner: win.at[p.seq_dev[at][0], owner]

    def wide_view(at):
        return lambda owner: wgu.at[p.seq_dev[at][0], owner]

    in_far, in_near, wide_far, wide_near = {}, [], {}, []
    arrived(first, 0)
    in_far[0] = push(in_view(0)(f))
    in_near += side(in_view(0)(f))
    for copy in gain_in:
        copy.wait_recv()
    gain_far = push(gain_all.at[:, f])
    gain_near = side(gain_all.at[:, f])
    for at in (1, 2, 3):
        arrived(first, at)
        in_near += side(in_view(at)(f))
        if at == 1:
            in_far[1] = push(in_view(1)(f))
    for micro in range(2):
        to = tok_full.at[pl.ds(micro * runs + s * 2, 2)]
        tok_x.append(wire.send(tokens.at[micro], to, p.x_dev))
    second = spread_columns((s_g, s_u), wgu)
    forward(lambda owner: gain_all.at[:, owner], gain_far, gain_near)
    forward(in_view(0), in_far[0], in_near)
    in_far[2] = push(in_view(2)(f))
    forward(in_view(1), in_far[1], in_near)
    in_far[3] = push(in_view(3)(f))
    settle(gain_near)
    table = gain_all[...].reshape(devices * 8, RUN).astype(BF16)
    gain_first = spread_gain(table, 0, devices, 1024)
    gain_post = spread_gain(table, 1, devices, 1024)
    gain_query = spread_gain(table, 2, devices, RUN)
    gain_key = spread_gain(table, 3, devices, RUN)
    gains[...] = jnp.zeros_like(gains)
    gains[0:1] = gain_first
    gains[1:2] = gain_post
    gains[2:3, 0:RUN] = gain_query
    gains[3:4, 0:RUN] = gain_key
    forward(in_view(2), in_far[2], in_near)
    out_far = [wire.send(s_o, wo.at[f], p.z_dev(step)) for step in range(1, planes)]
    forward(in_view(3), in_far[3], in_near)
    tok_fwd = []
    for micro in range(2):
        tok_x[micro].wait_recv()
        block = tok_full.at[pl.ds(micro * runs + p.x_dev[0] * 2, 2)]
        tok_fwd.append(wire.send(block, block, p.core_dev))
    for at in range(4):
        arrived(second, at)
        wide_near += side(wide_view(at)(f))
    for copy in staged:
        copy.wait()
    back_x, back_core, back_kept = [], [], []
    for micro in range(2):
        to = back_full.at[micro, mine]
        back_x.append(wire.send(cotangent.at[micro], to, p.x_dev))
        back_kept.append(wire.own(back_own.at[micro], to))
        back_core.append(wire.send(cotangent.at[micro], to, p.core_dev))
    wide_far[0] = push(wide_view(0)(f))
    down_far = [wire.send(s_d, wd.at[f], p.z_dev(step)) for step in range(1, planes)]
    settle(in_near)
    saved = [wire.own(win, win_out)]
    for copy in tok_here:
        copy.wait()
    for copy in tok_core + tok_fwd:
        copy.wait_recv()

    def project(step, carry):
        here = pl.ds(pl.multiple_of(step * BLOCK, BLOCK), BLOCK)
        raw = two_runs(tok_full, order[step * 2], order[step * 2 + 1]).astype(F32)
        root = lax.rsqrt(row_mean(raw * raw) + EPSILON)
        low = (raw * root * gains[0:1]).astype(BF16)
        normed[here] = low
        turn = pl.ds(pl.multiple_of(lax.rem(step, length // BLOCK) * BLOCK, BLOCK), BLOCK)
        cos, sin = cosine[turn], sine[turn]
        product = dot(low, flat(win))
        found, start = [], 0
        for low_ref, unit_ref, row in ((query, q_unit, 2), (key, k_unit, 3)):
            gain = gains[row : row + 1, 0:RUN]
            for head in range(low_ref.shape[1] // HEAD_DIM):
                at = slice(head * HEAD_DIM, (head + 1) * HEAD_DIM)
                one = product[:, start : start + HEAD_DIM]
                inverse = lax.rsqrt(row_mean(one * one) + EPSILON)
                unit = one * inverse
                unit_ref[here, at] = unit.astype(BF16)
                scaled = unit * gain
                low_ref[here, at] = (scaled * cos + pltpu.roll(scaled, HEAD_DIM // 2, 1) * sin).astype(BF16)
                found.append(inverse)
                start += HEAD_DIM
        roots[here, :] = jnp.zeros((BLOCK, roots.shape[1]), F32)
        for at, inverse in enumerate(found):
            roots[here, at : at + 1] = inverse
        value[here] = product[:, start:].astype(BF16)
        return carry

    def attend(step, carry):
        micro, head = step // 2, lax.rem(step, 2)
        keys_at = pl.ds(pl.multiple_of(head * HEAD_DIM, HEAD_DIM), HEAD_DIM)
        lanes = [pl.ds(pl.multiple_of(head * 2 * HEAD_DIM + g * HEAD_DIM, HEAD_DIM), HEAD_DIM) for g in range(2)]
        for block in range(length // BLOCK):
            here = pl.ds(pl.multiple_of(micro * length + block * BLOCK, BLOCK), BLOCK)
            seen = (block + 1) * BLOCK
            past = pl.ds(pl.multiple_of(micro * length, BLOCK), seen)
            asked = jnp.concatenate([query[here, lane] for lane in lanes], axis=0)
            scores = dot(asked, key[past, keys_at], NARROW)
            line = lax.broadcasted_iota(jnp.int32, (2 * BLOCK, seen), 0)
            line = jnp.where(line >= BLOCK, line - BLOCK, line) + block * BLOCK
            column = lax.broadcasted_iota(jnp.int32, (2 * BLOCK, seen), 1)
            scores = jnp.where(column <= line, scores, NEGATIVE)
            top = jnp.max(scores, axis=-1, keepdims=True)
            weight = jnp.exp2((scores - top) * (SCALE * LOG2E))
            total = jnp.sum(weight, axis=-1, keepdims=True)
            out = dot(weight.astype(BF16), value[past, keys_at]) * (1.0 / total)
            level = top * (SCALE * LOG2E) + jnp.log2(total)
            pair = pl.ds(micro * runs + block * 2, 2)
            held = roots[here, :]
            spot = lax.broadcasted_iota(jnp.int32, held.shape, 1)
            for g, lane in enumerate(lanes):
                half = slice(g * BLOCK, (g + 1) * BLOCK)
                mixed[pair, :, lane] = out[half].astype(BF16).reshape(2, RUN, HEAD_DIM)
                held = jnp.where(spot == LEVEL + head * 2 + g, level[half], held)
            roots[here, :] = held
        return carry

    def mix_out(step, carry):
        micro, block = reducer.block(step)
        at = micro * runs + block * 2
        low = two_runs(mixed, rank[at], rank[at + 1])
        part[...] = dot(low, flat(wo))
        reducer.take(step)
        return carry

    posts = []

    def finish(micro):
        own = joined(tok_full[pl.ds(micro * runs + s * 2, 2)]).astype(F32)
        total = own + reducer.total(micro)
        resid[micro] = total
        root = lax.rsqrt(row_mean(total * total) + EPSILON)
        post_own[micro] = (total * root * gains[1:2]).astype(BF16)
        to = post_full.at[micro, mine]
        posts.append((wire.send(post_own.at[micro], to, p.x_dev), wire.send(post_own.at[micro], to, p.core_dev),
                      wire.own(post_own.at[micro], to)))
        saved.append(wire.own(resid.at[micro], resid_out.at[micro]))

    steps = length // BLOCK
    lax.fori_loop(0, steps, project, 0)
    forward(lambda owner: wo.at[owner], out_far, out_near)
    wide_far[1] = push(wide_view(1)(f))
    lax.fori_loop(0, 2, attend, 0)
    lax.fori_loop(steps, 2 * steps, project, 0)
    saved += [wire.own(here, there) for here, there in (
        (normed, normed_out), (query, query_out), (key, key_out), (value, value_out),
        (q_unit, q_unit_out), (k_unit, k_unit_out))]
    out_kept.wait()
    settle(out_near)
    lax.fori_loop(0, 4, mix_out, 0)
    forward(wide_view(0), wide_far[0], wide_near)
    wide_far[2] = push(wide_view(2)(f))
    lax.fori_loop(2, 4, attend, 0)
    lax.fori_loop(4, 8, mix_out, 0)
    saved += [wire.own(mixed, mixed_out), wire.own(roots, roots_out), wire.own(wo, wo_out)]
    wide_far[3] = push(wide_view(3)(f))
    finish(0)
    forward(lambda owner: wd.at[owner], down_far, down_near)
    forward(wide_view(1), wide_far[1], wide_near)
    for micro in range(2):
        back_x[micro].wait_recv()
        block = back_full.at[micro, theirs]
        back_core.append(wire.send(block, block, p.core_dev))
    finish(1)
    forward(wide_view(2), wide_far[2], wide_near)
    forward(wide_view(3), wide_far[3], wide_near)
    last = []
    for micro in range(2):
        posts[micro][0].wait_recv()
        block = post_full.at[micro, theirs]
        last.append(wire.send(block, block, p.core_dev))
    for micro in range(2):
        last[micro].wait_recv()
        posts[micro][1].wait_recv()
        posts[micro][2].wait()
    for copy in back_core:
        copy.wait_recv()
    for copy in back_kept + saved + [down_kept]:
        copy.wait()
    settle(wide_near)
    settle(down_near)
    reducer.close()
    wire.close()


def front(planes, order, rank, tokens, cotangent, gain_tile, cosine, sine, shards):
    nf = 2 * planes
    rows = tokens.shape[1]
    length = 4 * rows
    total = 2 * length
    tokens = tokens.reshape(2, 2, RUN, tokens.shape[2])
    deep = shards[0].shape[0]

    def low(width):
        return jax.ShapeDtypeStruct((total, width), BF16)

    shapes = [
        jax.ShapeDtypeStruct((4, nf, deep, 1024), BF16), jax.ShapeDtypeStruct((nf, *shards[3].shape), BF16),
        jax.ShapeDtypeStruct((4, nf, deep, 2 * (shards[4].shape[1] // 4)), BF16),
        jax.ShapeDtypeStruct((nf, *shards[6].shape), BF16),
        low(1024), low(512), low(256), low(256), low(512), low(256),
        jax.ShapeDtypeStruct((total, 16), F32), jax.ShapeDtypeStruct((total // RUN, RUN, 512), BF16),
        jax.ShapeDtypeStruct((2, rows, 1024), F32),
        jax.ShapeDtypeStruct((2, length, 1024), BF16), jax.ShapeDtypeStruct((2, length, 1024), BF16),
        jax.ShapeDtypeStruct((8, 1024), F32)]
    held = [shapes[at] for at in (0, 1, *range(4, 13))]
    vm = pl.BlockSpec(memory_space=VMEM)
    hb = pl.BlockSpec(memory_space=ANY)
    sm = pl.BlockSpec(memory_space=pltpu.SMEM)
    return pl.pallas_call(
        functools.partial(front_kernel, planes),
        out_shape=shapes,
        in_specs=[sm, sm, hb, hb, vm, hb, hb, hb, hb, hb, hb, vm, vm, vm],
        out_specs=[hb] * (len(shapes) - 1) + [vm],
        scratch_shapes=[
            *[VMEM(item.shape, item.dtype) for item in held],
            VMEM((total // RUN, RUN, 1024), BF16), VMEM((4, nf, 8, RUN), F32), VMEM((2, rows, 1024), BF16),
            VMEM((2, rows, 1024), BF16), VMEM(cosine.shape, F32), VMEM(sine.shape, F32),
            VMEM((BLOCK, 1024), F32), *reducer_scratch(1024), *wire_scratch(130, 40),
        ],
        compiler_params=pltpu.CompilerParams(
            collective_id=0, has_side_effects=True, vmem_limit_bytes=VMEM_BYTES),
        name="front",
    )(order, rank, tokens, cotangent, gain_tile, cosine, sine, *shards)


GROUPS = (2, 3, 1, 0)


class RowHoming:
    def __init__(self, place, wire, grad, came, sums, far, home):
        self.p, self.wire, self.grad = place, wire, grad
        self.came, self.sums, self.far, self.home = came, sums, far, home

    def half(self, ref, at):
        return ref.at[pl.ds(at * (self.p.planes // 2), self.p.planes // 2)]

    def start(self):
        p = self.p
        self.kept = self.wire.own(self.grad.at[:, p.y], self.sums)
        self.sent = [
            self.wire.send(self.half(self.grad, at).at[:, p.other_y], self.half(self.came, at), p.y_dev)
            for at in range(2)
        ]
        self.out = [
            self.wire.send(self.sums.at[p.z_at(step)], self.far.at[step - 1], p.z_dev(step), start=False)
            for step in range(1, p.planes)
        ]

    def push(self, at):
        if at == 0:
            self.kept.wait()
        self.sent[at].wait_recv()
        share = self.p.planes // 2

        def add(z, carry):
            self.sums[z] = (self.sums[z].astype(F32) + self.came[z].astype(F32)).astype(BF16)
            return carry

        lax.fori_loop(at * share, (at + 1) * share, add, 0)
        for step, copy in enumerate(self.out, 1):
            @pl.when(self.p.z_at(step) // share == at)
            def _(copy=copy):
                copy.start()

    def gather(self):
        for copy in self.out:
            copy.wait_recv()
        total = self.sums[self.p.z].astype(F32)
        for step in range(1, self.p.planes):
            total = total + self.far[step - 1].astype(F32)
        self.home[...] = total


class ColumnHoming:
    def __init__(self, place, wire, came, sums, far, leave=None, arrive=None, homes=()):
        self.p, self.wire, self.came, self.sums, self.far = place, wire, came, sums, far
        self.leave, self.arrive, self.homes = leave, arrive, homes
        self.kept, self.sent, self.out, self.back = {}, {}, {}, {}

    def start(self, at, grad):
        self.kept[at] = self.wire.own(grad.at[:, self.p.y], self.sums.at[at])
        self.sent[at] = self.wire.send(grad.at[:, self.p.other_y], self.came.at[at], self.p.y_dev)

    def add(self, at):
        self.kept[at].wait()
        self.sent[at].wait_recv()

        def add(z, carry):
            self.sums[at, z] = (self.sums[at, z].astype(F32) + self.came[at, z].astype(F32)).astype(BF16)
            return carry

        lax.fori_loop(0, self.p.planes, add, 0)

    def push(self, at):
        self.out[at] = [
            self.wire.send(self.sums.at[at, self.p.z_at(step)], self.far.at[at, step - 1], self.p.z_dev(step))
            for step in range(1, self.p.planes)
        ]

    def put(self, owner, value):
        first = 0
        for home in self.homes:
            width = home.shape[1] // 4
            home[:, pl.ds(pl.multiple_of(owner * width, RUN), width)] = value[:, first : first + width]
            first += width

    def gather(self, at):
        for copy in self.out[at]:
            copy.wait_recv()
        total = self.sums[at, self.p.z].astype(F32)
        for step in range(1, self.p.planes):
            total = total + self.far[at, step - 1].astype(F32)
        if GROUPS[at] == 0:
            self.put(self.p.s, total)
            return
        self.leave[at] = total.astype(BF16)
        self.back[at] = self.wire.send(self.leave.at[at], self.arrive.at[at], self.p.seq_dev[GROUPS[at]])

    def finish(self):
        for at, copy in self.back.items():
            copy.wait_recv()
            self.put(self.p.seq_dev[GROUPS[at]][0], self.arrive[at].astype(F32))


def group_rows(place, at):
    owner = place.seq_dev[GROUPS[at]][0]
    return pl.ds(pl.multiple_of(owner * BLOCK, BLOCK), BLOCK)


def column_scratch(planes, deep, width, groups=4):
    return [
        VMEM((groups, planes, deep, width), BF16), VMEM((groups, planes, deep, width), BF16),
        VMEM((4, planes - 1, deep, width), BF16), VMEM((3, deep, width), BF16), VMEM((3, deep, width), BF16),
    ]


def row_scratch(planes, deep, width):
    return [VMEM((planes, deep, width), BF16), VMEM((planes, deep, width), BF16),
            VMEM((planes - 1, deep, width), BF16)]


def middle_kernel(
    planes,
    post_in, back_in, wgu_in, wd_in, resid_in, gains,
    ready, grad_rest, home_d, y_out, y_keep, d_resid, attn_full, sums,
    post, back, wgu, wd, resid, load_sems,
    grad_first, g_came, grad_d, d_came, d_sums, d_far, hidden, d_gu, part, attn_own,
    y_core_out, y_core_in,
    core_out, core_in, x_out, x_in, keep, core_s, core_r, x_s, x_r,
    y_core_s, y_core_r, out_sems, in_sems, own_sems,
):
    p = Place(planes)
    s = p.s
    wire = Wire(out_sems, in_sems, own_sems)
    into_post = Reducer(p, part, core_out, core_in, x_out, x_in, keep, (core_s, core_r, x_s, x_r))
    into_out = Reducer(p, part, y_core_out, y_core_in, y_out, None, y_keep, (y_core_s, y_core_r, None, None))
    rows = resid.shape[1]
    length = 4 * rows
    wide = hidden.shape[1]
    mine = pl.ds(s * rows, rows)
    theirs = pl.ds(p.x_dev[0] * rows, rows)
    loads = [wire.own(wgu_in, wgu), wire.own(wd_in, wd), wire.own(resid_in, resid)]

    def chunk(step):
        micro, block = into_post.block(step)
        here = pl.ds(pl.multiple_of(micro * length + block * BLOCK, BLOCK), BLOCK)
        return [pltpu.make_async_copy(far.at[here], near.at[here], load_sems.at[at, step])
                for at, (far, near) in enumerate(((post_in, post), (back_in, back)))]

    for step in range(8):
        for copy in chunk(step):
            copy.start()
    p.meet()
    for copy in loads:
        copy.wait()

    def feed(step, carry):
        micro, block = into_post.block(step)
        here = pl.ds(pl.multiple_of(micro * length + block * BLOCK, BLOCK), BLOCK)
        for copy in chunk(step):
            copy.wait()
        both = dot(post[here, :], wgu[...])
        d_hidden = dot(back[here, :], wd[...], NARROW)
        gate, upper = both[:, :wide], both[:, wide:]
        sigma = 1.0 / (1.0 + jnp.exp(-gate))
        lit = gate * sigma
        hidden[here] = (lit * upper).astype(BF16)
        d_gu[here, :wide] = (d_hidden * upper * (sigma + lit * (1.0 - sigma))).astype(BF16)
        d_gu[here, wide:] = (d_hidden * lit).astype(BF16)
        part[...] = dot(d_gu[here, :], wgu[...], NARROW)
        into_post.take(step)
        part[...] = dot(hidden[here, :], wd[...])
        into_out.take(step, send_x=False)
        return carry

    down = RowHoming(p, wire, grad_d, d_came, d_sums, d_far, home_d)
    columns = ColumnHoming(p, wire, g_came, ready, None)

    def down_tile(at, carry):
        tall = wide // 2
        cut = pl.ds(pl.multiple_of(at * tall, RUN), tall)
        found = dot(hidden[:, cut], back[...], TALL).astype(BF16)
        grad_d[pl.ds(at * (planes // 2), planes // 2)] = found.reshape(planes // 2, *grad_d.shape[1:])
        return carry

    def wide_tile(at):
        found = dot(post[:, group_rows(p, at)], d_gu[...], TALL).astype(BF16)
        return found.reshape(grad_first.shape)

    gain = gains[1:2]
    sends = []
    sums[...] = jnp.zeros_like(sums)

    def settle(micro):
        grad = into_post.total(micro)
        held = resid[micro]
        root = lax.rsqrt(row_mean(held * held) + EPSILON)
        unit = held * root
        sums[0:1] += jnp.sum(grad * unit, axis=0, keepdims=True)
        scaled = grad * gain
        own = back[pl.ds(pl.multiple_of(micro * length + s * rows, rows), rows), :].astype(F32)
        whole = own + root * (scaled - unit * row_mean(scaled * unit))
        d_resid[micro] = whole
        attn_own[micro] = whole.astype(BF16)
        to = attn_full.at[micro, mine]
        sends.append((wire.send(attn_own.at[micro], to, p.x_dev), wire.send(attn_own.at[micro], to, p.core_dev),
                      wire.own(attn_own.at[micro], to)))
        y_keep[micro] = y_keep[micro] + held

    lax.fori_loop(0, 7, feed, 0)
    settle(0)
    lax.fori_loop(7, 8, feed, 0)
    lax.fori_loop(0, 2, down_tile, 0)
    down.start()
    grad_first[...] = wide_tile(0)
    columns.start(0, grad_first)
    settle(1)
    grad_rest[0] = wide_tile(1)
    down.push(0)
    grad_rest[1] = wide_tile(2)
    grad_rest[2] = wide_tile(3)
    down.push(1)
    forwards = []
    for micro in range(2):
        sends[micro][0].wait_recv()
        block = attn_full.at[micro, theirs]
        forwards.append(wire.send(block, block, p.core_dev))
    columns.add(0)
    for micro in range(2):
        forwards[micro].wait_recv()
        sends[micro][1].wait_recv()
        sends[micro][2].wait()
    down.gather()
    into_post.close()
    into_out.close(send_x=False)
    wire.close()


def middle(planes, post, back, wgu, wd, resid, gains):
    rows = resid.shape[1]
    total = 8 * rows
    wide = wd.shape[0]
    deep = 1024 // (8 * planes)
    once = (planes, 2, deep, 2 * wide)
    slim = (planes, 2, wide // (2 * planes), 1024)
    shapes = [
        jax.ShapeDtypeStruct((1, planes, deep, 2 * wide), BF16), jax.ShapeDtypeStruct((3, *once), BF16),
        jax.ShapeDtypeStruct(slim[2:], F32),
        jax.ShapeDtypeStruct((2, rows, 1024), BF16), jax.ShapeDtypeStruct((2, rows, 1024), F32),
        jax.ShapeDtypeStruct((2, rows, 1024), F32), jax.ShapeDtypeStruct((2, 4 * rows, 1024), BF16),
        jax.ShapeDtypeStruct((8, 1024), F32),
    ]
    vm = pl.BlockSpec(memory_space=VMEM)
    hb = pl.BlockSpec(memory_space=ANY)
    return pl.pallas_call(
        functools.partial(middle_kernel, planes),
        out_shape=shapes,
        in_specs=[hb] * 5 + [vm],
        out_specs=[vm] * 6 + [hb, vm],
        scratch_shapes=[
            *[VMEM(item.shape, item.dtype) for item in (post, back, wgu, wd, resid)],
            pltpu.SemaphoreType.DMA((2, 8)),
            VMEM(once, BF16), VMEM((1, planes, deep, 2 * wide), BF16), VMEM(slim, BF16),
            *row_scratch(planes, *slim[2:]),
            VMEM((total, wide), BF16), VMEM((total, 2 * wide), BF16),
            VMEM((BLOCK, 1024), F32), VMEM((2, rows, 1024), BF16),
            VMEM((4, BLOCK, 1024), BF16), VMEM((4, BLOCK, 1024), BF16),
            *reducer_scratch(1024),
            pltpu.SemaphoreType.DMA((4,)), pltpu.SemaphoreType.DMA((4,)),
            *wire_scratch(16, 10),
        ],
        compiler_params=pltpu.CompilerParams(
            collective_id=1, has_side_effects=True, vmem_limit_bytes=VMEM_BYTES),
        name="middle",
    )(post, back, wgu, wd, resid, gains)


def rear_kernel(
    planes,
    order, rank, attn_in, query_in, key_in, value_in, q_unit_in, k_unit_in, roots_in, mixed_in, wo_in,
    normed_in, win_in, tokens_in, d_resid_in, cosine, sine, gains, y_out, y_keep_in, sums_in, ready, grad_rest,
    token_grad, sums, block_out, home_g, home_u, home_o, home_q, home_k, home_v,
    attn, query, key, value, q_unit, k_unit, roots, mixed, wo, win, tokens,
    rows_held, d_mixed, keys_grad, values_grad, y_in, grad_o, grad, part, sums_out, sums_came,
    g_came, g_sums, g_far, g_leave, g_arrive, o_came, o_sums, o_far,
    i_came, i_sums, i_far, i_leave, i_arrive,
    core_out, core_in, x_out, x_in, keep, core_s, core_r, x_s, x_r,
    out_sems, in_sems, own_sems,
):
    p = Place(planes)
    wire = Wire(out_sems, in_sems, own_sems)
    reducer = Reducer(p, part, core_out, core_in, x_out, x_in, keep, (core_s, core_r, x_s, x_r))
    rows = y_in.shape[1]
    length = 4 * rows
    loads = [wire.own(far, near) for far, near in (
        (attn_in, attn), (wo_in, wo), (mixed_in, mixed), (query_in, query), (key_in, key), (value_in, value),
        (q_unit_in, q_unit), (k_unit_in, k_unit), (roots_in, roots), (y_keep_in, keep), (win_in, win),
        (tokens_in, tokens), (d_resid_in, token_grad))]
    p.meet()
    wide = ColumnHoming(p, wire, g_came, g_sums, g_far, g_leave, g_arrive, (home_g, home_u))
    outer = RowHoming(p, wire, grad_o, o_came, o_sums, o_far, home_o)
    inner = ColumnHoming(p, wire, i_came, i_sums, i_far, i_leave, i_arrive, (home_q, home_k, home_v))
    wide.start(1, grad_rest.at[0])
    g_sums[0] = ready[0]
    wide.push(0)
    y_sent = [wire.send(y_out.at[micro], y_in.at[micro], p.x_dev) for micro in range(2)]
    loads[0].wait()
    loads[1].wait()

    def draw(step, carry):
        here = pl.ds(pl.multiple_of(step * BLOCK, BLOCK), BLOCK)
        low = two_runs(attn, order[step * 2], order[step * 2 + 1])
        rows_held[pl.ds(step * 2, 2)] = low.reshape(2, RUN, low.shape[1])
        d_mixed[here] = dot(low, wo[...], NARROW).astype(BF16)
        return carry

    lax.fori_loop(0, 2 * length // BLOCK, draw, 0)

    def out_tile(at, carry):
        cut = pl.ds(pl.multiple_of(at * BLOCK, BLOCK), BLOCK)
        found = dot(mixed[:, cut], flat(rows_held), TALL).astype(BF16)
        grad_o[pl.ds(at * (planes // 2), planes // 2)] = found.reshape(planes // 2, *grad_o.shape[1:])
        return carry

    loads[2].wait()
    lax.fori_loop(0, 2, out_tile, 0)
    wide.start(2, grad_rest.at[1])
    normed_load = wire.own(normed_in, attn)
    wide.add(1)
    wide.push(1)
    sums[...] = sums_in[...]

    def lane_of(ref, here, lane):
        held = ref[here, :]
        lanes = lax.broadcasted_iota(jnp.int32, held.shape, 1)
        return jnp.sum(jnp.where(lanes == lane, held, 0.0), axis=1, keepdims=True)

    def norm_home(grad, cos, sin, unit, root, gain):
        turned = grad * cos - pltpu.roll(grad, HEAD_DIM // 2, 1) * sin
        scaled = turned * gain
        back = root * (scaled - unit * row_mean(scaled * unit))
        return back, jnp.sum(turned * unit, axis=0, keepdims=True)

    def attend_back(step, carry):
        micro, head = step // 2, lax.rem(step, 2)
        keys_at = pl.ds(pl.multiple_of(head * HEAD_DIM, HEAD_DIM), HEAD_DIM)
        lanes = [pl.ds(pl.multiple_of(head * 2 * HEAD_DIM + g * HEAD_DIM, HEAD_DIM), HEAD_DIM) for g in range(2)]
        q_gain, k_gain = gains[2:3, 0:RUN], gains[3:4, 0:RUN]
        keys_grad[...] = jnp.zeros_like(keys_grad)
        values_grad[...] = jnp.zeros_like(values_grad)
        for block in range(length // BLOCK):
            here = pl.ds(pl.multiple_of(micro * length + block * BLOCK, BLOCK), BLOCK)
            seen = (block + 1) * BLOCK
            past = pl.ds(pl.multiple_of(micro * length, BLOCK), seen)
            asked = jnp.concatenate([query[here, lane] for lane in lanes], axis=0)
            pulled = jnp.concatenate([d_mixed[here, lane] for lane in lanes], axis=0)
            given = jnp.concatenate([mixed[here, lane] for lane in lanes], axis=0)
            level = jnp.concatenate(
                [lane_of(roots, here, LEVEL + head * 2 + g) for g in range(2)], axis=0)
            delta = jnp.sum(pulled.astype(F32) * given.astype(F32), axis=1, keepdims=True)
            scores = dot(asked, key[past, keys_at], NARROW)
            line = lax.broadcasted_iota(jnp.int32, (2 * BLOCK, seen), 0)
            line = jnp.where(line >= BLOCK, line - BLOCK, line) + block * BLOCK
            column = lax.broadcasted_iota(jnp.int32, (2 * BLOCK, seen), 1)
            weight = jnp.exp2(scores * (SCALE * LOG2E) - level)
            weight = jnp.where(column <= line, weight, 0.0)
            d_soft = dot(pulled, value[past, keys_at], NARROW)
            d_scores = (weight * (d_soft - delta)).astype(BF16)
            values_grad[0:seen] += dot(weight.astype(BF16), pulled, TALL)
            keys_grad[0:seen] += dot(d_scores, asked, TALL)
            moved = dot(d_scores, key[past, keys_at]) * SCALE
            spin = slice(block * BLOCK, (block + 1) * BLOCK)
            for g, lane in enumerate(lanes):
                root = lane_of(roots, here, head * 2 + g)
                unit = q_unit[here, lane].astype(F32)
                back, gained = norm_home(
                    moved[g * BLOCK : (g + 1) * BLOCK], cosine[spin], sine[spin], unit, root, q_gain)
                pair = pl.ds(micro * (length // RUN) + block * 2, 2)
                rows_held[pair, :, lane] = back.astype(BF16).reshape(2, RUN, HEAD_DIM)
                sums[1:2, 0:RUN] += gained
        everything = pl.ds(pl.multiple_of(micro * length, BLOCK), length)
        root = lane_of(roots, everything, head + 4)
        unit = k_unit[everything, keys_at].astype(F32)
        back, gained = norm_home(keys_grad[...] * SCALE, cosine[...], sine[...], unit, root, k_gain)
        at, whole = head * HEAD_DIM, pl.ds(micro * (length // RUN), length // RUN)
        tall = (length // RUN, RUN, HEAD_DIM)
        rows_held[whole, :, pl.ds(pl.multiple_of(512 + at, HEAD_DIM), HEAD_DIM)] = back.astype(BF16).reshape(tall)
        sums[2:3, 0:RUN] += gained
        low = values_grad[...].astype(BF16).reshape(tall)
        rows_held[whole, :, pl.ds(pl.multiple_of(768 + at, HEAD_DIM), HEAD_DIM)] = low
        return carry

    for copy in loads[3:9]:
        copy.wait()
    def pull(step, carry):
        micro, block = reducer.block(step)
        at = micro * (length // RUN) + block * 2
        runs = (rank[at], rank[at + 1])
        found = dot(two_runs(rows_held, *runs), win[...], NARROW)
        part[...] = found
        sums[3:4] += jnp.sum(found * two_runs(attn, *runs).astype(F32), axis=0, keepdims=True)
        reducer.take(step)
        return carry

    def tile(at):
        found = dot(joined(attn[:, :, group_rows(p, at)]), flat(rows_held), TALL).astype(BF16)
        grad[at] = found.reshape(grad.shape[1:])

    lax.fori_loop(0, 1, attend_back, 0)
    wide.start(3, grad_rest.at[2])
    wide.add(2)
    wide.push(2)
    lax.fori_loop(1, 2, attend_back, 0)
    outer.start()
    wide.add(3)
    wide.push(3)
    wide.gather(0)
    for copy in loads[9:]:
        copy.wait()
    for micro in range(2):
        y_sent[micro].wait_recv()
        block_out[micro] = (keep[micro] + y_in[micro].astype(F32)).astype(BF16)
    normed_load.wait()
    lax.fori_loop(0, 4, pull, 0)
    lax.fori_loop(2, 3, attend_back, 0)
    outer.push(0)
    outer.push(1)
    wide.gather(1)
    lax.fori_loop(3, 4, attend_back, 0)
    tile(0)
    inner.start(0, grad.at[0])
    tile(1)
    inner.start(1, grad.at[1])
    lax.fori_loop(4, 8, pull, 0)
    sums[3:4] = sums[3:4] / gains[0:1]

    def exchange(stage, devices, base):
        sums_out[stage] = sums[...]
        sent = [wire.send(sums_out.at[stage], sums_came.at[base + at], dev) for at, dev in enumerate(devices)]
        return base, sent

    def absorb(state):
        base, sent = state
        total = sums[...]
        for at, copy in enumerate(sent):
            copy.wait_recv()
            total = total + sums_came[base + at]
        sums[...] = total

    state = exchange(0, p.seq_dev[1:], 0)
    tile(2)
    tile(3)
    inner.add(0)
    inner.push(0)
    inner.start(2, grad.at[2])
    absorb(state)
    state = exchange(1, [p.z_dev(step) for step in range(1, planes)], 3)
    wide.gather(2)
    wide.gather(3)
    outer.gather()
    inner.add(1)
    inner.push(1)
    inner.start(3, grad.at[3])
    absorb(state)
    state = exchange(2, [p.y_dev], 2 + planes)
    inner.add(2)
    inner.push(2)
    inner.gather(0)
    for micro in range(2):
        grad_rows = reducer.total(micro)
        raw = tokens[micro].astype(F32)
        root = lax.rsqrt(row_mean(raw * raw) + EPSILON)
        unit = raw * root
        scaled = grad_rows * gains[0:1]
        token_grad[micro] = token_grad[micro] + root * (scaled - unit * row_mean(scaled * unit))
    inner.add(3)
    inner.push(3)
    wide.finish()
    inner.gather(1)
    absorb(state)
    inner.gather(2)
    inner.gather(3)
    inner.finish()
    reducer.close()
    wire.close()


def rear(planes, order, rank, attn, query, key, value, q_unit, k_unit, roots, mixed, wo, normed, win, tokens, d_resid,
         cosine, sine, gains, y_out, y_keep, sums, ready, grad_rest):
    rows = y_keep.shape[1]
    length = 4 * rows
    total = 2 * length
    deep, wide = grad_rest.shape[3:]
    slim = (planes, 2, 512 // (2 * planes), 1024)
    shapes = [
        jax.ShapeDtypeStruct((2, rows, 1024), F32), jax.ShapeDtypeStruct((8, 1024), F32),
        jax.ShapeDtypeStruct((2, rows, 1024), BF16),
        jax.ShapeDtypeStruct((deep, 2 * wide), F32), jax.ShapeDtypeStruct((deep, 2 * wide), F32),
        jax.ShapeDtypeStruct(slim[2:], F32), jax.ShapeDtypeStruct((deep, 2048), F32),
        jax.ShapeDtypeStruct((deep, 1024), F32), jax.ShapeDtypeStruct((deep, 1024), F32),
    ]
    held = (attn, query, key, value, q_unit, k_unit, roots, mixed, wo, win, tokens)
    vm = pl.BlockSpec(memory_space=VMEM)
    hb = pl.BlockSpec(memory_space=ANY)
    sm = pl.BlockSpec(memory_space=pltpu.SMEM)
    return pl.pallas_call(
        functools.partial(rear_kernel, planes),
        out_shape=shapes,
        in_specs=[sm, sm] + [hb] * 13 + [vm] * 3 + [hb, hb, vm, vm, hb],
        out_specs=[vm] * len(shapes),
        scratch_shapes=[
            *[VMEM(item.shape, item.dtype) for item in held],
            VMEM((total // RUN, RUN, 1024), BF16), VMEM((total, 512), BF16), VMEM((length, HEAD_DIM), F32),
            VMEM((length, HEAD_DIM), F32), VMEM((2, rows, 1024), BF16), VMEM(slim, BF16),
            VMEM((4, planes, 2, deep, 1024), BF16), VMEM((BLOCK, 1024), F32), VMEM((3, 8, 1024), F32),
            VMEM((3 + planes, 8, 1024), F32),
            *column_scratch(planes, deep, wide), *row_scratch(planes, *slim[2:]), *column_scratch(planes, deep, 1024),
            *reducer_scratch(1024), *wire_scratch(64, 40),
        ],
        compiler_params=pltpu.CompilerParams(
            collective_id=2, has_side_effects=True, vmem_limit_bytes=VMEM_BYTES),
        name="rear",
    )(order, rank, attn, query, key, value, q_unit, k_unit, roots, mixed, wo, normed, win, tokens, d_resid,
      cosine, sine, gains, y_out, y_keep, sums, ready, grad_rest)


def deliver_kernel(count, *refs):
    given, made, held, sems = refs[:count], refs[count : 2 * count], refs[2 * count : 3 * count], refs[3 * count]
    came = [pltpu.make_async_copy(src, mid, sems.at[0, at]) for at, (src, mid) in enumerate(zip(given, held))]
    gone = [pltpu.make_async_copy(mid, dst, sems.at[1, at]) for at, (mid, dst) in enumerate(zip(held, made))]
    for copy in came:
        copy.start()
    for first, second in zip(came, gone):
        first.wait()
        second.start()
    for copy in gone:
        copy.wait()


def deliver(*items):
    count = len(items)
    return pl.pallas_call(
        functools.partial(deliver_kernel, count),
        out_shape=[jax.ShapeDtypeStruct(item.shape, item.dtype) for item in items],
        in_specs=[pl.BlockSpec(memory_space=ANY)] * count,
        out_specs=[pl.BlockSpec(memory_space=ANY)] * count,
        scratch_shapes=[*[VMEM(item.shape, item.dtype) for item in items], pltpu.SemaphoreType.DMA((2, count))],
        compiler_params=pltpu.CompilerParams(vmem_limit_bytes=VMEM_BYTES),
        name="deliver",
    )(*items)


def run_tables(positions):
    runs = positions.shape[1] // RUN
    rank = positions[:, ::RUN] // RUN
    index = jnp.arange(runs, dtype=jnp.int32)
    order = jnp.sum(jnp.where(rank[:, :, None] == index, index[None, :, None], 0), axis=1)
    base = jnp.arange(positions.shape[0], dtype=jnp.int32)[:, None] * runs
    return (order + base).reshape(-1), (rank + base).reshape(-1)


def turn_tables(length):
    half = HEAD_DIM // 2
    frequency = (ROPE_BASE ** (-np.arange(half) * 2.0 / HEAD_DIM)).astype(np.float32)
    angles = (np.arange(length, dtype=np.float32)[:, None] * frequency[None, :]).astype(np.float64)
    cosine, sine = np.cos(angles), np.sin(angles)
    return (jnp.asarray(np.concatenate([cosine, cosine], axis=1).astype(np.float32)),
            jnp.asarray(np.concatenate([-sine, sine], axis=1).astype(np.float32)))


def kernel_body(tokens, positions, g_in, g_post, g_query, g_key, w_query, w_key, w_value,
                w_out, w_gate, w_up, w_down, cotangent):
    planes = lax.axis_size("fsdp") // 2
    length = positions.shape[2]
    order, rank = run_tables(positions[:, 0])
    tile = jnp.stack(
        [jnp.pad(item.astype(F32), (0, RUN - item.shape[0])) for item in (g_in, g_post, g_query, g_key)])
    tile = jnp.pad(tile, ((0, 4), (0, 0)))
    cosine, sine = turn_tables(length)
    near = tokens[:, 0]
    shards = (w_query, w_key, w_value, w_out, w_gate, w_up, w_down)
    (win, wo, wgu, wd, normed, query, key, value, q_unit, k_unit, roots, mixed,
     resid, post, back, gains) = front(
        planes, order, rank, near, cotangent[:, 0], tile, cosine, sine, shards)
    plain = lambda item: item.reshape(-1, item.shape[-1])
    apart = lambda item: item.reshape(-1, RUN, item.shape[-1])
    win, wo, wgu, wd, post, back = [plain(item) for item in (win, wo, wgu, wd, post, back)]
    ready, grad_rest, home_d, y_out, y_keep, d_resid, attn, sums = middle(
        planes, post, back, wgu, wd, resid, gains)
    token_grad, sums, block_out, home_g, home_u, home_o, home_q, home_k, home_v = rear(
        planes, order, rank, apart(attn), query, key, value, q_unit, k_unit, roots, plain(mixed), wo,
        apart(normed), win, near, d_resid, cosine, sine, gains, y_out, y_keep, sums, ready, grad_rest)
    me = lax.axis_index("seq") * (2 * planes) + lax.axis_index("fsdp")
    small = [
        lax.dynamic_slice(sums, (row, me * item.shape[0]), (1, item.shape[0]))[0]
        for row, item in ((3, g_in), (0, g_post), (1, g_query), (2, g_key))
    ]
    token_grad, block_out, *homes = deliver(
        token_grad, block_out, home_d, home_g, home_u, home_o, home_q, home_k, home_v)
    home_d, home_g, home_u, home_o, home_q, home_k, home_v = homes
    return (block_out[:, None], token_grad[:, None], *small, home_q, home_k, home_v, home_o,
            home_g, home_u, home_d)


def solution(mesh):
    both = ("seq", "fsdp")
    act = P(None, "fsdp", "seq", None)
    vec, mat = P(both), P(both, None)

    def body(*args):
        rows = args[6].shape[0]
        fits = mesh.shape["seq"] == 4 and mesh.shape["fsdp"] % 2 == 0 and rows % 16 == 0
        return (kernel_body if fits else plain_body)(*args)

    return jax.shard_map(
        body,
        mesh=mesh,
        in_specs=(act, P(None, "fsdp", None), *[vec] * 4, *[mat] * 7, act),
        out_specs=(act, act, *[vec] * 4, *[mat] * 7),
        check_vma=False,
    )
```

```python
import functools

import jax
import jax.numpy as jnp
import numpy as np
from jax import lax
from jax.experimental import pallas as pl
from jax.experimental.pallas import tpu as pltpu
from jax.sharding import PartitionSpec as P

HEADS = 16
KV_HEADS = 8
HEAD_DIM = 128
EPSILON = 1e-06
ROPE_BASE = 1000000.0
NEGATIVE = -1e30
F32 = jnp.float32
BF16 = jnp.bfloat16


def inverse_root(values):
    return lax.rsqrt(jnp.mean(values * values, axis=-1, keepdims=True) + EPSILON)


def rope_tables(token_pos):
    half_width = HEAD_DIM // 2
    frequency = ROPE_BASE ** (-(jnp.arange(half_width, dtype=F32) * 2.0 / HEAD_DIM))
    angles = token_pos.astype(F32)[:, None] * frequency[None, :]
    cosine = jnp.cos(angles)
    sine = jnp.sin(angles)
    return (
        jnp.concatenate([cosine, cosine], axis=-1)[:, None, :],
        jnp.concatenate([sine, sine], axis=-1)[:, None, :],
    )


def rotate(values, cosine, sine):
    half_width = values.shape[-1] // 2
    turned = jnp.concatenate([-values[..., half_width:], values[..., :half_width]], axis=-1)
    return values * cosine + turned * sine


def rotate_back(grads, cosine, sine):
    half_width = grads.shape[-1] // 2
    scaled = grads * sine
    turned = jnp.concatenate([scaled[..., half_width:], -scaled[..., :half_width]], axis=-1)
    return grads * cosine + turned


def norm_back(grads, values, inverse, gain):
    scaled = grads * gain
    return inverse * scaled - values * inverse**3 * jnp.mean(
        scaled * values, axis=-1, keepdims=True
    )


def mul(eq, left, right):
    return jnp.einsum(eq, left, right, preferred_element_type=F32)


def sum_scatter(part, axis):
    return lax.psum_scatter(part.astype(BF16), axis, scatter_dimension=0, tiled=True).astype(F32)


def slice_weights(item, ways):
    rows = item.shape[0]
    return item.reshape(rows, ways, -1).transpose(1, 0, 2)


def plain_body(tokens, positions, g_in, g_post, g_query, g_key, w_query, w_key, w_value,
               w_out, w_gate, w_up, w_down, cotangent):
    ways = lax.axis_size("seq")
    heads, kv_heads = HEADS // ways, KV_HEADS // ways
    micro, rows, width = tokens.shape[0], tokens.shape[2], tokens.shape[3]
    length = positions.shape[2]
    everyone = ("seq", "fsdp")
    gains = [
        lax.all_gather(item, everyone, axis=0, tiled=True).astype(F32)
        for item in (g_in, g_post, g_query, g_key)
    ]
    gain_in, gain_post, gain_query, gain_key = gains

    def spread(*items):
        packed = jnp.concatenate([slice_weights(item, ways) for item in items], axis=2)
        packed = lax.all_to_all(packed, "seq", 0, 0, tiled=True)
        packed = lax.all_gather(packed, "fsdp", axis=1, tiled=True)
        packed = packed.reshape(-1, packed.shape[2])
        sizes = [item.shape[1] // ways for item in items]
        cuts = [sum(sizes[: at + 1]) for at in range(len(sizes) - 1)]
        return jnp.split(packed, cuts, axis=1)

    wq, wk, wv = spread(w_query, w_key, w_value)
    wo = lax.all_gather(w_out, "fsdp", axis=0, tiled=True)
    wg, wu = spread(w_gate, w_up)
    wd = lax.all_gather(w_down, "fsdp", axis=0, tiled=True)
    scale = HEAD_DIM ** (-0.5)

    def gather_rows(item):
        return lax.all_gather(item, "seq", axis=0, tiled=True)

    grads = None
    outs, token_grads = [], []
    for at in range(micro):
        inputs = tokens[at, 0].astype(F32)
        pos = positions[at, 0]
        cosine, sine = rope_tables(pos)
        allowed = pos[None, :] <= pos[:, None]
        inv_in = inverse_root(inputs)
        normed = gather_rows((inputs * inv_in * gain_in).astype(BF16))
        q_raw = mul("td,df->tf", normed, wq).reshape(length, heads, HEAD_DIM)
        k_raw = mul("td,df->tf", normed, wk).reshape(length, kv_heads, HEAD_DIM)
        value = mul("td,df->tf", normed, wv).astype(BF16).reshape(length, kv_heads, HEAD_DIM)
        inv_q, inv_k = inverse_root(q_raw), inverse_root(k_raw)
        query = rotate(q_raw * inv_q * gain_query, cosine, sine).astype(BF16)
        query = query.reshape(length, kv_heads, heads // kv_heads, HEAD_DIM)
        key = rotate(k_raw * inv_k * gain_key, cosine, sine).astype(BF16)
        scores = jnp.where(allowed, mul("qjgd,kjd->jgqk", query, key) * scale, NEGATIVE)
        soft = jax.nn.softmax(scores, axis=-1)
        soft_low = soft.astype(BF16)
        mixed = mul("jgqk,kjd->qjgd", soft_low, value).astype(BF16).reshape(length, -1)
        resid = inputs + sum_scatter(mul("th,hd->td", mixed, wo), "seq")
        inv_post = inverse_root(resid)
        post = gather_rows((resid * inv_post * gain_post).astype(BF16))
        gate = mul("td,df->tf", post, wg)
        upper = mul("td,df->tf", post, wu)
        sigma = jax.nn.sigmoid(gate)
        hidden = (gate * sigma * upper).astype(BF16)
        outs.append((resid + sum_scatter(mul("tf,fd->td", hidden, wd), "seq")).astype(BF16))
        back_low = cotangent[at, 0]
        back = gather_rows(back_low)
        g_down = mul("tf,td->fd", hidden, back)
        d_hidden = mul("td,fd->tf", back, wd)
        d_gate = (d_hidden * upper * sigma * (1.0 + gate * (1.0 - sigma))).astype(BF16)
        d_upper = (d_hidden * gate * sigma).astype(BF16)
        g_gate = mul("td,tf->df", post, d_gate)
        g_up = mul("td,tf->df", post, d_upper)
        d_post = sum_scatter(mul("tf,df->td", d_gate, wg) + mul("tf,df->td", d_upper, wu), "seq")
        post_grad = jnp.sum(d_post * resid * inv_post, axis=0)
        d_resid = back_low.astype(F32) + norm_back(d_post, resid, inv_post, gain_post)
        d_attn = gather_rows(d_resid.astype(BF16))
        g_out = mul("th,td->hd", mixed, d_attn)
        d_mixed = mul("td,hd->th", d_attn, wo).astype(BF16)
        d_mixed = d_mixed.reshape(length, kv_heads, heads // kv_heads, HEAD_DIM)
        d_soft = mul("qjgd,kjd->jgqk", d_mixed, value)
        d_scores = (soft * (d_soft - jnp.sum(d_soft * soft, axis=-1, keepdims=True))).astype(BF16)
        d_query = mul("jgqk,kjd->qjgd", d_scores, key) * scale
        d_key = mul("jgqk,qjgd->kjd", d_scores, query) * scale
        d_value = mul("jgqk,qjgd->kjd", soft_low, d_mixed).astype(BF16).reshape(length, -1)
        key_turn = rotate_back(d_key, cosine, sine)
        query_turn = rotate_back(d_query.reshape(length, heads, HEAD_DIM), cosine, sine)
        key_grad = jnp.sum(key_turn * k_raw * inv_k, axis=(0, 1))
        query_grad = jnp.sum(query_turn * q_raw * inv_q, axis=(0, 1))
        d_key = norm_back(key_turn, k_raw, inv_k, gain_key).astype(BF16).reshape(length, -1)
        d_query = norm_back(query_turn, q_raw, inv_q, gain_query).astype(BF16).reshape(length, -1)
        g_query_w = mul("td,tf->df", normed, d_query)
        g_key_w = mul("td,tf->df", normed, d_key)
        g_value_w = mul("td,tf->df", normed, d_value)
        d_normed = mul("tf,df->td", d_query, wq) + mul("tf,df->td", d_key, wk)
        d_normed = sum_scatter(d_normed + mul("tf,df->td", d_value, wv), "seq")
        in_grad = jnp.sum(d_normed * inputs * inv_in, axis=0)
        token_grads.append(d_resid + norm_back(d_normed, inputs, inv_in, gain_in))
        found = [in_grad, post_grad, query_grad, key_grad, g_query_w, g_key_w, g_value_w,
                 g_out, g_gate, g_up, g_down]
        grads = found if grads is None else [left + right for left, right in zip(grads, found)]

    small = [lax.psum_scatter(item, everyone, scatter_dimension=0, tiled=True) for item in grads[:4]]

    def columns_home(item):
        full, wide = item.shape
        item = item.reshape(ways, -1, wide).astype(BF16)
        item = lax.psum_scatter(item, "fsdp", scatter_dimension=1, tiled=True)
        item = lax.all_to_all(item, "seq", 0, 0, tiled=True)
        return item.transpose(1, 0, 2).reshape(item.shape[1], ways * wide).astype(F32)

    def rows_home(item):
        return sum_scatter(item, "fsdp")

    large = [columns_home(item) for item in grads[4:7]] + [rows_home(grads[7])]
    large += [columns_home(item) for item in grads[8:10]] + [rows_home(grads[10])]
    return (jnp.stack(outs)[:, None], jnp.stack(token_grads)[:, None], *small, *large)


MESH = pl.DeviceIdType.MESH
ANY = pl.ANY
VMEM = pltpu.VMEM
RUN = 128
BLOCK = 256
NARROW = (((1,), (1,)), ((), ()))
TALL = (((0,), (0,)), ((), ()))
PLAIN = (((1,), (0,)), ((), ()))
LOG2E = 1.4426950408889634
SCALE = HEAD_DIM ** (-0.5)
LEVEL = 8
VMEM_BYTES = 63 * 2**20


def dot(left, right, dims=PLAIN):
    return lax.dot_general(left, right, dims, preferred_element_type=F32)


class Place:
    def __init__(self, planes):
        self.planes = planes
        self.s = lax.axis_index("seq")
        self.f = lax.axis_index("fsdp")
        self.x, self.c = self.s // 2, self.s % 2
        self.z, self.y = self.f // 2, self.f % 2
        self.other_y = 1 - self.y
        self.core_dev = (self.x * 2 + 1 - self.c, self.f)
        self.x_dev = ((1 - self.x) * 2 + self.c, self.f)
        self.far_dev = ((1 - self.x) * 2 + 1 - self.c, self.f)
        self.y_dev = (self.s, self.z * 2 + self.other_y)
        self.seq_dev = [(self.s, self.f), self.core_dev, self.x_dev, self.far_dev]

    def z_at(self, step):
        return lax.rem(self.z + step, self.planes)

    def z_dev(self, step):
        return (self.s, self.z_at(step) * 2 + self.y)

    def peers(self):
        return [self.core_dev, self.x_dev, self.far_dev, self.y_dev] + [
            self.z_dev(step) for step in range(1, self.planes)
        ]

    def meet(self):
        barrier = pltpu.get_barrier_semaphore()
        for peer in self.peers():
            pl.semaphore_signal(barrier, inc=1, device_id=peer, device_id_type=MESH)
        pl.semaphore_wait(barrier, 3 + self.planes)


def remote(src, dst, out_sem, in_sem, device):
    return pltpu.make_async_remote_copy(
        src_ref=src, dst_ref=dst, send_sem=out_sem, recv_sem=in_sem,
        device_id=device, device_id_type=MESH,
    )


class Wire:
    def __init__(self, out_sems, in_sems, own_sems):
        self.out_sems, self.in_sems, self.own_sems = out_sems, in_sems, own_sems
        self.sent, self.owned = [], 0

    def send(self, src, dst, device, start=True):
        at = len(self.sent)
        copy = remote(src, dst, self.out_sems.at[at], self.in_sems.at[at], device)
        if start:
            copy.start()
        self.sent.append(copy)
        return copy

    def own(self, src, dst):
        copy = pltpu.make_async_copy(src, dst, self.own_sems.at[self.owned])
        copy.start()
        self.owned += 1
        return copy

    def close(self):
        for copy in self.sent:
            copy.wait_send()


def wire_scratch(copies, owns):
    return [
        pltpu.SemaphoreType.DMA((copies,)),
        pltpu.SemaphoreType.DMA((copies,)),
        pltpu.SemaphoreType.DMA((owns,)),
    ]


class Reducer:
    def __init__(self, place, part, core_out, core_in, x_out, x_in, keep, sems):
        self.place, self.part = place, part
        self.core_out, self.core_in = core_out, core_in
        self.x_out, self.x_in, self.keep = x_out, x_in, keep
        self.core_s, self.core_r, self.x_s, self.x_r = sems

    def block(self, step):
        p = self.place
        turn = step % 4
        x = jnp.where(turn < 2, 1 - p.x, p.x)
        c = jnp.where(turn % 2 == 0, 1 - p.c, p.c)
        return step // 4, x * 2 + c

    def core_copy(self, slot):
        return remote(self.core_out.at[slot], self.core_in.at[slot], self.core_s.at[slot],
                      self.core_r.at[slot], self.place.core_dev)

    def x_copy(self, micro):
        return remote(self.x_out.at[micro], self.x_in.at[micro], self.x_s.at[micro],
                      self.x_r.at[micro], self.place.x_dev)

    def take(self, step, send_x=True):
        micro, turn = step // 4, step % 4

        @pl.when(turn % 2 == 0)
        def _():
            slot = micro * 2 + turn // 2
            self.core_out[slot] = self.part[...].astype(BF16)
            self.core_copy(slot).start()

        @pl.when(turn == 1)
        def _():
            slot = micro * 2
            self.core_copy(slot).wait_recv()
            self.x_out[micro] = (self.part[...] + self.core_in[slot].astype(F32)).astype(BF16)
            if send_x:
                self.x_copy(micro).start()

        @pl.when(turn == 3)
        def _():
            slot = micro * 2 + 1
            self.core_copy(slot).wait_recv()
            self.keep[micro] = self.part[...] + self.core_in[slot].astype(F32)

    def total(self, micro):
        self.x_copy(micro).wait_recv()
        return self.keep[micro] + self.x_in[micro].astype(F32)

    def close(self, send_x=True):
        for slot in range(4):
            self.core_copy(slot).wait_send()
        if send_x:
            for micro in range(2):
                self.x_copy(micro).wait_send()


def reducer_scratch(width):
    return [
        VMEM((4, BLOCK, width), BF16),
        VMEM((4, BLOCK, width), BF16),
        VMEM((2, BLOCK, width), BF16),
        VMEM((2, BLOCK, width), BF16),
        VMEM((2, BLOCK, width), F32),
        pltpu.SemaphoreType.DMA((4,)),
        pltpu.SemaphoreType.DMA((4,)),
        pltpu.SemaphoreType.DMA((2,)),
        pltpu.SemaphoreType.DMA((2,)),
    ]


def row_mean(values):
    return jnp.mean(values, axis=-1, keepdims=True)


def spread_gain(table, row, devices, width):
    per = width // devices
    lanes = lax.broadcasted_iota(jnp.int32, (RUN, width), 0)
    column = lax.broadcasted_iota(jnp.int32, (RUN, width), 1)
    pick = (lanes == lax.rem(column, per)).astype(BF16)
    picked = dot(table, pick)
    rows = lax.broadcasted_iota(jnp.int32, (devices * 8, width), 0)
    owner = lax.broadcasted_iota(jnp.int32, (devices * 8, width), 1) // per
    return jnp.sum(jnp.where(rows == owner * 8 + row, picked, 0.0), axis=0, keepdims=True)


def two_runs(ref, first, second):
    return jnp.concatenate([ref[first], ref[second]], axis=0)


def joined(value):
    return value.reshape(-1, value.shape[-1])


def flat(ref):
    return joined(ref[...])


def front_kernel(
    planes,
    order, rank, tokens, cotangent, gain_tile, cosine_in, sine_in,
    s_q, s_k, s_v, s_o, s_g, s_u, s_d,
    win_out, wo_out, wgu, wd,
    normed_out, query_out, key_out, value_out, q_unit_out, k_unit_out, roots_out, mixed_out,
    resid_out, post_full, back_full, gains,
    win, wo, normed, query, key, value, q_unit, k_unit, roots, mixed, resid,
    tok_full, gain_all, post_own, back_own, cosine, sine, part,
    core_out, core_in, x_out, x_in, keep, core_s, core_r, x_s, x_r,
    out_sems, in_sems, own_sems,
):
    p = Place(planes)
    s, f = p.s, p.f
    devices = 8 * planes
    wire = Wire(out_sems, in_sems, own_sems)
    reducer = Reducer(p, part, core_out, core_in, x_out, x_in, keep, (core_s, core_r, x_s, x_r))
    rows = BLOCK
    mine = pl.ds(s * rows, rows)
    theirs = pl.ds(p.x_dev[0] * rows, rows)
    length = 4 * rows
    runs = length // RUN
    p.meet()

    def spread_columns(items, full):
        came = [[] for _ in range(4)]
        for at in (0, 2, 3, 1):
            first = 0
            for item in items:
                wide = item.shape[1] // 4
                src = item.at[:, pl.ds(pl.multiple_of(p.seq_dev[at][0] * wide, RUN), wide)]
                dst = full.at[s, f, :, pl.ds(first, wide)]
                came[at].append(wire.send(src, dst, p.seq_dev[at]) if at else wire.own(src, dst))
                first += wide
        return came

    def arrived(copies, at):
        for copy in copies[at]:
            copy.wait_recv() if at else copy.wait()

    def side(here):
        return [wire.send(here, here, p.y_dev)]

    def push(here):
        return [wire.send(here, here, p.z_dev(step)) for step in range(1, planes)]

    def forward(view, far, near):
        for step, copy in enumerate(far, 1):
            copy.wait_recv()
            near += side(view(p.z_at(planes - step) * 2 + p.y))

    def settle(near):
        for copy in near:
            copy.wait_recv()

    gain_all[s, f] = gain_tile[...]
    gain_in = [wire.send(gain_all.at[s, f], gain_all.at[s, f], dev) for dev in p.seq_dev[1:]]
    first = spread_columns((s_q, s_k, s_v), win)
    out_near = [wire.send(s_o, wo.at[f], p.y_dev)]
    down_near = [wire.send(s_d, wd.at[f], p.y_dev)]
    tok_here, tok_x, tok_core = [], [], []
    for micro in range(2):
        to = tok_full.at[pl.ds(micro * runs + s * 2, 2)]
        tok_here.append(wire.own(tokens.at[micro], to))
        tok_core.append(wire.send(tokens.at[micro], to, p.core_dev))
    out_kept = wire.own(s_o, wo.at[f])
    down_kept = wire.own(s_d, wd.at[f])
    staged = [wire.own(cosine_in, cosine), wire.own(sine_in, sine), wire.own(cotangent, back_own)]

    def in_view(at):
        return lambda owner: win.at[p.seq_dev[at][0], owner]

    def wide_view(at):
        return lambda owner: wgu.at[p.seq_dev[at][0], owner]

    in_far, in_near, wide_far, wide_near = {}, [], {}, []
    arrived(first, 0)
    in_far[0] = push(in_view(0)(f))
    in_near += side(in_view(0)(f))
    for copy in gain_in:
        copy.wait_recv()
    gain_far = push(gain_all.at[:, f])
    gain_near = side(gain_all.at[:, f])
    for at in (1, 2, 3):
        arrived(first, at)
        in_near += side(in_view(at)(f))
        if at == 1:
            in_far[1] = push(in_view(1)(f))
    for micro in range(2):
        to = tok_full.at[pl.ds(micro * runs + s * 2, 2)]
        tok_x.append(wire.send(tokens.at[micro], to, p.x_dev))
    second = spread_columns((s_g, s_u), wgu)
    forward(lambda owner: gain_all.at[:, owner], gain_far, gain_near)
    forward(in_view(0), in_far[0], in_near)
    in_far[2] = push(in_view(2)(f))
    forward(in_view(1), in_far[1], in_near)
    in_far[3] = push(in_view(3)(f))
    settle(gain_near)
    table = gain_all[...].reshape(devices * 8, RUN).astype(BF16)
    gain_first = spread_gain(table, 0, devices, 1024)
    gain_post = spread_gain(table, 1, devices, 1024)
    gain_query = spread_gain(table, 2, devices, RUN)
    gain_key = spread_gain(table, 3, devices, RUN)
    gains[...] = jnp.zeros_like(gains)
    gains[0:1] = gain_first
    gains[1:2] = gain_post
    gains[2:3, 0:RUN] = gain_query
    gains[3:4, 0:RUN] = gain_key
    forward(in_view(2), in_far[2], in_near)
    out_far = [wire.send(s_o, wo.at[f], p.z_dev(step)) for step in range(1, planes)]
    forward(in_view(3), in_far[3], in_near)
    tok_fwd = []
    for micro in range(2):
        tok_x[micro].wait_recv()
        block = tok_full.at[pl.ds(micro * runs + p.x_dev[0] * 2, 2)]
        tok_fwd.append(wire.send(block, block, p.core_dev))
    for at in range(4):
        arrived(second, at)
        wide_near += side(wide_view(at)(f))
    for copy in staged:
        copy.wait()
    back_x, back_core, back_kept = [], [], []
    for micro in range(2):
        to = back_full.at[micro, mine]
        back_x.append(wire.send(cotangent.at[micro], to, p.x_dev))
        back_kept.append(wire.own(back_own.at[micro], to))
        back_core.append(wire.send(cotangent.at[micro], to, p.core_dev))
    wide_far[0] = push(wide_view(0)(f))
    down_far = [wire.send(s_d, wd.at[f], p.z_dev(step)) for step in range(1, planes)]
    settle(in_near)
    saved = [wire.own(win, win_out)]
    for copy in tok_here:
        copy.wait()
    for copy in tok_core + tok_fwd:
        copy.wait_recv()

    def project(step, carry):
        here = pl.ds(pl.multiple_of(step * BLOCK, BLOCK), BLOCK)
        raw = two_runs(tok_full, order[step * 2], order[step * 2 + 1]).astype(F32)
        root = lax.rsqrt(row_mean(raw * raw) + EPSILON)
        low = (raw * root * gains[0:1]).astype(BF16)
        normed[here] = low
        turn = pl.ds(pl.multiple_of(lax.rem(step, length // BLOCK) * BLOCK, BLOCK), BLOCK)
        cos, sin = cosine[turn], sine[turn]
        product = dot(low, flat(win))
        found, start = [], 0
        for low_ref, unit_ref, row in ((query, q_unit, 2), (key, k_unit, 3)):
            gain = gains[row : row + 1, 0:RUN]
            for head in range(low_ref.shape[1] // HEAD_DIM):
                at = slice(head * HEAD_DIM, (head + 1) * HEAD_DIM)
                one = product[:, start : start + HEAD_DIM]
                inverse = lax.rsqrt(row_mean(one * one) + EPSILON)
                unit = one * inverse
                unit_ref[here, at] = unit.astype(BF16)
                scaled = unit * gain
                low_ref[here, at] = (scaled * cos + pltpu.roll(scaled, HEAD_DIM // 2, 1) * sin).astype(BF16)
                found.append(inverse)
                start += HEAD_DIM
        roots[here, :] = jnp.zeros((BLOCK, roots.shape[1]), F32)
        for at, inverse in enumerate(found):
            roots[here, at : at + 1] = inverse
        value[here] = product[:, start:].astype(BF16)
        return carry

    def attend(step, carry):
        micro, head = step // 2, lax.rem(step, 2)
        keys_at = pl.ds(pl.multiple_of(head * HEAD_DIM, HEAD_DIM), HEAD_DIM)
        lanes = [pl.ds(pl.multiple_of(head * 2 * HEAD_DIM + g * HEAD_DIM, HEAD_DIM), HEAD_DIM) for g in range(2)]
        for block in range(length // BLOCK):
            here = pl.ds(pl.multiple_of(micro * length + block * BLOCK, BLOCK), BLOCK)
            seen = (block + 1) * BLOCK
            past = pl.ds(pl.multiple_of(micro * length, BLOCK), seen)
            asked = jnp.concatenate([query[here, lane] for lane in lanes], axis=0)
            scores = dot(asked, key[past, keys_at], NARROW)
            line = lax.broadcasted_iota(jnp.int32, (2 * BLOCK, seen), 0)
            line = jnp.where(line >= BLOCK, line - BLOCK, line) + block * BLOCK
            column = lax.broadcasted_iota(jnp.int32, (2 * BLOCK, seen), 1)
            scores = jnp.where(column <= line, scores, NEGATIVE)
            top = jnp.max(scores, axis=-1, keepdims=True)
            weight = jnp.exp2((scores - top) * (SCALE * LOG2E))
            total = jnp.sum(weight, axis=-1, keepdims=True)
            out = dot(weight.astype(BF16), value[past, keys_at]) * (1.0 / total)
            level = top * (SCALE * LOG2E) + jnp.log2(total)
            pair = pl.ds(micro * runs + block * 2, 2)
            held = roots[here, :]
            spot = lax.broadcasted_iota(jnp.int32, held.shape, 1)
            for g, lane in enumerate(lanes):
                half = slice(g * BLOCK, (g + 1) * BLOCK)
                mixed[pair, :, lane] = out[half].astype(BF16).reshape(2, RUN, HEAD_DIM)
                held = jnp.where(spot == LEVEL + head * 2 + g, level[half], held)
            roots[here, :] = held
        return carry

    def mix_out(step, carry):
        micro, block = reducer.block(step)
        at = micro * runs + block * 2
        low = two_runs(mixed, rank[at], rank[at + 1])
        part[...] = dot(low, flat(wo))
        reducer.take(step)
        return carry

    posts = []

    def finish(micro):
        own = joined(tok_full[pl.ds(micro * runs + s * 2, 2)]).astype(F32)
        total = own + reducer.total(micro)
        resid[micro] = total
        root = lax.rsqrt(row_mean(total * total) + EPSILON)
        post_own[micro] = (total * root * gains[1:2]).astype(BF16)
        to = post_full.at[micro, mine]
        posts.append((wire.send(post_own.at[micro], to, p.x_dev), wire.send(post_own.at[micro], to, p.core_dev),
                      wire.own(post_own.at[micro], to)))
        saved.append(wire.own(resid.at[micro], resid_out.at[micro]))

    steps = length // BLOCK
    lax.fori_loop(0, steps, project, 0)
    forward(lambda owner: wo.at[owner], out_far, out_near)
    wide_far[1] = push(wide_view(1)(f))
    lax.fori_loop(0, 2, attend, 0)
    lax.fori_loop(steps, 2 * steps, project, 0)
    saved += [wire.own(here, there) for here, there in (
        (normed, normed_out), (query, query_out), (key, key_out), (value, value_out),
        (q_unit, q_unit_out), (k_unit, k_unit_out))]
    out_kept.wait()
    settle(out_near)
    lax.fori_loop(0, 4, mix_out, 0)
    forward(wide_view(0), wide_far[0], wide_near)
    wide_far[2] = push(wide_view(2)(f))
    lax.fori_loop(2, 4, attend, 0)
    lax.fori_loop(4, 8, mix_out, 0)
    saved += [wire.own(mixed, mixed_out), wire.own(roots, roots_out), wire.own(wo, wo_out)]
    wide_far[3] = push(wide_view(3)(f))
    finish(0)
    forward(lambda owner: wd.at[owner], down_far, down_near)
    forward(wide_view(1), wide_far[1], wide_near)
    for micro in range(2):
        back_x[micro].wait_recv()
        block = back_full.at[micro, theirs]
        back_core.append(wire.send(block, block, p.core_dev))
    finish(1)
    forward(wide_view(2), wide_far[2], wide_near)
    forward(wide_view(3), wide_far[3], wide_near)
    last = []
    for micro in range(2):
        posts[micro][0].wait_recv()
        block = post_full.at[micro, theirs]
        last.append(wire.send(block, block, p.core_dev))
    for micro in range(2):
        last[micro].wait_recv()
        posts[micro][1].wait_recv()
        posts[micro][2].wait()
    for copy in back_core:
        copy.wait_recv()
    for copy in back_kept + saved + [down_kept]:
        copy.wait()
    settle(wide_near)
    settle(down_near)
    reducer.close()
    wire.close()


def front(planes, order, rank, tokens, cotangent, gain_tile, cosine, sine, shards):
    nf = 2 * planes
    rows = tokens.shape[1]
    length = 4 * rows
    total = 2 * length
    tokens = tokens.reshape(2, 2, RUN, tokens.shape[2])
    deep = shards[0].shape[0]

    def low(width):
        return jax.ShapeDtypeStruct((total, width), BF16)

    shapes = [
        jax.ShapeDtypeStruct((4, nf, deep, 1024), BF16), jax.ShapeDtypeStruct((nf, *shards[3].shape), BF16),
        jax.ShapeDtypeStruct((4, nf, deep, 2 * (shards[4].shape[1] // 4)), BF16),
        jax.ShapeDtypeStruct((nf, *shards[6].shape), BF16),
        low(1024), low(512), low(256), low(256), low(512), low(256),
        jax.ShapeDtypeStruct((total, 16), F32), jax.ShapeDtypeStruct((total // RUN, RUN, 512), BF16),
        jax.ShapeDtypeStruct((2, rows, 1024), F32),
        jax.ShapeDtypeStruct((2, length, 1024), BF16), jax.ShapeDtypeStruct((2, length, 1024), BF16),
        jax.ShapeDtypeStruct((8, 1024), F32)]
    held = [shapes[at] for at in (0, 1, *range(4, 13))]
    vm = pl.BlockSpec(memory_space=VMEM)
    hb = pl.BlockSpec(memory_space=ANY)
    sm = pl.BlockSpec(memory_space=pltpu.SMEM)
    return pl.pallas_call(
        functools.partial(front_kernel, planes),
        out_shape=shapes,
        in_specs=[sm, sm, hb, hb, vm, hb, hb, hb, hb, hb, hb, vm, vm, vm],
        out_specs=[hb] * (len(shapes) - 1) + [vm],
        scratch_shapes=[
            *[VMEM(item.shape, item.dtype) for item in held],
            VMEM((total // RUN, RUN, 1024), BF16), VMEM((4, nf, 8, RUN), F32), VMEM((2, rows, 1024), BF16),
            VMEM((2, rows, 1024), BF16), VMEM(cosine.shape, F32), VMEM(sine.shape, F32),
            VMEM((BLOCK, 1024), F32), *reducer_scratch(1024), *wire_scratch(130, 40),
        ],
        compiler_params=pltpu.CompilerParams(
            collective_id=0, has_side_effects=True, vmem_limit_bytes=VMEM_BYTES),
        name="front",
    )(order, rank, tokens, cotangent, gain_tile, cosine, sine, *shards)


GROUPS = (2, 3, 1, 0)


class RowHoming:
    def __init__(self, place, wire, grad, came, sums, far, home):
        self.p, self.wire, self.grad = place, wire, grad
        self.came, self.sums, self.far, self.home = came, sums, far, home

    def half(self, ref, at):
        return ref.at[pl.ds(at * (self.p.planes // 2), self.p.planes // 2)]

    def start(self):
        p = self.p
        self.kept = self.wire.own(self.grad.at[:, p.y], self.sums)
        self.sent = [
            self.wire.send(self.half(self.grad, at).at[:, p.other_y], self.half(self.came, at), p.y_dev)
            for at in range(2)
        ]
        self.out = [
            self.wire.send(self.sums.at[p.z_at(step)], self.far.at[step - 1], p.z_dev(step), start=False)
            for step in range(1, p.planes)
        ]

    def push(self, at):
        if at == 0:
            self.kept.wait()
        self.sent[at].wait_recv()
        share = self.p.planes // 2

        def add(z, carry):
            self.sums[z] = (self.sums[z].astype(F32) + self.came[z].astype(F32)).astype(BF16)
            return carry

        lax.fori_loop(at * share, (at + 1) * share, add, 0)
        for step, copy in enumerate(self.out, 1):
            @pl.when(self.p.z_at(step) // share == at)
            def _(copy=copy):
                copy.start()

    def gather(self):
        for copy in self.out:
            copy.wait_recv()
        total = self.sums[self.p.z].astype(F32)
        for step in range(1, self.p.planes):
            total = total + self.far[step - 1].astype(F32)
        self.home[...] = total


class ColumnHoming:
    def __init__(self, place, wire, came, sums, far, leave=None, arrive=None, homes=()):
        self.p, self.wire, self.came, self.sums, self.far = place, wire, came, sums, far
        self.leave, self.arrive, self.homes = leave, arrive, homes
        self.kept, self.sent, self.out, self.back = {}, {}, {}, {}

    def start(self, at, grad):
        self.kept[at] = self.wire.own(grad.at[:, self.p.y], self.sums.at[at])
        self.sent[at] = self.wire.send(grad.at[:, self.p.other_y], self.came.at[at], self.p.y_dev)

    def add(self, at):
        self.kept[at].wait()
        self.sent[at].wait_recv()

        def add(z, carry):
            self.sums[at, z] = (self.sums[at, z].astype(F32) + self.came[at, z].astype(F32)).astype(BF16)
            return carry

        lax.fori_loop(0, self.p.planes, add, 0)

    def push(self, at):
        self.out[at] = [
            self.wire.send(self.sums.at[at, self.p.z_at(step)], self.far.at[at, step - 1], self.p.z_dev(step))
            for step in range(1, self.p.planes)
        ]

    def put(self, owner, value):
        first = 0
        for home, start, width in self.homes:
            at = pl.multiple_of(owner * (home.shape[1] // 4) + start, RUN)
            home[:, pl.ds(at, width)] = value[:, first : first + width]
            first += width

    def gather(self, at):
        for copy in self.out[at]:
            copy.wait_recv()
        total = self.sums[at, self.p.z].astype(F32)
        for step in range(1, self.p.planes):
            total = total + self.far[at, step - 1].astype(F32)
        if GROUPS[at] == 0:
            self.put(self.p.s, total)
            return
        self.leave[at] = total.astype(BF16)
        self.back[at] = self.wire.send(self.leave.at[at], self.arrive.at[at], self.p.seq_dev[GROUPS[at]])

    def finish(self):
        for at, copy in self.back.items():
            copy.wait_recv()
            self.put(self.p.seq_dev[GROUPS[at]][0], self.arrive[at].astype(F32))


def group_rows(place, at):
    owner = place.seq_dev[GROUPS[at]][0]
    return pl.ds(pl.multiple_of(owner * BLOCK, BLOCK), BLOCK)


def column_scratch(planes, deep, width, groups=4):
    return [
        VMEM((groups, planes, deep, width), BF16), VMEM((groups, planes, deep, width), BF16),
        VMEM((4, planes - 1, deep, width), BF16), VMEM((3, deep, width), BF16), VMEM((3, deep, width), BF16),
    ]


def row_scratch(planes, deep, width):
    return [VMEM((planes, deep, width), BF16), VMEM((planes, deep, width), BF16),
            VMEM((planes - 1, deep, width), BF16)]


def middle_kernel(
    planes,
    post_in, back_in, wgu_in, wd_in, resid_in, gains,
    ready, grad_rest, home_d, y_out, y_keep, d_resid, attn_full, sums,
    post, back, wgu, wd, resid, load_sems,
    grad_first, g_came, grad_d, d_came, d_sums, d_far, hidden, d_gu, part, attn_own,
    y_core_out, y_core_in,
    core_out, core_in, x_out, x_in, keep, core_s, core_r, x_s, x_r,
    y_core_s, y_core_r, out_sems, in_sems, own_sems,
):
    p = Place(planes)
    s = p.s
    wire = Wire(out_sems, in_sems, own_sems)
    into_post = Reducer(p, part, core_out, core_in, x_out, x_in, keep, (core_s, core_r, x_s, x_r))
    into_out = Reducer(p, part, y_core_out, y_core_in, y_out, None, y_keep, (y_core_s, y_core_r, None, None))
    rows = resid.shape[1]
    length = 4 * rows
    wide = hidden.shape[1]
    mine = pl.ds(s * rows, rows)
    theirs = pl.ds(p.x_dev[0] * rows, rows)
    loads = [wire.own(wgu_in, wgu), wire.own(wd_in, wd), wire.own(resid_in, resid)]

    def chunk(step):
        micro, block = into_post.block(step)
        here = pl.ds(pl.multiple_of(micro * length + block * BLOCK, BLOCK), BLOCK)
        return [pltpu.make_async_copy(far.at[here], near.at[here], load_sems.at[at, step])
                for at, (far, near) in enumerate(((post_in, post), (back_in, back)))]

    for step in range(8):
        for copy in chunk(step):
            copy.start()
    p.meet()
    for copy in loads:
        copy.wait()

    def feed(step, carry):
        micro, block = into_post.block(step)
        here = pl.ds(pl.multiple_of(micro * length + block * BLOCK, BLOCK), BLOCK)
        for copy in chunk(step):
            copy.wait()
        both = dot(post[here, :], wgu[...])
        d_hidden = dot(back[here, :], wd[...], NARROW)
        gate, upper = both[:, :wide], both[:, wide:]
        sigma = 1.0 / (1.0 + jnp.exp(-gate))
        lit = gate * sigma
        hidden[here] = (lit * upper).astype(BF16)
        d_gu[here, :wide] = (d_hidden * upper * (sigma + lit * (1.0 - sigma))).astype(BF16)
        d_gu[here, wide:] = (d_hidden * lit).astype(BF16)
        part[...] = dot(d_gu[here, :], wgu[...], NARROW)
        into_post.take(step)
        part[...] = dot(hidden[here, :], wd[...])
        into_out.take(step, send_x=False)
        return carry

    down = RowHoming(p, wire, grad_d, d_came, d_sums, d_far, home_d)
    columns = ColumnHoming(p, wire, g_came, ready, None)

    def down_tile(at, carry):
        tall = wide // 2
        cut = pl.ds(pl.multiple_of(at * tall, RUN), tall)
        found = dot(hidden[:, cut], back[...], TALL).astype(BF16)
        grad_d[pl.ds(at * (planes // 2), planes // 2)] = found.reshape(planes // 2, *grad_d.shape[1:])
        return carry

    def wide_tile(at):
        found = dot(post[:, group_rows(p, at)], d_gu[...], TALL).astype(BF16)
        return found.reshape(grad_first.shape)

    gain = gains[1:2]
    sends = []
    sums[...] = jnp.zeros_like(sums)

    def settle(micro):
        grad = into_post.total(micro)
        held = resid[micro]
        root = lax.rsqrt(row_mean(held * held) + EPSILON)
        unit = held * root
        sums[0:1] += jnp.sum(grad * unit, axis=0, keepdims=True)
        scaled = grad * gain
        own = back[pl.ds(pl.multiple_of(micro * length + s * rows, rows), rows), :].astype(F32)
        whole = own + root * (scaled - unit * row_mean(scaled * unit))
        d_resid[micro] = whole
        attn_own[micro] = whole.astype(BF16)
        to = attn_full.at[micro, mine]
        sends.append((wire.send(attn_own.at[micro], to, p.x_dev), wire.send(attn_own.at[micro], to, p.core_dev),
                      wire.own(attn_own.at[micro], to)))
        y_keep[micro] = y_keep[micro] + held

    lax.fori_loop(0, 7, feed, 0)
    settle(0)
    lax.fori_loop(7, 8, feed, 0)
    lax.fori_loop(0, 2, down_tile, 0)
    down.start()
    grad_first[...] = wide_tile(0)
    columns.start(0, grad_first)
    settle(1)
    grad_rest[0] = wide_tile(1)
    down.push(0)
    grad_rest[1] = wide_tile(2)
    grad_rest[2] = wide_tile(3)
    down.push(1)
    forwards = []
    for micro in range(2):
        sends[micro][0].wait_recv()
        block = attn_full.at[micro, theirs]
        forwards.append(wire.send(block, block, p.core_dev))
    columns.add(0)
    for micro in range(2):
        forwards[micro].wait_recv()
        sends[micro][1].wait_recv()
        sends[micro][2].wait()
    down.gather()
    into_post.close()
    into_out.close(send_x=False)
    wire.close()


def middle(planes, post, back, wgu, wd, resid, gains):
    rows = resid.shape[1]
    total = 8 * rows
    wide = wd.shape[0]
    deep = 1024 // (8 * planes)
    once = (planes, 2, deep, 2 * wide)
    slim = (planes, 2, wide // (2 * planes), 1024)
    shapes = [
        jax.ShapeDtypeStruct((1, planes, deep, 2 * wide), BF16), jax.ShapeDtypeStruct((3, *once), BF16),
        jax.ShapeDtypeStruct(slim[2:], F32),
        jax.ShapeDtypeStruct((2, rows, 1024), BF16), jax.ShapeDtypeStruct((2, rows, 1024), F32),
        jax.ShapeDtypeStruct((2, rows, 1024), F32), jax.ShapeDtypeStruct((2, 4 * rows, 1024), BF16),
        jax.ShapeDtypeStruct((8, 1024), F32),
    ]
    vm = pl.BlockSpec(memory_space=VMEM)
    hb = pl.BlockSpec(memory_space=ANY)
    return pl.pallas_call(
        functools.partial(middle_kernel, planes),
        out_shape=shapes,
        in_specs=[hb] * 5 + [vm],
        out_specs=[vm] * 6 + [hb, vm],
        scratch_shapes=[
            *[VMEM(item.shape, item.dtype) for item in (post, back, wgu, wd, resid)],
            pltpu.SemaphoreType.DMA((2, 8)),
            VMEM(once, BF16), VMEM((1, planes, deep, 2 * wide), BF16), VMEM(slim, BF16),
            *row_scratch(planes, *slim[2:]),
            VMEM((total, wide), BF16), VMEM((total, 2 * wide), BF16),
            VMEM((BLOCK, 1024), F32), VMEM((2, rows, 1024), BF16),
            VMEM((4, BLOCK, 1024), BF16), VMEM((4, BLOCK, 1024), BF16),
            *reducer_scratch(1024),
            pltpu.SemaphoreType.DMA((4,)), pltpu.SemaphoreType.DMA((4,)),
            *wire_scratch(16, 10),
        ],
        compiler_params=pltpu.CompilerParams(
            collective_id=1, has_side_effects=True, vmem_limit_bytes=VMEM_BYTES),
        name="middle",
    )(post, back, wgu, wd, resid, gains)


def rear_kernel(
    planes,
    order, rank, attn_in, query_in, key_in, value_in, q_unit_in, k_unit_in, roots_in, mixed_in, wo_in,
    normed_in, win_in, tokens_in, d_resid_in, cosine, sine, gains, y_out, y_keep_in, sums_in, ready, grad_rest,
    token_grad, sums, block_out, home_g, home_u, home_o, home_q, home_k, home_v,
    attn, query, key, value, q_unit, k_unit, roots, mixed, wo, win, tokens,
    rows_held, d_mixed, keys_grad, values_grad, y_in, grad_o, grad, part, sums_out, sums_came,
    g_came, g_sums, g_far, g_leave, g_arrive, o_came, o_sums, o_far,
    a_came, a_sums, a_far, a_leave, a_arrive, b_came, b_sums, b_far, b_leave, b_arrive,
    core_out, core_in, x_out, x_in, keep, core_s, core_r, x_s, x_r,
    out_sems, in_sems, own_sems,
):
    p = Place(planes)
    wire = Wire(out_sems, in_sems, own_sems)
    reducer = Reducer(p, part, core_out, core_in, x_out, x_in, keep, (core_s, core_r, x_s, x_r))
    rows = y_in.shape[1]
    length = 4 * rows
    loads = [wire.own(far, near) for far, near in (
        (attn_in, attn), (wo_in, wo), (mixed_in, mixed), (query_in, query), (key_in, key), (value_in, value),
        (q_unit_in, q_unit), (k_unit_in, k_unit), (roots_in, roots), (y_keep_in, keep),
        (tokens_in, tokens), (d_resid_in, token_grad))]
    for far, near, span in ((0, 0, 256), (256, 512, 256), (512, 256, 128), (640, 768, 128), (768, 384, 128), (896, 896, 128)):
        loads.append(wire.own(win_in.at[:, far : far + span], win.at[:, near : near + span]))
    p.meet()
    wide = ColumnHoming(p, wire, g_came, g_sums, g_far, g_leave, g_arrive,
                        [(home, 0, home.shape[1] // 4) for home in (home_g, home_u)])
    outer = RowHoming(p, wire, grad_o, o_came, o_sums, o_far, home_o)
    inner = [
        ColumnHoming(p, wire, *refs, [(home_q, 256 * at, 256), (home_k, 128 * at, 128), (home_v, 128 * at, 128)])
        for at, refs in enumerate((
            (a_came, a_sums, a_far, a_leave, a_arrive), (b_came, b_sums, b_far, b_leave, b_arrive)))
    ]
    wide.start(1, grad_rest.at[0])
    g_sums[0] = ready[0]
    wide.push(0)
    y_sent = [wire.send(y_out.at[micro], y_in.at[micro], p.x_dev) for micro in range(2)]
    loads[0].wait()
    loads[1].wait()

    def draw(step, carry):
        here = pl.ds(pl.multiple_of(step * BLOCK, BLOCK), BLOCK)
        low = two_runs(attn, order[step * 2], order[step * 2 + 1])
        rows_held[pl.ds(step * 2, 2)] = low.reshape(2, RUN, low.shape[1])
        d_mixed[here] = dot(low, wo[...], NARROW).astype(BF16)
        return carry

    lax.fori_loop(0, 2 * length // BLOCK, draw, 0)

    def out_tile(at, carry):
        cut = pl.ds(pl.multiple_of(at * BLOCK, BLOCK), BLOCK)
        found = dot(mixed[:, cut], flat(rows_held), TALL).astype(BF16)
        grad_o[pl.ds(at * (planes // 2), planes // 2)] = found.reshape(planes // 2, *grad_o.shape[1:])
        return carry

    loads[2].wait()
    lax.fori_loop(0, 2, out_tile, 0)
    wide.start(2, grad_rest.at[1])
    normed_load = wire.own(normed_in, attn)
    wide.add(1)
    wide.push(1)
    sums[...] = sums_in[...]

    def lane_of(ref, here, lane):
        held = ref[here, :]
        lanes = lax.broadcasted_iota(jnp.int32, held.shape, 1)
        return jnp.sum(jnp.where(lanes == lane, held, 0.0), axis=1, keepdims=True)

    def norm_home(grad, cos, sin, unit, root, gain):
        turned = grad * cos - pltpu.roll(grad, HEAD_DIM // 2, 1) * sin
        scaled = turned * gain
        back = root * (scaled - unit * row_mean(scaled * unit))
        return back, jnp.sum(turned * unit, axis=0, keepdims=True)

    def attend_back(step, carry):
        micro, head = lax.rem(step, 2), step // 2
        keys_at = pl.ds(pl.multiple_of(head * HEAD_DIM, HEAD_DIM), HEAD_DIM)
        lanes = [pl.ds(pl.multiple_of(head * 2 * HEAD_DIM + g * HEAD_DIM, HEAD_DIM), HEAD_DIM) for g in range(2)]
        q_gain, k_gain = gains[2:3, 0:RUN], gains[3:4, 0:RUN]
        keys_grad[...] = jnp.zeros_like(keys_grad)
        values_grad[...] = jnp.zeros_like(values_grad)
        for block in range(length // BLOCK):
            here = pl.ds(pl.multiple_of(micro * length + block * BLOCK, BLOCK), BLOCK)
            seen = (block + 1) * BLOCK
            past = pl.ds(pl.multiple_of(micro * length, BLOCK), seen)
            asked = jnp.concatenate([query[here, lane] for lane in lanes], axis=0)
            pulled = jnp.concatenate([d_mixed[here, lane] for lane in lanes], axis=0)
            given = jnp.concatenate([mixed[here, lane] for lane in lanes], axis=0)
            level = jnp.concatenate(
                [lane_of(roots, here, LEVEL + head * 2 + g) for g in range(2)], axis=0)
            delta = jnp.sum(pulled.astype(F32) * given.astype(F32), axis=1, keepdims=True)
            scores = dot(asked, key[past, keys_at], NARROW)
            line = lax.broadcasted_iota(jnp.int32, (2 * BLOCK, seen), 0)
            line = jnp.where(line >= BLOCK, line - BLOCK, line) + block * BLOCK
            column = lax.broadcasted_iota(jnp.int32, (2 * BLOCK, seen), 1)
            weight = jnp.exp2(scores * (SCALE * LOG2E) - level)
            weight = jnp.where(column <= line, weight, 0.0)
            d_soft = dot(pulled, value[past, keys_at], NARROW)
            d_scores = (weight * (d_soft - delta)).astype(BF16)
            values_grad[0:seen] += dot(weight.astype(BF16), pulled, TALL)
            keys_grad[0:seen] += dot(d_scores, asked, TALL)
            moved = dot(d_scores, key[past, keys_at]) * SCALE
            spin = slice(block * BLOCK, (block + 1) * BLOCK)
            for g, lane in enumerate(lanes):
                root = lane_of(roots, here, head * 2 + g)
                unit = q_unit[here, lane].astype(F32)
                back, gained = norm_home(
                    moved[g * BLOCK : (g + 1) * BLOCK], cosine[spin], sine[spin], unit, root, q_gain)
                pair = pl.ds(micro * (length // RUN) + block * 2, 2)
                to = pl.ds(pl.multiple_of(head * 512 + g * HEAD_DIM, HEAD_DIM), HEAD_DIM)
                rows_held[pair, :, to] = back.astype(BF16).reshape(2, RUN, HEAD_DIM)
                sums[1:2, 0:RUN] += gained
        everything = pl.ds(pl.multiple_of(micro * length, BLOCK), length)
        root = lane_of(roots, everything, head + 4)
        unit = k_unit[everything, keys_at].astype(F32)
        back, gained = norm_home(keys_grad[...] * SCALE, cosine[...], sine[...], unit, root, k_gain)
        at, whole = head * 512 + 256, pl.ds(micro * (length // RUN), length // RUN)
        tall = (length // RUN, RUN, HEAD_DIM)
        rows_held[whole, :, pl.ds(pl.multiple_of(at, HEAD_DIM), HEAD_DIM)] = back.astype(BF16).reshape(tall)
        sums[2:3, 0:RUN] += gained
        low = values_grad[...].astype(BF16).reshape(tall)
        rows_held[whole, :, pl.ds(pl.multiple_of(at + HEAD_DIM, HEAD_DIM), HEAD_DIM)] = low
        return carry

    for copy in loads[3:9]:
        copy.wait()
    def pull(step, carry):
        micro, block = reducer.block(step)
        at = micro * (length // RUN) + block * 2
        runs = (rank[at], rank[at + 1])
        found = dot(two_runs(rows_held, *runs), win[...], NARROW)
        part[...] = found
        sums[3:4] += jnp.sum(found * two_runs(attn, *runs).astype(F32), axis=0, keepdims=True)
        reducer.take(step)
        return carry

    def tile(half, at):
        pulled = joined(rows_held[:, :, half * 512 : half * 512 + 512])
        found = dot(joined(attn[:, :, group_rows(p, at)]), pulled, TALL).astype(BF16)
        grad[half, at] = found.reshape(grad.shape[2:])
        inner[half].start(at, grad.at[half, at])

    lax.fori_loop(0, 1, attend_back, 0)
    wide.start(3, grad_rest.at[2])
    wide.add(2)
    wide.push(2)
    lax.fori_loop(1, 2, attend_back, 0)
    normed_load.wait()
    for at in range(4):
        tile(0, at)
    wide.add(3)
    wide.push(3)
    wide.gather(0)
    for copy in loads[9:]:
        copy.wait()
    for micro in range(2):
        y_sent[micro].wait_recv()
        block_out[micro] = (keep[micro] + y_in[micro].astype(F32)).astype(BF16)
    lax.fori_loop(2, 3, attend_back, 0)
    outer.start()
    lax.fori_loop(0, 4, pull, 0)
    for at in range(4):
        inner[0].add(at)
        inner[0].push(at)
    wide.gather(1)
    lax.fori_loop(3, 4, attend_back, 0)
    tile(1, 0)
    tile(1, 1)
    outer.push(0)
    outer.push(1)
    tile(1, 2)
    tile(1, 3)
    lax.fori_loop(4, 8, pull, 0)
    sums[3:4] = sums[3:4] / gains[0:1]

    def exchange(stage, devices, base):
        sums_out[stage] = sums[...]
        sent = [wire.send(sums_out.at[stage], sums_came.at[base + at], dev) for at, dev in enumerate(devices)]
        return base, sent

    def absorb(state):
        base, sent = state
        total = sums[...]
        for at, copy in enumerate(sent):
            copy.wait_recv()
            total = total + sums_came[base + at]
        sums[...] = total

    state = exchange(0, p.seq_dev[1:], 0)
    wide.gather(2)
    wide.gather(3)
    inner[1].add(0)
    inner[1].push(0)
    absorb(state)
    state = exchange(1, [p.z_dev(step) for step in range(1, planes)], 3)
    inner[1].add(1)
    inner[1].push(1)
    for at in range(4):
        inner[0].gather(at)
    inner[1].add(2)
    inner[1].push(2)
    absorb(state)
    state = exchange(2, [p.y_dev], 2 + planes)
    inner[1].add(3)
    inner[1].push(3)
    outer.gather()
    for micro in range(2):
        grad_rows = reducer.total(micro)
        raw = tokens[micro].astype(F32)
        root = lax.rsqrt(row_mean(raw * raw) + EPSILON)
        unit = raw * root
        scaled = grad_rows * gains[0:1]
        token_grad[micro] = token_grad[micro] + root * (scaled - unit * row_mean(scaled * unit))
    wide.finish()
    inner[0].finish()
    absorb(state)
    for at in range(4):
        inner[1].gather(at)
    inner[1].finish()
    reducer.close()
    wire.close()


def rear(planes, order, rank, attn, query, key, value, q_unit, k_unit, roots, mixed, wo, normed, win, tokens, d_resid,
         cosine, sine, gains, y_out, y_keep, sums, ready, grad_rest):
    rows = y_keep.shape[1]
    length = 4 * rows
    total = 2 * length
    deep, wide = grad_rest.shape[3:]
    slim = (planes, 2, 512 // (2 * planes), 1024)
    shapes = [
        jax.ShapeDtypeStruct((2, rows, 1024), F32), jax.ShapeDtypeStruct((8, 1024), F32),
        jax.ShapeDtypeStruct((2, rows, 1024), BF16),
        jax.ShapeDtypeStruct((deep, 2 * wide), F32), jax.ShapeDtypeStruct((deep, 2 * wide), F32),
        jax.ShapeDtypeStruct(slim[2:], F32), jax.ShapeDtypeStruct((deep, 2048), F32),
        jax.ShapeDtypeStruct((deep, 1024), F32), jax.ShapeDtypeStruct((deep, 1024), F32),
    ]
    held = (attn, query, key, value, q_unit, k_unit, roots, mixed, wo, win, tokens)
    vm = pl.BlockSpec(memory_space=VMEM)
    hb = pl.BlockSpec(memory_space=ANY)
    sm = pl.BlockSpec(memory_space=pltpu.SMEM)
    return pl.pallas_call(
        functools.partial(rear_kernel, planes),
        out_shape=shapes,
        in_specs=[sm, sm] + [hb] * 13 + [vm] * 3 + [hb, hb, vm, vm, hb],
        out_specs=[vm] * len(shapes),
        scratch_shapes=[
            *[VMEM(item.shape, item.dtype) for item in held],
            VMEM((total // RUN, RUN, 1024), BF16), VMEM((total, 512), BF16), VMEM((length, HEAD_DIM), F32),
            VMEM((length, HEAD_DIM), F32), VMEM((2, rows, 1024), BF16), VMEM(slim, BF16),
            VMEM((2, 4, planes, 2, deep, 512), BF16), VMEM((BLOCK, 1024), F32), VMEM((3, 8, 1024), F32),
            VMEM((3 + planes, 8, 1024), F32),
            *column_scratch(planes, deep, wide), *row_scratch(planes, *slim[2:]),
            *column_scratch(planes, deep, 512), *column_scratch(planes, deep, 512),
            *reducer_scratch(1024), *wire_scratch(96, 56),
        ],
        compiler_params=pltpu.CompilerParams(
            collective_id=2, has_side_effects=True, vmem_limit_bytes=VMEM_BYTES),
        name="rear",
    )(order, rank, attn, query, key, value, q_unit, k_unit, roots, mixed, wo, normed, win, tokens, d_resid,
      cosine, sine, gains, y_out, y_keep, sums, ready, grad_rest)


def deliver_kernel(count, planes, sums, *refs):
    given, rest = refs[:count], refs[count:]
    made, small, held, sems = rest[:count], rest[count : count + 4], rest[count + 4 : 2 * count + 4], rest[-1]
    came = [pltpu.make_async_copy(src, mid, sems.at[0, at]) for at, (src, mid) in enumerate(zip(given, held))]
    gone = [pltpu.make_async_copy(mid, dst, sems.at[1, at]) for at, (mid, dst) in enumerate(zip(held, made))]
    for copy in came:
        copy.start()
    me = lax.axis_index("seq") * (2 * planes) + lax.axis_index("fsdp")
    table = sums[...]
    for row, out in zip((3, 0, 1, 2), small):
        width = out.shape[1]
        turned = pltpu.roll(table, table.shape[1] - me * width, 1)
        out[...] = turned[row : row + 1, :width]
    for first, second in zip(came, gone):
        first.wait()
        second.start()
    for copy in gone:
        copy.wait()


def deliver(planes, sums, widths, *items):
    count = len(items)
    vm, hb = pl.BlockSpec(memory_space=VMEM), pl.BlockSpec(memory_space=ANY)
    return pl.pallas_call(
        functools.partial(deliver_kernel, count, planes),
        out_shape=[*[jax.ShapeDtypeStruct(item.shape, item.dtype) for item in items],
                   *[jax.ShapeDtypeStruct((1, width), F32) for width in widths]],
        in_specs=[vm] + [hb] * count,
        out_specs=[hb] * count + [vm] * 4,
        scratch_shapes=[*[VMEM(item.shape, item.dtype) for item in items], pltpu.SemaphoreType.DMA((2, count))],
        compiler_params=pltpu.CompilerParams(vmem_limit_bytes=VMEM_BYTES),
        name="deliver",
    )(sums, *items)


def run_tables(positions):
    runs = positions.shape[1] // RUN
    rank = positions[:, ::RUN] // RUN
    index = jnp.arange(runs, dtype=jnp.int32)
    order = jnp.sum(jnp.where(rank[:, :, None] == index, index[None, :, None], 0), axis=1)
    base = jnp.arange(positions.shape[0], dtype=jnp.int32)[:, None] * runs
    return (order + base).reshape(-1), (rank + base).reshape(-1)


def turn_tables(length):
    half = HEAD_DIM // 2
    frequency = (ROPE_BASE ** (-np.arange(half) * 2.0 / HEAD_DIM)).astype(np.float32)
    angles = (np.arange(length, dtype=np.float32)[:, None] * frequency[None, :]).astype(np.float64)
    cosine, sine = np.cos(angles), np.sin(angles)
    return (jnp.asarray(np.concatenate([cosine, cosine], axis=1).astype(np.float32)),
            jnp.asarray(np.concatenate([-sine, sine], axis=1).astype(np.float32)))


def kernel_body(tokens, positions, g_in, g_post, g_query, g_key, w_query, w_key, w_value,
                w_out, w_gate, w_up, w_down, cotangent):
    planes = lax.axis_size("fsdp") // 2
    length = positions.shape[2]
    order, rank = run_tables(positions[:, 0])
    tile = jnp.stack(
        [jnp.pad(item.astype(F32), (0, RUN - item.shape[0])) for item in (g_in, g_post, g_query, g_key)])
    tile = jnp.pad(tile, ((0, 4), (0, 0)))
    cosine, sine = turn_tables(length)
    near = tokens[:, 0]
    shards = (w_query, w_key, w_value, w_out, w_gate, w_up, w_down)
    (win, wo, wgu, wd, normed, query, key, value, q_unit, k_unit, roots, mixed,
     resid, post, back, gains) = front(
        planes, order, rank, near, cotangent[:, 0], tile, cosine, sine, shards)
    plain = lambda item: item.reshape(-1, item.shape[-1])
    apart = lambda item: item.reshape(-1, RUN, item.shape[-1])
    win, wo, wgu, wd, post, back = [plain(item) for item in (win, wo, wgu, wd, post, back)]
    ready, grad_rest, home_d, y_out, y_keep, d_resid, attn, sums = middle(
        planes, post, back, wgu, wd, resid, gains)
    token_grad, sums, block_out, home_g, home_u, home_o, home_q, home_k, home_v = rear(
        planes, order, rank, apart(attn), query, key, value, q_unit, k_unit, roots, plain(mixed), wo,
        apart(normed), win, near, d_resid, cosine, sine, gains, y_out, y_keep, sums, ready, grad_rest)
    widths = [item.shape[0] for item in (g_in, g_post, g_query, g_key)]
    found = deliver(planes, sums, widths, token_grad, block_out, home_d, home_g, home_u, home_o, home_q, home_k, home_v)
    token_grad, block_out, home_d, home_g, home_u, home_o, home_q, home_k, home_v = found[:9]
    small = [item[0] for item in found[9:]]
    return (block_out[:, None], token_grad[:, None], *small, home_q, home_k, home_v, home_o,
            home_g, home_u, home_d)


def solution(mesh):
    both = ("seq", "fsdp")
    act = P(None, "fsdp", "seq", None)
    vec, mat = P(both), P(both, None)

    def body(*args):
        rows = args[6].shape[0]
        fits = mesh.shape["seq"] == 4 and mesh.shape["fsdp"] % 2 == 0 and rows % 16 == 0
        return (kernel_body if fits else plain_body)(*args)

    return jax.shard_map(
        body,
        mesh=mesh,
        in_specs=(act, P(None, "fsdp", None), *[vec] * 4, *[mat] * 7, act),
        out_specs=(act, act, *[vec] * 4, *[mat] * 7),
        check_vma=False,
    )
```

```python
import functools

import jax
import jax.numpy as jnp
import numpy as np
from jax import lax
from jax.experimental import pallas as pl
from jax.experimental.pallas import tpu as pltpu
from jax.sharding import PartitionSpec as P

HEADS = 16
KV_HEADS = 8
HEAD_DIM = 128
EPSILON = 1e-06
ROPE_BASE = 1000000.0
NEGATIVE = -1e30
F32 = jnp.float32
BF16 = jnp.bfloat16


def inverse_root(values):
    return lax.rsqrt(jnp.mean(values * values, axis=-1, keepdims=True) + EPSILON)


def rope_tables(token_pos):
    half_width = HEAD_DIM // 2
    frequency = ROPE_BASE ** (-(jnp.arange(half_width, dtype=F32) * 2.0 / HEAD_DIM))
    angles = token_pos.astype(F32)[:, None] * frequency[None, :]
    cosine = jnp.cos(angles)
    sine = jnp.sin(angles)
    return (
        jnp.concatenate([cosine, cosine], axis=-1)[:, None, :],
        jnp.concatenate([sine, sine], axis=-1)[:, None, :],
    )


def rotate(values, cosine, sine):
    half_width = values.shape[-1] // 2
    turned = jnp.concatenate([-values[..., half_width:], values[..., :half_width]], axis=-1)
    return values * cosine + turned * sine


def rotate_back(grads, cosine, sine):
    half_width = grads.shape[-1] // 2
    scaled = grads * sine
    turned = jnp.concatenate([scaled[..., half_width:], -scaled[..., :half_width]], axis=-1)
    return grads * cosine + turned


def norm_back(grads, values, inverse, gain):
    scaled = grads * gain
    return inverse * scaled - values * inverse**3 * jnp.mean(
        scaled * values, axis=-1, keepdims=True
    )


def mul(eq, left, right):
    return jnp.einsum(eq, left, right, preferred_element_type=F32)


def sum_scatter(part, axis):
    return lax.psum_scatter(part.astype(BF16), axis, scatter_dimension=0, tiled=True).astype(F32)


def slice_weights(item, ways):
    rows = item.shape[0]
    return item.reshape(rows, ways, -1).transpose(1, 0, 2)


def plain_body(tokens, positions, g_in, g_post, g_query, g_key, w_query, w_key, w_value,
               w_out, w_gate, w_up, w_down, cotangent):
    ways = lax.axis_size("seq")
    heads, kv_heads = HEADS // ways, KV_HEADS // ways
    micro, rows, width = tokens.shape[0], tokens.shape[2], tokens.shape[3]
    length = positions.shape[2]
    everyone = ("seq", "fsdp")
    gains = [
        lax.all_gather(item, everyone, axis=0, tiled=True).astype(F32)
        for item in (g_in, g_post, g_query, g_key)
    ]
    gain_in, gain_post, gain_query, gain_key = gains

    def spread(*items):
        packed = jnp.concatenate([slice_weights(item, ways) for item in items], axis=2)
        packed = lax.all_to_all(packed, "seq", 0, 0, tiled=True)
        packed = lax.all_gather(packed, "fsdp", axis=1, tiled=True)
        packed = packed.reshape(-1, packed.shape[2])
        sizes = [item.shape[1] // ways for item in items]
        cuts = [sum(sizes[: at + 1]) for at in range(len(sizes) - 1)]
        return jnp.split(packed, cuts, axis=1)

    wq, wk, wv = spread(w_query, w_key, w_value)
    wo = lax.all_gather(w_out, "fsdp", axis=0, tiled=True)
    wg, wu = spread(w_gate, w_up)
    wd = lax.all_gather(w_down, "fsdp", axis=0, tiled=True)
    scale = HEAD_DIM ** (-0.5)

    def gather_rows(item):
        return lax.all_gather(item, "seq", axis=0, tiled=True)

    grads = None
    outs, token_grads = [], []
    for at in range(micro):
        inputs = tokens[at, 0].astype(F32)
        pos = positions[at, 0]
        cosine, sine = rope_tables(pos)
        allowed = pos[None, :] <= pos[:, None]
        inv_in = inverse_root(inputs)
        normed = gather_rows((inputs * inv_in * gain_in).astype(BF16))
        q_raw = mul("td,df->tf", normed, wq).reshape(length, heads, HEAD_DIM)
        k_raw = mul("td,df->tf", normed, wk).reshape(length, kv_heads, HEAD_DIM)
        value = mul("td,df->tf", normed, wv).astype(BF16).reshape(length, kv_heads, HEAD_DIM)
        inv_q, inv_k = inverse_root(q_raw), inverse_root(k_raw)
        query = rotate(q_raw * inv_q * gain_query, cosine, sine).astype(BF16)
        query = query.reshape(length, kv_heads, heads // kv_heads, HEAD_DIM)
        key = rotate(k_raw * inv_k * gain_key, cosine, sine).astype(BF16)
        scores = jnp.where(allowed, mul("qjgd,kjd->jgqk", query, key) * scale, NEGATIVE)
        soft = jax.nn.softmax(scores, axis=-1)
        soft_low = soft.astype(BF16)
        mixed = mul("jgqk,kjd->qjgd", soft_low, value).astype(BF16).reshape(length, -1)
        resid = inputs + sum_scatter(mul("th,hd->td", mixed, wo), "seq")
        inv_post = inverse_root(resid)
        post = gather_rows((resid * inv_post * gain_post).astype(BF16))
        gate = mul("td,df->tf", post, wg)
        upper = mul("td,df->tf", post, wu)
        sigma = jax.nn.sigmoid(gate)
        hidden = (gate * sigma * upper).astype(BF16)
        outs.append((resid + sum_scatter(mul("tf,fd->td", hidden, wd), "seq")).astype(BF16))
        back_low = cotangent[at, 0]
        back = gather_rows(back_low)
        g_down = mul("tf,td->fd", hidden, back)
        d_hidden = mul("td,fd->tf", back, wd)
        d_gate = (d_hidden * upper * sigma * (1.0 + gate * (1.0 - sigma))).astype(BF16)
        d_upper = (d_hidden * gate * sigma).astype(BF16)
        g_gate = mul("td,tf->df", post, d_gate)
        g_up = mul("td,tf->df", post, d_upper)
        d_post = sum_scatter(mul("tf,df->td", d_gate, wg) + mul("tf,df->td", d_upper, wu), "seq")
        post_grad = jnp.sum(d_post * resid * inv_post, axis=0)
        d_resid = back_low.astype(F32) + norm_back(d_post, resid, inv_post, gain_post)
        d_attn = gather_rows(d_resid.astype(BF16))
        g_out = mul("th,td->hd", mixed, d_attn)
        d_mixed = mul("td,hd->th", d_attn, wo).astype(BF16)
        d_mixed = d_mixed.reshape(length, kv_heads, heads // kv_heads, HEAD_DIM)
        d_soft = mul("qjgd,kjd->jgqk", d_mixed, value)
        d_scores = (soft * (d_soft - jnp.sum(d_soft * soft, axis=-1, keepdims=True))).astype(BF16)
        d_query = mul("jgqk,kjd->qjgd", d_scores, key) * scale
        d_key = mul("jgqk,qjgd->kjd", d_scores, query) * scale
        d_value = mul("jgqk,qjgd->kjd", soft_low, d_mixed).astype(BF16).reshape(length, -1)
        key_turn = rotate_back(d_key, cosine, sine)
        query_turn = rotate_back(d_query.reshape(length, heads, HEAD_DIM), cosine, sine)
        key_grad = jnp.sum(key_turn * k_raw * inv_k, axis=(0, 1))
        query_grad = jnp.sum(query_turn * q_raw * inv_q, axis=(0, 1))
        d_key = norm_back(key_turn, k_raw, inv_k, gain_key).astype(BF16).reshape(length, -1)
        d_query = norm_back(query_turn, q_raw, inv_q, gain_query).astype(BF16).reshape(length, -1)
        g_query_w = mul("td,tf->df", normed, d_query)
        g_key_w = mul("td,tf->df", normed, d_key)
        g_value_w = mul("td,tf->df", normed, d_value)
        d_normed = mul("tf,df->td", d_query, wq) + mul("tf,df->td", d_key, wk)
        d_normed = sum_scatter(d_normed + mul("tf,df->td", d_value, wv), "seq")
        in_grad = jnp.sum(d_normed * inputs * inv_in, axis=0)
        token_grads.append(d_resid + norm_back(d_normed, inputs, inv_in, gain_in))
        found = [in_grad, post_grad, query_grad, key_grad, g_query_w, g_key_w, g_value_w,
                 g_out, g_gate, g_up, g_down]
        grads = found if grads is None else [left + right for left, right in zip(grads, found)]

    small = [lax.psum_scatter(item, everyone, scatter_dimension=0, tiled=True) for item in grads[:4]]

    def columns_home(item):
        full, wide = item.shape
        item = item.reshape(ways, -1, wide).astype(BF16)
        item = lax.psum_scatter(item, "fsdp", scatter_dimension=1, tiled=True)
        item = lax.all_to_all(item, "seq", 0, 0, tiled=True)
        return item.transpose(1, 0, 2).reshape(item.shape[1], ways * wide).astype(F32)

    def rows_home(item):
        return sum_scatter(item, "fsdp")

    large = [columns_home(item) for item in grads[4:7]] + [rows_home(grads[7])]
    large += [columns_home(item) for item in grads[8:10]] + [rows_home(grads[10])]
    return (jnp.stack(outs)[:, None], jnp.stack(token_grads)[:, None], *small, *large)


MESH = pl.DeviceIdType.MESH
ANY = pl.ANY
VMEM = pltpu.VMEM
RUN = 128
BLOCK = 256
NARROW = (((1,), (1,)), ((), ()))
TALL = (((0,), (0,)), ((), ()))
PLAIN = (((1,), (0,)), ((), ()))
LOG2E = 1.4426950408889634
SCALE = HEAD_DIM ** (-0.5)
LEVEL = 8
VMEM_BYTES = 63 * 2**20


def dot(left, right, dims=PLAIN):
    return lax.dot_general(left, right, dims, preferred_element_type=F32)


class Place:
    def __init__(self, planes):
        self.planes = planes
        self.s = lax.axis_index("seq")
        self.f = lax.axis_index("fsdp")
        self.x, self.c = self.s // 2, self.s % 2
        self.z, self.y = self.f // 2, self.f % 2
        self.other_y = 1 - self.y
        self.core_dev = (self.x * 2 + 1 - self.c, self.f)
        self.x_dev = ((1 - self.x) * 2 + self.c, self.f)
        self.far_dev = ((1 - self.x) * 2 + 1 - self.c, self.f)
        self.y_dev = (self.s, self.z * 2 + self.other_y)
        self.seq_dev = [(self.s, self.f), self.core_dev, self.x_dev, self.far_dev]

    def z_at(self, step):
        return lax.rem(self.z + step, self.planes)

    def z_dev(self, step):
        return (self.s, self.z_at(step) * 2 + self.y)

    def peers(self):
        return [self.core_dev, self.x_dev, self.far_dev, self.y_dev] + [
            self.z_dev(step) for step in range(1, self.planes)
        ]

    def meet(self):
        barrier = pltpu.get_barrier_semaphore()
        for peer in self.peers():
            pl.semaphore_signal(barrier, inc=1, device_id=peer, device_id_type=MESH)
        pl.semaphore_wait(barrier, 3 + self.planes)


def remote(src, dst, out_sem, in_sem, device):
    return pltpu.make_async_remote_copy(
        src_ref=src, dst_ref=dst, send_sem=out_sem, recv_sem=in_sem,
        device_id=device, device_id_type=MESH,
    )


class Wire:
    def __init__(self, out_sems, in_sems, own_sems):
        self.out_sems, self.in_sems, self.own_sems = out_sems, in_sems, own_sems
        self.sent, self.owned = [], 0

    def send(self, src, dst, device, start=True):
        at = len(self.sent)
        copy = remote(src, dst, self.out_sems.at[at], self.in_sems.at[at], device)
        if start:
            copy.start()
        self.sent.append(copy)
        return copy

    def own(self, src, dst):
        copy = pltpu.make_async_copy(src, dst, self.own_sems.at[self.owned])
        copy.start()
        self.owned += 1
        return copy

    def close(self):
        for copy in self.sent:
            copy.wait_send()


def wire_scratch(copies, owns):
    return [
        pltpu.SemaphoreType.DMA((copies,)),
        pltpu.SemaphoreType.DMA((copies,)),
        pltpu.SemaphoreType.DMA((owns,)),
    ]


class Reducer:
    def __init__(self, place, part, core_out, core_in, x_out, x_in, keep, sems):
        self.place, self.part = place, part
        self.core_out, self.core_in = core_out, core_in
        self.x_out, self.x_in, self.keep = x_out, x_in, keep
        self.core_s, self.core_r, self.x_s, self.x_r = sems

    def block(self, step):
        p = self.place
        turn = step % 4
        x = jnp.where(turn < 2, 1 - p.x, p.x)
        c = jnp.where(turn % 2 == 0, 1 - p.c, p.c)
        return step // 4, x * 2 + c

    def core_copy(self, slot):
        return remote(self.core_out.at[slot], self.core_in.at[slot], self.core_s.at[slot],
                      self.core_r.at[slot], self.place.core_dev)

    def x_copy(self, micro):
        return remote(self.x_out.at[micro], self.x_in.at[micro], self.x_s.at[micro],
                      self.x_r.at[micro], self.place.x_dev)

    def take(self, step, send_x=True):
        micro, turn = step // 4, step % 4

        @pl.when(turn % 2 == 0)
        def _():
            slot = micro * 2 + turn // 2
            self.core_out[slot] = self.part[...].astype(BF16)
            self.core_copy(slot).start()

        @pl.when(turn == 1)
        def _():
            slot = micro * 2
            self.core_copy(slot).wait_recv()
            self.x_out[micro] = (self.part[...] + self.core_in[slot].astype(F32)).astype(BF16)
            if send_x:
                self.x_copy(micro).start()

        @pl.when(turn == 3)
        def _():
            slot = micro * 2 + 1
            self.core_copy(slot).wait_recv()
            self.keep[micro] = self.part[...] + self.core_in[slot].astype(F32)

    def total(self, micro):
        self.x_copy(micro).wait_recv()
        return self.keep[micro] + self.x_in[micro].astype(F32)

    def close(self, send_x=True):
        for slot in range(4):
            self.core_copy(slot).wait_send()
        if send_x:
            for micro in range(2):
                self.x_copy(micro).wait_send()


def reducer_scratch(width):
    return [
        VMEM((4, BLOCK, width), BF16),
        VMEM((4, BLOCK, width), BF16),
        VMEM((2, BLOCK, width), BF16),
        VMEM((2, BLOCK, width), BF16),
        VMEM((2, BLOCK, width), F32),
        pltpu.SemaphoreType.DMA((4,)),
        pltpu.SemaphoreType.DMA((4,)),
        pltpu.SemaphoreType.DMA((2,)),
        pltpu.SemaphoreType.DMA((2,)),
    ]


def row_mean(values):
    return jnp.mean(values, axis=-1, keepdims=True)


def spread_gain(table, row, devices, width):
    per = width // devices
    lanes = lax.broadcasted_iota(jnp.int32, (RUN, width), 0)
    column = lax.broadcasted_iota(jnp.int32, (RUN, width), 1)
    pick = (lanes == lax.rem(column, per)).astype(BF16)
    picked = dot(table, pick)
    rows = lax.broadcasted_iota(jnp.int32, (devices * 8, width), 0)
    owner = lax.broadcasted_iota(jnp.int32, (devices * 8, width), 1) // per
    return jnp.sum(jnp.where(rows == owner * 8 + row, picked, 0.0), axis=0, keepdims=True)


def two_runs(ref, first, second):
    return jnp.concatenate([ref[first], ref[second]], axis=0)


def joined(value):
    return value.reshape(-1, value.shape[-1])


def flat(ref):
    return joined(ref[...])


def front_kernel(
    planes,
    order, rank, tokens, cotangent, gain_tile, cosine_in, sine_in,
    s_q, s_k, s_v, s_o, s_g, s_u, s_d,
    win_out, wo_out, wgu, wd,
    normed_out, query_out, key_out, value_out, q_unit_out, k_unit_out, roots_out, mixed_out,
    resid_out, post_full, back_full, gains,
    win, wo, normed, query, key, value, q_unit, k_unit, roots, mixed, resid,
    tok_full, gain_all, post_own, back_own, cosine, sine, part,
    core_out, core_in, x_out, x_in, keep, core_s, core_r, x_s, x_r,
    out_sems, in_sems, own_sems,
):
    p = Place(planes)
    s, f = p.s, p.f
    devices = 8 * planes
    wire = Wire(out_sems, in_sems, own_sems)
    reducer = Reducer(p, part, core_out, core_in, x_out, x_in, keep, (core_s, core_r, x_s, x_r))
    rows = BLOCK
    mine = pl.ds(s * rows, rows)
    theirs = pl.ds(p.x_dev[0] * rows, rows)
    length = 4 * rows
    runs = length // RUN
    p.meet()

    def spread_columns(items, full):
        came = [[] for _ in range(4)]
        for at in (0, 2, 3, 1):
            first = 0
            for item in items:
                wide = item.shape[1] // 4
                src = item.at[:, pl.ds(pl.multiple_of(p.seq_dev[at][0] * wide, RUN), wide)]
                dst = full.at[s, f, :, pl.ds(first, wide)]
                came[at].append(wire.send(src, dst, p.seq_dev[at]) if at else wire.own(src, dst))
                first += wide
        return came

    def arrived(copies, at):
        for copy in copies[at]:
            copy.wait_recv() if at else copy.wait()

    def side(here):
        return [wire.send(here, here, p.y_dev)]

    def push(here):
        return [wire.send(here, here, p.z_dev(step)) for step in range(1, planes)]

    def forward(view, far, near):
        for step, copy in enumerate(far, 1):
            copy.wait_recv()
            near += side(view(p.z_at(planes - step) * 2 + p.y))

    def settle(near):
        for copy in near:
            copy.wait_recv()

    gain_all[s, f] = gain_tile[...]
    gain_in = [wire.send(gain_all.at[s, f], gain_all.at[s, f], dev) for dev in p.seq_dev[1:]]
    first = spread_columns((s_q, s_k, s_v), win)
    out_near = [wire.send(s_o, wo.at[f], p.y_dev)]
    down_near = [wire.send(s_d, wd.at[f], p.y_dev)]
    tok_here, tok_x, tok_core = [], [], []
    for micro in range(2):
        to = tok_full.at[pl.ds(micro * runs + s * 2, 2)]
        tok_here.append(wire.own(tokens.at[micro], to))
        tok_core.append(wire.send(tokens.at[micro], to, p.core_dev))
    out_kept = wire.own(s_o, wo.at[f])
    down_kept = wire.own(s_d, wd.at[f])
    staged = [wire.own(cosine_in, cosine), wire.own(sine_in, sine), wire.own(cotangent, back_own)]

    def in_view(at):
        return lambda owner: win.at[p.seq_dev[at][0], owner]

    def wide_view(at):
        return lambda owner: wgu.at[p.seq_dev[at][0], owner]

    in_far, in_near, wide_far, wide_near = {}, [], {}, []
    arrived(first, 0)
    in_far[0] = push(in_view(0)(f))
    in_near += side(in_view(0)(f))
    for copy in gain_in:
        copy.wait_recv()
    gain_far = push(gain_all.at[:, f])
    gain_near = side(gain_all.at[:, f])
    for at in (1, 2, 3):
        arrived(first, at)
        in_near += side(in_view(at)(f))
        if at == 1:
            in_far[1] = push(in_view(1)(f))
    for micro in range(2):
        to = tok_full.at[pl.ds(micro * runs + s * 2, 2)]
        tok_x.append(wire.send(tokens.at[micro], to, p.x_dev))
    second = spread_columns((s_g, s_u), wgu)
    forward(lambda owner: gain_all.at[:, owner], gain_far, gain_near)
    forward(in_view(0), in_far[0], in_near)
    in_far[2] = push(in_view(2)(f))
    forward(in_view(1), in_far[1], in_near)
    in_far[3] = push(in_view(3)(f))
    settle(gain_near)
    table = gain_all[...].reshape(devices * 8, RUN).astype(BF16)
    gain_first = spread_gain(table, 0, devices, 1024)
    gain_post = spread_gain(table, 1, devices, 1024)
    gain_query = spread_gain(table, 2, devices, RUN)
    gain_key = spread_gain(table, 3, devices, RUN)
    gains[...] = jnp.zeros_like(gains)
    gains[0:1] = gain_first
    gains[1:2] = gain_post
    gains[2:3, 0:RUN] = gain_query
    gains[3:4, 0:RUN] = gain_key
    forward(in_view(2), in_far[2], in_near)
    out_far = [wire.send(s_o, wo.at[f], p.z_dev(step)) for step in range(1, planes)]
    back_x = [wire.send(cotangent.at[0], back_full.at[0, mine], p.x_dev)]
    forward(in_view(3), in_far[3], in_near)
    tok_fwd = []
    for micro in range(2):
        tok_x[micro].wait_recv()
        block = tok_full.at[pl.ds(micro * runs + p.x_dev[0] * 2, 2)]
        tok_fwd.append(wire.send(block, block, p.core_dev))
    for at in range(4):
        arrived(second, at)
        wide_near += side(wide_view(at)(f))
    for copy in staged:
        copy.wait()
    back_core, back_kept = [], []
    for micro in range(2):
        to = back_full.at[micro, mine]
        if micro == 1:
            back_x.append(wire.send(cotangent.at[micro], to, p.x_dev))
        back_kept.append(wire.own(back_own.at[micro], to))
        back_core.append(wire.send(cotangent.at[micro], to, p.core_dev))
    wide_far[0] = push(wide_view(0)(f))
    down_far = [wire.send(s_d, wd.at[f], p.z_dev(step)) for step in range(1, planes)]
    settle(in_near)
    saved = [wire.own(win, win_out)]
    for copy in tok_here:
        copy.wait()
    for copy in tok_core + tok_fwd:
        copy.wait_recv()

    def project(step, carry):
        here = pl.ds(pl.multiple_of(step * BLOCK, BLOCK), BLOCK)
        raw = two_runs(tok_full, order[step * 2], order[step * 2 + 1]).astype(F32)
        root = lax.rsqrt(row_mean(raw * raw) + EPSILON)
        low = (raw * root * gains[0:1]).astype(BF16)
        normed[here] = low
        turn = pl.ds(pl.multiple_of(lax.rem(step, length // BLOCK) * BLOCK, BLOCK), BLOCK)
        cos, sin = cosine[turn], sine[turn]
        product = dot(low, flat(win))
        found, start = [], 0
        for low_ref, unit_ref, row in ((query, q_unit, 2), (key, k_unit, 3)):
            gain = gains[row : row + 1, 0:RUN]
            for head in range(low_ref.shape[1] // HEAD_DIM):
                at = slice(head * HEAD_DIM, (head + 1) * HEAD_DIM)
                one = product[:, start : start + HEAD_DIM]
                inverse = lax.rsqrt(row_mean(one * one) + EPSILON)
                unit = one * inverse
                unit_ref[here, at] = unit.astype(BF16)
                scaled = unit * gain
                low_ref[here, at] = (scaled * cos + pltpu.roll(scaled, HEAD_DIM // 2, 1) * sin).astype(BF16)
                found.append(inverse)
                start += HEAD_DIM
        roots[here, :] = jnp.zeros((BLOCK, roots.shape[1]), F32)
        for at, inverse in enumerate(found):
            roots[here, at : at + 1] = inverse
        value[here] = product[:, start:].astype(BF16)
        return carry

    def attend(step, carry):
        micro, head = step // 2, lax.rem(step, 2)
        keys_at = pl.ds(pl.multiple_of(head * HEAD_DIM, HEAD_DIM), HEAD_DIM)
        lanes = [pl.ds(pl.multiple_of(head * 2 * HEAD_DIM + g * HEAD_DIM, HEAD_DIM), HEAD_DIM) for g in range(2)]
        for block in range(length // BLOCK):
            here = pl.ds(pl.multiple_of(micro * length + block * BLOCK, BLOCK), BLOCK)
            seen = (block + 1) * BLOCK
            past = pl.ds(pl.multiple_of(micro * length, BLOCK), seen)
            asked = jnp.concatenate([query[here, lane] for lane in lanes], axis=0)
            scores = dot(asked, key[past, keys_at], NARROW)
            line = lax.broadcasted_iota(jnp.int32, (2 * BLOCK, seen), 0)
            line = jnp.where(line >= BLOCK, line - BLOCK, line) + block * BLOCK
            column = lax.broadcasted_iota(jnp.int32, (2 * BLOCK, seen), 1)
            scores = jnp.where(column <= line, scores, NEGATIVE)
            top = jnp.max(scores, axis=-1, keepdims=True)
            weight = jnp.exp2((scores - top) * (SCALE * LOG2E))
            total = jnp.sum(weight, axis=-1, keepdims=True)
            out = dot(weight.astype(BF16), value[past, keys_at]) * (1.0 / total)
            level = top * (SCALE * LOG2E) + jnp.log2(total)
            pair = pl.ds(micro * runs + block * 2, 2)
            held = roots[here, :]
            spot = lax.broadcasted_iota(jnp.int32, held.shape, 1)
            for g, lane in enumerate(lanes):
                half = slice(g * BLOCK, (g + 1) * BLOCK)
                mixed[pair, :, lane] = out[half].astype(BF16).reshape(2, RUN, HEAD_DIM)
                held = jnp.where(spot == LEVEL + head * 2 + g, level[half], held)
            roots[here, :] = held
        return carry

    def mix_out(step, carry):
        micro, block = reducer.block(step)
        at = micro * runs + block * 2
        low = two_runs(mixed, rank[at], rank[at + 1])
        part[...] = dot(low, flat(wo))
        reducer.take(step)
        return carry

    posts = []

    def finish(micro):
        own = joined(tok_full[pl.ds(micro * runs + s * 2, 2)]).astype(F32)
        total = own + reducer.total(micro)
        resid[micro] = total
        root = lax.rsqrt(row_mean(total * total) + EPSILON)
        post_own[micro] = (total * root * gains[1:2]).astype(BF16)
        to = post_full.at[micro, mine]
        posts.append((wire.send(post_own.at[micro], to, p.x_dev), wire.send(post_own.at[micro], to, p.core_dev),
                      wire.own(post_own.at[micro], to)))
        saved.append(wire.own(resid.at[micro], resid_out.at[micro]))

    steps = length // BLOCK
    lax.fori_loop(0, steps, project, 0)
    forward(lambda owner: wo.at[owner], out_far, out_near)
    wide_far[1] = push(wide_view(1)(f))
    lax.fori_loop(0, 2, attend, 0)
    lax.fori_loop(steps, 2 * steps, project, 0)
    saved += [wire.own(here, there) for here, there in (
        (normed, normed_out), (query, query_out), (key, key_out), (value, value_out),
        (q_unit, q_unit_out), (k_unit, k_unit_out))]
    out_kept.wait()
    settle(out_near)
    lax.fori_loop(0, 4, mix_out, 0)
    forward(wide_view(0), wide_far[0], wide_near)
    wide_far[2] = push(wide_view(2)(f))
    lax.fori_loop(2, 4, attend, 0)
    lax.fori_loop(4, 8, mix_out, 0)
    saved += [wire.own(mixed, mixed_out), wire.own(roots, roots_out), wire.own(wo, wo_out)]
    wide_far[3] = push(wide_view(3)(f))
    finish(0)
    forward(lambda owner: wd.at[owner], down_far, down_near)
    forward(wide_view(1), wide_far[1], wide_near)
    for micro in range(2):
        back_x[micro].wait_recv()
        block = back_full.at[micro, theirs]
        back_core.append(wire.send(block, block, p.core_dev))
    finish(1)
    forward(wide_view(2), wide_far[2], wide_near)
    forward(wide_view(3), wide_far[3], wide_near)
    last = []
    for micro in range(2):
        posts[micro][0].wait_recv()
        block = post_full.at[micro, theirs]
        last.append(wire.send(block, block, p.core_dev))
    for micro in range(2):
        last[micro].wait_recv()
        posts[micro][1].wait_recv()
        posts[micro][2].wait()
    for copy in back_core:
        copy.wait_recv()
    for copy in back_kept + saved + [down_kept]:
        copy.wait()
    settle(wide_near)
    settle(down_near)
    reducer.close()
    wire.close()


def front(planes, order, rank, tokens, cotangent, gain_tile, cosine, sine, shards):
    nf = 2 * planes
    rows = tokens.shape[1]
    length = 4 * rows
    total = 2 * length
    tokens = tokens.reshape(2, 2, RUN, tokens.shape[2])
    deep = shards[0].shape[0]

    def low(width):
        return jax.ShapeDtypeStruct((total, width), BF16)

    shapes = [
        jax.ShapeDtypeStruct((4, nf, deep, 1024), BF16), jax.ShapeDtypeStruct((nf, *shards[3].shape), BF16),
        jax.ShapeDtypeStruct((4, nf, deep, 2 * (shards[4].shape[1] // 4)), BF16),
        jax.ShapeDtypeStruct((nf, *shards[6].shape), BF16),
        low(1024), low(512), low(256), low(256), low(512), low(256),
        jax.ShapeDtypeStruct((total, 16), F32), jax.ShapeDtypeStruct((total // RUN, RUN, 512), BF16),
        jax.ShapeDtypeStruct((2, rows, 1024), F32),
        jax.ShapeDtypeStruct((2, length, 1024), BF16), jax.ShapeDtypeStruct((2, length, 1024), BF16),
        jax.ShapeDtypeStruct((8, 1024), F32)]
    held = [shapes[at] for at in (0, 1, *range(4, 13))]
    vm = pl.BlockSpec(memory_space=VMEM)
    hb = pl.BlockSpec(memory_space=ANY)
    sm = pl.BlockSpec(memory_space=pltpu.SMEM)
    return pl.pallas_call(
        functools.partial(front_kernel, planes),
        out_shape=shapes,
        in_specs=[sm, sm, hb, hb, vm, hb, hb, hb, hb, hb, hb, vm, vm, vm],
        out_specs=[hb] * (len(shapes) - 1) + [vm],
        scratch_shapes=[
            *[VMEM(item.shape, item.dtype) for item in held],
            VMEM((total // RUN, RUN, 1024), BF16), VMEM((4, nf, 8, RUN), F32), VMEM((2, rows, 1024), BF16),
            VMEM((2, rows, 1024), BF16), VMEM(cosine.shape, F32), VMEM(sine.shape, F32),
            VMEM((BLOCK, 1024), F32), *reducer_scratch(1024), *wire_scratch(130, 40),
        ],
        compiler_params=pltpu.CompilerParams(
            collective_id=0, has_side_effects=True, vmem_limit_bytes=VMEM_BYTES),
        name="front",
    )(order, rank, tokens, cotangent, gain_tile, cosine, sine, *shards)


GROUPS = (2, 3, 1, 0)


class RowHoming:
    def __init__(self, place, wire, grad, came, sums, far, home):
        self.p, self.wire, self.grad = place, wire, grad
        self.came, self.sums, self.far, self.home = came, sums, far, home

    def half(self, ref, at):
        return ref.at[pl.ds(at * (self.p.planes // 2), self.p.planes // 2)]

    def start(self):
        p = self.p
        self.kept = self.wire.own(self.grad.at[:, p.y], self.sums)
        self.sent = [
            self.wire.send(self.half(self.grad, at).at[:, p.other_y], self.half(self.came, at), p.y_dev)
            for at in range(2)
        ]
        self.out = [
            self.wire.send(self.sums.at[p.z_at(step)], self.far.at[step - 1], p.z_dev(step), start=False)
            for step in range(1, p.planes)
        ]

    def push(self, at):
        if at == 0:
            self.kept.wait()
        self.sent[at].wait_recv()
        share = self.p.planes // 2

        def add(z, carry):
            self.sums[z] = (self.sums[z].astype(F32) + self.came[z].astype(F32)).astype(BF16)
            return carry

        lax.fori_loop(at * share, (at + 1) * share, add, 0)
        for step, copy in enumerate(self.out, 1):
            @pl.when(self.p.z_at(step) // share == at)
            def _(copy=copy):
                copy.start()

    def gather(self):
        for copy in self.out:
            copy.wait_recv()
        total = self.sums[self.p.z].astype(F32)
        for step in range(1, self.p.planes):
            total = total + self.far[step - 1].astype(F32)
        self.home[...] = total


class ColumnHoming:
    def __init__(self, place, wire, came, sums, far, leave=None, arrive=None, homes=()):
        self.p, self.wire, self.came, self.sums, self.far = place, wire, came, sums, far
        self.leave, self.arrive, self.homes = leave, arrive, homes
        self.kept, self.sent, self.out, self.back = {}, {}, {}, {}

    def start(self, at, grad):
        self.kept[at] = self.wire.own(grad.at[:, self.p.y], self.sums.at[at])
        self.sent[at] = self.wire.send(grad.at[:, self.p.other_y], self.came.at[at], self.p.y_dev)

    def add(self, at):
        self.kept[at].wait()
        self.sent[at].wait_recv()

        def add(z, carry):
            self.sums[at, z] = (self.sums[at, z].astype(F32) + self.came[at, z].astype(F32)).astype(BF16)
            return carry

        lax.fori_loop(0, self.p.planes, add, 0)

    def push(self, at):
        self.out[at] = [
            self.wire.send(self.sums.at[at, self.p.z_at(step)], self.far.at[at, step - 1], self.p.z_dev(step))
            for step in range(1, self.p.planes)
        ]

    def put(self, owner, value):
        first = 0
        for home, start, width in self.homes:
            at = pl.multiple_of(owner * (home.shape[1] // 4) + start, RUN)
            home[:, pl.ds(at, width)] = value[:, first : first + width]
            first += width

    def gather(self, at):
        for copy in self.out[at]:
            copy.wait_recv()
        total = self.sums[at, self.p.z].astype(F32)
        for step in range(1, self.p.planes):
            total = total + self.far[at, step - 1].astype(F32)
        if GROUPS[at] == 0:
            self.put(self.p.s, total)
            return
        self.leave[at] = total.astype(BF16)
        self.back[at] = self.wire.send(self.leave.at[at], self.arrive.at[at], self.p.seq_dev[GROUPS[at]])

    def finish(self):
        for at, copy in self.back.items():
            copy.wait_recv()
            self.put(self.p.seq_dev[GROUPS[at]][0], self.arrive[at].astype(F32))


def group_rows(place, at):
    owner = place.seq_dev[GROUPS[at]][0]
    return pl.ds(pl.multiple_of(owner * BLOCK, BLOCK), BLOCK)


def column_scratch(planes, deep, width, groups=4):
    return [
        VMEM((groups, planes, deep, width), BF16), VMEM((groups, planes, deep, width), BF16),
        VMEM((4, planes - 1, deep, width), BF16), VMEM((3, deep, width), BF16), VMEM((3, deep, width), BF16),
    ]


def row_scratch(planes, deep, width):
    return [VMEM((planes, deep, width), BF16), VMEM((planes, deep, width), BF16),
            VMEM((planes - 1, deep, width), BF16)]


def middle_kernel(
    planes,
    post_in, back_in, wgu_in, wd_in, resid_in, gains,
    ready, grad_rest, home_d, y_out, y_keep, d_resid, attn_full, sums,
    post, back, wgu, wd, resid, load_sems,
    grad_first, g_came, grad_d, d_came, d_sums, d_far, hidden, d_gu, part, attn_own,
    y_core_out, y_core_in,
    core_out, core_in, x_out, x_in, keep, core_s, core_r, x_s, x_r,
    y_core_s, y_core_r, out_sems, in_sems, own_sems,
):
    p = Place(planes)
    s = p.s
    wire = Wire(out_sems, in_sems, own_sems)
    into_post = Reducer(p, part, core_out, core_in, x_out, x_in, keep, (core_s, core_r, x_s, x_r))
    into_out = Reducer(p, part, y_core_out, y_core_in, y_out, None, y_keep, (y_core_s, y_core_r, None, None))
    rows = resid.shape[1]
    length = 4 * rows
    wide = hidden.shape[1]
    mine = pl.ds(s * rows, rows)
    theirs = pl.ds(p.x_dev[0] * rows, rows)
    loads = [wire.own(wgu_in, wgu), wire.own(wd_in, wd), wire.own(resid_in, resid)]

    def chunk(step):
        micro, block = into_post.block(step)
        here = pl.ds(pl.multiple_of(micro * length + block * BLOCK, BLOCK), BLOCK)
        return [pltpu.make_async_copy(far.at[here], near.at[here], load_sems.at[at, step])
                for at, (far, near) in enumerate(((post_in, post), (back_in, back)))]

    for step in range(8):
        for copy in chunk(step):
            copy.start()
    p.meet()
    for copy in loads:
        copy.wait()

    def feed(step, carry):
        micro, block = into_post.block(step)
        here = pl.ds(pl.multiple_of(micro * length + block * BLOCK, BLOCK), BLOCK)
        for copy in chunk(step):
            copy.wait()
        both = dot(post[here, :], wgu[...])
        d_hidden = dot(back[here, :], wd[...], NARROW)
        gate, upper = both[:, :wide], both[:, wide:]
        sigma = 1.0 / (1.0 + jnp.exp(-gate))
        lit = gate * sigma
        hidden[here] = (lit * upper).astype(BF16)
        d_gu[here, :wide] = (d_hidden * upper * (sigma + lit * (1.0 - sigma))).astype(BF16)
        d_gu[here, wide:] = (d_hidden * lit).astype(BF16)
        part[...] = dot(d_gu[here, :], wgu[...], NARROW)
        into_post.take(step)
        part[...] = dot(hidden[here, :], wd[...])
        into_out.take(step, send_x=False)
        return carry

    down = RowHoming(p, wire, grad_d, d_came, d_sums, d_far, home_d)
    columns = ColumnHoming(p, wire, g_came, ready, None)

    def down_tile(at, carry):
        tall = wide // 2
        cut = pl.ds(pl.multiple_of(at * tall, RUN), tall)
        found = dot(hidden[:, cut], back[...], TALL).astype(BF16)
        grad_d[pl.ds(at * (planes // 2), planes // 2)] = found.reshape(planes // 2, *grad_d.shape[1:])
        return carry

    def wide_tile(at):
        found = dot(post[:, group_rows(p, at)], d_gu[...], TALL).astype(BF16)
        return found.reshape(grad_first.shape)

    gain = gains[1:2]
    sends = []
    sums[...] = jnp.zeros_like(sums)

    def settle(micro):
        grad = into_post.total(micro)
        held = resid[micro]
        root = lax.rsqrt(row_mean(held * held) + EPSILON)
        unit = held * root
        sums[0:1] += jnp.sum(grad * unit, axis=0, keepdims=True)
        scaled = grad * gain
        own = back[pl.ds(pl.multiple_of(micro * length + s * rows, rows), rows), :].astype(F32)
        whole = own + root * (scaled - unit * row_mean(scaled * unit))
        d_resid[micro] = whole
        attn_own[micro] = whole.astype(BF16)
        to = attn_full.at[micro, mine]
        sends.append((wire.send(attn_own.at[micro], to, p.x_dev), wire.send(attn_own.at[micro], to, p.core_dev),
                      wire.own(attn_own.at[micro], to)))
        y_keep[micro] = y_keep[micro] + held

    lax.fori_loop(0, 7, feed, 0)
    settle(0)
    lax.fori_loop(7, 8, feed, 0)
    lax.fori_loop(0, 2, down_tile, 0)
    down.start()
    grad_first[...] = wide_tile(0)
    columns.start(0, grad_first)
    settle(1)
    grad_rest[0] = wide_tile(1)
    down.push(0)
    grad_rest[1] = wide_tile(2)
    grad_rest[2] = wide_tile(3)
    down.push(1)
    forwards = []
    for micro in range(2):
        sends[micro][0].wait_recv()
        block = attn_full.at[micro, theirs]
        forwards.append(wire.send(block, block, p.core_dev))
    columns.add(0)
    for micro in range(2):
        forwards[micro].wait_recv()
        sends[micro][1].wait_recv()
        sends[micro][2].wait()
    down.gather()
    into_post.close()
    into_out.close(send_x=False)
    wire.close()


def middle(planes, post, back, wgu, wd, resid, gains):
    rows = resid.shape[1]
    total = 8 * rows
    wide = wd.shape[0]
    deep = 1024 // (8 * planes)
    once = (planes, 2, deep, 2 * wide)
    slim = (planes, 2, wide // (2 * planes), 1024)
    shapes = [
        jax.ShapeDtypeStruct((1, planes, deep, 2 * wide), BF16), jax.ShapeDtypeStruct((3, *once), BF16),
        jax.ShapeDtypeStruct(slim[2:], F32),
        jax.ShapeDtypeStruct((2, rows, 1024), BF16), jax.ShapeDtypeStruct((2, rows, 1024), F32),
        jax.ShapeDtypeStruct((2, rows, 1024), F32), jax.ShapeDtypeStruct((2, 4 * rows, 1024), BF16),
        jax.ShapeDtypeStruct((8, 1024), F32),
    ]
    vm = pl.BlockSpec(memory_space=VMEM)
    hb = pl.BlockSpec(memory_space=ANY)
    return pl.pallas_call(
        functools.partial(middle_kernel, planes),
        out_shape=shapes,
        in_specs=[hb] * 5 + [vm],
        out_specs=[vm] * 6 + [hb, vm],
        scratch_shapes=[
            *[VMEM(item.shape, item.dtype) for item in (post, back, wgu, wd, resid)],
            pltpu.SemaphoreType.DMA((2, 8)),
            VMEM(once, BF16), VMEM((1, planes, deep, 2 * wide), BF16), VMEM(slim, BF16),
            *row_scratch(planes, *slim[2:]),
            VMEM((total, wide), BF16), VMEM((total, 2 * wide), BF16),
            VMEM((BLOCK, 1024), F32), VMEM((2, rows, 1024), BF16),
            VMEM((4, BLOCK, 1024), BF16), VMEM((4, BLOCK, 1024), BF16),
            *reducer_scratch(1024),
            pltpu.SemaphoreType.DMA((4,)), pltpu.SemaphoreType.DMA((4,)),
            *wire_scratch(16, 10),
        ],
        compiler_params=pltpu.CompilerParams(
            collective_id=1, has_side_effects=True, vmem_limit_bytes=VMEM_BYTES),
        name="middle",
    )(post, back, wgu, wd, resid, gains)


def rear_kernel(
    planes,
    order, rank, attn_in, query_in, key_in, value_in, q_unit_in, k_unit_in, roots_in, mixed_in, wo_in,
    normed_in, win_in, tokens_in, d_resid_in, cosine, sine, gains, y_out, y_keep_in, sums_in, ready, grad_rest,
    token_grad, sums, block_out, home_g, home_u, home_o, home_q, home_k, home_v,
    attn, query, key, value, q_unit, k_unit, roots, mixed, wo, win, tokens,
    rows_held, d_mixed, keys_grad, values_grad, y_in, grad_o, grad, part, sums_out, sums_came,
    g_came, g_sums, g_far, g_leave, g_arrive, o_came, o_sums, o_far,
    a_came, a_sums, a_far, a_leave, a_arrive, b_came, b_sums, b_far, b_leave, b_arrive,
    core_out, core_in, x_out, x_in, keep, core_s, core_r, x_s, x_r,
    out_sems, in_sems, own_sems,
):
    p = Place(planes)
    wire = Wire(out_sems, in_sems, own_sems)
    reducer = Reducer(p, part, core_out, core_in, x_out, x_in, keep, (core_s, core_r, x_s, x_r))
    rows = y_in.shape[1]
    length = 4 * rows
    loads = [wire.own(far, near) for far, near in (
        (attn_in, attn), (wo_in, wo), (mixed_in, mixed), (query_in, query), (key_in, key), (value_in, value),
        (q_unit_in, q_unit), (k_unit_in, k_unit), (roots_in, roots), (y_keep_in, keep),
        (tokens_in, tokens), (d_resid_in, token_grad))]
    for far, near, span in ((0, 0, 256), (256, 512, 256), (512, 256, 128), (640, 768, 128), (768, 384, 128), (896, 896, 128)):
        loads.append(wire.own(win_in.at[:, far : far + span], win.at[:, near : near + span]))
    p.meet()
    wide = ColumnHoming(p, wire, g_came, g_sums, g_far, g_leave, g_arrive,
                        [(home, 0, home.shape[1] // 4) for home in (home_g, home_u)])
    outer = RowHoming(p, wire, grad_o, o_came, o_sums, o_far, home_o)
    inner = [
        ColumnHoming(p, wire, *refs, [(home_q, 256 * at, 256), (home_k, 128 * at, 128), (home_v, 128 * at, 128)])
        for at, refs in enumerate((
            (a_came, a_sums, a_far, a_leave, a_arrive), (b_came, b_sums, b_far, b_leave, b_arrive)))
    ]
    wide.start(1, grad_rest.at[0])
    g_sums[0] = ready[0]
    wide.push(0)
    y_sent = [wire.send(y_out.at[micro], y_in.at[micro], p.x_dev) for micro in range(2)]
    loads[0].wait()
    loads[1].wait()

    def draw(step, carry):
        here = pl.ds(pl.multiple_of(step * BLOCK, BLOCK), BLOCK)
        low = two_runs(attn, order[step * 2], order[step * 2 + 1])
        rows_held[pl.ds(step * 2, 2)] = low.reshape(2, RUN, low.shape[1])
        d_mixed[here] = dot(low, wo[...], NARROW).astype(BF16)
        return carry

    lax.fori_loop(0, 2 * length // BLOCK, draw, 0)

    def out_tile(at, carry):
        cut = pl.ds(pl.multiple_of(at * BLOCK, BLOCK), BLOCK)
        found = dot(mixed[:, cut], flat(rows_held), TALL).astype(BF16)
        grad_o[pl.ds(at * (planes // 2), planes // 2)] = found.reshape(planes // 2, *grad_o.shape[1:])
        return carry

    loads[2].wait()
    lax.fori_loop(0, 2, out_tile, 0)
    wide.start(2, grad_rest.at[1])
    normed_load = wire.own(normed_in, attn)
    wide.add(1)
    wide.push(1)
    sums[...] = sums_in[...]

    def lane_of(ref, here, lane):
        held = ref[here, :]
        lanes = lax.broadcasted_iota(jnp.int32, held.shape, 1)
        return jnp.sum(jnp.where(lanes == lane, held, 0.0), axis=1, keepdims=True)

    def norm_home(grad, cos, sin, unit, root, gain):
        turned = grad * cos - pltpu.roll(grad, HEAD_DIM // 2, 1) * sin
        scaled = turned * gain
        back = root * (scaled - unit * row_mean(scaled * unit))
        return back, jnp.sum(turned * unit, axis=0, keepdims=True)

    def attend_back(step, carry):
        micro, head = lax.rem(step, 2), step // 2
        keys_at = pl.ds(pl.multiple_of(head * HEAD_DIM, HEAD_DIM), HEAD_DIM)
        lanes = [pl.ds(pl.multiple_of(head * 2 * HEAD_DIM + g * HEAD_DIM, HEAD_DIM), HEAD_DIM) for g in range(2)]
        q_gain, k_gain = gains[2:3, 0:RUN], gains[3:4, 0:RUN]
        keys_grad[...] = jnp.zeros_like(keys_grad)
        values_grad[...] = jnp.zeros_like(values_grad)
        for block in range(length // BLOCK):
            here = pl.ds(pl.multiple_of(micro * length + block * BLOCK, BLOCK), BLOCK)
            seen = (block + 1) * BLOCK
            past = pl.ds(pl.multiple_of(micro * length, BLOCK), seen)
            asked = jnp.concatenate([query[here, lane] for lane in lanes], axis=0)
            pulled = jnp.concatenate([d_mixed[here, lane] for lane in lanes], axis=0)
            given = jnp.concatenate([mixed[here, lane] for lane in lanes], axis=0)
            level = jnp.concatenate(
                [lane_of(roots, here, LEVEL + head * 2 + g) for g in range(2)], axis=0)
            delta = jnp.sum(pulled.astype(F32) * given.astype(F32), axis=1, keepdims=True)
            scores = dot(asked, key[past, keys_at], NARROW)
            line = lax.broadcasted_iota(jnp.int32, (2 * BLOCK, seen), 0)
            line = jnp.where(line >= BLOCK, line - BLOCK, line) + block * BLOCK
            column = lax.broadcasted_iota(jnp.int32, (2 * BLOCK, seen), 1)
            weight = jnp.exp2(scores * (SCALE * LOG2E) - level)
            weight = jnp.where(column <= line, weight, 0.0)
            d_soft = dot(pulled, value[past, keys_at], NARROW)
            d_scores = (weight * (d_soft - delta)).astype(BF16)
            values_grad[0:seen] += dot(weight.astype(BF16), pulled, TALL)
            keys_grad[0:seen] += dot(d_scores, asked, TALL)
            moved = dot(d_scores, key[past, keys_at]) * SCALE
            spin = slice(block * BLOCK, (block + 1) * BLOCK)
            for g, lane in enumerate(lanes):
                root = lane_of(roots, here, head * 2 + g)
                unit = q_unit[here, lane].astype(F32)
                back, gained = norm_home(
                    moved[g * BLOCK : (g + 1) * BLOCK], cosine[spin], sine[spin], unit, root, q_gain)
                pair = pl.ds(micro * (length // RUN) + block * 2, 2)
                to = pl.ds(pl.multiple_of(head * 512 + g * HEAD_DIM, HEAD_DIM), HEAD_DIM)
                rows_held[pair, :, to] = back.astype(BF16).reshape(2, RUN, HEAD_DIM)
                sums[1:2, 0:RUN] += gained
        everything = pl.ds(pl.multiple_of(micro * length, BLOCK), length)
        root = lane_of(roots, everything, head + 4)
        unit = k_unit[everything, keys_at].astype(F32)
        back, gained = norm_home(keys_grad[...] * SCALE, cosine[...], sine[...], unit, root, k_gain)
        at, whole = head * 512 + 256, pl.ds(micro * (length // RUN), length // RUN)
        tall = (length // RUN, RUN, HEAD_DIM)
        rows_held[whole, :, pl.ds(pl.multiple_of(at, HEAD_DIM), HEAD_DIM)] = back.astype(BF16).reshape(tall)
        sums[2:3, 0:RUN] += gained
        low = values_grad[...].astype(BF16).reshape(tall)
        rows_held[whole, :, pl.ds(pl.multiple_of(at + HEAD_DIM, HEAD_DIM), HEAD_DIM)] = low
        return carry

    for copy in loads[3:9]:
        copy.wait()
    def pull(step, carry):
        micro, block = reducer.block(step)
        at = micro * (length // RUN) + block * 2
        runs = (rank[at], rank[at + 1])
        found = dot(two_runs(rows_held, *runs), win[...], NARROW)
        part[...] = found
        sums[3:4] += jnp.sum(found * two_runs(attn, *runs).astype(F32), axis=0, keepdims=True)
        reducer.take(step)
        return carry

    def tile(half, at):
        pulled = joined(rows_held[:, :, half * 512 : half * 512 + 512])
        found = dot(joined(attn[:, :, group_rows(p, at)]), pulled, TALL).astype(BF16)
        grad[half, at] = found.reshape(grad.shape[2:])
        inner[half].start(at, grad.at[half, at])

    lax.fori_loop(0, 1, attend_back, 0)
    wide.start(3, grad_rest.at[2])
    wide.add(2)
    wide.push(2)
    lax.fori_loop(1, 2, attend_back, 0)
    normed_load.wait()
    for at in range(4):
        tile(0, at)
    wide.add(3)
    wide.push(3)
    wide.gather(0)
    for copy in loads[9:]:
        copy.wait()
    for micro in range(2):
        y_sent[micro].wait_recv()
        block_out[micro] = (keep[micro] + y_in[micro].astype(F32)).astype(BF16)
    lax.fori_loop(2, 3, attend_back, 0)
    outer.start()
    lax.fori_loop(0, 4, pull, 0)
    for at in range(4):
        inner[0].add(at)
        inner[0].push(at)
    wide.gather(1)
    lax.fori_loop(3, 4, attend_back, 0)
    tile(1, 0)
    tile(1, 1)
    outer.push(0)
    outer.push(1)
    tile(1, 2)
    tile(1, 3)
    lax.fori_loop(4, 8, pull, 0)
    sums[3:4] = sums[3:4] / gains[0:1]

    def exchange(stage, devices, base):
        sums_out[stage] = sums[...]
        sent = [wire.send(sums_out.at[stage], sums_came.at[base + at], dev) for at, dev in enumerate(devices)]
        return base, sent

    def absorb(state):
        base, sent = state
        total = sums[...]
        for at, copy in enumerate(sent):
            copy.wait_recv()
            total = total + sums_came[base + at]
        sums[...] = total

    state = exchange(0, p.seq_dev[1:], 0)
    wide.gather(2)
    wide.gather(3)
    inner[1].add(0)
    inner[1].push(0)
    absorb(state)
    state = exchange(1, [p.z_dev(step) for step in range(1, planes)], 3)
    inner[1].add(1)
    inner[1].push(1)
    for at in range(4):
        inner[0].gather(at)
    inner[1].add(2)
    inner[1].push(2)
    absorb(state)
    state = exchange(2, [p.y_dev], 2 + planes)
    inner[1].add(3)
    inner[1].push(3)
    outer.gather()
    for micro in range(2):
        grad_rows = reducer.total(micro)
        raw = tokens[micro].astype(F32)
        root = lax.rsqrt(row_mean(raw * raw) + EPSILON)
        unit = raw * root
        scaled = grad_rows * gains[0:1]
        token_grad[micro] = token_grad[micro] + root * (scaled - unit * row_mean(scaled * unit))
    wide.finish()
    inner[0].finish()
    absorb(state)
    for at in range(4):
        inner[1].gather(at)
    inner[1].finish()
    reducer.close()
    wire.close()


def rear(planes, order, rank, attn, query, key, value, q_unit, k_unit, roots, mixed, wo, normed, win, tokens, d_resid,
         cosine, sine, gains, y_out, y_keep, sums, ready, grad_rest):
    rows = y_keep.shape[1]
    length = 4 * rows
    total = 2 * length
    deep, wide = grad_rest.shape[3:]
    slim = (planes, 2, 512 // (2 * planes), 1024)
    shapes = [
        jax.ShapeDtypeStruct((2, rows, 1024), F32), jax.ShapeDtypeStruct((8, 1024), F32),
        jax.ShapeDtypeStruct((2, rows, 1024), BF16),
        jax.ShapeDtypeStruct((deep, 2 * wide), F32), jax.ShapeDtypeStruct((deep, 2 * wide), F32),
        jax.ShapeDtypeStruct(slim[2:], F32), jax.ShapeDtypeStruct((deep, 2048), F32),
        jax.ShapeDtypeStruct((deep, 1024), F32), jax.ShapeDtypeStruct((deep, 1024), F32),
    ]
    held = (attn, query, key, value, q_unit, k_unit, roots, mixed, wo, win, tokens)
    vm = pl.BlockSpec(memory_space=VMEM)
    hb = pl.BlockSpec(memory_space=ANY)
    sm = pl.BlockSpec(memory_space=pltpu.SMEM)
    return pl.pallas_call(
        functools.partial(rear_kernel, planes),
        out_shape=shapes,
        in_specs=[sm, sm] + [hb] * 13 + [vm] * 3 + [hb, hb, vm, vm, hb],
        out_specs=[vm] * len(shapes),
        scratch_shapes=[
            *[VMEM(item.shape, item.dtype) for item in held],
            VMEM((total // RUN, RUN, 1024), BF16), VMEM((total, 512), BF16), VMEM((length, HEAD_DIM), F32),
            VMEM((length, HEAD_DIM), F32), VMEM((2, rows, 1024), BF16), VMEM(slim, BF16),
            VMEM((2, 4, planes, 2, deep, 512), BF16), VMEM((BLOCK, 1024), F32), VMEM((3, 8, 1024), F32),
            VMEM((3 + planes, 8, 1024), F32),
            *column_scratch(planes, deep, wide), *row_scratch(planes, *slim[2:]),
            *column_scratch(planes, deep, 512), *column_scratch(planes, deep, 512),
            *reducer_scratch(1024), *wire_scratch(96, 56),
        ],
        compiler_params=pltpu.CompilerParams(
            collective_id=2, has_side_effects=True, vmem_limit_bytes=VMEM_BYTES),
        name="rear",
    )(order, rank, attn, query, key, value, q_unit, k_unit, roots, mixed, wo, normed, win, tokens, d_resid,
      cosine, sine, gains, y_out, y_keep, sums, ready, grad_rest)


def deliver_kernel(count, planes, sums, *refs):
    given, rest = refs[:count], refs[count:]
    made, small, held, sems = rest[:count], rest[count : count + 4], rest[count + 4 : 2 * count + 4], rest[-1]
    came = [pltpu.make_async_copy(src, mid, sems.at[0, at]) for at, (src, mid) in enumerate(zip(given, held))]
    gone = [pltpu.make_async_copy(mid, dst, sems.at[1, at]) for at, (mid, dst) in enumerate(zip(held, made))]
    for copy in came:
        copy.start()
    me = lax.axis_index("seq") * (2 * planes) + lax.axis_index("fsdp")
    table = sums[...]
    for row, out in zip((3, 0, 1, 2), small):
        width = out.shape[1]
        turned = pltpu.roll(table, table.shape[1] - me * width, 1)
        out[...] = turned[row : row + 1, :width]
    for first, second in zip(came, gone):
        first.wait()
        second.start()
    for copy in gone:
        copy.wait()


def deliver(planes, sums, widths, *items):
    count = len(items)
    vm, hb = pl.BlockSpec(memory_space=VMEM), pl.BlockSpec(memory_space=ANY)
    return pl.pallas_call(
        functools.partial(deliver_kernel, count, planes),
        out_shape=[*[jax.ShapeDtypeStruct(item.shape, item.dtype) for item in items],
                   *[jax.ShapeDtypeStruct((1, width), F32) for width in widths]],
        in_specs=[vm] + [hb] * count,
        out_specs=[hb] * count + [vm] * 4,
        scratch_shapes=[*[VMEM(item.shape, item.dtype) for item in items], pltpu.SemaphoreType.DMA((2, count))],
        compiler_params=pltpu.CompilerParams(vmem_limit_bytes=VMEM_BYTES),
        name="deliver",
    )(sums, *items)


def run_tables(positions):
    runs = positions.shape[1] // RUN
    rank = positions[:, ::RUN] // RUN
    index = jnp.arange(runs, dtype=jnp.int32)
    order = jnp.sum(jnp.where(rank[:, :, None] == index, index[None, :, None], 0), axis=1)
    base = jnp.arange(positions.shape[0], dtype=jnp.int32)[:, None] * runs
    return (order + base).reshape(-1), (rank + base).reshape(-1)


def turn_tables(length):
    half = HEAD_DIM // 2
    frequency = (ROPE_BASE ** (-np.arange(half) * 2.0 / HEAD_DIM)).astype(np.float32)
    angles = (np.arange(length, dtype=np.float32)[:, None] * frequency[None, :]).astype(np.float64)
    cosine, sine = np.cos(angles), np.sin(angles)
    return (jnp.asarray(np.concatenate([cosine, cosine], axis=1).astype(np.float32)),
            jnp.asarray(np.concatenate([-sine, sine], axis=1).astype(np.float32)))


def kernel_body(tokens, positions, g_in, g_post, g_query, g_key, w_query, w_key, w_value,
                w_out, w_gate, w_up, w_down, cotangent):
    planes = lax.axis_size("fsdp") // 2
    length = positions.shape[2]
    order, rank = run_tables(positions[:, 0])
    tile = jnp.stack(
        [jnp.pad(item.astype(F32), (0, RUN - item.shape[0])) for item in (g_in, g_post, g_query, g_key)])
    tile = jnp.pad(tile, ((0, 4), (0, 0)))
    cosine, sine = turn_tables(length)
    near = tokens[:, 0]
    shards = (w_query, w_key, w_value, w_out, w_gate, w_up, w_down)
    (win, wo, wgu, wd, normed, query, key, value, q_unit, k_unit, roots, mixed,
     resid, post, back, gains) = front(
        planes, order, rank, near, cotangent[:, 0], tile, cosine, sine, shards)
    plain = lambda item: item.reshape(-1, item.shape[-1])
    apart = lambda item: item.reshape(-1, RUN, item.shape[-1])
    win, wo, wgu, wd, post, back = [plain(item) for item in (win, wo, wgu, wd, post, back)]
    ready, grad_rest, home_d, y_out, y_keep, d_resid, attn, sums = middle(
        planes, post, back, wgu, wd, resid, gains)
    token_grad, sums, block_out, home_g, home_u, home_o, home_q, home_k, home_v = rear(
        planes, order, rank, apart(attn), query, key, value, q_unit, k_unit, roots, plain(mixed), wo,
        apart(normed), win, near, d_resid, cosine, sine, gains, y_out, y_keep, sums, ready, grad_rest)
    widths = [item.shape[0] for item in (g_in, g_post, g_query, g_key)]
    found = deliver(planes, sums, widths, token_grad, block_out, home_d, home_g, home_u, home_o, home_q, home_k, home_v)
    token_grad, block_out, home_d, home_g, home_u, home_o, home_q, home_k, home_v = found[:9]
    small = [item[0] for item in found[9:]]
    return (block_out[:, None], token_grad[:, None], *small, home_q, home_k, home_v, home_o,
            home_g, home_u, home_d)


def solution(mesh):
    both = ("seq", "fsdp")
    act = P(None, "fsdp", "seq", None)
    vec, mat = P(both), P(both, None)

    def body(*args):
        rows = args[6].shape[0]
        fits = mesh.shape["seq"] == 4 and mesh.shape["fsdp"] % 2 == 0 and rows % 16 == 0
        return (kernel_body if fits else plain_body)(*args)

    return jax.shard_map(
        body,
        mesh=mesh,
        in_specs=(act, P(None, "fsdp", None), *[vec] * 4, *[mat] * 7, act),
        out_specs=(act, act, *[vec] * 4, *[mat] * 7),
        check_vma=False,
    )
```

```python
import functools

import jax
import jax.numpy as jnp
import numpy as np
from jax import lax
from jax.experimental import pallas as pl
from jax.experimental.pallas import tpu as pltpu
from jax.sharding import PartitionSpec as P

HEADS = 16
KV_HEADS = 8
HEAD_DIM = 128
EPSILON = 1e-06
ROPE_BASE = 1000000.0
NEGATIVE = -1e30
F32 = jnp.float32
BF16 = jnp.bfloat16


def inverse_root(values):
    return lax.rsqrt(jnp.mean(values * values, axis=-1, keepdims=True) + EPSILON)


def rope_tables(token_pos):
    half_width = HEAD_DIM // 2
    frequency = ROPE_BASE ** (-(jnp.arange(half_width, dtype=F32) * 2.0 / HEAD_DIM))
    angles = token_pos.astype(F32)[:, None] * frequency[None, :]
    cosine = jnp.cos(angles)
    sine = jnp.sin(angles)
    return (
        jnp.concatenate([cosine, cosine], axis=-1)[:, None, :],
        jnp.concatenate([sine, sine], axis=-1)[:, None, :],
    )


def rotate(values, cosine, sine):
    half_width = values.shape[-1] // 2
    turned = jnp.concatenate([-values[..., half_width:], values[..., :half_width]], axis=-1)
    return values * cosine + turned * sine


def rotate_back(grads, cosine, sine):
    half_width = grads.shape[-1] // 2
    scaled = grads * sine
    turned = jnp.concatenate([scaled[..., half_width:], -scaled[..., :half_width]], axis=-1)
    return grads * cosine + turned


def norm_back(grads, values, inverse, gain):
    scaled = grads * gain
    return inverse * scaled - values * inverse**3 * jnp.mean(
        scaled * values, axis=-1, keepdims=True
    )


def mul(eq, left, right):
    return jnp.einsum(eq, left, right, preferred_element_type=F32)


def sum_scatter(part, axis):
    return lax.psum_scatter(part.astype(BF16), axis, scatter_dimension=0, tiled=True).astype(F32)


def slice_weights(item, ways):
    rows = item.shape[0]
    return item.reshape(rows, ways, -1).transpose(1, 0, 2)


def plain_body(tokens, positions, g_in, g_post, g_query, g_key, w_query, w_key, w_value,
               w_out, w_gate, w_up, w_down, cotangent):
    ways = lax.axis_size("seq")
    heads, kv_heads = HEADS // ways, KV_HEADS // ways
    micro, rows, width = tokens.shape[0], tokens.shape[2], tokens.shape[3]
    length = positions.shape[2]
    everyone = ("seq", "fsdp")
    gains = [
        lax.all_gather(item, everyone, axis=0, tiled=True).astype(F32)
        for item in (g_in, g_post, g_query, g_key)
    ]
    gain_in, gain_post, gain_query, gain_key = gains

    def spread(*items):
        packed = jnp.concatenate([slice_weights(item, ways) for item in items], axis=2)
        packed = lax.all_to_all(packed, "seq", 0, 0, tiled=True)
        packed = lax.all_gather(packed, "fsdp", axis=1, tiled=True)
        packed = packed.reshape(-1, packed.shape[2])
        sizes = [item.shape[1] // ways for item in items]
        cuts = [sum(sizes[: at + 1]) for at in range(len(sizes) - 1)]
        return jnp.split(packed, cuts, axis=1)

    wq, wk, wv = spread(w_query, w_key, w_value)
    wo = lax.all_gather(w_out, "fsdp", axis=0, tiled=True)
    wg, wu = spread(w_gate, w_up)
    wd = lax.all_gather(w_down, "fsdp", axis=0, tiled=True)
    scale = HEAD_DIM ** (-0.5)

    def gather_rows(item):
        return lax.all_gather(item, "seq", axis=0, tiled=True)

    grads = None
    outs, token_grads = [], []
    for at in range(micro):
        inputs = tokens[at, 0].astype(F32)
        pos = positions[at, 0]
        cosine, sine = rope_tables(pos)
        allowed = pos[None, :] <= pos[:, None]
        inv_in = inverse_root(inputs)
        normed = gather_rows((inputs * inv_in * gain_in).astype(BF16))
        q_raw = mul("td,df->tf", normed, wq).reshape(length, heads, HEAD_DIM)
        k_raw = mul("td,df->tf", normed, wk).reshape(length, kv_heads, HEAD_DIM)
        value = mul("td,df->tf", normed, wv).astype(BF16).reshape(length, kv_heads, HEAD_DIM)
        inv_q, inv_k = inverse_root(q_raw), inverse_root(k_raw)
        query = rotate(q_raw * inv_q * gain_query, cosine, sine).astype(BF16)
        query = query.reshape(length, kv_heads, heads // kv_heads, HEAD_DIM)
        key = rotate(k_raw * inv_k * gain_key, cosine, sine).astype(BF16)
        scores = jnp.where(allowed, mul("qjgd,kjd->jgqk", query, key) * scale, NEGATIVE)
        soft = jax.nn.softmax(scores, axis=-1)
        soft_low = soft.astype(BF16)
        mixed = mul("jgqk,kjd->qjgd", soft_low, value).astype(BF16).reshape(length, -1)
        resid = inputs + sum_scatter(mul("th,hd->td", mixed, wo), "seq")
        inv_post = inverse_root(resid)
        post = gather_rows((resid * inv_post * gain_post).astype(BF16))
        gate = mul("td,df->tf", post, wg)
        upper = mul("td,df->tf", post, wu)
        sigma = jax.nn.sigmoid(gate)
        hidden = (gate * sigma * upper).astype(BF16)
        outs.append((resid + sum_scatter(mul("tf,fd->td", hidden, wd), "seq")).astype(BF16))
        back_low = cotangent[at, 0]
        back = gather_rows(back_low)
        g_down = mul("tf,td->fd", hidden, back)
        d_hidden = mul("td,fd->tf", back, wd)
        d_gate = (d_hidden * upper * sigma * (1.0 + gate * (1.0 - sigma))).astype(BF16)
        d_upper = (d_hidden * gate * sigma).astype(BF16)
        g_gate = mul("td,tf->df", post, d_gate)
        g_up = mul("td,tf->df", post, d_upper)
        d_post = sum_scatter(mul("tf,df->td", d_gate, wg) + mul("tf,df->td", d_upper, wu), "seq")
        post_grad = jnp.sum(d_post * resid * inv_post, axis=0)
        d_resid = back_low.astype(F32) + norm_back(d_post, resid, inv_post, gain_post)
        d_attn = gather_rows(d_resid.astype(BF16))
        g_out = mul("th,td->hd", mixed, d_attn)
        d_mixed = mul("td,hd->th", d_attn, wo).astype(BF16)
        d_mixed = d_mixed.reshape(length, kv_heads, heads // kv_heads, HEAD_DIM)
        d_soft = mul("qjgd,kjd->jgqk", d_mixed, value)
        d_scores = (soft * (d_soft - jnp.sum(d_soft * soft, axis=-1, keepdims=True))).astype(BF16)
        d_query = mul("jgqk,kjd->qjgd", d_scores, key) * scale
        d_key = mul("jgqk,qjgd->kjd", d_scores, query) * scale
        d_value = mul("jgqk,qjgd->kjd", soft_low, d_mixed).astype(BF16).reshape(length, -1)
        key_turn = rotate_back(d_key, cosine, sine)
        query_turn = rotate_back(d_query.reshape(length, heads, HEAD_DIM), cosine, sine)
        key_grad = jnp.sum(key_turn * k_raw * inv_k, axis=(0, 1))
        query_grad = jnp.sum(query_turn * q_raw * inv_q, axis=(0, 1))
        d_key = norm_back(key_turn, k_raw, inv_k, gain_key).astype(BF16).reshape(length, -1)
        d_query = norm_back(query_turn, q_raw, inv_q, gain_query).astype(BF16).reshape(length, -1)
        g_query_w = mul("td,tf->df", normed, d_query)
        g_key_w = mul("td,tf->df", normed, d_key)
        g_value_w = mul("td,tf->df", normed, d_value)
        d_normed = mul("tf,df->td", d_query, wq) + mul("tf,df->td", d_key, wk)
        d_normed = sum_scatter(d_normed + mul("tf,df->td", d_value, wv), "seq")
        in_grad = jnp.sum(d_normed * inputs * inv_in, axis=0)
        token_grads.append(d_resid + norm_back(d_normed, inputs, inv_in, gain_in))
        found = [in_grad, post_grad, query_grad, key_grad, g_query_w, g_key_w, g_value_w,
                 g_out, g_gate, g_up, g_down]
        grads = found if grads is None else [left + right for left, right in zip(grads, found)]

    small = [lax.psum_scatter(item, everyone, scatter_dimension=0, tiled=True) for item in grads[:4]]

    def columns_home(item):
        full, wide = item.shape
        item = item.reshape(ways, -1, wide).astype(BF16)
        item = lax.psum_scatter(item, "fsdp", scatter_dimension=1, tiled=True)
        item = lax.all_to_all(item, "seq", 0, 0, tiled=True)
        return item.transpose(1, 0, 2).reshape(item.shape[1], ways * wide).astype(F32)

    def rows_home(item):
        return sum_scatter(item, "fsdp")

    large = [columns_home(item) for item in grads[4:7]] + [rows_home(grads[7])]
    large += [columns_home(item) for item in grads[8:10]] + [rows_home(grads[10])]
    return (jnp.stack(outs)[:, None], jnp.stack(token_grads)[:, None], *small, *large)


MESH = pl.DeviceIdType.MESH
ANY = pl.ANY
VMEM = pltpu.VMEM
RUN = 128
BLOCK = 256
NARROW = (((1,), (1,)), ((), ()))
TALL = (((0,), (0,)), ((), ()))
PLAIN = (((1,), (0,)), ((), ()))
LOG2E = 1.4426950408889634
SCALE = HEAD_DIM ** (-0.5)
LEVEL = 8
VMEM_BYTES = 63 * 2**20


def dot(left, right, dims=PLAIN):
    return lax.dot_general(left, right, dims, preferred_element_type=F32)


class Place:
    def __init__(self, planes):
        self.planes = planes
        self.s = lax.axis_index("seq")
        self.f = lax.axis_index("fsdp")
        self.x, self.c = self.s // 2, self.s % 2
        self.z, self.y = self.f // 2, self.f % 2
        self.other_y = 1 - self.y
        self.core_dev = (self.x * 2 + 1 - self.c, self.f)
        self.x_dev = ((1 - self.x) * 2 + self.c, self.f)
        self.far_dev = ((1 - self.x) * 2 + 1 - self.c, self.f)
        self.y_dev = (self.s, self.z * 2 + self.other_y)
        self.seq_dev = [(self.s, self.f), self.core_dev, self.x_dev, self.far_dev]

    def z_at(self, step):
        return lax.rem(self.z + step, self.planes)

    def z_dev(self, step):
        return (self.s, self.z_at(step) * 2 + self.y)

    def peers(self):
        return [self.core_dev, self.x_dev, self.far_dev, self.y_dev] + [
            self.z_dev(step) for step in range(1, self.planes)
        ]

    def meet(self):
        barrier = pltpu.get_barrier_semaphore()
        for peer in self.peers():
            pl.semaphore_signal(barrier, inc=1, device_id=peer, device_id_type=MESH)
        pl.semaphore_wait(barrier, 3 + self.planes)


def remote(src, dst, out_sem, in_sem, device):
    return pltpu.make_async_remote_copy(
        src_ref=src, dst_ref=dst, send_sem=out_sem, recv_sem=in_sem,
        device_id=device, device_id_type=MESH,
    )


class Wire:
    def __init__(self, out_sems, in_sems, own_sems):
        self.out_sems, self.in_sems, self.own_sems = out_sems, in_sems, own_sems
        self.sent, self.owned = [], 0

    def send(self, src, dst, device, start=True):
        at = len(self.sent)
        copy = remote(src, dst, self.out_sems.at[at], self.in_sems.at[at], device)
        if start:
            copy.start()
        self.sent.append(copy)
        return copy

    def own(self, src, dst):
        copy = pltpu.make_async_copy(src, dst, self.own_sems.at[self.owned])
        copy.start()
        self.owned += 1
        return copy

    def close(self):
        for copy in self.sent:
            copy.wait_send()


def wire_scratch(copies, owns):
    return [
        pltpu.SemaphoreType.DMA((copies,)),
        pltpu.SemaphoreType.DMA((copies,)),
        pltpu.SemaphoreType.DMA((owns,)),
    ]


class Reducer:
    def __init__(self, place, part, core_out, core_in, x_out, x_in, keep, sems):
        self.place, self.part = place, part
        self.core_out, self.core_in = core_out, core_in
        self.x_out, self.x_in, self.keep = x_out, x_in, keep
        self.core_s, self.core_r, self.x_s, self.x_r = sems

    def block(self, step):
        p = self.place
        turn = step % 4
        x = jnp.where(turn < 2, 1 - p.x, p.x)
        c = jnp.where(turn % 2 == 0, 1 - p.c, p.c)
        return step // 4, x * 2 + c

    def core_copy(self, slot):
        return remote(self.core_out.at[slot], self.core_in.at[slot], self.core_s.at[slot],
                      self.core_r.at[slot], self.place.core_dev)

    def x_copy(self, micro):
        return remote(self.x_out.at[micro], self.x_in.at[micro], self.x_s.at[micro],
                      self.x_r.at[micro], self.place.x_dev)

    def take(self, step, send_x=True):
        micro, turn = step // 4, step % 4

        @pl.when(turn % 2 == 0)
        def _():
            slot = micro * 2 + turn // 2
            self.core_out[slot] = self.part[...].astype(BF16)
            self.core_copy(slot).start()

        @pl.when(turn == 1)
        def _():
            slot = micro * 2
            self.core_copy(slot).wait_recv()
            self.x_out[micro] = (self.part[...] + self.core_in[slot].astype(F32)).astype(BF16)
            if send_x:
                self.x_copy(micro).start()

        @pl.when(turn == 3)
        def _():
            slot = micro * 2 + 1
            self.core_copy(slot).wait_recv()
            self.keep[micro] = self.part[...] + self.core_in[slot].astype(F32)

    def total(self, micro):
        self.x_copy(micro).wait_recv()
        return self.keep[micro] + self.x_in[micro].astype(F32)

    def close(self, send_x=True):
        for slot in range(4):
            self.core_copy(slot).wait_send()
        if send_x:
            for micro in range(2):
                self.x_copy(micro).wait_send()


def reducer_scratch(width):
    return [
        VMEM((4, BLOCK, width), BF16),
        VMEM((4, BLOCK, width), BF16),
        VMEM((2, BLOCK, width), BF16),
        VMEM((2, BLOCK, width), BF16),
        VMEM((2, BLOCK, width), F32),
        pltpu.SemaphoreType.DMA((4,)),
        pltpu.SemaphoreType.DMA((4,)),
        pltpu.SemaphoreType.DMA((2,)),
        pltpu.SemaphoreType.DMA((2,)),
    ]


def row_mean(values):
    return jnp.mean(values, axis=-1, keepdims=True)


def spread_gain(table, row, devices, width):
    per = width // devices
    lanes = lax.broadcasted_iota(jnp.int32, (RUN, width), 0)
    column = lax.broadcasted_iota(jnp.int32, (RUN, width), 1)
    pick = (lanes == lax.rem(column, per)).astype(BF16)
    picked = dot(table, pick)
    rows = lax.broadcasted_iota(jnp.int32, (devices * 8, width), 0)
    owner = lax.broadcasted_iota(jnp.int32, (devices * 8, width), 1) // per
    return jnp.sum(jnp.where(rows == owner * 8 + row, picked, 0.0), axis=0, keepdims=True)


def two_runs(ref, first, second):
    return jnp.concatenate([ref[first], ref[second]], axis=0)


def joined(value):
    return value.reshape(-1, value.shape[-1])


def flat(ref):
    return joined(ref[...])


def front_kernel(
    planes,
    order, rank, tokens, cotangent, gain_tile, cosine_in, sine_in,
    s_q, s_k, s_v, s_o, s_g, s_u, s_d,
    win_out, wo_out, wgu, wd,
    normed_out, query_out, key_out, value_out, q_unit_out, k_unit_out, roots_out, mixed_out,
    resid_out, post_full, back_full, gains,
    win, wo, normed, query, key, value, q_unit, k_unit, roots, mixed, resid,
    tok_full, gain_all, post_own, back_own, cosine, sine, part,
    core_out, core_in, x_out, x_in, keep, core_s, core_r, x_s, x_r,
    out_sems, in_sems, own_sems,
):
    p = Place(planes)
    s, f = p.s, p.f
    devices = 8 * planes
    wire = Wire(out_sems, in_sems, own_sems)
    reducer = Reducer(p, part, core_out, core_in, x_out, x_in, keep, (core_s, core_r, x_s, x_r))
    rows = BLOCK
    mine = pl.ds(s * rows, rows)
    theirs = pl.ds(p.x_dev[0] * rows, rows)
    length = 4 * rows
    runs = length // RUN
    p.meet()

    def spread_columns(items, full):
        came = [[] for _ in range(4)]
        for at in (0, 2, 3, 1):
            first = 0
            for item in items:
                wide = item.shape[1] // 4
                src = item.at[:, pl.ds(pl.multiple_of(p.seq_dev[at][0] * wide, RUN), wide)]
                dst = full.at[s, f, :, pl.ds(first, wide)]
                came[at].append(wire.send(src, dst, p.seq_dev[at]) if at else wire.own(src, dst))
                first += wide
        return came

    def arrived(copies, at):
        for copy in copies[at]:
            copy.wait_recv() if at else copy.wait()

    def side(here):
        return [wire.send(here, here, p.y_dev)]

    def push(here):
        return [wire.send(here, here, p.z_dev(step)) for step in range(1, planes)]

    def forward(view, far, near):
        for step, copy in enumerate(far, 1):
            copy.wait_recv()
            near += side(view(p.z_at(planes - step) * 2 + p.y))

    def settle(near):
        for copy in near:
            copy.wait_recv()

    gain_all[s, f] = gain_tile[...]
    gain_in = [wire.send(gain_all.at[s, f], gain_all.at[s, f], dev) for dev in p.seq_dev[1:]]
    first = spread_columns((s_q, s_k, s_v), win)
    out_near = [wire.send(s_o, wo.at[f], p.y_dev)]
    down_near = [wire.send(s_d, wd.at[f], p.y_dev)]
    tok_here, tok_x, tok_core = [], [], []
    for micro in range(2):
        to = tok_full.at[pl.ds(micro * runs + s * 2, 2)]
        tok_here.append(wire.own(tokens.at[micro], to))
        tok_core.append(wire.send(tokens.at[micro], to, p.core_dev))
    out_kept = wire.own(s_o, wo.at[f])
    down_kept = wire.own(s_d, wd.at[f])
    staged = [wire.own(cosine_in, cosine), wire.own(sine_in, sine), wire.own(cotangent, back_own)]

    def in_view(at):
        return lambda owner: win.at[p.seq_dev[at][0], owner]

    def wide_view(at):
        return lambda owner: wgu.at[p.seq_dev[at][0], owner]

    in_far, in_near, wide_far, wide_near = {}, [], {}, []
    arrived(first, 0)
    in_far[0] = push(in_view(0)(f))
    in_near += side(in_view(0)(f))
    for copy in gain_in:
        copy.wait_recv()
    gain_far = push(gain_all.at[:, f])
    gain_near = side(gain_all.at[:, f])
    for at in (1, 2, 3):
        arrived(first, at)
        in_near += side(in_view(at)(f))
        if at == 1:
            in_far[1] = push(in_view(1)(f))
    for micro in range(2):
        to = tok_full.at[pl.ds(micro * runs + s * 2, 2)]
        tok_x.append(wire.send(tokens.at[micro], to, p.x_dev))
    second = spread_columns((s_g, s_u), wgu)
    forward(lambda owner: gain_all.at[:, owner], gain_far, gain_near)
    forward(in_view(0), in_far[0], in_near)
    in_far[2] = push(in_view(2)(f))
    forward(in_view(1), in_far[1], in_near)
    in_far[3] = push(in_view(3)(f))
    settle(gain_near)
    table = gain_all[...].reshape(devices * 8, RUN).astype(BF16)
    gain_first = spread_gain(table, 0, devices, 1024)
    gain_post = spread_gain(table, 1, devices, 1024)
    gain_query = spread_gain(table, 2, devices, RUN)
    gain_key = spread_gain(table, 3, devices, RUN)
    gains[...] = jnp.zeros_like(gains)
    gains[0:1] = gain_first
    gains[1:2] = gain_post
    gains[2:3, 0:RUN] = gain_query
    gains[3:4, 0:RUN] = gain_key
    forward(in_view(2), in_far[2], in_near)
    out_far = [wire.send(s_o, wo.at[f], p.z_dev(step)) for step in range(1, planes)]
    back_x = [wire.send(cotangent.at[0], back_full.at[0, mine], p.x_dev)]
    forward(in_view(3), in_far[3], in_near)
    tok_fwd = []
    for micro in range(2):
        tok_x[micro].wait_recv()
        block = tok_full.at[pl.ds(micro * runs + p.x_dev[0] * 2, 2)]
        tok_fwd.append(wire.send(block, block, p.core_dev))
    for at in range(4):
        arrived(second, at)
        wide_near += side(wide_view(at)(f))
    for copy in staged:
        copy.wait()
    back_core, back_kept = [], []
    for micro in range(2):
        to = back_full.at[micro, mine]
        if micro == 1:
            back_x.append(wire.send(cotangent.at[micro], to, p.x_dev))
        back_kept.append(wire.own(back_own.at[micro], to))
        back_core.append(wire.send(cotangent.at[micro], to, p.core_dev))
    wide_far[0] = push(wide_view(0)(f))
    down_far = [wire.send(s_d, wd.at[f], p.z_dev(step)) for step in range(1, planes)]
    settle(in_near)
    saved = [wire.own(win, win_out)]
    for copy in tok_here:
        copy.wait()
    for copy in tok_core + tok_fwd:
        copy.wait_recv()

    def project(step, carry):
        here = pl.ds(pl.multiple_of(step * BLOCK, BLOCK), BLOCK)
        raw = two_runs(tok_full, order[step * 2], order[step * 2 + 1]).astype(F32)
        root = lax.rsqrt(row_mean(raw * raw) + EPSILON)
        low = (raw * root * gains[0:1]).astype(BF16)
        normed[here] = low
        turn = pl.ds(pl.multiple_of(lax.rem(step, length // BLOCK) * BLOCK, BLOCK), BLOCK)
        cos, sin = cosine[turn], sine[turn]
        product = dot(low, flat(win))
        found, start = [], 0
        for low_ref, unit_ref, row in ((query, q_unit, 2), (key, k_unit, 3)):
            gain = gains[row : row + 1, 0:RUN]
            for head in range(low_ref.shape[1] // HEAD_DIM):
                at = slice(head * HEAD_DIM, (head + 1) * HEAD_DIM)
                one = product[:, start : start + HEAD_DIM]
                inverse = lax.rsqrt(row_mean(one * one) + EPSILON)
                unit = one * inverse
                unit_ref[here, at] = unit.astype(BF16)
                scaled = unit * gain
                low_ref[here, at] = (scaled * cos + pltpu.roll(scaled, HEAD_DIM // 2, 1) * sin).astype(BF16)
                found.append(inverse)
                start += HEAD_DIM
        roots[here, :] = jnp.zeros((BLOCK, roots.shape[1]), F32)
        for at, inverse in enumerate(found):
            roots[here, at : at + 1] = inverse
        value[here] = product[:, start:].astype(BF16)
        return carry

    def attend(step, carry):
        micro, head = step // 2, lax.rem(step, 2)
        keys_at = pl.ds(pl.multiple_of(head * HEAD_DIM, HEAD_DIM), HEAD_DIM)
        lanes = [pl.ds(pl.multiple_of(head * 2 * HEAD_DIM + g * HEAD_DIM, HEAD_DIM), HEAD_DIM) for g in range(2)]
        for block in range(length // BLOCK):
            here = pl.ds(pl.multiple_of(micro * length + block * BLOCK, BLOCK), BLOCK)
            seen = (block + 1) * BLOCK
            past = pl.ds(pl.multiple_of(micro * length, BLOCK), seen)
            asked = jnp.concatenate([query[here, lane] for lane in lanes], axis=0)
            scores = dot(asked, key[past, keys_at], NARROW)
            line = lax.broadcasted_iota(jnp.int32, (2 * BLOCK, seen), 0)
            line = jnp.where(line >= BLOCK, line - BLOCK, line) + block * BLOCK
            column = lax.broadcasted_iota(jnp.int32, (2 * BLOCK, seen), 1)
            scores = jnp.where(column <= line, scores, NEGATIVE)
            top = jnp.max(scores, axis=-1, keepdims=True)
            weight = jnp.exp2((scores - top) * (SCALE * LOG2E))
            total = jnp.sum(weight, axis=-1, keepdims=True)
            out = dot(weight.astype(BF16), value[past, keys_at]) * (1.0 / total)
            level = top * (SCALE * LOG2E) + jnp.log2(total)
            pair = pl.ds(micro * runs + block * 2, 2)
            held = roots[here, :]
            spot = lax.broadcasted_iota(jnp.int32, held.shape, 1)
            for g, lane in enumerate(lanes):
                half = slice(g * BLOCK, (g + 1) * BLOCK)
                mixed[pair, :, lane] = out[half].astype(BF16).reshape(2, RUN, HEAD_DIM)
                held = jnp.where(spot == LEVEL + head * 2 + g, level[half], held)
            roots[here, :] = held
        return carry

    def mix_out(step, carry):
        micro, block = reducer.block(step)
        at = micro * runs + block * 2
        low = two_runs(mixed, rank[at], rank[at + 1])
        part[...] = dot(low, flat(wo))
        reducer.take(step)
        return carry

    posts = []

    def finish(micro):
        own = joined(tok_full[pl.ds(micro * runs + s * 2, 2)]).astype(F32)
        total = own + reducer.total(micro)
        resid[micro] = total
        root = lax.rsqrt(row_mean(total * total) + EPSILON)
        post_own[micro] = (total * root * gains[1:2]).astype(BF16)
        to = post_full.at[micro, mine]
        posts.append((wire.send(post_own.at[micro], to, p.x_dev), wire.send(post_own.at[micro], to, p.core_dev),
                      wire.own(post_own.at[micro], to)))
        saved.append(wire.own(resid.at[micro], resid_out.at[micro]))

    steps = length // BLOCK
    lax.fori_loop(0, steps, project, 0)
    forward(lambda owner: wo.at[owner], out_far, out_near)
    wide_far[1] = push(wide_view(1)(f))
    lax.fori_loop(0, 2, attend, 0)
    lax.fori_loop(steps, 2 * steps, project, 0)
    saved += [wire.own(here, there) for here, there in (
        (normed, normed_out), (query, query_out), (key, key_out), (value, value_out),
        (q_unit, q_unit_out), (k_unit, k_unit_out))]
    out_kept.wait()
    settle(out_near)
    lax.fori_loop(0, 4, mix_out, 0)
    forward(wide_view(0), wide_far[0], wide_near)
    wide_far[2] = push(wide_view(2)(f))
    lax.fori_loop(2, 4, attend, 0)
    lax.fori_loop(4, 8, mix_out, 0)
    saved += [wire.own(mixed, mixed_out), wire.own(roots, roots_out), wire.own(wo, wo_out)]
    wide_far[3] = push(wide_view(3)(f))
    finish(0)
    forward(lambda owner: wd.at[owner], down_far, down_near)
    forward(wide_view(1), wide_far[1], wide_near)
    for micro in range(2):
        back_x[micro].wait_recv()
        block = back_full.at[micro, theirs]
        back_core.append(wire.send(block, block, p.core_dev))
    finish(1)
    forward(wide_view(2), wide_far[2], wide_near)
    forward(wide_view(3), wide_far[3], wide_near)
    last = []
    for micro in range(2):
        posts[micro][0].wait_recv()
        block = post_full.at[micro, theirs]
        last.append(wire.send(block, block, p.core_dev))
    for micro in range(2):
        last[micro].wait_recv()
        posts[micro][1].wait_recv()
        posts[micro][2].wait()
    for copy in back_core:
        copy.wait_recv()
    for copy in back_kept + saved + [down_kept]:
        copy.wait()
    settle(wide_near)
    settle(down_near)
    reducer.close()
    wire.close()


def front(planes, order, rank, tokens, cotangent, gain_tile, cosine, sine, shards):
    nf = 2 * planes
    rows = tokens.shape[1]
    length = 4 * rows
    total = 2 * length
    tokens = tokens.reshape(2, 2, RUN, tokens.shape[2])
    deep = shards[0].shape[0]

    def low(width):
        return jax.ShapeDtypeStruct((total, width), BF16)

    shapes = [
        jax.ShapeDtypeStruct((4, nf, deep, 1024), BF16), jax.ShapeDtypeStruct((nf, *shards[3].shape), BF16),
        jax.ShapeDtypeStruct((4, nf, deep, 2 * (shards[4].shape[1] // 4)), BF16),
        jax.ShapeDtypeStruct((nf, *shards[6].shape), BF16),
        low(1024), low(512), low(256), low(256), low(512), low(256),
        jax.ShapeDtypeStruct((total, 16), F32), jax.ShapeDtypeStruct((total // RUN, RUN, 512), BF16),
        jax.ShapeDtypeStruct((2, rows, 1024), F32),
        jax.ShapeDtypeStruct((2, length, 1024), BF16), jax.ShapeDtypeStruct((2, length, 1024), BF16),
        jax.ShapeDtypeStruct((8, 1024), F32)]
    held = [shapes[at] for at in (0, 1, *range(4, 13))]
    vm = pl.BlockSpec(memory_space=VMEM)
    hb = pl.BlockSpec(memory_space=ANY)
    sm = pl.BlockSpec(memory_space=pltpu.SMEM)
    return pl.pallas_call(
        functools.partial(front_kernel, planes),
        out_shape=shapes,
        in_specs=[sm, sm, hb, hb, vm, hb, hb, hb, hb, hb, hb, vm, vm, vm],
        out_specs=[hb] * (len(shapes) - 1) + [vm],
        scratch_shapes=[
            *[VMEM(item.shape, item.dtype) for item in held],
            VMEM((total // RUN, RUN, 1024), BF16), VMEM((4, nf, 8, RUN), F32), VMEM((2, rows, 1024), BF16),
            VMEM((2, rows, 1024), BF16), VMEM(cosine.shape, F32), VMEM(sine.shape, F32),
            VMEM((BLOCK, 1024), F32), *reducer_scratch(1024), *wire_scratch(130, 40),
        ],
        compiler_params=pltpu.CompilerParams(
            collective_id=0, has_side_effects=True, vmem_limit_bytes=VMEM_BYTES),
        name="front",
    )(order, rank, tokens, cotangent, gain_tile, cosine, sine, *shards)


GROUPS = (2, 3, 1, 0)


class RowHoming:
    def __init__(self, place, wire, grad, came, sums, far, home):
        self.p, self.wire, self.grad = place, wire, grad
        self.came, self.sums, self.far, self.home = came, sums, far, home

    def half(self, ref, at):
        return ref.at[pl.ds(at * (self.p.planes // 2), self.p.planes // 2)]

    def start(self):
        p = self.p
        self.kept = self.wire.own(self.grad.at[:, p.y], self.sums)
        self.sent = [
            self.wire.send(self.half(self.grad, at).at[:, p.other_y], self.half(self.came, at), p.y_dev)
            for at in range(2)
        ]
        self.out = [
            self.wire.send(self.sums.at[p.z_at(step)], self.far.at[step - 1], p.z_dev(step), start=False)
            for step in range(1, p.planes)
        ]

    def push(self, at):
        if at == 0:
            self.kept.wait()
        self.sent[at].wait_recv()
        share = self.p.planes // 2

        def add(z, carry):
            self.sums[z] = (self.sums[z].astype(F32) + self.came[z].astype(F32)).astype(BF16)
            return carry

        lax.fori_loop(at * share, (at + 1) * share, add, 0)
        for step, copy in enumerate(self.out, 1):
            @pl.when(self.p.z_at(step) // share == at)
            def _(copy=copy):
                copy.start()

    def gather(self):
        for copy in self.out:
            copy.wait_recv()
        total = self.sums[self.p.z].astype(F32)
        for step in range(1, self.p.planes):
            total = total + self.far[step - 1].astype(F32)
        self.home[...] = total


class ColumnHoming:
    def __init__(self, place, wire, came, sums, far, leave=None, arrive=None, homes=()):
        self.p, self.wire, self.came, self.sums, self.far = place, wire, came, sums, far
        self.leave, self.arrive, self.homes = leave, arrive, homes
        self.kept, self.sent, self.out, self.back = {}, {}, {}, {}

    def start(self, at, grad):
        self.kept[at] = self.wire.own(grad.at[:, self.p.y], self.sums.at[at])
        self.sent[at] = self.wire.send(grad.at[:, self.p.other_y], self.came.at[at], self.p.y_dev)

    def add(self, at):
        self.kept[at].wait()
        self.sent[at].wait_recv()

        def add(z, carry):
            self.sums[at, z] = (self.sums[at, z].astype(F32) + self.came[at, z].astype(F32)).astype(BF16)
            return carry

        lax.fori_loop(0, self.p.planes, add, 0)

    def push(self, at):
        self.out[at] = [
            self.wire.send(self.sums.at[at, self.p.z_at(step)], self.far.at[at, step - 1], self.p.z_dev(step))
            for step in range(1, self.p.planes)
        ]

    def put(self, owner, value):
        first = 0
        for home, start, width in self.homes:
            at = pl.multiple_of(owner * (home.shape[1] // 4) + start, RUN)
            home[:, pl.ds(at, width)] = value[:, first : first + width]
            first += width

    def gather(self, at):
        for copy in self.out[at]:
            copy.wait_recv()
        total = self.sums[at, self.p.z].astype(F32)
        for step in range(1, self.p.planes):
            total = total + self.far[at, step - 1].astype(F32)
        if GROUPS[at] == 0:
            self.put(self.p.s, total)
            return
        self.leave[at] = total.astype(BF16)
        self.back[at] = self.wire.send(self.leave.at[at], self.arrive.at[at], self.p.seq_dev[GROUPS[at]])

    def finish(self):
        for at, copy in self.back.items():
            copy.wait_recv()
            self.put(self.p.seq_dev[GROUPS[at]][0], self.arrive[at].astype(F32))


def group_rows(place, at):
    owner = place.seq_dev[GROUPS[at]][0]
    return pl.ds(pl.multiple_of(owner * BLOCK, BLOCK), BLOCK)


def column_scratch(planes, deep, width, groups=4):
    return [
        VMEM((groups, planes, deep, width), BF16), VMEM((groups, planes, deep, width), BF16),
        VMEM((4, planes - 1, deep, width), BF16), VMEM((3, deep, width), BF16), VMEM((3, deep, width), BF16),
    ]


def row_scratch(planes, deep, width):
    return [VMEM((planes, deep, width), BF16), VMEM((planes, deep, width), BF16),
            VMEM((planes - 1, deep, width), BF16)]


def middle_kernel(
    planes,
    post_in, back_in, wgu_in, wd_in, resid_in, gains,
    ready, grad_rest, home_d, y_out, y_keep, d_resid, attn_full, sums,
    post, back, wgu, wd, resid, load_sems,
    grad_first, g_came, grad_d, d_came, d_sums, d_far, hidden, d_gu, part, attn_own,
    y_core_out, y_core_in,
    core_out, core_in, x_out, x_in, keep, core_s, core_r, x_s, x_r,
    y_core_s, y_core_r, out_sems, in_sems, own_sems,
):
    p = Place(planes)
    s = p.s
    wire = Wire(out_sems, in_sems, own_sems)
    into_post = Reducer(p, part, core_out, core_in, x_out, x_in, keep, (core_s, core_r, x_s, x_r))
    into_out = Reducer(p, part, y_core_out, y_core_in, y_out, None, y_keep, (y_core_s, y_core_r, None, None))
    rows = resid.shape[1]
    length = 4 * rows
    wide = hidden.shape[1]
    mine = pl.ds(s * rows, rows)
    theirs = pl.ds(p.x_dev[0] * rows, rows)
    loads = [wire.own(wgu_in, wgu), wire.own(wd_in, wd), wire.own(resid_in, resid)]

    def chunk(step):
        micro, block = into_post.block(step)
        here = pl.ds(pl.multiple_of(micro * length + block * BLOCK, BLOCK), BLOCK)
        return [pltpu.make_async_copy(far.at[here], near.at[here], load_sems.at[at, step])
                for at, (far, near) in enumerate(((post_in, post), (back_in, back)))]

    for step in range(8):
        for copy in chunk(step):
            copy.start()
    p.meet()
    for copy in loads:
        copy.wait()

    def feed(step, carry):
        micro, block = into_post.block(step)
        here = pl.ds(pl.multiple_of(micro * length + block * BLOCK, BLOCK), BLOCK)
        for copy in chunk(step):
            copy.wait()
        both = dot(post[here, :], wgu[...])
        d_hidden = dot(back[here, :], wd[...], NARROW)
        gate, upper = both[:, :wide], both[:, wide:]
        sigma = 1.0 / (1.0 + jnp.exp(-gate))
        lit = gate * sigma
        hidden[here] = (lit * upper).astype(BF16)
        d_gu[here, :wide] = (d_hidden * upper * (sigma + lit * (1.0 - sigma))).astype(BF16)
        d_gu[here, wide:] = (d_hidden * lit).astype(BF16)
        part[...] = dot(d_gu[here, :], wgu[...], NARROW)
        into_post.take(step)
        part[...] = dot(hidden[here, :], wd[...])
        into_out.take(step, send_x=False)
        return carry

    down = RowHoming(p, wire, grad_d, d_came, d_sums, d_far, home_d)
    columns = ColumnHoming(p, wire, g_came, ready, None)

    def down_tile(at, carry):
        tall = wide // 2
        cut = pl.ds(pl.multiple_of(at * tall, RUN), tall)
        found = dot(hidden[:, cut], back[...], TALL).astype(BF16)
        grad_d[pl.ds(at * (planes // 2), planes // 2)] = found.reshape(planes // 2, *grad_d.shape[1:])
        return carry

    def wide_tile(at):
        found = dot(post[:, group_rows(p, at)], d_gu[...], TALL).astype(BF16)
        return found.reshape(grad_first.shape)

    gain = gains[1:2]
    sends = []
    sums[...] = jnp.zeros_like(sums)

    def settle(micro):
        grad = into_post.total(micro)
        held = resid[micro]
        root = lax.rsqrt(row_mean(held * held) + EPSILON)
        unit = held * root
        sums[0:1] += jnp.sum(grad * unit, axis=0, keepdims=True)
        scaled = grad * gain
        own = back[pl.ds(pl.multiple_of(micro * length + s * rows, rows), rows), :].astype(F32)
        whole = own + root * (scaled - unit * row_mean(scaled * unit))
        d_resid[micro] = whole
        attn_own[micro] = whole.astype(BF16)
        to = attn_full.at[micro, mine]
        sends.append((wire.send(attn_own.at[micro], to, p.x_dev), wire.send(attn_own.at[micro], to, p.core_dev),
                      wire.own(attn_own.at[micro], to)))
        y_keep[micro] = y_keep[micro] + held

    lax.fori_loop(0, 7, feed, 0)
    settle(0)
    lax.fori_loop(7, 8, feed, 0)
    lax.fori_loop(0, 2, down_tile, 0)
    down.start()
    grad_first[...] = wide_tile(0)
    columns.start(0, grad_first)
    grad_rest[0] = wide_tile(1)
    down.push(0)
    settle(1)
    grad_rest[1] = wide_tile(2)
    grad_rest[2] = wide_tile(3)
    down.push(1)
    forwards = []
    for micro in range(2):
        sends[micro][0].wait_recv()
        block = attn_full.at[micro, theirs]
        forwards.append(wire.send(block, block, p.core_dev))
    columns.add(0)
    for micro in range(2):
        forwards[micro].wait_recv()
        sends[micro][1].wait_recv()
        sends[micro][2].wait()
    down.gather()
    into_post.close()
    into_out.close(send_x=False)
    wire.close()


def middle(planes, post, back, wgu, wd, resid, gains):
    rows = resid.shape[1]
    total = 8 * rows
    wide = wd.shape[0]
    deep = 1024 // (8 * planes)
    once = (planes, 2, deep, 2 * wide)
    slim = (planes, 2, wide // (2 * planes), 1024)
    shapes = [
        jax.ShapeDtypeStruct((1, planes, deep, 2 * wide), BF16), jax.ShapeDtypeStruct((3, *once), BF16),
        jax.ShapeDtypeStruct(slim[2:], F32),
        jax.ShapeDtypeStruct((2, rows, 1024), BF16), jax.ShapeDtypeStruct((2, rows, 1024), F32),
        jax.ShapeDtypeStruct((2, rows, 1024), F32), jax.ShapeDtypeStruct((2, 4 * rows, 1024), BF16),
        jax.ShapeDtypeStruct((8, 1024), F32),
    ]
    vm = pl.BlockSpec(memory_space=VMEM)
    hb = pl.BlockSpec(memory_space=ANY)
    return pl.pallas_call(
        functools.partial(middle_kernel, planes),
        out_shape=shapes,
        in_specs=[hb] * 5 + [vm],
        out_specs=[vm] * 6 + [hb, vm],
        scratch_shapes=[
            *[VMEM(item.shape, item.dtype) for item in (post, back, wgu, wd, resid)],
            pltpu.SemaphoreType.DMA((2, 8)),
            VMEM(once, BF16), VMEM((1, planes, deep, 2 * wide), BF16), VMEM(slim, BF16),
            *row_scratch(planes, *slim[2:]),
            VMEM((total, wide), BF16), VMEM((total, 2 * wide), BF16),
            VMEM((BLOCK, 1024), F32), VMEM((2, rows, 1024), BF16),
            VMEM((4, BLOCK, 1024), BF16), VMEM((4, BLOCK, 1024), BF16),
            *reducer_scratch(1024),
            pltpu.SemaphoreType.DMA((4,)), pltpu.SemaphoreType.DMA((4,)),
            *wire_scratch(16, 10),
        ],
        compiler_params=pltpu.CompilerParams(
            collective_id=1, has_side_effects=True, vmem_limit_bytes=VMEM_BYTES),
        name="middle",
    )(post, back, wgu, wd, resid, gains)


def rear_kernel(
    planes,
    order, rank, attn_in, query_in, key_in, value_in, q_unit_in, k_unit_in, roots_in, mixed_in, wo_in,
    normed_in, win_in, tokens_in, d_resid_in, cosine, sine, gains, y_out, y_keep_in, sums_in, ready, grad_rest,
    token_grad, sums, block_out, home_g, home_u, home_o, home_q, home_k, home_v,
    attn, query, key, value, q_unit, k_unit, roots, mixed, wo, win, tokens,
    rows_held, d_mixed, keys_grad, values_grad, y_in, grad_o, grad, part, sums_out, sums_came,
    g_came, g_sums, g_far, g_leave, g_arrive, o_came, o_sums, o_far,
    a_came, a_sums, a_far, a_leave, a_arrive, b_came, b_sums, b_far, b_leave, b_arrive,
    core_out, core_in, x_out, x_in, keep, core_s, core_r, x_s, x_r,
    out_sems, in_sems, own_sems,
):
    p = Place(planes)
    wire = Wire(out_sems, in_sems, own_sems)
    reducer = Reducer(p, part, core_out, core_in, x_out, x_in, keep, (core_s, core_r, x_s, x_r))
    rows = y_in.shape[1]
    length = 4 * rows
    loads = [wire.own(far, near) for far, near in (
        (attn_in, attn), (wo_in, wo), (mixed_in, mixed), (query_in, query), (key_in, key), (value_in, value),
        (q_unit_in, q_unit), (k_unit_in, k_unit), (roots_in, roots), (y_keep_in, keep),
        (tokens_in, tokens), (d_resid_in, token_grad))]
    for far, near, span in ((0, 0, 256), (256, 512, 256), (512, 256, 128), (640, 768, 128), (768, 384, 128), (896, 896, 128)):
        loads.append(wire.own(win_in.at[:, far : far + span], win.at[:, near : near + span]))
    p.meet()
    wide = ColumnHoming(p, wire, g_came, g_sums, g_far, g_leave, g_arrive,
                        [(home, 0, home.shape[1] // 4) for home in (home_g, home_u)])
    outer = RowHoming(p, wire, grad_o, o_came, o_sums, o_far, home_o)
    inner = [
        ColumnHoming(p, wire, *refs, [(home_q, 256 * at, 256), (home_k, 128 * at, 128), (home_v, 128 * at, 128)])
        for at, refs in enumerate((
            (a_came, a_sums, a_far, a_leave, a_arrive), (b_came, b_sums, b_far, b_leave, b_arrive)))
    ]
    wide.start(1, grad_rest.at[0])
    g_sums[0] = ready[0]
    wide.push(0)
    y_sent = [wire.send(y_out.at[micro], y_in.at[micro], p.x_dev) for micro in range(2)]
    loads[0].wait()
    loads[1].wait()

    def draw(step, carry):
        here = pl.ds(pl.multiple_of(step * BLOCK, BLOCK), BLOCK)
        low = two_runs(attn, order[step * 2], order[step * 2 + 1])
        rows_held[pl.ds(step * 2, 2)] = low.reshape(2, RUN, low.shape[1])
        d_mixed[here] = dot(low, wo[...], NARROW).astype(BF16)
        return carry

    lax.fori_loop(0, 2 * length // BLOCK, draw, 0)

    def out_tile(at, carry):
        cut = pl.ds(pl.multiple_of(at * BLOCK, BLOCK), BLOCK)
        found = dot(mixed[:, cut], flat(rows_held), TALL).astype(BF16)
        grad_o[pl.ds(at * (planes // 2), planes // 2)] = found.reshape(planes // 2, *grad_o.shape[1:])
        return carry

    loads[2].wait()
    lax.fori_loop(0, 2, out_tile, 0)
    wide.start(2, grad_rest.at[1])
    normed_load = wire.own(normed_in, attn)
    wide.add(1)
    wide.push(1)
    sums[...] = sums_in[...]

    def lane_of(ref, here, lane):
        held = ref[here, :]
        lanes = lax.broadcasted_iota(jnp.int32, held.shape, 1)
        return jnp.sum(jnp.where(lanes == lane, held, 0.0), axis=1, keepdims=True)

    def norm_home(grad, cos, sin, unit, root, gain):
        turned = grad * cos - pltpu.roll(grad, HEAD_DIM // 2, 1) * sin
        scaled = turned * gain
        back = root * (scaled - unit * row_mean(scaled * unit))
        return back, jnp.sum(turned * unit, axis=0, keepdims=True)

    def attend_back(step, carry):
        micro, head = lax.rem(step, 2), step // 2
        keys_at = pl.ds(pl.multiple_of(head * HEAD_DIM, HEAD_DIM), HEAD_DIM)
        lanes = [pl.ds(pl.multiple_of(head * 2 * HEAD_DIM + g * HEAD_DIM, HEAD_DIM), HEAD_DIM) for g in range(2)]
        q_gain, k_gain = gains[2:3, 0:RUN], gains[3:4, 0:RUN]
        keys_grad[...] = jnp.zeros_like(keys_grad)
        values_grad[...] = jnp.zeros_like(values_grad)
        for block in range(length // BLOCK):
            here = pl.ds(pl.multiple_of(micro * length + block * BLOCK, BLOCK), BLOCK)
            seen = (block + 1) * BLOCK
            past = pl.ds(pl.multiple_of(micro * length, BLOCK), seen)
            asked = jnp.concatenate([query[here, lane] for lane in lanes], axis=0)
            pulled = jnp.concatenate([d_mixed[here, lane] for lane in lanes], axis=0)
            given = jnp.concatenate([mixed[here, lane] for lane in lanes], axis=0)
            level = jnp.concatenate(
                [lane_of(roots, here, LEVEL + head * 2 + g) for g in range(2)], axis=0)
            delta = jnp.sum(pulled.astype(F32) * given.astype(F32), axis=1, keepdims=True)
            scores = dot(asked, key[past, keys_at], NARROW)
            line = lax.broadcasted_iota(jnp.int32, (2 * BLOCK, seen), 0)
            line = jnp.where(line >= BLOCK, line - BLOCK, line) + block * BLOCK
            column = lax.broadcasted_iota(jnp.int32, (2 * BLOCK, seen), 1)
            weight = jnp.exp2(scores * (SCALE * LOG2E) - level)
            weight = jnp.where(column <= line, weight, 0.0)
            d_soft = dot(pulled, value[past, keys_at], NARROW)
            d_scores = (weight * (d_soft - delta)).astype(BF16)
            values_grad[0:seen] += dot(weight.astype(BF16), pulled, TALL)
            keys_grad[0:seen] += dot(d_scores, asked, TALL)
            moved = dot(d_scores, key[past, keys_at]) * SCALE
            spin = slice(block * BLOCK, (block + 1) * BLOCK)
            for g, lane in enumerate(lanes):
                root = lane_of(roots, here, head * 2 + g)
                unit = q_unit[here, lane].astype(F32)
                back, gained = norm_home(
                    moved[g * BLOCK : (g + 1) * BLOCK], cosine[spin], sine[spin], unit, root, q_gain)
                pair = pl.ds(micro * (length // RUN) + block * 2, 2)
                to = pl.ds(pl.multiple_of(head * 512 + g * HEAD_DIM, HEAD_DIM), HEAD_DIM)
                rows_held[pair, :, to] = back.astype(BF16).reshape(2, RUN, HEAD_DIM)
                sums[1:2, 0:RUN] += gained
        everything = pl.ds(pl.multiple_of(micro * length, BLOCK), length)
        root = lane_of(roots, everything, head + 4)
        unit = k_unit[everything, keys_at].astype(F32)
        back, gained = norm_home(keys_grad[...] * SCALE, cosine[...], sine[...], unit, root, k_gain)
        at, whole = head * 512 + 256, pl.ds(micro * (length // RUN), length // RUN)
        tall = (length // RUN, RUN, HEAD_DIM)
        rows_held[whole, :, pl.ds(pl.multiple_of(at, HEAD_DIM), HEAD_DIM)] = back.astype(BF16).reshape(tall)
        sums[2:3, 0:RUN] += gained
        low = values_grad[...].astype(BF16).reshape(tall)
        rows_held[whole, :, pl.ds(pl.multiple_of(at + HEAD_DIM, HEAD_DIM), HEAD_DIM)] = low
        return carry

    for copy in loads[3:9]:
        copy.wait()
    def pull(step, carry):
        micro, block = reducer.block(step)
        at = micro * (length // RUN) + block * 2
        runs = (rank[at], rank[at + 1])
        found = dot(two_runs(rows_held, *runs), win[...], NARROW)
        part[...] = found
        sums[3:4] += jnp.sum(found * two_runs(attn, *runs).astype(F32), axis=0, keepdims=True)
        reducer.take(step)
        return carry

    def tile(half, at):
        pulled = joined(rows_held[:, :, half * 512 : half * 512 + 512])
        found = dot(joined(attn[:, :, group_rows(p, at)]), pulled, TALL).astype(BF16)
        grad[half, at] = found.reshape(grad.shape[2:])
        inner[half].start(at, grad.at[half, at])

    lax.fori_loop(0, 1, attend_back, 0)
    wide.start(3, grad_rest.at[2])
    wide.add(2)
    wide.push(2)
    lax.fori_loop(1, 2, attend_back, 0)
    normed_load.wait()
    for at in range(4):
        tile(0, at)
    wide.add(3)
    wide.push(3)
    wide.gather(0)
    for copy in loads[9:]:
        copy.wait()
    for micro in range(2):
        y_sent[micro].wait_recv()
        block_out[micro] = (keep[micro] + y_in[micro].astype(F32)).astype(BF16)
    lax.fori_loop(2, 3, attend_back, 0)
    outer.start()
    lax.fori_loop(0, 4, pull, 0)
    for at in range(4):
        inner[0].add(at)
        inner[0].push(at)
    wide.gather(1)
    lax.fori_loop(3, 4, attend_back, 0)
    tile(1, 0)
    tile(1, 1)
    outer.push(0)
    outer.push(1)
    tile(1, 2)
    tile(1, 3)
    lax.fori_loop(4, 8, pull, 0)
    sums[3:4] = sums[3:4] / gains[0:1]

    def exchange(stage, devices, base):
        sums_out[stage] = sums[...]
        sent = [wire.send(sums_out.at[stage], sums_came.at[base + at], dev) for at, dev in enumerate(devices)]
        return base, sent

    def absorb(state):
        base, sent = state
        total = sums[...]
        for at, copy in enumerate(sent):
            copy.wait_recv()
            total = total + sums_came[base + at]
        sums[...] = total

    state = exchange(0, p.seq_dev[1:], 0)
    wide.gather(2)
    wide.gather(3)
    inner[1].add(0)
    inner[1].push(0)
    absorb(state)
    state = exchange(1, [p.z_dev(step) for step in range(1, planes)], 3)
    inner[1].add(1)
    inner[1].push(1)
    for at in range(4):
        inner[0].gather(at)
    inner[1].add(2)
    inner[1].push(2)
    absorb(state)
    state = exchange(2, [p.y_dev], 2 + planes)
    inner[1].add(3)
    inner[1].push(3)
    outer.gather()
    for micro in range(2):
        grad_rows = reducer.total(micro)
        raw = tokens[micro].astype(F32)
        root = lax.rsqrt(row_mean(raw * raw) + EPSILON)
        unit = raw * root
        scaled = grad_rows * gains[0:1]
        token_grad[micro] = token_grad[micro] + root * (scaled - unit * row_mean(scaled * unit))
    wide.finish()
    inner[0].finish()
    absorb(state)
    for at in range(4):
        inner[1].gather(at)
    inner[1].finish()
    reducer.close()
    wire.close()


def rear(planes, order, rank, attn, query, key, value, q_unit, k_unit, roots, mixed, wo, normed, win, tokens, d_resid,
         cosine, sine, gains, y_out, y_keep, sums, ready, grad_rest):
    rows = y_keep.shape[1]
    length = 4 * rows
    total = 2 * length
    deep, wide = grad_rest.shape[3:]
    slim = (planes, 2, 512 // (2 * planes), 1024)
    shapes = [
        jax.ShapeDtypeStruct((2, rows, 1024), F32), jax.ShapeDtypeStruct((8, 1024), F32),
        jax.ShapeDtypeStruct((2, rows, 1024), BF16),
        jax.ShapeDtypeStruct((deep, 2 * wide), F32), jax.ShapeDtypeStruct((deep, 2 * wide), F32),
        jax.ShapeDtypeStruct(slim[2:], F32), jax.ShapeDtypeStruct((deep, 2048), F32),
        jax.ShapeDtypeStruct((deep, 1024), F32), jax.ShapeDtypeStruct((deep, 1024), F32),
    ]
    held = (attn, query, key, value, q_unit, k_unit, roots, mixed, wo, win, tokens)
    vm = pl.BlockSpec(memory_space=VMEM)
    hb = pl.BlockSpec(memory_space=ANY)
    sm = pl.BlockSpec(memory_space=pltpu.SMEM)
    return pl.pallas_call(
        functools.partial(rear_kernel, planes),
        out_shape=shapes,
        in_specs=[sm, sm] + [hb] * 13 + [vm] * 3 + [hb, hb, vm, vm, hb],
        out_specs=[vm] * len(shapes),
        scratch_shapes=[
            *[VMEM(item.shape, item.dtype) for item in held],
            VMEM((total // RUN, RUN, 1024), BF16), VMEM((total, 512), BF16), VMEM((length, HEAD_DIM), F32),
            VMEM((length, HEAD_DIM), F32), VMEM((2, rows, 1024), BF16), VMEM(slim, BF16),
            VMEM((2, 4, planes, 2, deep, 512), BF16), VMEM((BLOCK, 1024), F32), VMEM((3, 8, 1024), F32),
            VMEM((3 + planes, 8, 1024), F32),
            *column_scratch(planes, deep, wide), *row_scratch(planes, *slim[2:]),
            *column_scratch(planes, deep, 512), *column_scratch(planes, deep, 512),
            *reducer_scratch(1024), *wire_scratch(96, 56),
        ],
        compiler_params=pltpu.CompilerParams(
            collective_id=2, has_side_effects=True, vmem_limit_bytes=VMEM_BYTES),
        name="rear",
    )(order, rank, attn, query, key, value, q_unit, k_unit, roots, mixed, wo, normed, win, tokens, d_resid,
      cosine, sine, gains, y_out, y_keep, sums, ready, grad_rest)


def deliver_kernel(count, planes, sums, *refs):
    given, rest = refs[:count], refs[count:]
    made, small, held, sems = rest[:count], rest[count : count + 4], rest[count + 4 : 2 * count + 4], rest[-1]
    came = [pltpu.make_async_copy(src, mid, sems.at[0, at]) for at, (src, mid) in enumerate(zip(given, held))]
    gone = [pltpu.make_async_copy(mid, dst, sems.at[1, at]) for at, (mid, dst) in enumerate(zip(held, made))]
    for copy in came:
        copy.start()
    me = lax.axis_index("seq") * (2 * planes) + lax.axis_index("fsdp")
    table = sums[...]
    for row, out in zip((3, 0, 1, 2), small):
        width = out.shape[1]
        turned = pltpu.roll(table, table.shape[1] - me * width, 1)
        out[...] = turned[row : row + 1, :width]
    for first, second in zip(came, gone):
        first.wait()
        second.start()
    for copy in gone:
        copy.wait()


def deliver(planes, sums, widths, *items):
    count = len(items)
    vm, hb = pl.BlockSpec(memory_space=VMEM), pl.BlockSpec(memory_space=ANY)
    return pl.pallas_call(
        functools.partial(deliver_kernel, count, planes),
        out_shape=[*[jax.ShapeDtypeStruct(item.shape, item.dtype) for item in items],
                   *[jax.ShapeDtypeStruct((1, width), F32) for width in widths]],
        in_specs=[vm] + [hb] * count,
        out_specs=[hb] * count + [vm] * 4,
        scratch_shapes=[*[VMEM(item.shape, item.dtype) for item in items], pltpu.SemaphoreType.DMA((2, count))],
        compiler_params=pltpu.CompilerParams(vmem_limit_bytes=VMEM_BYTES),
        name="deliver",
    )(sums, *items)


def run_tables(positions):
    runs = positions.shape[1] // RUN
    rank = positions[:, ::RUN] // RUN
    index = jnp.arange(runs, dtype=jnp.int32)
    order = jnp.sum(jnp.where(rank[:, :, None] == index, index[None, :, None], 0), axis=1)
    base = jnp.arange(positions.shape[0], dtype=jnp.int32)[:, None] * runs
    return (order + base).reshape(-1), (rank + base).reshape(-1)


def turn_tables(length):
    half = HEAD_DIM // 2
    frequency = (ROPE_BASE ** (-np.arange(half) * 2.0 / HEAD_DIM)).astype(np.float32)
    angles = (np.arange(length, dtype=np.float32)[:, None] * frequency[None, :]).astype(np.float64)
    cosine, sine = np.cos(angles), np.sin(angles)
    return (jnp.asarray(np.concatenate([cosine, cosine], axis=1).astype(np.float32)),
            jnp.asarray(np.concatenate([-sine, sine], axis=1).astype(np.float32)))


def kernel_body(tokens, positions, g_in, g_post, g_query, g_key, w_query, w_key, w_value,
                w_out, w_gate, w_up, w_down, cotangent):
    planes = lax.axis_size("fsdp") // 2
    length = positions.shape[2]
    order, rank = run_tables(positions[:, 0])
    tile = jnp.stack(
        [jnp.pad(item.astype(F32), (0, RUN - item.shape[0])) for item in (g_in, g_post, g_query, g_key)])
    tile = jnp.pad(tile, ((0, 4), (0, 0)))
    cosine, sine = turn_tables(length)
    near = tokens[:, 0]
    shards = (w_query, w_key, w_value, w_out, w_gate, w_up, w_down)
    (win, wo, wgu, wd, normed, query, key, value, q_unit, k_unit, roots, mixed,
     resid, post, back, gains) = front(
        planes, order, rank, near, cotangent[:, 0], tile, cosine, sine, shards)
    plain = lambda item: item.reshape(-1, item.shape[-1])
    apart = lambda item: item.reshape(-1, RUN, item.shape[-1])
    win, wo, wgu, wd, post, back = [plain(item) for item in (win, wo, wgu, wd, post, back)]
    ready, grad_rest, home_d, y_out, y_keep, d_resid, attn, sums = middle(
        planes, post, back, wgu, wd, resid, gains)
    token_grad, sums, block_out, home_g, home_u, home_o, home_q, home_k, home_v = rear(
        planes, order, rank, apart(attn), query, key, value, q_unit, k_unit, roots, plain(mixed), wo,
        apart(normed), win, near, d_resid, cosine, sine, gains, y_out, y_keep, sums, ready, grad_rest)
    widths = [item.shape[0] for item in (g_in, g_post, g_query, g_key)]
    found = deliver(planes, sums, widths, token_grad, block_out, home_d, home_g, home_u, home_o, home_q, home_k, home_v)
    token_grad, block_out, home_d, home_g, home_u, home_o, home_q, home_k, home_v = found[:9]
    small = [item[0] for item in found[9:]]
    return (block_out[:, None], token_grad[:, None], *small, home_q, home_k, home_v, home_o,
            home_g, home_u, home_d)


def solution(mesh):
    both = ("seq", "fsdp")
    act = P(None, "fsdp", "seq", None)
    vec, mat = P(both), P(both, None)

    def body(*args):
        rows = args[6].shape[0]
        fits = mesh.shape["seq"] == 4 and mesh.shape["fsdp"] % 2 == 0 and rows % 16 == 0
        return (kernel_body if fits else plain_body)(*args)

    return jax.shard_map(
        body,
        mesh=mesh,
        in_specs=(act, P(None, "fsdp", None), *[vec] * 4, *[mat] * 7, act),
        out_specs=(act, act, *[vec] * 4, *[mat] * 7),
        check_vma=False,
    )
```
